32 devices in a mesh: dp: 4 (over y, core), hid: 8 (over z, x).
Axes of the slice: x: 2, y: 2, z: 4, core: 2. Of those that a mesh axis runs over, the one named last changes fastest.
Arguments:
- history: bfloat16 [8, 4096, 2048], P(None, None, ('dp', 'hid')), may hold values from -24 to 24
- mix: float32 [4096, 32], P(('dp', 'hid')), may hold values from -1.5 to 1.5
- segment_ids: int32 [4096], P(('dp', 'hid')), may hold values from 0 to 7, never falling along the last dimension, each value on 1 to 1024 neighbouring positions
- norm_gains: bfloat16 [2048, 4], P('dp'), may hold values from 0.099609375 to 1.8984375
- w_query: bfloat16 [2048, 2048], P('dp'), may hold values from -0.125 to 0.125
- w_key: bfloat16 [2048, 2048], P('dp'), may hold values from -0.125 to 0.125
- w_value: bfloat16 [2048, 2048], P('dp'), may hold values from -0.125 to 0.125
- w_out: bfloat16 [2048, 2048], P('dp'), may hold values from -1 to 1
- w_up: bfloat16 [2048, 8192], P('dp'), may hold values from -0.125 to 0.125
- w_down: bfloat16 [8192, 2048], P('dp'), may hold values from -0.0625 to 0.0625
- w_mixer: bfloat16 [2048, 36], P('dp'), may hold values from -0.125 to 0.125
- mixer_out: float32 [36, 36], replicated, may hold values from -1 to 1
- mix_static: float32 [36], replicated, may hold values from -3 to 3
- out_cotangent: bfloat16 [4096, 2048], P(None, ('dp', 'hid')), may hold values from -6 to 6
- mix_cotangent: float32 [4096, 36], P(('dp', 'hid')), may hold values from -16 to 16
Outputs:
- block_output: bfloat16 [4096, 2048], P(None, ('dp', 'hid'))
- mix_next: float32 [4096, 36], P(('dp', 'hid'))
- history_grad: float32 [8, 4096, 2048], P(None, None, ('dp', 'hid'))
- mix_grad: float32 [4096, 32], P(('dp', 'hid'))
- norm_gains_grad: float32 [2048, 4], P('dp')
- w_query_grad: float32 [2048, 2048], P('dp')
- w_key_grad: float32 [2048, 2048], P('dp')
- w_value_grad: float32 [2048, 2048], P('dp')
- w_out_grad: float32 [2048, 2048], P('dp')
- w_up_grad: float32 [2048, 8192], P('dp')
- w_down_grad: float32 [8192, 2048], P('dp')
- w_mixer_grad: float32 [2048, 36], P('dp')
- mixer_out_grad: float32 [36, 36], replicated
- mix_static_grad: float32 [36], replicated
The draws below stay inside these ranges and needn't reach their ends.
Inputs may be any that keep to these rules, and one draw needn't show every extreme that they name: `segment_ids`: segment ids never fall along the tokens; each id names 1 to 1024 consecutive tokens, and one names exactly 1024.
All inputs are finite; a program needn't handle non-finite values.
Results may differ from the reference program's by a relative error of at most 0.02.
Values may be sent and summed in bfloat16 or wider, within the bound.
A program may use at most 512 MiB of HBM per device.

```python
import math
import jax
import jax.numpy as jnp
import numpy as np
from jax import lax

D = 2048
HEADS = 16
HEAD = 128
FF = 8192
ROT = 32
HIST = 8
STREAMS = 4
MIXH = 36
NMIX = 36
TOKENS = 4096
ROW = 1024
DOCS = 8
DOC_MOST = 1024


def draw_history(key, part):
    noise_key = jax.random.fold_in(key, 11)
    drift_key = jax.random.fold_in(key, 14)
    token_ramp = 1.0 + 2.0 * jnp.arange(TOKENS, dtype=jnp.float32) / TOKENS
    drift_part = jax.random.normal(drift_key, (HIST, 1, D), jnp.float32) * (token_ramp[None, :, None] - 1.0) * 0.5
    noise_part = jax.random.normal(noise_key, (HIST, TOKENS, D), jnp.float32)
    values = noise_part * token_ramp[None, :, None] + drift_part
    return jnp.clip(values, -24.0, 24.0).astype(jnp.bfloat16)


def draw_mix_cotangent(key, part):
    noise_key = jax.random.fold_in(key, 21)
    token_ramp = 1.0 + 2.0 * jnp.arange(TOKENS, dtype=jnp.float32) / TOKENS
    noise_part = jax.random.normal(noise_key, (TOKENS, NMIX), jnp.float32)
    values = noise_part * token_ramp[:, None]
    return jnp.clip(values, -16.0, 16.0)


def shard_levels(own_key, extent, pieces, smallest, high):
    def one(dim, shards_of):
        steps = jax.random.uniform(jax.random.fold_in(jax.random.fold_in(own_key, 6), dim), (shards_of,), jnp.float32, smallest / len(pieces), high / len(pieces))
        return jnp.repeat(jnp.exp(steps), extent[dim] // shards_of).reshape((-1,) + (1,) * (len(extent) - dim - 1))

    loudness = one(*pieces[0])
    for cut in pieces[1:]:
        loudness = loudness * one(*cut)
    return loudness


def split_up(number_of, total, bound, lean):
    loads = [(1 << 20) // math.isqrt(standing ** lean) + 1 for standing in range(2, number_of + 1)]
    rest, counts = total - bound - (number_of - 1), [1] * (number_of - 1)
    while rest > 0:
        free = [i for i in range(number_of - 1) if counts[i] < bound]
        pool, left = sum([loads[i] for i in free]), rest
        for i in free:
            extra = min(bound - counts[i], max(1, left * loads[i] // pool), rest)
            counts[i] = counts[i] + extra
            rest = rest - extra
    return np.array([bound] + counts)


def ragged_sizes(key, amount, total, limit, lean):
    if amount == 2:
        one = jax.random.randint(key, (), max(1, total - limit), min(limit, total - 1) + 1)
        return jnp.stack([one, total - one])
    lengths = jnp.asarray(split_up(amount, total, limit, lean), jnp.int32)
    twos = (amount - 1) // 2
    giver, receiver = lengths[1:1 + 2 * twos:2], lengths[2:2 + 2 * twos:2]
    margin = jnp.minimum(giver - 1, limit - receiver)
    shifted = jax.random.randint(jax.random.fold_in(key, 1), (twos,), 0, 1 << 20) % (margin + 1)
    lengths = lengths.at[1:1 + 2 * twos:2].set(giver - shifted).at[2:2 + 2 * twos:2].set(receiver + shifted)
    return lengths[jax.random.permutation(jax.random.fold_in(key, 2), amount)]


def gaussian(stream_key, dims, deviation, bound, shards=(), kind=jnp.bfloat16):
    factor_of = shard_levels(stream_key, dims, shards, -0.22, 0.18) if shards else 1.0
    values = jax.random.normal(stream_key, dims, jnp.float32) * deviation * factor_of
    return jnp.minimum(jnp.maximum(values, -bound), bound).astype(kind)


def setup_inputs(seed: int = 0) -> dict:
    key_of = jax.random.split(jax.random.key(seed), 16)
    return {
        "history": draw_history(jax.random.fold_in(key_of[15], 71), 0),
        "mix": gaussian(key_of[1], (TOKENS, STREAMS * HIST), 0.25, 1.5, ((0, 32),), jnp.float32),
        "segment_ids": jnp.searchsorted(jnp.cumsum(ragged_sizes(key_of[2], DOCS, TOKENS, DOC_MOST, 1)), jnp.arange(TOKENS), side="right").astype(jnp.int32),
        "norm_gains": jnp.clip(1.0 + 0.18 * jax.random.normal(key_of[3], (D, STREAMS), jnp.float32), 0.099609375, 1.8984375).astype(jnp.bfloat16),
        "w_query": gaussian(key_of[4], (D, D), D ** -0.5, 0.125, ((0, 4),)),
        "w_key": gaussian(key_of[5], (D, D), D ** -0.5, 0.125, ((0, 4),)),
        "w_value": gaussian(key_of[6], (D, D), D ** -0.5, 0.125, ((0, 4),)),
        "w_out": gaussian(key_of[7], (D, D), (D // 64) ** -0.5, 1.0, ((0, 4),)),
        "w_up": gaussian(key_of[8], (D, FF), D ** -0.5, 0.125, ((0, 4),)),
        "w_down": gaussian(key_of[9], (FF, D), FF ** -0.5, 0.0625, ((0, 4),)),
        "w_mixer": gaussian(key_of[10], (D, MIXH), D ** -0.5, 0.125, ((0, 4),)),
        "mixer_out": gaussian(key_of[11], (MIXH, NMIX), MIXH ** -0.5, 1.0, (), jnp.float32),
        "mix_static": gaussian(key_of[12], (NMIX,), 0.5, 3.0, (), jnp.float32),
        "out_cotangent": gaussian(key_of[13], (TOKENS, D), 1.0, 6.0, ((1, 32),)),
        "mix_cotangent": draw_mix_cotangent(jax.random.fold_in(key_of[15], 71), 0),
    }


@jax.custom_vjp
def low(v):
    return lax.optimization_barrier(v.astype(jnp.bfloat16)).astype(jnp.float32)

@jax.custom_vjp
def low_back(v):
    return v

def low_keep(v):
    return (low(v), None)

def low_pass(kept, grad):
    return (grad,)

def back_keep(v):
    return (v, None)

def back_low(kept, grad):
    return (low(grad),)
low.defvjp(low_keep, low_pass)
low_back.defvjp(back_keep, back_low)
highest = lax.Precision.HIGHEST
rope_base = 10000.0

def matmul_high(left, right):
    return jnp.dot(left, right, precision=highest, preferred_element_type=jnp.float32)

def layer_norm(values_in, gain):
    average = lax.optimization_barrier(jnp.mean(values_in, axis=-1, keepdims=True))
    centred = values_in - average
    variance = lax.optimization_barrier(jnp.mean(centred * centred, axis=-1, keepdims=True))
    return centred * lax.rsqrt(variance + 1e-05) * gain

def gelu_exact(values_in):
    return jax.nn.gelu(values_in, approximate=False)

def rotate(values_in, cosine, sine_table):
    half_rot = ROT // 2
    front_half = values_in[..., :half_rot]
    back_half = values_in[..., half_rot:ROT]
    cos_heads = cosine[:, None, :]
    sin_heads = sine_table[:, None, :]
    return jnp.concatenate([front_half * cos_heads - back_half * sin_heads, back_half * cos_heads + front_half * sin_heads, values_in[..., ROT:]], axis=-1)

def tables(segment_ids):
    row_ids = segment_ids.reshape(TOKENS // ROW, ROW)
    positions_in_row = jnp.arange(ROW, dtype=jnp.int32)

    def one_row(row_segments):
        same_doc = row_segments[:, None] == row_segments[None, :]
        doc_start = lax.optimization_barrier(jnp.min(jnp.where(same_doc, positions_in_row[None, :], ROW), axis=1))
        return positions_in_row - doc_start
    position = lax.map(one_row, row_ids).reshape(TOKENS).astype(jnp.float32)
    frequency = rope_base ** (-jnp.arange(ROT // 2, dtype=jnp.float32) * 2.0 / ROT)
    angle = position[:, None] * frequency[None, :]
    return (jnp.cos(angle), jnp.sin(angle))

def attend_row(queries, key_heads, value_heads, row_segments):
    score_scale = 1.0 / math.sqrt(HEAD)
    scores = jnp.einsum('qhd,khd->hqk', queries, key_heads, precision=highest) * score_scale
    scores = low_back(scores)
    positions_in_row = jnp.arange(ROW, dtype=jnp.int32)
    visible = (row_segments[:, None] == row_segments[None, :]) & (positions_in_row[None, :] <= positions_in_row[:, None])
    scores = jnp.where(visible[None], scores, -1e+30)
    weights = low(jax.nn.softmax(scores, axis=-1))
    return jnp.einsum('hqk,khd->qhd', weights, value_heads, precision=highest)

def forward(params, cosine, sine_table, row_ids):
    history_f, mix, gains, wq_f, wk_f, wv_f, wo_f, wup_f, wdown_f, wmix_f, mixer_out, mix_static = params
    mix_table = mix.reshape(TOKENS, STREAMS, HIST)
    streams = [jnp.einsum('tj,jtd->td', mix_table[:, stream, :], history_f, precision=highest) for stream in range(STREAMS)]
    normed = [low(layer_norm(streams[stream], gains[:, stream])) for stream in range(STREAMS)]

    def to_heads(values_in):
        return values_in.reshape(TOKENS, HEADS, HEAD)

    def by_rows(values_in):
        return values_in.reshape(TOKENS // ROW, ROW, HEADS, HEAD)
    queries = low(rotate(to_heads(low_back(matmul_high(normed[0], wq_f))), cosine, sine_table))
    key_heads = low(rotate(to_heads(low_back(matmul_high(normed[1], wk_f))), cosine, sine_table))
    value_heads = low(to_heads(low_back(matmul_high(normed[2], wv_f))))
    attended = lax.map(jax.checkpoint(lambda packed: attend_row(*packed)), (by_rows(queries), by_rows(key_heads), by_rows(value_heads), row_ids))
    attended = low(low_back(attended.reshape(TOKENS, D)))
    branch = low_back(matmul_high(attended, wo_f))
    hidden = low_back(matmul_high(normed[3], wup_f))
    active = low(gelu_exact(hidden))
    feed_out = low_back(matmul_high(active, wdown_f))
    output = streams[3] + branch + feed_out
    scaled = low(output * lax.rsqrt(lax.optimization_barrier(jnp.mean(output * output, axis=-1, keepdims=True)) + 1e-06))
    inner_pre = low_back(matmul_high(scaled, wmix_f))
    raw_mix = matmul_high(gelu_exact(inner_pre), mixer_out)
    average = lax.optimization_barrier(jnp.mean(raw_mix, axis=0))
    variance = lax.optimization_barrier(jnp.mean(raw_mix * raw_mix, axis=0)) - average * average
    mix_next = mix_static + (raw_mix - average) * lax.rsqrt(variance + 1e-05)
    return (output, mix_next)

def reference(history, mix, segment_ids, norm_gains, w_query, w_key, w_value, w_out, w_up, w_down, w_mixer, mixer_out, mix_static, out_cotangent, mix_cotangent):
    cosine, sine_table = tables(segment_ids)
    row_ids = segment_ids.reshape(TOKENS // ROW, ROW)
    params = (history.astype(jnp.float32), mix, norm_gains.astype(jnp.float32), w_query.astype(jnp.float32), w_key.astype(jnp.float32), w_value.astype(jnp.float32), w_out.astype(jnp.float32), w_up.astype(jnp.float32), w_down.astype(jnp.float32), w_mixer.astype(jnp.float32), mixer_out, mix_static)
    results, pullback = jax.vjp(lambda packed: forward(packed, cosine, sine_table, row_ids), params)
    output, mix_next = results
    grads = pullback((out_cotangent.astype(jnp.float32), mix_cotangent))[0]
    return (output.astype(jnp.bfloat16), mix_next, grads[0], grads[1], grads[2], grads[3], grads[4], grads[5], grads[6], grads[7], grads[8], grads[9], grads[10], grads[11])
```

```python
import functools
import math

import jax
import jax.numpy as jnp
from jax import lax
from jax.experimental import pallas as pl
from jax.experimental.pallas import tpu as pltpu
from jax.sharding import PartitionSpec as P

HEADS = 16
HEAD = 128
ROT = 32
HIST = 8
STREAMS = 4
CORES = 2
CHUNK = 1 << 16
SLACK = 5

highest = lax.Precision.HIGHEST
rope_base = 10000.0
low = jnp.bfloat16
full = jnp.float32


def contract(left, right, left_dim, right_dim):
    return lax.dot_general(
        left, right, (((left_dim,), (right_dim,)), ((), ())), preferred_element_type=full
    )


def contract_high(left, right, left_dim, right_dim):
    return lax.dot_general(
        left,
        right,
        (((left_dim,), (right_dim,)), ((), ())),
        precision=highest,
        preferred_element_type=full,
    )


def batched(left, right, left_dim, right_dim):
    return lax.dot_general(
        left, right, (((left_dim,), (right_dim,)), ((0,), (0,))), preferred_element_type=full
    )


def gelu_exact(values_in):
    return jax.nn.gelu(values_in, approximate=False)


def core_swap(values_in):
    size = lax.axis_size("dp")
    return lax.ppermute(values_in, "dp", [(i, i ^ 1) for i in range(size)])


def outer_shift(values_in, step):
    size = lax.axis_size("dp")
    outer = size // CORES
    pairs = [
        (o * CORES + c, ((o + step) % outer) * CORES + c) for o in range(outer) for c in range(CORES)
    ]
    return lax.ppermute(values_in, "dp", pairs)


def hid_swap(values_in, bit):
    size = lax.axis_size("hid")
    return lax.ppermute(values_in, "hid", [(i, i ^ bit) for i in range(size)])


def ordered(first, values_in, other, axis):
    return jnp.stack(
        [jnp.where(first, values_in, other), jnp.where(first, other, values_in)], axis=axis
    )


def take(values_in, index):
    return lax.dynamic_index_in_dim(values_in, index, 0, keepdims=False)


def put(target, values_in, index):
    return lax.dynamic_update_index_in_dim(target, values_in, index, 0)


def split_ways():
    return 2 if HEADS // lax.axis_size("dp") >= 2 else 1


def gather_ways(values_in, axis):
    if split_ways() == 1:
        return jnp.expand_dims(values_in, axis)
    return ordered(lax.axis_index("hid") % 2 == 0, values_in, hid_swap(values_in, 1), axis)


def gather_dp(values_in):
    size = lax.axis_size("dp")
    outer = size // CORES
    me = lax.axis_index("dp")
    mine, core = me // CORES, me % CORES
    if outer == 2:
        held = ordered(mine == 0, values_in, outer_shift(values_in, 1), 0)
    else:
        held = jnp.zeros((outer,) + values_in.shape, values_in.dtype)
        held = put(held, values_in, mine)
        for step in range(1, outer):
            held = put(held, outer_shift(values_in, step), (mine - step) % outer)
    pair = ordered(core == 0, held, core_swap(held), 1)
    return pair.reshape((size,) + values_in.shape)


def sum_features(values_in):
    if split_ways() == 2:
        values_in = values_in + hid_swap(values_in, 1)
    parts = gather_dp(values_in)
    total = parts[0]
    for i in range(1, parts.shape[0]):
        total = total + parts[i]
    return total


def sum_tokens(values_in):
    size = lax.axis_size("hid")
    bit = split_ways()
    while bit < size:
        values_in = values_in + hid_swap(values_in, bit)
        bit *= 2
    return values_in


def gather_all(values_in):
    for axis in ("hid", "dp"):
        size, me = lax.axis_size(axis), lax.axis_index(axis)
        bit = 1
        while bit < size:
            other = lax.ppermute(values_in, axis, [(i, i ^ bit) for i in range(size)])
            both = ordered(me // bit % 2 == 0, values_in, other, 0)
            values_in = both.reshape((2 * values_in.shape[0],) + values_in.shape[1:])
            bit *= 2
    return values_in


def scatter_dp(make):
    size = lax.axis_size("dp")
    outer = size // CORES
    me = lax.axis_index("dp")
    mine, core = me // CORES, me % CORES
    total = None
    for step in list(range(1, outer)) + [0]:
        there = (mine + step) % outer
        away = core_swap(make(there * CORES + 1 - core).astype(low))
        block = make(there * CORES + core) + away.astype(full)
        if step:
            block = outer_shift(block.astype(low), step).astype(full)
        total = block if total is None else total + block
    return total


def exchange(values_in):
    ways, size = split_ways(), lax.axis_size("hid")
    groups = None
    if ways > 1:
        groups = [[t * ways + w for t in range(size // ways)] for w in range(ways)]
    return lax.all_to_all(
        values_in, "hid", split_axis=0, concat_axis=0, tiled=True, axis_index_groups=groups
    )


def chain_kernel(
    ways,
    places,
    part_ref,
    out_ref,
    landed,
    sums,
    up_send,
    up_recv,
    down_send,
    down_recv,
    side_send,
    side_recv,
    kept,
):
    count = part_ref.shape[0]
    last = places - 1
    me = lax.axis_index("hid")
    if ways == 2:
        place, way = me // 2, me % 2
        above, below, beside = me + 2, me - 2, me + 1 - 2 * way
    else:
        odd, half = me % 2, places // 2
        place, way = (1 - odd) * (me // 2) + odd * (last - me // 2), 0
        turn_up = (place + 1) // half
        turn_down = (place - 1 + places) // half - 2
        above = (1 - turn_up) * 2 * (place + 1) + turn_up * (2 * (last - place - 1) + 1)
        below = (1 - turn_down) * 2 * (place - 1) + turn_down * (2 * (last - place + 1) + 1)
        beside = me

    def remote(source, target, send, recv, device):
        return pltpu.make_async_remote_copy(
            src_ref=source,
            dst_ref=target,
            send_sem=send,
            recv_sem=recv,
            device_id={"hid": device},
            device_id_type=pl.DeviceIdType.MESH,
        )

    def up_copy(i):
        return remote(sums.at[i], landed.at[i], up_send, up_recv.at[i], above)

    def down_copy(source, i):
        return remote(source, out_ref.at[way, i], down_send, down_recv.at[i], below)

    def side_copy(source, i):
        return remote(source, out_ref.at[way, i], side_send, side_recv, beside)

    barrier = pltpu.get_barrier_semaphore()

    def greet(device):
        pl.semaphore_signal(
            barrier, inc=1, device_id={"hid": device}, device_id_type=pl.DeviceIdType.MESH
        )

    @pl.when(place > 0)
    def _():
        greet(below)

    @pl.when(place < last)
    def _():
        greet(above)

    if ways == 2:
        greet(beside)
    met = jnp.where(place > 0, 1, 0) + jnp.where(place < last, 1, 0) + (ways - 1)
    pl.semaphore_wait(barrier, met)

    def upward(i):
        @pl.when(place == 0)
        def _():
            remote(part_ref.at[i], landed.at[i], up_send, up_recv.at[i], above).start()

        @pl.when(place > 0)
        def _():
            up_copy(i).wait_recv()
            sums[i] = (landed[i].astype(full) + part_ref[i].astype(full)).astype(low)

            @pl.when(place < last)
            def _():
                up_copy(i).start()

            @pl.when(place == last)
            def _():
                down_copy(sums.at[i], i).start()
                if ways == 2:
                    side_copy(sums.at[i], i).start()
                pltpu.make_async_copy(sums.at[i], out_ref.at[way, i], kept).start()

    def downward(i):
        down_copy(sums.at[i], i).wait_recv()

        @pl.when(place > 0)
        def _():
            down_copy(out_ref.at[way, i], i).start()

        if ways == 2:
            side_copy(out_ref.at[way, i], i).start()

    lag = SLACK * (last - place) + 2

    def step(i, carry):
        @pl.when(i < count)
        def _():
            upward(i)

        behind = i - lag

        @pl.when((behind >= 0) & (behind < count) & (place < last))
        def _():
            downward(behind)

        return carry

    lax.fori_loop(0, count + SLACK * last + 2, step, 0)

    @pl.when(place < last)
    def _():
        remote(sums, landed, up_send, kept, above).wait_send()

    @pl.when(place > 0)
    def _():
        remote(sums, out_ref.at[way], down_send, kept, below).wait_send()

    @pl.when(place == last)
    def _():
        pltpu.make_async_copy(sums, out_ref.at[way], kept).wait()

    if ways == 2:
        remote(sums, out_ref.at[way], side_send, kept, beside).wait_send()
        remote(sums, out_ref.at[1 - way], kept, side_recv, beside).wait_recv()


def chain_sum(part, collective_id):
    ways, size = split_ways(), lax.axis_size("hid")
    rows, columns = part.shape
    depth = max(16, CHUNK // columns)
    count = rows // depth
    return pl.pallas_call(
        functools.partial(chain_kernel, ways, size // ways),
        out_shape=jax.ShapeDtypeStruct((ways, count, depth, columns), low),
        in_specs=[pl.BlockSpec(memory_space=pltpu.VMEM)],
        out_specs=pl.BlockSpec(memory_space=pl.ANY),
        scratch_shapes=[
            pltpu.VMEM((count, depth, columns), low),
            pltpu.VMEM((count, depth, columns), low),
            pltpu.SemaphoreType.DMA,
            pltpu.SemaphoreType.DMA((count,)),
            pltpu.SemaphoreType.DMA,
            pltpu.SemaphoreType.DMA((count,)),
            pltpu.SemaphoreType.DMA,
            pltpu.SemaphoreType.DMA,
            pltpu.SemaphoreType.DMA,
        ],
        compiler_params=pltpu.CompilerParams(
            collective_id=collective_id, has_side_effects=True, vmem_limit_bytes=48 << 20
        ),
        cost_estimate=pl.CostEstimate(
            flops=rows * columns, bytes_accessed=300 * rows * columns, transcendentals=0
        ),
    )(part.reshape(count, depth, columns))


def to_owner(values_in):
    dp, hid, ways = lax.axis_size("dp"), lax.axis_size("hid"), split_ways()
    index = lax.axis_index("dp") * ways + lax.axis_index("hid") % ways
    mine = lax.dynamic_index_in_dim(values_in, index, 1, keepdims=False)
    pairs = [
        (d * hid + t * ways + w, (t * dp + d) * ways + w)
        for d in range(dp)
        for t in range(hid // ways)
        for w in range(ways)
    ]
    return lax.ppermute(mine, ("dp", "hid"), pairs)


def rotate(values_in, cosine, sine):
    half = cosine.shape[1]
    front, back = values_in[:, :half], values_in[:, half : 2 * half]
    return jnp.concatenate(
        [
            front * cosine - back * sine,
            back * cosine + front * sine,
            values_in[:, 2 * half :],
        ],
        axis=1,
    )


def local(
    history,
    mix,
    segment_ids,
    norm_gains,
    w_query,
    w_key,
    w_value,
    w_out,
    w_up,
    w_down,
    w_mixer,
    mixer_out,
    mix_static,
    out_cotangent,
    mix_cotangent,
):
    dp, hid, ways = lax.axis_size("dp"), lax.axis_size("hid"), split_ways()
    places = hid // ways
    my_hid = lax.axis_index("hid")
    place, way = my_hid // ways, my_hid % ways
    block = segment_ids.shape[0]
    total_tokens = block * dp * hid
    row = total_tokens // dp
    group = total_tokens // places
    rows = group // row
    piece = history.shape[2]
    mine = piece * places
    feats = piece * hid
    width = feats * dp
    heads = HEADS // dp // ways
    n_mix = mix.shape[1]
    n_cot = mix_cotangent.shape[1]

    def by_place(values_in):
        return jnp.stack(
            [values_in[..., p * group : (p + 1) * group] for p in range(places)], axis=0
        )

    stored = exchange(by_place(history.swapaxes(1, 2)))
    upstream = exchange(by_place(out_cotangent.T))
    upstream = upstream.reshape(mine, group).astype(full)

    table = jnp.concatenate(
        [mix.T, mix_cotangent.T, segment_ids.astype(full)[None]], axis=0
    )
    table = gather_all(table[None])
    table = lax.dynamic_slice_in_dim(table, place * dp * ways, dp * ways, 0)
    table = table.transpose(1, 0, 2).reshape(table.shape[1], group)
    mix_t = table[:n_mix]
    cot_t = table[n_mix : n_mix + n_cot]
    ids = table[-1].reshape(rows, row)

    there = jnp.arange(row, dtype=jnp.int32)
    same_doc = ids[:, :, None] == ids[:, None, :]
    doc_start = jnp.min(jnp.where(same_doc, there[None, None], row), axis=2)
    position = (there[None] - doc_start).astype(full).reshape(group)
    visible = same_doc & (there[None, None] <= there[None, :, None])
    frequency = rope_base ** (-jnp.arange(ROT // 2, dtype=full) * 2.0 / ROT)
    angle = frequency[:, None] * position[None, :]
    cosine, sine = jnp.cos(angle)[None], jnp.sin(angle)[None]

    streams = []
    for s in range(STREAMS):
        total = mix_t[s * HIST] * stored[:, 0].astype(full)
        for j in range(1, HIST):
            total = total + mix_t[s * HIST + j] * stored[:, j].astype(full)
        streams.append(total.reshape(mine, group))
    local_means = [jnp.mean(v, axis=0) for v in streams]
    local_devs = [jnp.sum(jnp.square(v - m), axis=0) for v, m in zip(streams, local_means)]
    moments = gather_dp(gather_ways(jnp.stack(local_means + local_devs, axis=0), 0))
    moments = moments.reshape((dp * ways,) + moments.shape[2:])
    mean_parts, dev_parts = moments[:, :STREAMS], moments[:, STREAMS:]
    means = jnp.sum(mean_parts, axis=0) / (dp * ways)
    variance = (
        jnp.sum(dev_parts, axis=0) + mine * jnp.sum(jnp.square(mean_parts - means), axis=0)
    ) / width
    inv_scales = lax.rsqrt(variance + 1e-05)

    def own_rows(values_in):
        parts = values_in.reshape((places, ways, piece) + values_in.shape[1:])
        part = lax.dynamic_index_in_dim(parts, way, 1, keepdims=False)
        return part.reshape((mine,) + values_in.shape[1:])

    def all_rows(values_in):
        parts = values_in.reshape((places, piece) + values_in.shape[1:])
        return gather_ways(parts, 1).reshape((feats,) + values_in.shape[1:])

    own_gains = own_rows(norm_gains).astype(full)
    gains = [own_gains[:, s][:, None] for s in range(STREAMS)]
    units = [(streams[s] - means[s]) * inv_scales[s] for s in range(STREAMS)]
    normed = [all_rows((units[s] * gains[s]).astype(low)) for s in range(STREAMS)]

    def project(weight, left):
        columns = weight.shape[1] // dp // ways

        def make(index):
            start = (index * ways + way) * columns
            part = lax.dynamic_slice_in_dim(weight, start, columns, 1)
            return contract(part, left, 0, 0)

        return scatter_dp(make)

    def way_columns(weight):
        if ways == 1:
            return weight
        size = weight.shape[1] // dp // ways
        parts = [weight[:, i * size : (i + 1) * size] for i in range(dp * ways)]
        pairs = zip(parts[::2], parts[1::2])
        return jnp.concatenate([jnp.where(way == 0, a, b) for a, b in pairs], axis=1)

    def way_rows(weight):
        size = weight.shape[0] // ways
        return lax.dynamic_slice_in_dim(weight, way * size, size, 0)

    def by_head(values_in):
        return values_in.reshape(heads, HEAD, group)

    queries = rotate(by_head(project(w_query, normed[0])), cosine, sine).astype(low)
    keys = rotate(by_head(project(w_key, normed[1])), cosine, sine).astype(low)
    values = by_head(project(w_value, normed[2])).astype(low)
    hidden = project(w_up, normed[3])

    def by_row(values_in):
        if rows == 1:
            return values_in
        return (
            values_in.reshape(heads, HEAD, rows, row)
            .transpose(0, 2, 1, 3)
            .reshape(heads * rows, HEAD, row)
        )

    def from_row(values_in):
        if rows == 1:
            return values_in
        return (
            values_in.reshape(heads, rows, HEAD, row)
            .transpose(0, 2, 1, 3)
            .reshape(heads, HEAD, group)
        )

    q_rows, k_rows, v_rows = by_row(queries), by_row(keys), by_row(values)
    score_scale = 1.0 / math.sqrt(HEAD)
    scores = batched(q_rows, k_rows, 1, 1) * score_scale
    mask = jnp.broadcast_to(visible[None], (heads, rows, row, row)).reshape(scores.shape)
    scores = jnp.where(mask, scores, -1e30)
    probs = jax.nn.softmax(scores, axis=-1)
    probs_low = probs.astype(low)
    attended = from_row(batched(v_rows, probs_low, 2, 2).astype(low)).reshape(heads * HEAD, group)

    active, hidden_pull = jax.vjp(gelu_exact, hidden)
    active = active.astype(low)
    (slope,) = hidden_pull(jnp.ones_like(hidden))
    out_rows, down_rows = way_rows(w_out), way_rows(w_down)

    def make_out(index):
        start = index * feats
        left = lax.dynamic_slice_in_dim(out_rows, start, feats, 1)
        other = lax.dynamic_slice_in_dim(down_rows, start, feats, 1)
        return contract(left, attended, 0, 0) + contract(other, active, 0, 0)

    branches = scatter_dp(make_out).reshape(places, ways, piece, group)
    kept = lax.dynamic_index_in_dim(branches, way, 1, keepdims=False)
    if ways == 2:
        given = lax.dynamic_index_in_dim(branches, 1 - way, 1, keepdims=False).astype(low)
        kept = kept + hid_swap(given, 1).astype(full)
    output = streams[3] + kept.reshape(mine, group)
    output_rounded = output.astype(low)

    block_output = exchange(output_rounded.reshape(places, piece, group))
    block_output = block_output.transpose(1, 0, 2).reshape(piece, total_tokens).T

    square = jnp.sum(output * output, axis=0, keepdims=True)
    mixer_rows = own_rows(w_mixer)
    mixer_part = contract(mixer_rows, output_rounded, 0, 0)
    sums = sum_features(jnp.concatenate([mixer_part, square], axis=0))
    inv_rms = lax.rsqrt(sums[-1] / width + 1e-06)
    inner_raw = sums[:-1]
    inner_pre = inner_raw * inv_rms
    inner_act, inner_pull = jax.vjp(gelu_exact, inner_pre)
    raw_mix = contract_high(mixer_out, inner_act, 0, 0)
    column = jnp.stack(
        [
            jnp.sum(raw_mix, axis=1),
            jnp.sum(raw_mix * raw_mix, axis=1),
            jnp.sum(cot_t, axis=1),
            jnp.sum(cot_t * raw_mix, axis=1),
        ],
        axis=0,
    )
    act_total = jnp.sum(inner_act, axis=1)
    act_cot = contract_high(inner_act, cot_t, 1, 1)
    act_raw = contract_high(inner_act, raw_mix, 1, 1)
    n_inner = act_total.shape[0]
    flat = sum_tokens(
        jnp.concatenate([column.reshape(-1), act_total, act_cot.reshape(-1), act_raw.reshape(-1)])
    )
    sum_raw, sum_square, sum_grad, sum_grad_raw = flat[: 4 * n_cot].reshape(4, n_cot)
    start = 4 * n_cot
    act_total = flat[start : start + n_inner]
    start += n_inner
    act_cot = flat[start : start + n_inner * n_cot].reshape(n_inner, n_cot)
    start += n_inner * n_cot
    act_raw = flat[start:].reshape(n_inner, n_cot)
    average = sum_raw / total_tokens
    variance_mix = sum_square / total_tokens - average * average
    inv_spread = lax.rsqrt(variance_mix + 1e-05)
    unit_mix = (raw_mix - average[:, None]) * inv_spread[:, None]
    mix_next = mix_static[:, None] + unit_mix
    mix_next = to_owner(mix_next.reshape(n_cot, dp * ways, block)).T
    mean_grad = sum_grad / total_tokens
    sum_grad_unit = inv_spread * (sum_grad_raw - average * sum_grad)
    mean_grad_unit = sum_grad_unit / total_tokens
    raw_grad = inv_spread[:, None] * (
        cot_t - mean_grad[:, None] - unit_mix * mean_grad_unit[:, None]
    )
    act_unit = inv_spread[None, :] * (act_raw - act_total[:, None] * average[None, :])
    mixer_out_grad = inv_spread[None, :] * (
        act_cot - act_total[:, None] * mean_grad[None, :] - act_unit * mean_grad_unit[None, :]
    )
    act_grad = contract_high(mixer_out, raw_grad, 1, 0)
    inner_low = inner_pull(act_grad)[0].astype(low)
    scaled = (output * inv_rms).astype(low)
    mixer_grad_part = contract(inner_low, scaled, 1, 1)
    scaled_grad = contract(mixer_rows, inner_low, 1, 0)
    along = jnp.sum(inner_low.astype(full) * inner_raw, axis=0) / width
    output_grad = upstream + inv_rms * scaled_grad - output * (inv_rms * inv_rms * inv_rms) * along
    output_low = gather_dp(all_rows(output_grad.astype(low))).reshape(width, group)

    branch_part = jnp.concatenate(
        [
            contract(attended, output_low, 1, 1).astype(low),
            contract(active, output_low, 1, 1).astype(low),
        ],
        axis=0,
    )
    hidden_low = (contract(down_rows, output_low, 1, 0) * slope).astype(low)

    attended_grad = contract(out_rows, output_low, 1, 0).astype(low)
    a_rows = by_row(by_head(attended_grad))
    prob_grad = batched(a_rows, v_rows, 1, 1)
    row_total = jnp.sum(probs * prob_grad, axis=-1, keepdims=True)
    score_grad = (probs * (prob_grad - row_total)).astype(low)
    query_grad = from_row(batched(k_rows, score_grad, 2, 2) * score_scale)
    key_grad = from_row(batched(q_rows, score_grad, 2, 1) * score_scale)
    value_grad = from_row(batched(a_rows, probs_low, 2, 1))
    query_low = rotate(query_grad, cosine, -sine).astype(low).reshape(heads * HEAD, group)
    key_low = rotate(key_grad, cosine, -sine).astype(low).reshape(heads * HEAD, group)
    value_low = value_grad.astype(low).reshape(heads * HEAD, group)

    lows_mine, hidden_mine = (query_low, key_low, value_low), hidden_low
    branch_part, hidden_mine, lows_mine = lax.optimization_barrier(
        (branch_part, hidden_mine, lows_mine)
    )
    hidden_all = gather_dp(hidden_mine).reshape(-1, group)
    lows = [gather_dp(v).reshape(-1, group) for v in lows_mine]
    branch_sum = chain_sum(branch_part, 0)
    n_out = out_rows.shape[0] // branch_sum.shape[2]
    w_out_grad = branch_sum[:, :n_out].astype(full).reshape(w_out.shape)
    w_down_grad = branch_sum[:, n_out:].astype(full).reshape(w_down.shape)

    def unsplit(total, weight):
        total = total.reshape(ways, weight.shape[0], -1)
        size = total.shape[2] // dp
        parts = [total[w, :, d * size : (d + 1) * size] for d in range(dp) for w in range(ways)]
        return jnp.concatenate([v.astype(full) for v in parts], axis=1)

    up_part = contract(normed[3], hidden_all, 1, 1).astype(low)
    w_up_grad = unsplit(chain_sum(up_part, 1), w_up)
    parts = [contract(normed[s], lows[s], 1, 1).astype(low) for s in range(3)]
    head_sum = chain_sum(jnp.concatenate(parts, axis=0), 2)
    head_sum = head_sum.reshape(ways, 3, -1, head_sum.shape[2], head_sum.shape[3])
    w_query_grad, w_key_grad, w_value_grad = [
        unsplit(head_sum[:, s], w) for s, w in enumerate((w_query, w_key, w_value))
    ]

    normed_grads = []
    for s, weight in enumerate((w_query, w_key, w_value, w_up)):
        right = lows[s] if s < 3 else hidden_all
        part = contract(way_columns(weight), right, 1, 0).reshape(places, ways, piece, group)
        kept = lax.dynamic_index_in_dim(part, way, 1, keepdims=False)
        if ways == 2:
            given = lax.dynamic_index_in_dim(part, 1 - way, 1, keepdims=False).astype(low)
            kept = kept + hid_swap(given, 1).astype(full)
        normed_grads.append(kept.reshape(mine, group))
    weighted = [normed_grads[s] * gains[s] for s in range(STREAMS)]
    means_back = sum_features(
        jnp.stack(
            [jnp.sum(e, axis=0) for e in weighted]
            + [jnp.sum(e * u, axis=0) for e, u in zip(weighted, units)],
            axis=0,
        )
    ) / width
    gain_parts = [jnp.sum(g * u, axis=1) for g, u in zip(normed_grads, units)]
    stream_grads = [
        (weighted[s] - means_back[s] - units[s] * means_back[STREAMS + s]) * inv_scales[s]
        for s in range(STREAMS)
    ]
    stream_grads[3] = stream_grads[3] + output_grad
    smalls = sum_tokens(jnp.concatenate([mixer_grad_part, jnp.stack(gain_parts, axis=0)], axis=0))
    smalls = gather_ways(smalls.reshape(-1, places, piece), 2).reshape(-1, feats)
    w_mixer_grad = smalls[:n_inner].T
    norm_gains_grad = smalls[n_inner:].T

    split = [v.reshape(places, piece, group) for v in stream_grads]
    layers = []
    for j in range(HIST):
        total = mix_t[j] * split[0]
        for s in range(1, STREAMS):
            total = total + mix_t[s * HIST + j] * split[s]
        layers.append(total.astype(low))
    history_grad = exchange(jnp.stack(layers, axis=1))
    history_grad = (
        history_grad.transpose(1, 2, 0, 3)
        .reshape(HIST, piece, total_tokens)
        .astype(full)
        .swapaxes(1, 2)
    )
    mix_parts = jnp.stack(
        [
            jnp.sum(split[s] * stored[:, j].astype(full), axis=(0, 1))
            for s in range(STREAMS)
            for j in range(HIST)
        ],
        axis=0,
    )
    mix_grad = to_owner(sum_features(mix_parts).reshape(n_mix, dp * ways, block)).T

    return (
        block_output,
        mix_next,
        history_grad,
        mix_grad,
        norm_gains_grad,
        w_query_grad,
        w_key_grad,
        w_value_grad,
        w_out_grad,
        w_up_grad,
        w_down_grad,
        w_mixer_grad,
        mixer_out_grad,
        sum_grad,
    )


def solution(mesh):
    everywhere = ("dp", "hid")
    placed = (
        P(None, None, everywhere),
        P(everywhere, None),
        P(everywhere),
        P("dp", None),
        P("dp", None),
        P("dp", None),
        P("dp", None),
        P("dp", None),
        P("dp", None),
        P("dp", None),
        P("dp", None),
        P(),
        P(),
        P(None, everywhere),
        P(everywhere, None),
    )
    return jax.shard_map(
        local,
        mesh=mesh,
        in_specs=placed,
        out_specs=(
            P(None, everywhere),
            P(everywhere, None),
            P(None, None, everywhere),
            P(everywhere, None),
            P("dp", None),
            P("dp", None),
            P("dp", None),
            P("dp", None),
            P("dp", None),
            P("dp", None),
            P("dp", None),
            P("dp", None),
            P(),
            P(),
        ),
        check_vma=False,
    )
```

```python
import functools
import math

import jax
import jax.numpy as jnp
from jax import lax
from jax.experimental import pallas as pl
from jax.experimental.pallas import tpu as pltpu
from jax.sharding import PartitionSpec as P

HEADS = 16
HEAD = 128
ROT = 32
HIST = 8
STREAMS = 4
CORES = 2
CHUNK = 1 << 15
SLACK = 4

highest = lax.Precision.HIGHEST
rope_base = 10000.0
low = jnp.bfloat16
full = jnp.float32


def contract(left, right, left_dim, right_dim):
    return lax.dot_general(
        left, right, (((left_dim,), (right_dim,)), ((), ())), preferred_element_type=full
    )


def contract_high(left, right, left_dim, right_dim):
    return lax.dot_general(
        left,
        right,
        (((left_dim,), (right_dim,)), ((), ())),
        precision=highest,
        preferred_element_type=full,
    )


def batched(left, right, left_dim, right_dim):
    return lax.dot_general(
        left, right, (((left_dim,), (right_dim,)), ((0,), (0,))), preferred_element_type=full
    )


def gelu_exact(values_in):
    return jax.nn.gelu(values_in, approximate=False)


def core_swap(values_in):
    size = lax.axis_size("dp")
    return lax.ppermute(values_in, "dp", [(i, i ^ 1) for i in range(size)])


def outer_shift(values_in, step):
    size = lax.axis_size("dp")
    outer = size // CORES
    pairs = [
        (o * CORES + c, ((o + step) % outer) * CORES + c) for o in range(outer) for c in range(CORES)
    ]
    return lax.ppermute(values_in, "dp", pairs)


def hid_swap(values_in, bit):
    size = lax.axis_size("hid")
    return lax.ppermute(values_in, "hid", [(i, i ^ bit) for i in range(size)])


def ordered(first, values_in, other, axis):
    return jnp.stack(
        [jnp.where(first, values_in, other), jnp.where(first, other, values_in)], axis=axis
    )


def take(values_in, index):
    return lax.dynamic_index_in_dim(values_in, index, 0, keepdims=False)


def put(target, values_in, index):
    return lax.dynamic_update_index_in_dim(target, values_in, index, 0)


def split_ways():
    return 2 if HEADS // lax.axis_size("dp") >= 2 else 1


def gather_ways(values_in, axis):
    if split_ways() == 1:
        return jnp.expand_dims(values_in, axis)
    return ordered(lax.axis_index("hid") % 2 == 0, values_in, hid_swap(values_in, 1), axis)


def gather_dp(values_in):
    size = lax.axis_size("dp")
    outer = size // CORES
    me = lax.axis_index("dp")
    mine, core = me // CORES, me % CORES
    if outer == 2:
        held = ordered(mine == 0, values_in, outer_shift(values_in, 1), 0)
    else:
        held = jnp.zeros((outer,) + values_in.shape, values_in.dtype)
        held = put(held, values_in, mine)
        for step in range(1, outer):
            held = put(held, outer_shift(values_in, step), (mine - step) % outer)
    pair = ordered(core == 0, held, core_swap(held), 1)
    return pair.reshape((size,) + values_in.shape)


def sum_features(values_in):
    if split_ways() == 2:
        values_in = values_in + hid_swap(values_in, 1)
    parts = gather_dp(values_in)
    total = parts[0]
    for i in range(1, parts.shape[0]):
        total = total + parts[i]
    return total


def sum_tokens(values_in):
    size = lax.axis_size("hid")
    bit = split_ways()
    while bit < size:
        values_in = values_in + hid_swap(values_in, bit)
        bit *= 2
    return values_in


def gather_all(values_in):
    count = lax.axis_size("dp") * lax.axis_size("hid")
    copies = jnp.broadcast_to(values_in[None], (count,) + values_in.shape)
    held = lax.all_to_all(copies, ("dp", "hid"), split_axis=0, concat_axis=0, tiled=True)
    return held.transpose(1, 0, 2).reshape(values_in.shape[0], -1)


def scatter_dp(make):
    size = lax.axis_size("dp")
    outer = size // CORES
    me = lax.axis_index("dp")
    mine, core = me // CORES, me % CORES
    total = None
    for step in list(range(1, outer)) + [0]:
        there = (mine + step) % outer
        away = core_swap(make(there * CORES + 1 - core).astype(low))
        block = make(there * CORES + core) + away.astype(full)
        if step:
            block = outer_shift(block.astype(low), step).astype(full)
        total = block if total is None else total + block
    return total


def exchange(values_in):
    ways, size = split_ways(), lax.axis_size("hid")
    groups = None
    if ways > 1:
        groups = [[t * ways + w for t in range(size // ways)] for w in range(ways)]
    return lax.all_to_all(
        values_in, "hid", split_axis=0, concat_axis=0, tiled=True, axis_index_groups=groups
    )


def chain_kernel(
    ways,
    places,
    part_ref,
    out_ref,
    landed,
    sums,
    up_send,
    up_recv,
    down_send,
    down_recv,
    side_send,
    side_recv,
    kept,
):
    count = part_ref.shape[0]
    last = places - 1
    me = lax.axis_index("hid")
    if ways == 2:
        place, way = me // 2, me % 2
        above, below, beside = me + 2, me - 2, me + 1 - 2 * way
    else:
        odd, half = me % 2, places // 2
        place, way = (1 - odd) * (me // 2) + odd * (last - me // 2), 0
        turn_up = (place + 1) // half
        turn_down = (place - 1 + places) // half - 2
        above = (1 - turn_up) * 2 * (place + 1) + turn_up * (2 * (last - place - 1) + 1)
        below = (1 - turn_down) * 2 * (place - 1) + turn_down * (2 * (last - place + 1) + 1)
        beside = me

    def remote(source, target, send, recv, device):
        return pltpu.make_async_remote_copy(
            src_ref=source,
            dst_ref=target,
            send_sem=send,
            recv_sem=recv,
            device_id={"hid": device},
            device_id_type=pl.DeviceIdType.MESH,
        )

    def up_copy(i):
        return remote(sums.at[i], landed.at[i], up_send, up_recv.at[i], above)

    def down_copy(source, i):
        return remote(source, out_ref.at[way, i], down_send, down_recv.at[i], below)

    def side_copy(source, i):
        return remote(source, out_ref.at[way, i], side_send, side_recv, beside)

    barrier = pltpu.get_barrier_semaphore()

    def greet(device):
        pl.semaphore_signal(
            barrier, inc=1, device_id={"hid": device}, device_id_type=pl.DeviceIdType.MESH
        )

    @pl.when(place > 0)
    def _():
        greet(below)

    @pl.when(place < last)
    def _():
        greet(above)

    if ways == 2:
        greet(beside)
    met = jnp.where(place > 0, 1, 0) + jnp.where(place < last, 1, 0) + (ways - 1)
    pl.semaphore_wait(barrier, met)

    def upward(i):
        @pl.when(place == 0)
        def _():
            remote(part_ref.at[i], landed.at[i], up_send, up_recv.at[i], above).start()

        @pl.when(place > 0)
        def _():
            up_copy(i).wait_recv()
            sums[i] = (landed[i].astype(full) + part_ref[i].astype(full)).astype(low)

            @pl.when(place < last)
            def _():
                up_copy(i).start()

            @pl.when(place == last)
            def _():
                down_copy(sums.at[i], i).start()
                if ways == 2:
                    side_copy(sums.at[i], i).start()
                pltpu.make_async_copy(sums.at[i], out_ref.at[way, i], kept).start()

    def downward(i):
        down_copy(sums.at[i], i).wait_recv()

        @pl.when(place > 0)
        def _():
            down_copy(out_ref.at[way, i], i).start()

        if ways == 2:
            side_copy(out_ref.at[way, i], i).start()

    lag = SLACK * (last - place) + 2

    def step(i, carry):
        @pl.when(i < count)
        def _():
            upward(i)

        behind = i - lag

        @pl.when((behind >= 0) & (behind < count) & (place < last))
        def _():
            downward(behind)

        return carry

    lax.fori_loop(0, count + SLACK * last + 2, step, 0)

    @pl.when(place < last)
    def _():
        remote(sums, landed, up_send, kept, above).wait_send()

    @pl.when(place > 0)
    def _():
        remote(sums, out_ref.at[way], down_send, kept, below).wait_send()

    @pl.when(place == last)
    def _():
        pltpu.make_async_copy(sums, out_ref.at[way], kept).wait()

    if ways == 2:
        remote(sums, out_ref.at[way], side_send, kept, beside).wait_send()
        remote(sums, out_ref.at[1 - way], kept, side_recv, beside).wait_recv()


def chain_sum(part, collective_id):
    ways, size = split_ways(), lax.axis_size("hid")
    rows, columns = part.shape
    depth = max(16, CHUNK // columns)
    count = rows // depth
    return pl.pallas_call(
        functools.partial(chain_kernel, ways, size // ways),
        out_shape=jax.ShapeDtypeStruct((ways, count, depth, columns), low),
        in_specs=[pl.BlockSpec(memory_space=pltpu.VMEM)],
        out_specs=pl.BlockSpec(memory_space=pl.ANY),
        scratch_shapes=[
            pltpu.VMEM((count, depth, columns), low),
            pltpu.VMEM((count, depth, columns), low),
            pltpu.SemaphoreType.DMA,
            pltpu.SemaphoreType.DMA((count,)),
            pltpu.SemaphoreType.DMA,
            pltpu.SemaphoreType.DMA((count,)),
            pltpu.SemaphoreType.DMA,
            pltpu.SemaphoreType.DMA,
            pltpu.SemaphoreType.DMA,
        ],
        compiler_params=pltpu.CompilerParams(
            collective_id=collective_id, has_side_effects=True, vmem_limit_bytes=48 << 20
        ),
        cost_estimate=pl.CostEstimate(
            flops=rows * columns, bytes_accessed=300 * rows * columns, transcendentals=0
        ),
    )(part.reshape(count, depth, columns))


def assemble_kernel(ways, dp, own_ref, *refs):
    halves, (up_ref, *head_refs, out_ref) = refs[:ways], refs[ways:]
    wide = own_ref.shape[3]
    size = up_ref.shape[1] // dp // ways
    blocks = dp * size // wide
    for w in range(ways):
        for d in range(dp):
            start = d * size
            part = own_ref[w, start // wide, :, start % wide : start % wide + size]
            place = (d * ways + w) * size
            up_ref[:, place : place + size] = part.astype(full)
        for s, ref in enumerate(head_refs):
            own = wide // dp
            for d in range(dp):
                place = (d * ways + w) * own
                part = own_ref[w, blocks + s, :, d * own : (d + 1) * own]
                ref[:, place : place + own] = part.astype(full)
    for w in range(ways):
        out_ref[:, w * wide : (w + 1) * wide] = halves[w][0, 0].astype(full)


def assemble(total, w_up):
    ways, dp = split_ways(), lax.axis_size("dp")
    blocks, rows, wide = total.shape[1:]
    depth = min(64, rows // ways)
    share = rows // ways // depth

    def half_map(half):
        return lambda i: (i // share, blocks - 1, half * share + i % share, 0)

    widths = [w_up.shape[1]] + [ways * wide] * 4
    return pl.pallas_call(
        functools.partial(assemble_kernel, ways, dp),
        grid=(rows // depth,),
        out_shape=[jax.ShapeDtypeStruct((rows, n), full) for n in widths],
        in_specs=[pl.BlockSpec((ways, blocks, depth, wide), lambda i: (0, 0, i, 0))]
        + [pl.BlockSpec((1, 1, depth, wide), half_map(half)) for half in range(ways)],
        out_specs=[pl.BlockSpec((depth, n), lambda i: (i, 0)) for n in widths],
        compiler_params=pltpu.CompilerParams(vmem_limit_bytes=48 << 20),
        cost_estimate=pl.CostEstimate(
            flops=0, bytes_accessed=6 * total.size, transcendentals=0
        ),
    )(total, *[total] * ways)


def to_owner(values_in):
    dp, hid, ways = lax.axis_size("dp"), lax.axis_size("hid"), split_ways()
    index = lax.axis_index("dp") * ways + lax.axis_index("hid") % ways
    mine = lax.dynamic_index_in_dim(values_in, index, 1, keepdims=False)
    pairs = [
        (d * hid + t * ways + w, (t * dp + d) * ways + w)
        for d in range(dp)
        for t in range(hid // ways)
        for w in range(ways)
    ]
    return lax.ppermute(mine, ("dp", "hid"), pairs)


def rotate(values_in, cosine, sine):
    half = cosine.shape[1]
    front, back = values_in[:, :half], values_in[:, half : 2 * half]
    return jnp.concatenate(
        [
            front * cosine - back * sine,
            back * cosine + front * sine,
            values_in[:, 2 * half :],
        ],
        axis=1,
    )


def local(
    history,
    mix,
    segment_ids,
    norm_gains,
    w_query,
    w_key,
    w_value,
    w_out,
    w_up,
    w_down,
    w_mixer,
    mixer_out,
    mix_static,
    out_cotangent,
    mix_cotangent,
):
    dp, hid, ways = lax.axis_size("dp"), lax.axis_size("hid"), split_ways()
    places = hid // ways
    my_hid = lax.axis_index("hid")
    place, way = my_hid // ways, my_hid % ways
    block = segment_ids.shape[0]
    total_tokens = block * dp * hid
    row = total_tokens // dp
    group = total_tokens // places
    rows = group // row
    piece = history.shape[2]
    mine = piece * places
    feats = piece * hid
    width = feats * dp
    heads = HEADS // dp // ways
    n_mix = mix.shape[1]
    n_cot = mix_cotangent.shape[1]

    def by_place(values_in):
        return jnp.stack(
            [values_in[..., p * group : (p + 1) * group] for p in range(places)], axis=0
        )

    stored = history.swapaxes(1, 2)
    mix_all = gather_all(mix.T)
    own_means, own_devs, deviations = [], [], []
    for s in range(STREAMS):
        total = mix_all[s * HIST] * stored[0].astype(full)
        for j in range(1, HIST):
            total = total + mix_all[s * HIST + j] * stored[j].astype(full)
        own_means.append(jnp.mean(total, axis=0))
        off = total - own_means[s]
        own_devs.append(jnp.sum(off * off, axis=0))
        deviations.append(off.astype(low))
    moments = exchange(by_place(jnp.stack(own_means + own_devs, axis=0)))
    deviations[3] = exchange(by_place(deviations[3]))
    for s in range(3):
        deviations[s] = exchange(by_place(deviations[s]))
    upstream = exchange(by_place(out_cotangent.T))
    upstream = upstream.reshape(mine, group).astype(full)

    def join_moments(mean_parts, dev_parts, size):
        mean = jnp.mean(mean_parts, axis=0)
        spread = size * jnp.sum(jnp.square(mean_parts - mean), axis=0)
        return mean, jnp.sum(dev_parts, axis=0) + spread

    block_means = moments[:, :STREAMS]
    joined = join_moments(block_means, moments[:, STREAMS:], piece)
    joined = gather_dp(gather_ways(jnp.concatenate(joined, axis=0), 0))
    joined = joined.reshape((dp * ways,) + joined.shape[2:])
    means, variance = join_moments(joined[:, :STREAMS], joined[:, STREAMS:], mine)
    inv_scales = lax.rsqrt(variance / width + 1e-05)
    all_means = gather_ways(block_means, 1)

    table = jnp.concatenate([mix_cotangent.T, segment_ids.astype(full)[None]], axis=0)
    table = lax.dynamic_slice_in_dim(gather_all(table), place * group, group, 1)
    cot_t = table[:n_cot]
    ids = table[-1].reshape(rows, row)

    there = jnp.arange(row, dtype=jnp.int32)
    same_doc = ids[:, :, None] == ids[:, None, :]
    doc_start = jnp.min(jnp.where(same_doc, there[None, None], row), axis=2)
    position = (there[None] - doc_start).astype(full).reshape(group)
    visible = same_doc & (there[None, None] <= there[None, :, None])
    frequency = rope_base ** (-jnp.arange(ROT // 2, dtype=full) * 2.0 / ROT)
    angle = frequency[:, None] * position[None, :]
    cosine, sine = jnp.cos(angle)[None], jnp.sin(angle)[None]

    def own_rows(values_in):
        parts = values_in.reshape((places, ways, piece) + values_in.shape[1:])
        part = lax.dynamic_index_in_dim(parts, way, 1, keepdims=False)
        return part.reshape((mine,) + values_in.shape[1:])

    def all_rows(values_in):
        parts = values_in.reshape((places, piece) + values_in.shape[1:])
        return gather_ways(parts, 1).reshape((feats,) + values_in.shape[1:])

    def unit(values_in, block_mean, s):
        return (values_in.astype(full) + (block_mean - means[s])[..., None, :]) * inv_scales[s]

    own_gains = own_rows(norm_gains).astype(full)
    gains = [own_gains[:, s][:, None] for s in range(STREAMS)]
    all_gains = norm_gains.astype(full)
    units = [
        unit(deviations[s], block_means[:, s], s).reshape(mine, group) for s in range(STREAMS)
    ]
    normed = []
    for s in range(STREAMS):
        both = unit(gather_ways(deviations[s], 1), all_means[:, :, s], s).reshape(feats, group)
        normed.append((both * all_gains[:, s][:, None]).astype(low))
    residual = (deviations[3].astype(full) + block_means[:, 3][:, None]).reshape(mine, group)

    def project(weight, left):
        columns = weight.shape[1] // dp // ways

        def make(index):
            start = (index * ways + way) * columns
            part = lax.dynamic_slice_in_dim(weight, start, columns, 1)
            return contract(part, left, 0, 0)

        return scatter_dp(make)

    def way_columns(weight):
        if ways == 1:
            return weight
        size = weight.shape[1] // dp // ways
        parts = [weight[:, i * size : (i + 1) * size] for i in range(dp * ways)]
        pairs = zip(parts[::2], parts[1::2])
        return jnp.concatenate([jnp.where(way == 0, a, b) for a, b in pairs], axis=1)

    def way_rows(weight):
        size = weight.shape[0] // ways
        return lax.dynamic_slice_in_dim(weight, way * size, size, 0)

    def by_head(values_in):
        return values_in.reshape(heads, HEAD, group)

    hidden = project(w_up, normed[3])
    queries = rotate(by_head(project(w_query, normed[0])), cosine, sine).astype(low)
    keys = rotate(by_head(project(w_key, normed[1])), cosine, sine).astype(low)
    values = by_head(project(w_value, normed[2])).astype(low)
    queries, upstream = lax.optimization_barrier((queries, upstream))

    def by_row(values_in):
        if rows == 1:
            return values_in
        return (
            values_in.reshape(heads, HEAD, rows, row)
            .transpose(0, 2, 1, 3)
            .reshape(heads * rows, HEAD, row)
        )

    def from_row(values_in):
        if rows == 1:
            return values_in
        return (
            values_in.reshape(heads, rows, HEAD, row)
            .transpose(0, 2, 1, 3)
            .reshape(heads, HEAD, group)
        )

    q_rows, k_rows, v_rows = by_row(queries), by_row(keys), by_row(values)
    score_scale = 1.0 / math.sqrt(HEAD)
    scores = batched(q_rows, k_rows, 1, 1) * score_scale
    mask = jnp.broadcast_to(visible[None], (heads, rows, row, row)).reshape(scores.shape)
    scores = jnp.where(mask, scores, -1e30)
    probs = jax.nn.softmax(scores, axis=-1)
    probs_low = probs.astype(low)
    attended = from_row(batched(v_rows, probs_low, 2, 2).astype(low)).reshape(heads * HEAD, group)

    active, hidden_pull = jax.vjp(gelu_exact, hidden)
    active = active.astype(low)
    (slope,) = hidden_pull(jnp.ones_like(hidden))
    out_rows, down_rows = way_rows(w_out), way_rows(w_down)

    def make_out(index):
        start = index * feats
        left = lax.dynamic_slice_in_dim(out_rows, start, feats, 1)
        other = lax.dynamic_slice_in_dim(down_rows, start, feats, 1)
        return contract(left, attended, 0, 0) + contract(other, active, 0, 0)

    branches = scatter_dp(make_out).reshape(places, ways, piece, group)
    kept = lax.dynamic_index_in_dim(branches, way, 1, keepdims=False)
    if ways == 2:
        given = lax.dynamic_index_in_dim(branches, 1 - way, 1, keepdims=False).astype(low)
        kept = kept + hid_swap(given, 1).astype(full)
    output = residual + kept.reshape(mine, group)
    output_rounded = output.astype(low)

    block_output = exchange(output_rounded.reshape(places, piece, group))
    block_output = block_output.transpose(1, 0, 2).reshape(piece, total_tokens).T

    square = jnp.sum(output * output, axis=0, keepdims=True)
    mixer_rows = own_rows(w_mixer)
    mixer_part = contract(mixer_rows, output_rounded, 0, 0)
    sums = sum_features(jnp.concatenate([mixer_part, square], axis=0))
    inv_rms = lax.rsqrt(sums[-1] / width + 1e-06)
    inner_raw = sums[:-1]
    inner_pre = inner_raw * inv_rms
    inner_act, inner_pull = jax.vjp(gelu_exact, inner_pre)
    raw_mix = contract_high(mixer_out, inner_act, 0, 0)
    column = jnp.stack(
        [
            jnp.sum(raw_mix, axis=1),
            jnp.sum(raw_mix * raw_mix, axis=1),
            jnp.sum(cot_t, axis=1),
            jnp.sum(cot_t * raw_mix, axis=1),
        ],
        axis=0,
    )
    act_total = jnp.sum(inner_act, axis=1)
    act_cot = contract_high(inner_act, cot_t, 1, 1)
    act_raw = contract_high(inner_act, raw_mix, 1, 1)
    n_inner = act_total.shape[0]
    flat = sum_tokens(
        jnp.concatenate([column.reshape(-1), act_total, act_cot.reshape(-1), act_raw.reshape(-1)])
    )
    sum_raw, sum_square, sum_grad, sum_grad_raw = flat[: 4 * n_cot].reshape(4, n_cot)
    start = 4 * n_cot
    act_total = flat[start : start + n_inner]
    start += n_inner
    act_cot = flat[start : start + n_inner * n_cot].reshape(n_inner, n_cot)
    start += n_inner * n_cot
    act_raw = flat[start:].reshape(n_inner, n_cot)
    average = sum_raw / total_tokens
    variance_mix = sum_square / total_tokens - average * average
    inv_spread = lax.rsqrt(variance_mix + 1e-05)
    unit_mix = (raw_mix - average[:, None]) * inv_spread[:, None]
    mix_next = mix_static[:, None] + unit_mix
    mix_next = to_owner(mix_next.reshape(n_cot, dp * ways, block)).T
    mean_grad = sum_grad / total_tokens
    sum_grad_unit = inv_spread * (sum_grad_raw - average * sum_grad)
    mean_grad_unit = sum_grad_unit / total_tokens
    raw_grad = inv_spread[:, None] * (
        cot_t - mean_grad[:, None] - unit_mix * mean_grad_unit[:, None]
    )
    act_unit = inv_spread[None, :] * (act_raw - act_total[:, None] * average[None, :])
    mixer_out_grad = inv_spread[None, :] * (
        act_cot - act_total[:, None] * mean_grad[None, :] - act_unit * mean_grad_unit[None, :]
    )
    act_grad = contract_high(mixer_out, raw_grad, 1, 0)
    inner_low = inner_pull(act_grad)[0].astype(low)
    scaled = (output * inv_rms).astype(low)
    mixer_grad_part = contract(inner_low, scaled, 1, 1)
    scaled_grad = contract(mixer_rows, inner_low, 1, 0)
    along = jnp.sum(inner_low.astype(full) * inner_raw, axis=0) / width
    output_grad = upstream + inv_rms * scaled_grad - output * (inv_rms * inv_rms * inv_rms) * along
    output_low = gather_dp(all_rows(output_grad.astype(low))).reshape(width, group)

    branch_part = contract(active, output_low, 1, 1).astype(low)
    hidden_low = (contract(down_rows, output_low, 1, 0) * slope).astype(low)

    attended_grad = contract(out_rows, output_low, 1, 0).astype(low)
    a_rows = by_row(by_head(attended_grad))
    prob_grad = batched(a_rows, v_rows, 1, 1)
    row_total = jnp.sum(probs * prob_grad, axis=-1, keepdims=True)
    score_grad = (probs * (prob_grad - row_total)).astype(low)
    query_grad = from_row(batched(k_rows, score_grad, 2, 2) * score_scale)
    key_grad = from_row(batched(q_rows, score_grad, 2, 1) * score_scale)
    value_grad = from_row(batched(a_rows, probs_low, 2, 1))
    query_low = rotate(query_grad, cosine, -sine).astype(low).reshape(heads * HEAD, group)
    key_low = rotate(key_grad, cosine, -sine).astype(low).reshape(heads * HEAD, group)
    value_low = value_grad.astype(low).reshape(heads * HEAD, group)

    lows_mine, hidden_mine = (query_low, key_low, value_low), hidden_low
    branch_part, hidden_mine, lows_mine = lax.optimization_barrier(
        (branch_part, hidden_mine, lows_mine)
    )
    hidden_all = gather_dp(hidden_mine).reshape(-1, group)
    lows = [gather_dp(v).reshape(-1, group) for v in lows_mine]
    branch_sum = chain_sum(branch_part, 0)
    w_down_grad = branch_sum.astype(full).reshape(w_down.shape)

    normed_grads, alongs = [], []
    for s, weight in enumerate((w_query, w_key, w_value, w_up)):
        right = lows[s] if s < 3 else hidden_all
        part = contract(way_columns(weight), right, 1, 0)
        alongs.append(jnp.sum(part * all_gains[:, s][:, None], axis=0))
        alongs.append(jnp.sum(part * normed[s].astype(full), axis=0))
        part = part.reshape(places, ways, piece, group)
        kept = lax.dynamic_index_in_dim(part, way, 1, keepdims=False)
        if ways == 2:
            given = lax.dynamic_index_in_dim(part, 1 - way, 1, keepdims=False).astype(low)
            kept = kept + hid_swap(given, 1).astype(full)
        normed_grads.append(kept.reshape(mine, group))
    weighted = [normed_grads[s] * gains[s] for s in range(STREAMS)]
    means_back = sum_features(jnp.stack(alongs, axis=0)) / width
    gain_parts = [jnp.sum(g * u, axis=1) for g, u in zip(normed_grads, units)]
    stream_grads = [
        (weighted[s] - means_back[2 * s] - units[s] * means_back[2 * s + 1]) * inv_scales[s]
        for s in range(STREAMS)
    ]
    stream_grads[3] = stream_grads[3] + output_grad
    smalls = sum_tokens(jnp.concatenate([mixer_grad_part, jnp.stack(gain_parts, axis=0)], axis=0))
    smalls = gather_ways(smalls.reshape(-1, places, piece), 2).reshape(-1, feats)

    split = jnp.stack([v.astype(low).reshape(places, piece, group) for v in stream_grads], axis=1)
    split = exchange(split)
    split = jnp.concatenate([split[p] for p in range(places)], axis=-1).astype(full)
    mix_layers = mix_all.reshape(STREAMS, HIST, total_tokens)
    history_grad = sum(mix_layers[s][:, None] * split[s][None] for s in range(STREAMS))
    history_grad = history_grad.swapaxes(1, 2)
    mix_parts = jnp.concatenate(
        [jnp.sum(split[s][None] * stored.astype(full), axis=1) for s in range(STREAMS)], axis=0
    )
    mix_parts = mix_parts.reshape(n_mix, dp * hid, block).transpose(1, 0, 2)

    wide = w_query.shape[1] // ways
    pairs = [(normed[3], hidden_all[i : i + wide]) for i in range(0, hidden_all.shape[0], wide)]
    pairs += [(normed[s], lows[s]) for s in range(3)]
    pairs += [(attended, output_low[i : i + wide]) for i in range(0, width, wide)]
    parts = [contract(left, right, 1, 1).astype(low) for left, right in pairs]
    late_part = jnp.concatenate(parts, axis=0)
    late_part, mix_parts, smalls = lax.optimization_barrier((late_part, mix_parts, smalls))
    mix_parts = lax.all_to_all(mix_parts, ("dp", "hid"), split_axis=0, concat_axis=0, tiled=True)
    mix_grad = jnp.sum(mix_parts, axis=0).T
    w_mixer_grad = smalls[:n_inner].T
    norm_gains_grad = smalls[n_inner:].T
    late_sum = chain_sum(late_part, 1).reshape(ways, -1, feats, wide)
    w_up_grad, w_query_grad, w_key_grad, w_value_grad, w_out_grad = assemble(late_sum, w_up)

    return (
        block_output,
        mix_next,
        history_grad,
        mix_grad,
        norm_gains_grad,
        w_query_grad,
        w_key_grad,
        w_value_grad,
        w_out_grad,
        w_up_grad,
        w_down_grad,
        w_mixer_grad,
        mixer_out_grad,
        sum_grad,
    )


def solution(mesh):
    everywhere = ("dp", "hid")
    placed = (
        P(None, None, everywhere),
        P(everywhere, None),
        P(everywhere),
        P("dp", None),
        P("dp", None),
        P("dp", None),
        P("dp", None),
        P("dp", None),
        P("dp", None),
        P("dp", None),
        P("dp", None),
        P(),
        P(),
        P(None, everywhere),
        P(everywhere, None),
    )
    return jax.shard_map(
        local,
        mesh=mesh,
        in_specs=placed,
        out_specs=(
            P(None, everywhere),
            P(everywhere, None),
            P(None, None, everywhere),
            P(everywhere, None),
            P("dp", None),
            P("dp", None),
            P("dp", None),
            P("dp", None),
            P("dp", None),
            P("dp", None),
            P("dp", None),
            P("dp", None),
            P(),
            P(),
        ),
        check_vma=False,
    )
```

```python
import functools
import math

import jax
import jax.numpy as jnp
from jax import lax
from jax.experimental import pallas as pl
from jax.experimental.pallas import tpu as pltpu
from jax.sharding import PartitionSpec as P

HEADS = 16
HEAD = 128
ROT = 32
HIST = 8
STREAMS = 4
CORES = 2
CHUNK = 1 << 15
SLACK = 6
TILE = 128
VMEM = 52 << 20

highest = lax.Precision.HIGHEST
rope_base = 10000.0
low = jnp.bfloat16
full = jnp.float32


def contract(left, right, left_dim, right_dim):
    return lax.dot_general(
        left, right, (((left_dim,), (right_dim,)), ((), ())), preferred_element_type=full
    )


def contract_high(left, right, left_dim, right_dim):
    return lax.dot_general(
        left,
        right,
        (((left_dim,), (right_dim,)), ((), ())),
        precision=highest,
        preferred_element_type=full,
    )


def batched(left, right, left_dim, right_dim):
    return lax.dot_general(
        left, right, (((left_dim,), (right_dim,)), ((0,), (0,))), preferred_element_type=full
    )


def gelu_exact(values_in):
    return jax.nn.gelu(values_in, approximate=False)


def core_swap(values_in):
    size = lax.axis_size("dp")
    return lax.ppermute(values_in, "dp", [(i, i ^ 1) for i in range(size)])


def outer_shift(values_in, step):
    size = lax.axis_size("dp")
    outer = size // CORES
    pairs = [
        (o * CORES + c, ((o + step) % outer) * CORES + c) for o in range(outer) for c in range(CORES)
    ]
    return lax.ppermute(values_in, "dp", pairs)


def hid_swap(values_in, bit):
    size = lax.axis_size("hid")
    return lax.ppermute(values_in, "hid", [(i, i ^ bit) for i in range(size)])


def ordered(first, values_in, other, axis):
    return jnp.stack(
        [jnp.where(first, values_in, other), jnp.where(first, other, values_in)], axis=axis
    )


def take(values_in, index):
    return lax.dynamic_index_in_dim(values_in, index, 0, keepdims=False)


def put(target, values_in, index):
    return lax.dynamic_update_index_in_dim(target, values_in, index, 0)


def split_ways():
    return 2 if HEADS // lax.axis_size("dp") >= 2 else 1


def gather_ways(values_in, axis):
    if split_ways() == 1:
        return jnp.expand_dims(values_in, axis)
    return ordered(lax.axis_index("hid") % 2 == 0, values_in, hid_swap(values_in, 1), axis)


def gather_dp(values_in):
    size = lax.axis_size("dp")
    outer = size // CORES
    me = lax.axis_index("dp")
    mine, core = me // CORES, me % CORES
    if outer == 2:
        held = ordered(mine == 0, values_in, outer_shift(values_in, 1), 0)
    else:
        held = jnp.zeros((outer,) + values_in.shape, values_in.dtype)
        held = put(held, values_in, mine)
        for step in range(1, outer):
            held = put(held, outer_shift(values_in, step), (mine - step) % outer)
    pair = ordered(core == 0, held, core_swap(held), 1)
    return pair.reshape((size,) + values_in.shape)


def gather_outer(values_in):
    steps = range(1, lax.axis_size("dp") // CORES)
    return [values_in] + [outer_shift(values_in, step) for step in steps]


def gather_cores(held):
    return [v for h in held for v in (h, core_swap(h))]


def gather_turns(values_in):
    return gather_cores(gather_outer(values_in))


def turn_source(turn):
    outer, me = lax.axis_size("dp") // CORES, lax.axis_index("dp")
    there = (me // CORES + outer - turn // CORES) % outer
    return there * CORES + (me + turn) % CORES


def turn_of(index):
    outer, me = lax.axis_size("dp") // CORES, lax.axis_index("dp")
    step = (me // CORES + outer - index // CORES) % outer
    return step * CORES + (me + index) % CORES


def sum_features(values_in):
    if split_ways() == 2:
        values_in = values_in + hid_swap(values_in, 1)
    parts = gather_dp(values_in)
    total = parts[0]
    for i in range(1, parts.shape[0]):
        total = total + parts[i]
    return total


def sum_tokens(values_in):
    size = lax.axis_size("hid")
    bit = split_ways()
    while bit < size:
        values_in = values_in + hid_swap(values_in, bit)
        bit *= 2
    return values_in


def gather_all(values_in):
    count = lax.axis_size("dp") * lax.axis_size("hid")
    copies = jnp.broadcast_to(values_in[None], (count,) + values_in.shape)
    held = lax.all_to_all(copies, ("dp", "hid"), split_axis=0, concat_axis=0, tiled=True)
    return held.transpose(1, 0, 2).reshape(values_in.shape[0], -1)


def scatter_dp(make):
    size = lax.axis_size("dp")
    outer = size // CORES
    me = lax.axis_index("dp")
    mine, core = me // CORES, me % CORES
    total = None
    for step in list(range(1, outer)) + [0]:
        there = (mine + step) % outer
        away = core_swap(make(there * CORES + 1 - core).astype(low))
        block = make(there * CORES + core) + away.astype(full)
        if step:
            block = outer_shift(block.astype(low), step).astype(full)
        total = block if total is None else total + block
    return total


def exchange(values_in):
    ways, size = split_ways(), lax.axis_size("hid")
    groups = None
    if ways > 1:
        groups = [[t * ways + w for t in range(size // ways)] for w in range(ways)]
    return lax.all_to_all(
        values_in, "hid", split_axis=0, concat_axis=0, tiled=True, axis_index_groups=groups
    )


def chain_kernel(ways, places, blocks, n_operands, depth, *refs):
    operand_refs, refs = refs[:n_operands], refs[n_operands:]
    out_ref, refs = refs[0], refs[1:]
    operands, refs = refs[:n_operands], refs[n_operands:]
    (
        own,
        landed,
        sums,
        fetched,
        up_send,
        up_recv,
        down_send,
        down_recv,
        side_send,
        side_recv,
        kept,
    ) = refs
    count = sums.shape[0]
    per_tile = TILE // depth
    last = places - 1
    me = lax.axis_index("hid")
    if ways == 2:
        place, way = me // 2, me % 2
        above, below, beside = me + 2, me - 2, me + 1 - 2 * way
    else:
        odd, half = me % 2, places // 2
        place, way = (1 - odd) * (me // 2) + odd * (last - me // 2), 0
        turn_up = (place + 1) // half
        turn_down = (place - 1 + places) // half - 2
        above = (1 - turn_up) * 2 * (place + 1) + turn_up * (2 * (last - place - 1) + 1)
        below = (1 - turn_down) * 2 * (place - 1) + turn_down * (2 * (last - place + 1) + 1)
        beside = me

    def remote(source, target, send, recv, device):
        return pltpu.make_async_remote_copy(
            src_ref=source,
            dst_ref=target,
            send_sem=send,
            recv_sem=recv,
            device_id={"hid": device},
            device_id_type=pl.DeviceIdType.MESH,
        )

    def up_copy(i):
        return remote(sums.at[i], landed.at[i], up_send, up_recv.at[i], above)

    def down_copy(source, i):
        return remote(source, out_ref.at[way, i], down_send, down_recv.at[i], below)

    def side_copy(source, i):
        return remote(source, out_ref.at[way, i], side_send, side_recv, beside)

    def fetch(n):
        return pltpu.make_async_copy(operand_refs[n], operands[n], fetched.at[n])

    for n in range(n_operands):
        fetch(n).start()

    barrier = pltpu.get_barrier_semaphore()

    def greet(device):
        pl.semaphore_signal(
            barrier, inc=1, device_id={"hid": device}, device_id_type=pl.DeviceIdType.MESH
        )

    @pl.when(place > 0)
    def _():
        greet(below)

    @pl.when(place < last)
    def _():
        greet(above)

    if ways == 2:
        greet(beside)
    met = jnp.where(place > 0, 1, 0) + jnp.where(place < last, 1, 0) + (ways - 1)
    pl.semaphore_wait(barrier, met)

    def compute(tile):
        seen, first = set(), 0
        for rows, segments in blocks:
            start = first
            first = first + rows // TILE
            fresh = [n for seg in segments for n in (seg[0], seg[2])]
            fresh = [n for n in dict.fromkeys(fresh) if n not in seen]
            seen.update(fresh)

            @pl.when(tile == start)
            def _(fresh=fresh):
                for n in fresh:
                    fetch(n).wait()

            @pl.when((tile >= start) & (tile < first))
            def _(start=start, segments=segments):
                column = 0
                for left, left_row, right, right_row, size in segments:
                    row = pl.multiple_of(left_row + (tile - start) * TILE, TILE)
                    own[:, column : column + size] = lax.dot_general(
                        operands[left][pl.ds(row, TILE), :],
                        operands[right][right_row : right_row + size, :],
                        (((1,), (1,)), ((), ())),
                        preferred_element_type=full,
                    )
                    column += size

    def upward(i):
        @pl.when(i % per_tile == 0)
        def _():
            compute(i // per_tile)

        mine = own[pl.ds(pl.multiple_of(i % per_tile * depth, depth), depth), :]

        @pl.when(place == 0)
        def _():
            sums[i] = mine.astype(low)
            up_copy(i).start()

        @pl.when(place > 0)
        def _():
            up_copy(i).wait_recv()
            sums[i] = (landed[i].astype(full) + mine).astype(low)

            @pl.when(place < last)
            def _():
                up_copy(i).start()

            @pl.when(place == last)
            def _():
                down_copy(sums.at[i], i).start()
                if ways == 2:
                    side_copy(sums.at[i], i).start()
                pltpu.make_async_copy(sums.at[i], out_ref.at[way, i], kept).start()

    def downward(i):
        down_copy(sums.at[i], i).wait_recv()

        @pl.when(place > 0)
        def _():
            down_copy(out_ref.at[way, i], i).start()

        if ways == 2:
            side_copy(out_ref.at[way, i], i).start()

    lag = SLACK * (last - place) + 2

    def step(i, carry):
        @pl.when(i < count)
        def _():
            upward(i)

        behind = i - lag

        @pl.when((behind >= 0) & (behind < count) & (place < last))
        def _():
            downward(behind)

        return carry

    lax.fori_loop(0, count + SLACK * last + 2, step, 0)

    @pl.when(place < last)
    def _():
        remote(sums, landed, up_send, kept, above).wait_send()

    @pl.when(place > 0)
    def _():
        remote(sums, out_ref.at[way], down_send, kept, below).wait_send()

    @pl.when(place == last)
    def _():
        pltpu.make_async_copy(sums, out_ref.at[way], kept).wait()

    if ways == 2:
        remote(sums, out_ref.at[way], side_send, kept, beside).wait_send()
        remote(sums, out_ref.at[1 - way], kept, side_recv, beside).wait_recv()


def chain_sum(operands, blocks, collective_id):
    ways, size = split_ways(), lax.axis_size("hid")
    columns = sum(seg[4] for seg in blocks[0][1])
    rows = sum(block[0] for block in blocks)
    depth = max(16, CHUNK // columns)
    count = rows // depth
    tokens = operands[0].shape[1]
    return pl.pallas_call(
        functools.partial(chain_kernel, ways, size // ways, blocks, len(operands), depth),
        out_shape=jax.ShapeDtypeStruct((ways, count, depth, columns), low),
        in_specs=[pl.BlockSpec(memory_space=pl.ANY)] * len(operands),
        out_specs=pl.BlockSpec(memory_space=pl.ANY),
        scratch_shapes=[pltpu.VMEM(v.shape, low) for v in operands]
        + [
            pltpu.VMEM((TILE, columns), full),
            pltpu.VMEM((count, depth, columns), low),
            pltpu.VMEM((count, depth, columns), low),
            pltpu.SemaphoreType.DMA((len(operands),)),
            pltpu.SemaphoreType.DMA,
            pltpu.SemaphoreType.DMA((count,)),
            pltpu.SemaphoreType.DMA,
            pltpu.SemaphoreType.DMA((count,)),
            pltpu.SemaphoreType.DMA,
            pltpu.SemaphoreType.DMA,
            pltpu.SemaphoreType.DMA,
        ],
        compiler_params=pltpu.CompilerParams(
            collective_id=collective_id, has_side_effects=True, vmem_limit_bytes=60 << 20
        ),
        cost_estimate=pl.CostEstimate(
            flops=2 * rows * columns * tokens,
            bytes_accessed=300 * rows * columns,
            transcendentals=0,
        ),
    )(*operands)


def chain_sums(operands, blocks, collective_id):
    groups, held, size = [[]], set(), 0
    for rows, segments in blocks:
        used = {n for seg in segments for n in (seg[0], seg[2])}
        more = sum(2 * operands[n].size for n in used - held)
        more += 4 * rows * sum(seg[4] for seg in segments)
        if groups[-1] and size + more > VMEM:
            groups.append([])
            held, size = set(), 0
            more = sum(2 * operands[n].size for n in used)
            more += 4 * rows * sum(seg[4] for seg in segments)
        groups[-1].append((rows, segments))
        held |= used
        size += more
    totals = []
    for i, group in enumerate(groups):
        used = sorted({n for _, segments in group for seg in segments for n in (seg[0], seg[2])})
        place = {n: k for k, n in enumerate(used)}
        own = [
            (rows, [(place[a], b, place[c], d, e) for a, b, c, d, e in segments])
            for rows, segments in group
        ]
        total = chain_sum([operands[n] for n in used], own, collective_id + i)
        totals.append(total.reshape(total.shape[0], -1, total.shape[3]))
    return totals[0] if len(totals) == 1 else jnp.concatenate(totals, axis=1)


def assemble_kernel(ways, dp, own_ref, *refs):
    halves, (up_ref, *head_refs, out_ref) = refs[:ways], refs[ways:]
    rows, wide = own_ref.shape[2:]
    size = up_ref.shape[1] // dp // ways
    blocks = dp * size // wide
    own = wide // dp
    feats = out_ref.shape[1] // dp
    for d in range(dp):
        turn = turn_of(d)
        for w in range(ways):
            start = turn * size
            lanes = pl.ds(pl.multiple_of(start % wide, size), size)
            place = (d * ways + w) * size
            up_ref[:, place : place + size] = own_ref[w, start // wide, :, lanes].astype(full)
            for s, ref in enumerate(head_refs):
                lanes = pl.ds(pl.multiple_of(turn * own, own), own)
                place = (d * ways + w) * own
                ref[:, place : place + own] = own_ref[w, blocks + s, :, lanes].astype(full)
        start = turn * feats
        lanes = pl.ds(pl.multiple_of(start % wide, feats), feats)
        for w in range(ways):

            @pl.when(start // wide == w)
            def _(w=w, d=d, lanes=lanes):
                out_ref[:, d * feats : (d + 1) * feats] = halves[w][0, 0, :, lanes].astype(full)


def assemble(total, w_up):
    ways, dp = split_ways(), lax.axis_size("dp")
    blocks, rows, wide = total.shape[1:]
    depth = min(64, rows // ways)
    share = rows // ways // depth

    def half_map(half):
        return lambda i: (i // share, blocks - 1, half * share + i % share, 0)

    widths = [w_up.shape[1]] + [ways * wide] * 4
    return pl.pallas_call(
        functools.partial(assemble_kernel, ways, dp),
        grid=(rows // depth,),
        out_shape=[jax.ShapeDtypeStruct((rows, n), full) for n in widths],
        in_specs=[pl.BlockSpec((ways, blocks, depth, wide), lambda i: (0, 0, i, 0))]
        + [pl.BlockSpec((1, 1, depth, wide), half_map(half)) for half in range(ways)],
        out_specs=[pl.BlockSpec((depth, n), lambda i: (i, 0)) for n in widths],
        compiler_params=pltpu.CompilerParams(vmem_limit_bytes=48 << 20),
        cost_estimate=pl.CostEstimate(
            flops=0, bytes_accessed=6 * total.size, transcendentals=0
        ),
    )(total, *[total] * ways)


def unturn_kernel(dp, own_ref, out_ref):
    size = out_ref.shape[1] // dp
    for d in range(dp):
        lanes = pl.ds(pl.multiple_of(turn_of(d) * size, size), size)
        out_ref[:, d * size : (d + 1) * size] = own_ref[:, lanes].astype(full)


def unturn(total):
    rows, columns = total.shape
    depth = 256
    return pl.pallas_call(
        functools.partial(unturn_kernel, lax.axis_size("dp")),
        grid=(rows // depth,),
        out_shape=jax.ShapeDtypeStruct((rows, columns), full),
        in_specs=[pl.BlockSpec((depth, columns), lambda i: (i, 0))],
        out_specs=pl.BlockSpec((depth, columns), lambda i: (i, 0)),
        cost_estimate=pl.CostEstimate(
            flops=0, bytes_accessed=6 * total.size, transcendentals=0
        ),
    )(total)


def to_owner(values_in):
    dp, hid, ways = lax.axis_size("dp"), lax.axis_size("hid"), split_ways()
    index = lax.axis_index("dp") * ways + lax.axis_index("hid") % ways
    mine = lax.dynamic_index_in_dim(values_in, index, 1, keepdims=False)
    pairs = [
        (d * hid + t * ways + w, (t * dp + d) * ways + w)
        for d in range(dp)
        for t in range(hid // ways)
        for w in range(ways)
    ]
    return lax.ppermute(mine, ("dp", "hid"), pairs)


def rotate(values_in, cosine, sine):
    half = cosine.shape[1]
    front, back = values_in[:, :half], values_in[:, half : 2 * half]
    return jnp.concatenate(
        [
            front * cosine - back * sine,
            back * cosine + front * sine,
            values_in[:, 2 * half :],
        ],
        axis=1,
    )


def local(
    history,
    mix,
    segment_ids,
    norm_gains,
    w_query,
    w_key,
    w_value,
    w_out,
    w_up,
    w_down,
    w_mixer,
    mixer_out,
    mix_static,
    out_cotangent,
    mix_cotangent,
):
    dp, hid, ways = lax.axis_size("dp"), lax.axis_size("hid"), split_ways()
    places = hid // ways
    my_hid = lax.axis_index("hid")
    place, way = my_hid // ways, my_hid % ways
    block = segment_ids.shape[0]
    total_tokens = block * dp * hid
    row = total_tokens // dp
    group = total_tokens // places
    rows = group // row
    piece = history.shape[2]
    mine = piece * places
    feats = piece * hid
    width = feats * dp
    heads = HEADS // dp // ways
    n_mix = mix.shape[1]
    n_cot = mix_cotangent.shape[1]

    def by_place(values_in):
        return jnp.stack(
            [values_in[..., p * group : (p + 1) * group] for p in range(places)], axis=0
        )

    stored = history.swapaxes(1, 2)
    mix_all = gather_all(mix.T)
    own_means, own_devs, deviations = [], [], []
    for s in range(STREAMS):
        total = mix_all[s * HIST] * stored[0].astype(full)
        for j in range(1, HIST):
            total = total + mix_all[s * HIST + j] * stored[j].astype(full)
        own_means.append(jnp.mean(total, axis=0))
        off = total - own_means[s]
        own_devs.append(jnp.sum(off * off, axis=0))
        deviations.append(off.astype(low))
    moments = exchange(by_place(jnp.stack(own_means + own_devs, axis=0)))
    deviations[3] = exchange(by_place(deviations[3]))
    for s in range(3):
        deviations[s] = exchange(by_place(deviations[s]))
    def join_moments(mean_parts, dev_parts, size):
        mean = jnp.mean(mean_parts, axis=0)
        spread = size * jnp.sum(jnp.square(mean_parts - mean), axis=0)
        return mean, jnp.sum(dev_parts, axis=0) + spread

    block_means = moments[:, :STREAMS]
    joined = join_moments(block_means, moments[:, STREAMS:], piece)
    joined = gather_dp(gather_ways(jnp.concatenate(joined, axis=0), 0))
    joined = joined.reshape((dp * ways,) + joined.shape[2:])
    means, variance = join_moments(joined[:, :STREAMS], joined[:, STREAMS:], mine)
    inv_scales = lax.rsqrt(variance / width + 1e-05)
    all_means = gather_ways(block_means, 1)

    table = jnp.concatenate([mix_cotangent.T, segment_ids.astype(full)[None]], axis=0)
    table = lax.dynamic_slice_in_dim(gather_all(table), place * group, group, 1)
    cot_t = table[:n_cot]
    ids = table[-1].reshape(rows, row)

    there = jnp.arange(row, dtype=jnp.int32)
    same_doc = ids[:, :, None] == ids[:, None, :]
    doc_start = jnp.min(jnp.where(same_doc, there[None, None], row), axis=2)
    position = (there[None] - doc_start).astype(full).reshape(group)
    visible = same_doc & (there[None, None] <= there[None, :, None])
    frequency = rope_base ** (-jnp.arange(ROT // 2, dtype=full) * 2.0 / ROT)
    angle = frequency[:, None] * position[None, :]
    cosine, sine = jnp.cos(angle)[None], jnp.sin(angle)[None]

    def own_rows(values_in):
        parts = values_in.reshape((places, ways, piece) + values_in.shape[1:])
        part = lax.dynamic_index_in_dim(parts, way, 1, keepdims=False)
        return part.reshape((mine,) + values_in.shape[1:])

    def all_rows(values_in):
        parts = values_in.reshape((places, piece) + values_in.shape[1:])
        return gather_ways(parts, 1).reshape((feats,) + values_in.shape[1:])

    def unit(values_in, block_mean, s):
        return (values_in.astype(full) + (block_mean - means[s])[..., None, :]) * inv_scales[s]

    own_gains = own_rows(norm_gains).astype(full)
    gains = [own_gains[:, s][:, None] for s in range(STREAMS)]
    all_gains = norm_gains.astype(full)
    units = [
        unit(deviations[s], block_means[:, s], s).reshape(mine, group) for s in range(STREAMS)
    ]
    normed = []
    for s in range(STREAMS):
        both = unit(gather_ways(deviations[s], 1), all_means[:, :, s], s).reshape(feats, group)
        normed.append((both * all_gains[:, s][:, None]).astype(low))
    residual = (deviations[3].astype(full) + block_means[:, 3][:, None]).reshape(mine, group)

    def project(weight, left):
        columns = weight.shape[1] // dp // ways

        def make(index):
            start = (index * ways + way) * columns
            part = lax.dynamic_slice_in_dim(weight, start, columns, 1)
            return contract(part, left, 0, 0)

        return scatter_dp(make)

    def way_columns(weight):
        if ways == 1:
            return weight
        size = weight.shape[1] // dp // ways
        parts = [weight[:, i * size : (i + 1) * size] for i in range(dp * ways)]
        pairs = zip(parts[::2], parts[1::2])
        return jnp.concatenate([jnp.where(way == 0, a, b) for a, b in pairs], axis=1)

    def way_rows(weight):
        size = weight.shape[0] // ways
        return lax.dynamic_slice_in_dim(weight, way * size, size, 0)

    def by_head(values_in):
        return values_in.reshape(heads, HEAD, group)

    hidden = project(w_up, normed[3])
    queries = rotate(by_head(project(w_query, normed[0])), cosine, sine).astype(low)
    keys = rotate(by_head(project(w_key, normed[1])), cosine, sine).astype(low)
    values = by_head(project(w_value, normed[2])).astype(low)
    cotangent, queries = lax.optimization_barrier((out_cotangent, queries))
    upstream = exchange(by_place(cotangent.T)).reshape(mine, group)

    def turned(weight, stride, offset, size):
        starts = [turn_source(turn) * stride + offset for turn in range(dp)]
        parts = [lax.dynamic_slice_in_dim(weight, start, size, 1) for start in starts]
        return jnp.concatenate(parts, axis=1)

    n_head = heads * HEAD
    n_units = hidden.shape[0]
    out_rows, down_rows = way_rows(w_out), way_rows(w_down)
    turned_weights = (
        turned(w_query, ways * n_head, way * n_head, n_head),
        turned(w_key, ways * n_head, way * n_head, n_head),
        turned(w_value, ways * n_head, way * n_head, n_head),
        turned(w_up, ways * n_units, way * n_units, n_units),
        turned(out_rows, feats, 0, feats),
        turned(down_rows, feats, 0, feats),
    )
    hidden, turned_weights = lax.optimization_barrier((hidden, turned_weights))

    def by_row(values_in):
        if rows == 1:
            return values_in
        return (
            values_in.reshape(heads, HEAD, rows, row)
            .transpose(0, 2, 1, 3)
            .reshape(heads * rows, HEAD, row)
        )

    def from_row(values_in):
        if rows == 1:
            return values_in
        return (
            values_in.reshape(heads, rows, HEAD, row)
            .transpose(0, 2, 1, 3)
            .reshape(heads, HEAD, group)
        )

    q_rows, k_rows, v_rows = by_row(queries), by_row(keys), by_row(values)
    score_scale = 1.0 / math.sqrt(HEAD)
    scores = batched(q_rows, k_rows, 1, 1) * score_scale
    mask = jnp.broadcast_to(visible[None], (heads, rows, row, row)).reshape(scores.shape)
    scores = jnp.where(mask, scores, -1e30)
    probs = jax.nn.softmax(scores, axis=-1)
    probs_low = probs.astype(low)
    attended = from_row(batched(v_rows, probs_low, 2, 2).astype(low)).reshape(heads * HEAD, group)

    active, hidden_pull = jax.vjp(gelu_exact, hidden)
    active = active.astype(low)
    (slope,) = hidden_pull(jnp.ones_like(hidden))

    def make_out(index):
        start = index * feats
        left = lax.dynamic_slice_in_dim(out_rows, start, feats, 1)
        other = lax.dynamic_slice_in_dim(down_rows, start, feats, 1)
        return contract(left, attended, 0, 0) + contract(other, active, 0, 0)

    branches = scatter_dp(make_out).reshape(places, ways, piece, group)
    kept = lax.dynamic_index_in_dim(branches, way, 1, keepdims=False)
    if ways == 2:
        given = lax.dynamic_index_in_dim(branches, 1 - way, 1, keepdims=False).astype(low)
        kept = kept + hid_swap(given, 1).astype(full)
    output = residual + kept.reshape(mine, group)
    output, upstream = lax.optimization_barrier((output, upstream))
    upstream = upstream.astype(full)
    output_rounded = output.astype(low)

    block_output = exchange(output_rounded.reshape(places, piece, group))

    square = jnp.sum(output * output, axis=0, keepdims=True)
    mixer_rows = own_rows(w_mixer)
    mixer_part = contract(mixer_rows, output_rounded, 0, 0)
    sums = sum_features(jnp.concatenate([mixer_part, square], axis=0))
    inv_rms = lax.rsqrt(sums[-1] / width + 1e-06)
    inner_raw = sums[:-1]
    inner_pre = inner_raw * inv_rms
    inner_act, inner_pull = jax.vjp(gelu_exact, inner_pre)
    raw_mix = contract_high(mixer_out, inner_act, 0, 0)
    column = jnp.stack(
        [
            jnp.sum(raw_mix, axis=1),
            jnp.sum(raw_mix * raw_mix, axis=1),
            jnp.sum(cot_t, axis=1),
            jnp.sum(cot_t * raw_mix, axis=1),
        ],
        axis=0,
    )
    act_total = jnp.sum(inner_act, axis=1)
    act_cot = contract_high(inner_act, cot_t, 1, 1)
    act_raw = contract_high(inner_act, raw_mix, 1, 1)
    n_inner = act_total.shape[0]
    flat = sum_tokens(
        jnp.concatenate([column.reshape(-1), act_total, act_cot.reshape(-1), act_raw.reshape(-1)])
    )
    sum_raw, sum_square, sum_grad, sum_grad_raw = flat[: 4 * n_cot].reshape(4, n_cot)
    start = 4 * n_cot
    act_total = flat[start : start + n_inner]
    start += n_inner
    act_cot = flat[start : start + n_inner * n_cot].reshape(n_inner, n_cot)
    start += n_inner * n_cot
    act_raw = flat[start:].reshape(n_inner, n_cot)
    average = sum_raw / total_tokens
    variance_mix = sum_square / total_tokens - average * average
    inv_spread = lax.rsqrt(variance_mix + 1e-05)
    unit_mix = (raw_mix - average[:, None]) * inv_spread[:, None]
    mix_next = mix_static[:, None] + unit_mix
    mix_next = to_owner(mix_next.reshape(n_cot, dp * ways, block)).T
    mean_grad = sum_grad / total_tokens
    sum_grad_unit = inv_spread * (sum_grad_raw - average * sum_grad)
    mean_grad_unit = sum_grad_unit / total_tokens
    raw_grad = inv_spread[:, None] * (
        cot_t - mean_grad[:, None] - unit_mix * mean_grad_unit[:, None]
    )
    act_unit = inv_spread[None, :] * (act_raw - act_total[:, None] * average[None, :])
    mixer_out_grad = inv_spread[None, :] * (
        act_cot - act_total[:, None] * mean_grad[None, :] - act_unit * mean_grad_unit[None, :]
    )
    act_grad = contract_high(mixer_out, raw_grad, 1, 0)
    inner_low = inner_pull(act_grad)[0].astype(low)
    scaled = (output * inv_rms).astype(low)
    mixer_grad_part = contract(inner_low, scaled, 1, 1)
    scaled_grad = contract(mixer_rows, inner_low, 1, 0)
    along = jnp.sum(inner_low.astype(full) * inner_raw, axis=0) / width
    output_grad = upstream + inv_rms * scaled_grad - output * (inv_rms * inv_rms * inv_rms) * along
    output_lows = gather_turns(all_rows(output_grad.astype(low)))

    output_low = jnp.concatenate(output_lows, axis=0)

    hidden_low = (contract(turned_weights[5], output_low, 1, 0) * slope).astype(low)

    attended_grad = contract(turned_weights[4], output_low, 1, 0).astype(low)
    a_rows = by_row(by_head(attended_grad))
    prob_grad = batched(a_rows, v_rows, 1, 1)
    row_total = jnp.sum(probs * prob_grad, axis=-1, keepdims=True)
    score_grad = (probs * (prob_grad - row_total)).astype(low)
    query_grad = from_row(batched(k_rows, score_grad, 2, 2) * score_scale)
    key_grad = from_row(batched(q_rows, score_grad, 2, 1) * score_scale)
    value_grad = from_row(batched(a_rows, probs_low, 2, 1))
    query_low = rotate(query_grad, cosine, -sine).astype(low).reshape(heads * HEAD, group)
    key_low = rotate(key_grad, cosine, -sine).astype(low).reshape(heads * HEAD, group)
    value_low = value_grad.astype(low).reshape(heads * HEAD, group)

    lows_mine = jnp.concatenate([query_low, key_low, value_low], axis=0)
    active_kept, hidden_low, lows_mine = lax.optimization_barrier((active, hidden_low, lows_mine))
    hidden_lows, lows = gather_outer(hidden_low), gather_outer(lows_mine)
    blocks = [(active.shape[0], [(0, 0, 1, 0, width)])]
    branch_sum = chain_sum([active_kept, output_low], blocks, 0)
    branch_sum, block_output, hidden_lows, lows = lax.optimization_barrier(
        (branch_sum, block_output, hidden_lows, lows)
    )
    block_output = block_output.transpose(1, 0, 2).reshape(piece, total_tokens).T
    hidden_lows, lows = gather_cores(hidden_lows), gather_cores(lows)

    normed_grads, alongs, rights = [], [], []
    for s in range(STREAMS):
        if s < 3:
            right = jnp.concatenate([v[s * n_head : (s + 1) * n_head] for v in lows], axis=0)
        else:
            right = jnp.concatenate(hidden_lows, axis=0)
        rights.append(right)
        part = contract(turned_weights[s], right, 1, 0)
        alongs.append(jnp.sum(part * all_gains[:, s][:, None], axis=0))
        alongs.append(jnp.sum(part * normed[s].astype(full), axis=0))
        part = part.reshape(places, ways, piece, group)
        kept = lax.dynamic_index_in_dim(part, way, 1, keepdims=False)
        if ways == 2:
            given = lax.dynamic_index_in_dim(part, 1 - way, 1, keepdims=False).astype(low)
            kept = kept + hid_swap(given, 1).astype(full)
        normed_grads.append(kept.reshape(mine, group))
    weighted = [normed_grads[s] * gains[s] for s in range(STREAMS)]
    means_back = sum_features(jnp.stack(alongs, axis=0)) / width
    gain_parts = [jnp.sum(g * u, axis=1) for g, u in zip(normed_grads, units)]
    stream_grads = [
        (weighted[s] - means_back[2 * s] - units[s] * means_back[2 * s + 1]) * inv_scales[s]
        for s in range(STREAMS)
    ]
    stream_grads[3] = stream_grads[3] + output_grad
    smalls = jnp.concatenate([mixer_grad_part, jnp.stack(gain_parts, axis=0)], axis=0)

    split = jnp.stack([v.astype(low).reshape(places, piece, group) for v in stream_grads], axis=1)
    attended, split, smalls = lax.optimization_barrier((attended, split, smalls))
    split = exchange(split)
    split = jnp.concatenate([split[p] for p in range(places)], axis=-1).astype(full)
    mix_layers = mix_all.reshape(STREAMS, HIST, total_tokens)
    history_grad = sum(mix_layers[s][:, None] * split[s][None] for s in range(STREAMS))
    history_grad = history_grad.swapaxes(1, 2)
    mix_parts = jnp.concatenate(
        [jnp.sum(split[s][None] * stored.astype(full), axis=1) for s in range(STREAMS)], axis=0
    )
    mix_parts = mix_parts.reshape(n_mix, dp * hid, block).transpose(1, 0, 2)

    wide = w_query.shape[1] // ways
    operands = [rights[3]] + rights[:3] + [output_low, normed[3]] + normed[:3] + [attended]
    blocks = [(feats, [(5, 0, 0, i, wide)]) for i in range(0, rights[3].shape[0], wide)]
    blocks += [(feats, [(6 + s, 0, 1 + s, 0, wide)]) for s in range(3)]
    blocks += [(n_head, [(9, 0, 4, i, wide)]) for i in range(0, width, wide)]
    late_sum = chain_sums(operands, blocks, 1)
    late_sum, mix_parts, smalls = lax.optimization_barrier((late_sum, mix_parts, smalls))
    smalls = sum_tokens(smalls)
    smalls = gather_ways(smalls.reshape(-1, places, piece), 2).reshape(-1, feats)
    w_mixer_grad = smalls[:n_inner].T
    norm_gains_grad = smalls[n_inner:].T
    mix_parts = lax.all_to_all(mix_parts, ("dp", "hid"), split_axis=0, concat_axis=0, tiled=True)
    mix_grad = jnp.sum(mix_parts, axis=0).T
    w_down_grad = unturn(branch_sum.reshape(w_down.shape))
    late_sum = late_sum.reshape(ways, -1, feats, wide)
    w_up_grad, w_query_grad, w_key_grad, w_value_grad, w_out_grad = assemble(late_sum, w_up)

    return (
        block_output,
        mix_next,
        history_grad,
        mix_grad,
        norm_gains_grad,
        w_query_grad,
        w_key_grad,
        w_value_grad,
        w_out_grad,
        w_up_grad,
        w_down_grad,
        w_mixer_grad,
        mixer_out_grad,
        sum_grad,
    )


def solution(mesh):
    everywhere = ("dp", "hid")
    placed = (
        P(None, None, everywhere),
        P(everywhere, None),
        P(everywhere),
        P("dp", None),
        P("dp", None),
        P("dp", None),
        P("dp", None),
        P("dp", None),
        P("dp", None),
        P("dp", None),
        P("dp", None),
        P(),
        P(),
        P(None, everywhere),
        P(everywhere, None),
    )
    return jax.shard_map(
        local,
        mesh=mesh,
        in_specs=placed,
        out_specs=(
            P(None, everywhere),
            P(everywhere, None),
            P(None, None, everywhere),
            P(everywhere, None),
            P("dp", None),
            P("dp", None),
            P("dp", None),
            P("dp", None),
            P("dp", None),
            P("dp", None),
            P("dp", None),
            P("dp", None),
            P(),
            P(),
        ),
        check_vma=False,
    )
```

```python
import functools
import math

import jax
import jax.numpy as jnp
from jax import lax
from jax.experimental import pallas as pl
from jax.experimental.pallas import tpu as pltpu
from jax.sharding import PartitionSpec as P

HEADS = 16
HEAD = 128
ROT = 32
HIST = 8
STREAMS = 4
CORES = 2
CHUNK = 1 << 15
SLACK = 6
TILE = 128
VMEM = 52 << 20

highest = lax.Precision.HIGHEST
rope_base = 10000.0
low = jnp.bfloat16
full = jnp.float32


def contract(left, right, left_dim, right_dim):
    return lax.dot_general(
        left, right, (((left_dim,), (right_dim,)), ((), ())), preferred_element_type=full
    )


def contract_high(left, right, left_dim, right_dim):
    return lax.dot_general(
        left,
        right,
        (((left_dim,), (right_dim,)), ((), ())),
        precision=highest,
        preferred_element_type=full,
    )


def batched(left, right, left_dim, right_dim):
    return lax.dot_general(
        left, right, (((left_dim,), (right_dim,)), ((0,), (0,))), preferred_element_type=full
    )


def gelu_exact(values_in):
    return jax.nn.gelu(values_in, approximate=False)


def core_swap(values_in):
    size = lax.axis_size("dp")
    return lax.ppermute(values_in, "dp", [(i, i ^ 1) for i in range(size)])


def outer_shift(values_in, step):
    size = lax.axis_size("dp")
    outer = size // CORES
    pairs = [
        (o * CORES + c, ((o + step) % outer) * CORES + c) for o in range(outer) for c in range(CORES)
    ]
    return lax.ppermute(values_in, "dp", pairs)


def hid_swap(values_in, bit):
    size = lax.axis_size("hid")
    return lax.ppermute(values_in, "hid", [(i, i ^ bit) for i in range(size)])


def ordered(first, values_in, other, axis):
    return jnp.stack(
        [jnp.where(first, values_in, other), jnp.where(first, other, values_in)], axis=axis
    )


def take(values_in, index):
    return lax.dynamic_index_in_dim(values_in, index, 0, keepdims=False)


def put(target, values_in, index):
    return lax.dynamic_update_index_in_dim(target, values_in, index, 0)


def split_ways():
    return 2 if HEADS // lax.axis_size("dp") >= 2 else 1


def gather_ways(values_in, axis):
    if split_ways() == 1:
        return jnp.expand_dims(values_in, axis)
    return ordered(lax.axis_index("hid") % 2 == 0, values_in, hid_swap(values_in, 1), axis)


def gather_dp(values_in):
    size = lax.axis_size("dp")
    outer = size // CORES
    me = lax.axis_index("dp")
    mine, core = me // CORES, me % CORES
    if outer == 2:
        held = ordered(mine == 0, values_in, outer_shift(values_in, 1), 0)
    else:
        held = jnp.zeros((outer,) + values_in.shape, values_in.dtype)
        held = put(held, values_in, mine)
        for step in range(1, outer):
            held = put(held, outer_shift(values_in, step), (mine - step) % outer)
    pair = ordered(core == 0, held, core_swap(held), 1)
    return pair.reshape((size,) + values_in.shape)


def gather_outer(values_in):
    steps = range(1, lax.axis_size("dp") // CORES)
    return [values_in] + [outer_shift(values_in, step) for step in steps]


def gather_cores(held):
    return [v for h in held for v in (h, core_swap(h))]


def gather_turns(values_in):
    return gather_cores(gather_outer(values_in))


def turn_source(turn):
    outer, me = lax.axis_size("dp") // CORES, lax.axis_index("dp")
    there = (me // CORES + outer - turn // CORES) % outer
    return there * CORES + (me + turn) % CORES


def turn_of(index):
    outer, me = lax.axis_size("dp") // CORES, lax.axis_index("dp")
    step = (me // CORES + outer - index // CORES) % outer
    return step * CORES + (me + index) % CORES


def sum_features(values_in):
    if split_ways() == 2:
        values_in = values_in + hid_swap(values_in, 1)
    parts = gather_dp(values_in)
    total = parts[0]
    for i in range(1, parts.shape[0]):
        total = total + parts[i]
    return total


def sum_tokens(values_in):
    size = lax.axis_size("hid")
    bit = split_ways()
    while bit < size:
        values_in = values_in + hid_swap(values_in, bit)
        bit *= 2
    return values_in


def gather_all(values_in):
    count = lax.axis_size("dp") * lax.axis_size("hid")
    copies = jnp.broadcast_to(values_in[None], (count,) + values_in.shape)
    held = lax.all_to_all(copies, ("dp", "hid"), split_axis=0, concat_axis=0, tiled=True)
    return held.transpose(1, 0, 2).reshape(values_in.shape[0], -1)


def scatter_dp(make):
    size = lax.axis_size("dp")
    outer = size // CORES
    me = lax.axis_index("dp")
    mine, core = me // CORES, me % CORES
    total = None
    for step in list(range(1, outer)) + [0]:
        there = (mine + step) % outer
        away = core_swap(make(there * CORES + 1 - core).astype(low))
        block = make(there * CORES + core) + away.astype(full)
        if step:
            block = outer_shift(block.astype(low), step).astype(full)
        total = block if total is None else total + block
    return total


def exchange(values_in):
    ways, size = split_ways(), lax.axis_size("hid")
    groups = None
    if ways > 1:
        groups = [[t * ways + w for t in range(size // ways)] for w in range(ways)]
    return lax.all_to_all(
        values_in, "hid", split_axis=0, concat_axis=0, tiled=True, axis_index_groups=groups
    )


def forward_kernel(dims, *refs):
    places, piece, group, n_head, n_units = dims
    (send_ref, mom_ref, gains_ref, query_ref, key_ref, value_ref, up_ref), refs = refs[:7], refs[7:]
    (
        normed_ref,
        own_ref,
        shift_ref,
        active_ref,
        slope_ref,
        heads_ref,
        turned_ref,
        turned_up_ref,
    ), refs = refs[:8], refs[8:]
    (
        devs,
        moms,
        joins,
        weights,
        core_out,
        core_in,
        outer_out,
        outer_in,
        mom_send,
        mom_recv,
        dev_send,
        dev_recv,
        way_send,
        way_recv,
        pair_send,
        pair_recv,
        join_send,
        join_recv,
        weight_sem,
        turned_sem,
        core_send,
        core_recv,
        outer_send,
        outer_recv,
    ) = refs
    count = weights.shape[0]
    ups = n_units // n_head
    index, hid = lax.axis_index("dp"), lax.axis_index("hid")
    outer, core = index // 2, index % 2
    place, way = hid // 2, hid % 2
    me = index * 2 + way
    partner = {"hid": hid + 1 - 2 * way}
    core_peer = {"dp": index + 1 - 2 * core}
    outer_peer = {"dp": (index + 2) % 4}

    def remote(source, target, send, recv, device):
        return pltpu.make_async_remote_copy(
            src_ref=source,
            dst_ref=target,
            send_sem=send,
            recv_sem=recv,
            device_id=device,
            device_id_type=pl.DeviceIdType.MESH,
        )

    def peer(k):
        return (place + k) % places

    def z_device(k):
        return {"hid": peer(k) * 2 + way}

    others = [(i, j) for i in range(4) for j in range(2) if i or j]

    def join_device(i, j):
        return {"dp": (index + i) % 4, "hid": place * 2 + (way + j) % 2}

    def weight_copy(unit, t):
        there = (1 - outer if t < 2 else outer) * 2 + (core if t % 2 else 1 - core)
        block = there * 2 + way
        if unit < ups:
            source, start = up_ref, block * n_units + unit * n_head
        else:
            source, start = (query_ref, key_ref, value_ref)[unit - ups], block * n_head
        start = pl.multiple_of(start, n_head)
        return pltpu.make_async_copy(
            source.at[:, pl.ds(start, n_head)], weights.at[unit, t], weight_sem.at[unit]
        )

    for unit in range(count):
        for t in range(4):
            weight_copy(unit, t).start()

    barrier = pltpu.get_barrier_semaphore()

    def greet(device):
        pl.semaphore_signal(barrier, inc=1, device_id=device, device_id_type=pl.DeviceIdType.MESH)

    for k in range(1, places):
        greet(z_device(k))
    for i, j in others:
        greet(join_device(i, j))
    pl.semaphore_wait(barrier, places - 1 + len(others))

    def mom_copy(k, sender, target):
        return remote(
            mom_ref.at[target], moms.at[way, sender], mom_send, mom_recv.at[sender], z_device(k)
        )

    def dev_copy(s, k, sender, target):
        return remote(
            send_ref.at[target, s],
            devs.at[s, way, sender],
            dev_send,
            dev_recv.at[s, sender],
            z_device(k),
        )

    for k in range(1, places):
        mom_copy(k, place, peer(k)).start()
    for s in (3, 0, 1, 2):
        for k in range(1, places):
            dev_copy(s, k, place, peer(k)).start()
    moms[way, place] = mom_ref[place]
    for s in range(STREAMS):
        devs[s, way, place] = send_ref[place, s]

    def way_copy(source, s, q):
        return remote(source, devs.at[s, way, q], way_send, way_recv.at[s], partner)

    def forward(s):
        way_copy(send_ref.at[place, s], s, place).start()
        for k in range(1, places):
            q = peer(k)
            dev_copy(s, k, q, q).wait_recv()
            way_copy(devs.at[s, way, q], s, q).start()

    def join_parts(means, parts, size):
        mean = means[0]
        for m in means[1:]:
            mean = mean + m
        mean = mean / len(means)
        total = parts[0]
        for v in parts[1:]:
            total = total + v
        for m in means:
            total = total + size * (m - mean) * (m - mean)
        return mean, total

    for k in range(1, places):
        mom_copy(k, peer(k), place).wait_recv()
    remote(moms.at[way], moms.at[way], pair_send, pair_recv, partner).start()
    mean, total = join_parts(
        [moms[way, q, :STREAMS, :] for q in range(places)],
        [moms[way, q, STREAMS:, :] for q in range(places)],
        piece,
    )
    joins[me, :STREAMS, :] = mean
    joins[me, STREAMS:, :] = total
    for i, j in others:
        remote(joins.at[me], joins.at[me], join_send, join_recv, join_device(i, j)).start()
    forward(3)
    n_others = len(others)
    remote(
        joins.at[pl.ds(0, n_others)], joins.at[pl.ds(0, n_others)], join_send, join_recv, partner
    ).wait_recv()
    remote(moms.at[way], moms.at[1 - way], pair_send, pair_recv, partner).wait_recv()
    mean, total = join_parts(
        [joins[i, :STREAMS, :] for i in range(n_others + 1)],
        [joins[i, STREAMS:, :] for i in range(n_others + 1)],
        piece * places,
    )
    scale = lax.rsqrt(total / (piece * places * (n_others + 1)) + 1e-05)
    for s in range(STREAMS):
        for q in range(places):
            for w in range(2):
                off = moms[w, q, s : s + 1, :] - mean[s : s + 1]
                shift_ref[s, 2 * q + w : 2 * q + w + 1, :] = off * scale[s : s + 1]
        shift_ref[s, 2 * places : 2 * places + 1, :] = scale[s : s + 1]
        shift_ref[s, 2 * places + 1 : 2 * places + 2, :] = mean[s : s + 1]

    def normalize(s):
        remote(devs.at[s, 1 - way], devs.at[s, 1 - way], way_send, way_recv.at[s], partner).wait_recv()
        size = shift_ref[s, 2 * places : 2 * places + 1, :]
        for q in range(places):
            for w in range(2):
                block = 2 * q + w
                rows = slice(block * piece, (block + 1) * piece)
                unit = devs[s, w, q].astype(full) * size + shift_ref[s, block : block + 1, :]
                normed_ref[s, rows, :] = (unit * gains_ref[s, rows, :]).astype(low)

    def core_copy(unit, half):
        return remote(
            core_out.at[unit, half],
            core_in.at[unit, half],
            core_send,
            core_recv.at[unit, half],
            core_peer,
        )

    def outer_copy(unit):
        return remote(
            outer_out.at[unit], outer_in.at[unit], outer_send, outer_recv.at[unit], outer_peer
        )

    def project(unit, carry):
        @pl.when(unit == 0)
        def _():
            normalize(3)
            forward(0)

        for s in (1, 2):

            @pl.when(unit == s)
            def _(s=s):
                forward(s)

        @pl.when(unit >= ups)
        def _():
            normalize(unit - ups)

        stream = jnp.where(unit < ups, 3, unit - ups)
        pltpu.make_async_copy(weights.at[unit], weights.at[unit], weight_sem.at[unit]).wait()

        def product(t):
            return lax.dot_general(
                weights[unit, t],
                normed_ref[stream],
                (((0,), (0,)), ((), ())),
                preferred_element_type=full,
            )

        core_out[unit, 0] = product(0).astype(low)
        core_copy(unit, 0).start()
        passing = product(1)
        core_out[unit, 1] = product(2).astype(low)
        core_copy(unit, 1).start()
        core_copy(unit, 0).wait_recv()
        outer_out[unit] = (passing + core_in[unit, 0].astype(full)).astype(low)
        outer_copy(unit).start()
        kept = product(3)
        core_copy(unit, 1).wait_recv()
        kept = kept + core_in[unit, 1].astype(full)

        @pl.when(unit < ups)
        def _():
            slope_ref[pl.ds(pl.multiple_of(unit * n_head, n_head), n_head), :] = kept

        @pl.when(unit >= ups)
        def _():
            heads_ref[unit - ups] = kept

        return carry

    lax.fori_loop(0, count, project, 0)

    def turned_copies():
        for unit in range(count):
            for t in range(4):
                turn = 3 - t
                if unit < ups:
                    start = turn * n_units + unit * n_head
                    target = turned_up_ref.at[:, start : start + n_head]
                else:
                    target = turned_ref.at[unit - ups, :, turn * n_head : (turn + 1) * n_head]
                yield pltpu.make_async_copy(weights.at[unit, t], target, turned_sem)

    for copy in turned_copies():
        copy.start()
    for s in range(STREAMS):
        own_ref[s] = devs[s, way]

    step = 32

    def finish_up(unit, carry):
        outer_copy(unit).wait_recv()

        def part(i, carry):
            inner = pl.ds(pl.multiple_of(i * step, step), step)
            rows = pl.ds(pl.multiple_of(unit * n_head + i * step, step), step)
            hidden = slope_ref[rows, :] + outer_in[unit, inner, :].astype(full)
            half = 0.5 + 0.5 * lax.erf(hidden * math.sqrt(0.5))
            active_ref[rows, :] = (hidden * half).astype(low)
            bell = jnp.exp(-0.5 * hidden * hidden) * (1.0 / math.sqrt(2.0 * math.pi))
            slope_ref[rows, :] = half + hidden * bell
            return carry

        return lax.fori_loop(0, n_head // step, part, carry)

    lax.fori_loop(0, ups, finish_up, 0)

    def finish_head(unit, carry):
        outer_copy(unit).wait_recv()
        heads_ref[unit - ups] = heads_ref[unit - ups] + outer_in[unit].astype(full)
        return carry

    lax.fori_loop(ups, count, finish_head, 0)

    def sent(ref, sem):
        remote(ref, ref, sem, join_recv, partner).wait_send()

    sent(moms.at[0, pl.ds(0, places - 1)], mom_send)
    sent(send_ref.at[pl.ds(0, places - 1)], dev_send)
    sent(send_ref, way_send)
    sent(moms.at[0], pair_send)
    sent(joins.at[pl.ds(0, n_others)], join_send)
    sent(core_out, core_send)
    sent(outer_out, outer_send)
    pltpu.make_async_copy(weights, weights, turned_sem).wait()


def forward_projections(deviations, moments, norm_gains, w_query, w_key, w_value, w_up):
    places, _, piece, group = deviations.shape
    feats = norm_gains.shape[0]
    n_head = w_query.shape[1] // 8
    n_units = w_up.shape[1] // 8
    count = n_units // n_head + 3
    vmem, dma = pltpu.VMEM, pltpu.SemaphoreType.DMA
    out_types = [
        ((STREAMS, feats, group), low),
        ((STREAMS, places, piece, group), low),
        ((STREAMS, 2 * places + 8, group), full),
        ((n_units, group), low),
        ((n_units, group), full),
        ((3, n_head, group), full),
        ((3, feats, 4 * n_head), low),
        ((feats, 4 * n_units), low),
    ]
    spaces = [vmem] * 6 + [pl.ANY] * 2
    return pl.pallas_call(
        functools.partial(forward_kernel, (places, piece, group, n_head, n_units)),
        out_shape=[jax.ShapeDtypeStruct(*t) for t in out_types],
        in_specs=[pl.BlockSpec(memory_space=vmem)] * 3 + [pl.BlockSpec(memory_space=pl.ANY)] * 4,
        out_specs=[pl.BlockSpec(memory_space=m) for m in spaces],
        scratch_shapes=[
            vmem((STREAMS, 2, places, piece, group), low),
            vmem((2, places, 2 * STREAMS, group), full),
            vmem((8, 2 * STREAMS, group), full),
            vmem((count, 4, feats, n_head), low),
            vmem((count, 2, n_head, group), low),
            vmem((count, 2, n_head, group), low),
            vmem((count, n_head, group), low),
            vmem((count, n_head, group), low),
            dma,
            dma((places,)),
            dma,
            dma((STREAMS, places)),
            dma,
            dma((STREAMS,)),
            dma,
            dma,
            dma,
            dma,
            dma((count,)),
            dma,
            dma,
            dma((count, 2)),
            dma,
            dma((count,)),
        ],
        compiler_params=pltpu.CompilerParams(
            collective_id=7, has_side_effects=True, vmem_limit_bytes=62 << 20
        ),
        cost_estimate=pl.CostEstimate(
            flops=8 * count * n_head * feats * group,
            bytes_accessed=300 << 20,
            transcendentals=2 * n_units * group,
        ),
    )(
        deviations,
        moments,
        norm_gains.T.astype(full)[:, :, None],
        w_query,
        w_key,
        w_value,
        w_up,
    )


def chain_kernel(ways, places, blocks, n_operands, depth, *refs):
    operand_refs, refs = refs[:n_operands], refs[n_operands:]
    out_ref, refs = refs[0], refs[1:]
    operands, refs = refs[:n_operands], refs[n_operands:]
    (
        own,
        landed,
        sums,
        fetched,
        up_send,
        up_recv,
        down_send,
        down_recv,
        side_send,
        side_recv,
        kept,
    ) = refs
    count = sums.shape[0]
    per_tile = TILE // depth
    last = places - 1
    me = lax.axis_index("hid")
    if ways == 2:
        place, way = me // 2, me % 2
        above, below, beside = me + 2, me - 2, me + 1 - 2 * way
    else:
        odd, half = me % 2, places // 2
        place, way = (1 - odd) * (me // 2) + odd * (last - me // 2), 0
        turn_up = (place + 1) // half
        turn_down = (place - 1 + places) // half - 2
        above = (1 - turn_up) * 2 * (place + 1) + turn_up * (2 * (last - place - 1) + 1)
        below = (1 - turn_down) * 2 * (place - 1) + turn_down * (2 * (last - place + 1) + 1)
        beside = me

    def remote(source, target, send, recv, device):
        return pltpu.make_async_remote_copy(
            src_ref=source,
            dst_ref=target,
            send_sem=send,
            recv_sem=recv,
            device_id={"hid": device},
            device_id_type=pl.DeviceIdType.MESH,
        )

    def up_copy(i):
        return remote(sums.at[i], landed.at[i], up_send, up_recv.at[i], above)

    def down_copy(source, i):
        return remote(source, out_ref.at[way, i], down_send, down_recv.at[i], below)

    def side_copy(source, i):
        return remote(source, out_ref.at[way, i], side_send, side_recv, beside)

    def fetch(n):
        return pltpu.make_async_copy(operand_refs[n], operands[n], fetched.at[n])

    for n in range(n_operands):
        fetch(n).start()

    barrier = pltpu.get_barrier_semaphore()

    def greet(device):
        pl.semaphore_signal(
            barrier, inc=1, device_id={"hid": device}, device_id_type=pl.DeviceIdType.MESH
        )

    @pl.when(place > 0)
    def _():
        greet(below)

    @pl.when(place < last)
    def _():
        greet(above)

    if ways == 2:
        greet(beside)
    met = jnp.where(place > 0, 1, 0) + jnp.where(place < last, 1, 0) + (ways - 1)
    pl.semaphore_wait(barrier, met)

    def compute(tile):
        seen, first = set(), 0
        for rows, segments in blocks:
            start = first
            first = first + rows // TILE
            fresh = [n for seg in segments for n in (seg[0], seg[2])]
            fresh = [n for n in dict.fromkeys(fresh) if n not in seen]
            seen.update(fresh)

            @pl.when(tile == start)
            def _(fresh=fresh):
                for n in fresh:
                    fetch(n).wait()

            @pl.when((tile >= start) & (tile < first))
            def _(start=start, segments=segments):
                column = 0
                for left, left_row, right, right_row, size in segments:
                    row = pl.multiple_of(left_row + (tile - start) * TILE, TILE)
                    own[:, column : column + size] = lax.dot_general(
                        operands[left][pl.ds(row, TILE), :],
                        operands[right][right_row : right_row + size, :],
                        (((1,), (1,)), ((), ())),
                        preferred_element_type=full,
                    )
                    column += size

    def upward(i):
        @pl.when(i % per_tile == 0)
        def _():
            compute(i // per_tile)

        mine = own[pl.ds(pl.multiple_of(i % per_tile * depth, depth), depth), :]

        @pl.when(place == 0)
        def _():
            sums[i] = mine.astype(low)
            up_copy(i).start()

        @pl.when(place > 0)
        def _():
            up_copy(i).wait_recv()
            sums[i] = (landed[i].astype(full) + mine).astype(low)

            @pl.when(place < last)
            def _():
                up_copy(i).start()

            @pl.when(place == last)
            def _():
                down_copy(sums.at[i], i).start()
                if ways == 2:
                    side_copy(sums.at[i], i).start()
                pltpu.make_async_copy(sums.at[i], out_ref.at[way, i], kept).start()

    def downward(i):
        down_copy(sums.at[i], i).wait_recv()

        @pl.when(place > 0)
        def _():
            down_copy(out_ref.at[way, i], i).start()

        if ways == 2:
            side_copy(out_ref.at[way, i], i).start()

    lag = SLACK * (last - place) + 2

    def step(i, carry):
        @pl.when(i < count)
        def _():
            upward(i)

        behind = i - lag

        @pl.when((behind >= 0) & (behind < count) & (place < last))
        def _():
            downward(behind)

        return carry

    lax.fori_loop(0, count + SLACK * last + 2, step, 0)

    @pl.when(place < last)
    def _():
        remote(sums, landed, up_send, kept, above).wait_send()

    @pl.when(place > 0)
    def _():
        remote(sums, out_ref.at[way], down_send, kept, below).wait_send()

    @pl.when(place == last)
    def _():
        pltpu.make_async_copy(sums, out_ref.at[way], kept).wait()

    if ways == 2:
        remote(sums, out_ref.at[way], side_send, kept, beside).wait_send()
        remote(sums, out_ref.at[1 - way], kept, side_recv, beside).wait_recv()


def chain_sum(operands, blocks, collective_id):
    ways, size = split_ways(), lax.axis_size("hid")
    columns = sum(seg[4] for seg in blocks[0][1])
    rows = sum(block[0] for block in blocks)
    depth = max(16, CHUNK // columns)
    count = rows // depth
    tokens = operands[0].shape[1]
    return pl.pallas_call(
        functools.partial(chain_kernel, ways, size // ways, blocks, len(operands), depth),
        out_shape=jax.ShapeDtypeStruct((ways, count, depth, columns), low),
        in_specs=[pl.BlockSpec(memory_space=pl.ANY)] * len(operands),
        out_specs=pl.BlockSpec(memory_space=pl.ANY),
        scratch_shapes=[pltpu.VMEM(v.shape, low) for v in operands]
        + [
            pltpu.VMEM((TILE, columns), full),
            pltpu.VMEM((count, depth, columns), low),
            pltpu.VMEM((count, depth, columns), low),
            pltpu.SemaphoreType.DMA((len(operands),)),
            pltpu.SemaphoreType.DMA,
            pltpu.SemaphoreType.DMA((count,)),
            pltpu.SemaphoreType.DMA,
            pltpu.SemaphoreType.DMA((count,)),
            pltpu.SemaphoreType.DMA,
            pltpu.SemaphoreType.DMA,
            pltpu.SemaphoreType.DMA,
        ],
        compiler_params=pltpu.CompilerParams(
            collective_id=collective_id, has_side_effects=True, vmem_limit_bytes=60 << 20
        ),
        cost_estimate=pl.CostEstimate(
            flops=2 * rows * columns * tokens,
            bytes_accessed=300 * rows * columns,
            transcendentals=0,
        ),
    )(*operands)


def chain_sums(operands, blocks, collective_id):
    groups, held, size = [[]], set(), 0
    for rows, segments in blocks:
        used = {n for seg in segments for n in (seg[0], seg[2])}
        more = sum(2 * operands[n].size for n in used - held)
        more += 4 * rows * sum(seg[4] for seg in segments)
        if groups[-1] and size + more > VMEM:
            groups.append([])
            held, size = set(), 0
            more = sum(2 * operands[n].size for n in used)
            more += 4 * rows * sum(seg[4] for seg in segments)
        groups[-1].append((rows, segments))
        held |= used
        size += more
    totals = []
    for i, group in enumerate(groups):
        used = sorted({n for _, segments in group for seg in segments for n in (seg[0], seg[2])})
        place = {n: k for k, n in enumerate(used)}
        own = [
            (rows, [(place[a], b, place[c], d, e) for a, b, c, d, e in segments])
            for rows, segments in group
        ]
        total = chain_sum([operands[n] for n in used], own, collective_id + i)
        totals.append(total.reshape(total.shape[0], -1, total.shape[3]))
    return totals[0] if len(totals) == 1 else jnp.concatenate(totals, axis=1)


def assemble_kernel(ways, dp, own_ref, *refs):
    halves, (up_ref, *head_refs, out_ref) = refs[:ways], refs[ways:]
    rows, wide = own_ref.shape[2:]
    size = up_ref.shape[1] // dp // ways
    blocks = dp * size // wide
    own = wide // dp
    feats = out_ref.shape[1] // dp
    for d in range(dp):
        turn = turn_of(d)
        for w in range(ways):
            start = turn * size
            lanes = pl.ds(pl.multiple_of(start % wide, size), size)
            place = (d * ways + w) * size
            up_ref[:, place : place + size] = own_ref[w, start // wide, :, lanes].astype(full)
            for s, ref in enumerate(head_refs):
                lanes = pl.ds(pl.multiple_of(turn * own, own), own)
                place = (d * ways + w) * own
                ref[:, place : place + own] = own_ref[w, blocks + s, :, lanes].astype(full)
        start = turn * feats
        lanes = pl.ds(pl.multiple_of(start % wide, feats), feats)
        for w in range(ways):

            @pl.when(start // wide == w)
            def _(w=w, d=d, lanes=lanes):
                out_ref[:, d * feats : (d + 1) * feats] = halves[w][0, 0, :, lanes].astype(full)


def assemble(total, w_up):
    ways, dp = split_ways(), lax.axis_size("dp")
    blocks, rows, wide = total.shape[1:]
    depth = min(64, rows // ways)
    share = rows // ways // depth

    def half_map(half):
        return lambda i: (i // share, blocks - 1, half * share + i % share, 0)

    widths = [w_up.shape[1]] + [ways * wide] * 4
    return pl.pallas_call(
        functools.partial(assemble_kernel, ways, dp),
        grid=(rows // depth,),
        out_shape=[jax.ShapeDtypeStruct((rows, n), full) for n in widths],
        in_specs=[pl.BlockSpec((ways, blocks, depth, wide), lambda i: (0, 0, i, 0))]
        + [pl.BlockSpec((1, 1, depth, wide), half_map(half)) for half in range(ways)],
        out_specs=[pl.BlockSpec((depth, n), lambda i: (i, 0)) for n in widths],
        compiler_params=pltpu.CompilerParams(vmem_limit_bytes=48 << 20),
        cost_estimate=pl.CostEstimate(
            flops=0, bytes_accessed=6 * total.size, transcendentals=0
        ),
    )(total, *[total] * ways)


def unturn_kernel(dp, own_ref, out_ref):
    size = out_ref.shape[1] // dp
    for d in range(dp):
        lanes = pl.ds(pl.multiple_of(turn_of(d) * size, size), size)
        out_ref[:, d * size : (d + 1) * size] = own_ref[:, lanes].astype(full)


def unturn(total):
    rows, columns = total.shape
    depth = 256
    return pl.pallas_call(
        functools.partial(unturn_kernel, lax.axis_size("dp")),
        grid=(rows // depth,),
        out_shape=jax.ShapeDtypeStruct((rows, columns), full),
        in_specs=[pl.BlockSpec((depth, columns), lambda i: (i, 0))],
        out_specs=pl.BlockSpec((depth, columns), lambda i: (i, 0)),
        cost_estimate=pl.CostEstimate(
            flops=0, bytes_accessed=6 * total.size, transcendentals=0
        ),
    )(total)


def to_owner(values_in):
    dp, hid, ways = lax.axis_size("dp"), lax.axis_size("hid"), split_ways()
    index = lax.axis_index("dp") * ways + lax.axis_index("hid") % ways
    mine = lax.dynamic_index_in_dim(values_in, index, 1, keepdims=False)
    pairs = [
        (d * hid + t * ways + w, (t * dp + d) * ways + w)
        for d in range(dp)
        for t in range(hid // ways)
        for w in range(ways)
    ]
    return lax.ppermute(mine, ("dp", "hid"), pairs)


def rotate(values_in, cosine, sine):
    half = cosine.shape[1]
    front, back = values_in[:, :half], values_in[:, half : 2 * half]
    return jnp.concatenate(
        [
            front * cosine - back * sine,
            back * cosine + front * sine,
            values_in[:, 2 * half :],
        ],
        axis=1,
    )


def local(
    history,
    mix,
    segment_ids,
    norm_gains,
    w_query,
    w_key,
    w_value,
    w_out,
    w_up,
    w_down,
    w_mixer,
    mixer_out,
    mix_static,
    out_cotangent,
    mix_cotangent,
):
    dp, hid, ways = lax.axis_size("dp"), lax.axis_size("hid"), split_ways()
    places = hid // ways
    my_hid = lax.axis_index("hid")
    place, way = my_hid // ways, my_hid % ways
    block = segment_ids.shape[0]
    total_tokens = block * dp * hid
    row = total_tokens // dp
    group = total_tokens // places
    rows = group // row
    piece = history.shape[2]
    mine = piece * places
    feats = piece * hid
    width = feats * dp
    heads = HEADS // dp // ways
    n_mix = mix.shape[1]
    n_cot = mix_cotangent.shape[1]

    def by_place(values_in):
        return jnp.stack(
            [values_in[..., p * group : (p + 1) * group] for p in range(places)], axis=0
        )

    stored = history.swapaxes(1, 2)
    mix_all = gather_all(mix.T)
    own_means, own_devs, deviations = [], [], []
    for s in range(STREAMS):
        total = mix_all[s * HIST] * stored[0].astype(full)
        for j in range(1, HIST):
            total = total + mix_all[s * HIST + j] * stored[j].astype(full)
        own_means.append(jnp.mean(total, axis=0))
        off = total - own_means[s]
        own_devs.append(jnp.sum(off * off, axis=0))
        deviations.append(off.astype(low))
    moments = by_place(jnp.stack(own_means + own_devs, axis=0))
    deviations = by_place(jnp.stack(deviations, axis=0))
    fused = dp == 4 and ways == 2 and rows == 1

    table = jnp.concatenate([mix_cotangent.T, segment_ids.astype(full)[None]], axis=0)
    table = lax.dynamic_slice_in_dim(gather_all(table), place * group, group, 1)
    cot_t = table[:n_cot]
    ids = table[-1].reshape(rows, row)

    there = jnp.arange(row, dtype=jnp.int32)
    same_doc = ids[:, :, None] == ids[:, None, :]
    doc_start = jnp.min(jnp.where(same_doc, there[None, None], row), axis=2)
    position = (there[None] - doc_start).astype(full).reshape(group)
    visible = same_doc & (there[None, None] <= there[None, :, None])
    frequency = rope_base ** (-jnp.arange(ROT // 2, dtype=full) * 2.0 / ROT)
    angle = frequency[:, None] * position[None, :]
    cosine, sine = jnp.cos(angle)[None], jnp.sin(angle)[None]

    def own_rows(values_in):
        parts = values_in.reshape((places, ways, piece) + values_in.shape[1:])
        part = lax.dynamic_index_in_dim(parts, way, 1, keepdims=False)
        return part.reshape((mine,) + values_in.shape[1:])

    def all_rows(values_in):
        parts = values_in.reshape((places, piece) + values_in.shape[1:])
        return gather_ways(parts, 1).reshape((feats,) + values_in.shape[1:])

    own_gains = own_rows(norm_gains).astype(full)
    gains = [own_gains[:, s][:, None] for s in range(STREAMS)]
    all_gains = norm_gains.astype(full)

    def project(weight, left):
        columns = weight.shape[1] // dp // ways

        def make(index):
            start = (index * ways + way) * columns
            part = lax.dynamic_slice_in_dim(weight, start, columns, 1)
            return contract(part, left, 0, 0)

        return scatter_dp(make)

    def way_columns(weight):
        if ways == 1:
            return weight
        size = weight.shape[1] // dp // ways
        parts = [weight[:, i * size : (i + 1) * size] for i in range(dp * ways)]
        pairs = zip(parts[::2], parts[1::2])
        return jnp.concatenate([jnp.where(way == 0, a, b) for a, b in pairs], axis=1)

    def way_rows(weight):
        size = weight.shape[0] // ways
        return lax.dynamic_slice_in_dim(weight, way * size, size, 0)

    def by_head(values_in):
        return values_in.reshape(heads, HEAD, group)

    def turned(weight, stride, offset, size):
        starts = [turn_source(turn) * stride + offset for turn in range(dp)]
        parts = [lax.dynamic_slice_in_dim(weight, start, size, 1) for start in starts]
        return jnp.concatenate(parts, axis=1)

    n_head = heads * HEAD
    n_units = w_up.shape[1] // dp // ways
    if fused:
        normed, deviations, shifts, active, slope, products, turned_heads, turned_up = (
            forward_projections(deviations, moments, norm_gains, w_query, w_key, w_value, w_up)
        )
        inv_scales = shifts[:, 2 * places]
        own_shifts = shifts[:, : 2 * places].reshape(STREAMS, places, ways, group)
        own_shifts = lax.dynamic_index_in_dim(own_shifts, way, 2, keepdims=False)
        offset = own_shifts[3] / inv_scales[3] + shifts[3, 2 * places + 1]
        residual = (deviations[3].astype(full) + offset[:, None]).reshape(mine, group)
        units = [
            (deviations[s].astype(full) * inv_scales[s] + own_shifts[s][:, None]).reshape(mine, group)
            for s in range(STREAMS)
        ]
        normed = [normed[s] for s in range(STREAMS)]
        products = [by_head(v) for v in products]
        turned_weights = [turned_heads[s] for s in range(3)] + [turned_up]
    else:
        moments = exchange(moments)
        deviations = exchange(deviations)
        deviations = [deviations[:, s] for s in range(STREAMS)]
        def join_moments(mean_parts, dev_parts, size):
            mean = jnp.mean(mean_parts, axis=0)
            spread = size * jnp.sum(jnp.square(mean_parts - mean), axis=0)
            return mean, jnp.sum(dev_parts, axis=0) + spread

        block_means = moments[:, :STREAMS]
        joined = join_moments(block_means, moments[:, STREAMS:], piece)
        joined = gather_dp(gather_ways(jnp.concatenate(joined, axis=0), 0))
        joined = joined.reshape((dp * ways,) + joined.shape[2:])
        means, variance = join_moments(joined[:, :STREAMS], joined[:, STREAMS:], mine)
        inv_scales = lax.rsqrt(variance / width + 1e-05)
        all_means = gather_ways(block_means, 1)

        def unit(values_in, block_mean, s):
            return (values_in.astype(full) + (block_mean - means[s])[..., None, :]) * inv_scales[s]

        units = [
            unit(deviations[s], block_means[:, s], s).reshape(mine, group) for s in range(STREAMS)
        ]
        normed = []
        for s in range(STREAMS):
            both = unit(gather_ways(deviations[s], 1), all_means[:, :, s], s).reshape(feats, group)
            normed.append((both * all_gains[:, s][:, None]).astype(low))
        residual = (deviations[3].astype(full) + block_means[:, 3][:, None]).reshape(mine, group)
        products = [
            by_head(project(w, normed[s])) for s, w in enumerate((w_query, w_key, w_value))
        ]
        hidden = project(w_up, normed[3])
        active, hidden_pull = jax.vjp(gelu_exact, hidden)
        active = active.astype(low)
        (slope,) = hidden_pull(jnp.ones_like(hidden))
        turned_weights = [
            turned(w, ways * n_head, way * n_head, n_head) for w in (w_query, w_key, w_value)
        ] + [turned(w_up, ways * n_units, way * n_units, n_units)]
    queries = rotate(products[0], cosine, sine).astype(low)
    keys = rotate(products[1], cosine, sine).astype(low)
    values = products[2].astype(low)
    cotangent, queries = lax.optimization_barrier((out_cotangent, queries))
    upstream = exchange(by_place(cotangent.T)).reshape(mine, group)

    out_rows, down_rows = way_rows(w_out), way_rows(w_down)
    turned_weights += [turned(out_rows, feats, 0, feats), turned(down_rows, feats, 0, feats)]

    def by_row(values_in):
        if rows == 1:
            return values_in
        return (
            values_in.reshape(heads, HEAD, rows, row)
            .transpose(0, 2, 1, 3)
            .reshape(heads * rows, HEAD, row)
        )

    def from_row(values_in):
        if rows == 1:
            return values_in
        return (
            values_in.reshape(heads, rows, HEAD, row)
            .transpose(0, 2, 1, 3)
            .reshape(heads, HEAD, group)
        )

    q_rows, k_rows, v_rows = by_row(queries), by_row(keys), by_row(values)
    score_scale = 1.0 / math.sqrt(HEAD)
    scores = batched(q_rows, k_rows, 1, 1) * score_scale
    mask = jnp.broadcast_to(visible[None], (heads, rows, row, row)).reshape(scores.shape)
    scores = jnp.where(mask, scores, -1e30)
    probs = jax.nn.softmax(scores, axis=-1)
    probs_low = probs.astype(low)
    attended = from_row(batched(v_rows, probs_low, 2, 2).astype(low)).reshape(heads * HEAD, group)

    def make_out(index):
        start = index * feats
        left = lax.dynamic_slice_in_dim(out_rows, start, feats, 1)
        other = lax.dynamic_slice_in_dim(down_rows, start, feats, 1)
        return contract(left, attended, 0, 0) + contract(other, active, 0, 0)

    branches = scatter_dp(make_out).reshape(places, ways, piece, group)
    kept = lax.dynamic_index_in_dim(branches, way, 1, keepdims=False)
    if ways == 2:
        given = lax.dynamic_index_in_dim(branches, 1 - way, 1, keepdims=False).astype(low)
        kept = kept + hid_swap(given, 1).astype(full)
    output = residual + kept.reshape(mine, group)
    output, upstream, turned_weights = lax.optimization_barrier(
        (output, upstream, turned_weights)
    )
    upstream = upstream.astype(full)
    output_rounded = output.astype(low)

    block_output = exchange(output_rounded.reshape(places, piece, group))

    square = jnp.sum(output * output, axis=0, keepdims=True)
    mixer_rows = own_rows(w_mixer)
    mixer_part = contract(mixer_rows, output_rounded, 0, 0)
    sums = sum_features(jnp.concatenate([mixer_part, square], axis=0))
    inv_rms = lax.rsqrt(sums[-1] / width + 1e-06)
    inner_raw = sums[:-1]
    inner_pre = inner_raw * inv_rms
    inner_act, inner_pull = jax.vjp(gelu_exact, inner_pre)
    raw_mix = contract_high(mixer_out, inner_act, 0, 0)
    column = jnp.stack(
        [
            jnp.sum(raw_mix, axis=1),
            jnp.sum(raw_mix * raw_mix, axis=1),
            jnp.sum(cot_t, axis=1),
            jnp.sum(cot_t * raw_mix, axis=1),
        ],
        axis=0,
    )
    act_total = jnp.sum(inner_act, axis=1)
    act_cot = contract_high(inner_act, cot_t, 1, 1)
    act_raw = contract_high(inner_act, raw_mix, 1, 1)
    n_inner = act_total.shape[0]
    flat = sum_tokens(
        jnp.concatenate([column.reshape(-1), act_total, act_cot.reshape(-1), act_raw.reshape(-1)])
    )
    sum_raw, sum_square, sum_grad, sum_grad_raw = flat[: 4 * n_cot].reshape(4, n_cot)
    start = 4 * n_cot
    act_total = flat[start : start + n_inner]
    start += n_inner
    act_cot = flat[start : start + n_inner * n_cot].reshape(n_inner, n_cot)
    start += n_inner * n_cot
    act_raw = flat[start:].reshape(n_inner, n_cot)
    average = sum_raw / total_tokens
    variance_mix = sum_square / total_tokens - average * average
    inv_spread = lax.rsqrt(variance_mix + 1e-05)
    unit_mix = (raw_mix - average[:, None]) * inv_spread[:, None]
    mix_next = mix_static[:, None] + unit_mix
    mix_next = to_owner(mix_next.reshape(n_cot, dp * ways, block)).T
    mean_grad = sum_grad / total_tokens
    sum_grad_unit = inv_spread * (sum_grad_raw - average * sum_grad)
    mean_grad_unit = sum_grad_unit / total_tokens
    raw_grad = inv_spread[:, None] * (
        cot_t - mean_grad[:, None] - unit_mix * mean_grad_unit[:, None]
    )
    act_unit = inv_spread[None, :] * (act_raw - act_total[:, None] * average[None, :])
    mixer_out_grad = inv_spread[None, :] * (
        act_cot - act_total[:, None] * mean_grad[None, :] - act_unit * mean_grad_unit[None, :]
    )
    act_grad = contract_high(mixer_out, raw_grad, 1, 0)
    inner_low = inner_pull(act_grad)[0].astype(low)
    scaled = (output * inv_rms).astype(low)
    mixer_grad_part = contract(inner_low, scaled, 1, 1)
    scaled_grad = contract(mixer_rows, inner_low, 1, 0)
    along = jnp.sum(inner_low.astype(full) * inner_raw, axis=0) / width
    output_grad = upstream + inv_rms * scaled_grad - output * (inv_rms * inv_rms * inv_rms) * along
    output_lows = gather_turns(all_rows(output_grad.astype(low)))

    output_low = jnp.concatenate(output_lows, axis=0)

    hidden_low = (contract(turned_weights[5], output_low, 1, 0) * slope).astype(low)

    attended_grad = contract(turned_weights[4], output_low, 1, 0).astype(low)
    a_rows = by_row(by_head(attended_grad))
    prob_grad = batched(a_rows, v_rows, 1, 1)
    row_total = jnp.sum(probs * prob_grad, axis=-1, keepdims=True)
    score_grad = (probs * (prob_grad - row_total)).astype(low)
    query_grad = from_row(batched(k_rows, score_grad, 2, 2) * score_scale)
    key_grad = from_row(batched(q_rows, score_grad, 2, 1) * score_scale)
    value_grad = from_row(batched(a_rows, probs_low, 2, 1))
    query_low = rotate(query_grad, cosine, -sine).astype(low).reshape(heads * HEAD, group)
    key_low = rotate(key_grad, cosine, -sine).astype(low).reshape(heads * HEAD, group)
    value_low = value_grad.astype(low).reshape(heads * HEAD, group)

    lows_mine = jnp.concatenate([query_low, key_low, value_low], axis=0)
    active_kept, hidden_low, lows_mine = lax.optimization_barrier((active, hidden_low, lows_mine))
    hidden_lows, lows = gather_outer(hidden_low), gather_outer(lows_mine)
    blocks = [(active.shape[0], [(0, 0, 1, 0, width)])]
    branch_sum = chain_sum([active_kept, output_low], blocks, 0)
    branch_sum, block_output, hidden_lows, lows = lax.optimization_barrier(
        (branch_sum, block_output, hidden_lows, lows)
    )
    block_output = block_output.transpose(1, 0, 2).reshape(piece, total_tokens).T
    hidden_lows, lows = gather_cores(hidden_lows), gather_cores(lows)

    normed_grads, alongs, rights = [], [], []
    for s in range(STREAMS):
        if s < 3:
            right = jnp.concatenate([v[s * n_head : (s + 1) * n_head] for v in lows], axis=0)
        else:
            right = jnp.concatenate(hidden_lows, axis=0)
        rights.append(right)
        part = contract(turned_weights[s], right, 1, 0)
        alongs.append(jnp.sum(part * all_gains[:, s][:, None], axis=0))
        alongs.append(jnp.sum(part * normed[s].astype(full), axis=0))
        part = part.reshape(places, ways, piece, group)
        kept = lax.dynamic_index_in_dim(part, way, 1, keepdims=False)
        if ways == 2:
            given = lax.dynamic_index_in_dim(part, 1 - way, 1, keepdims=False).astype(low)
            kept = kept + hid_swap(given, 1).astype(full)
        normed_grads.append(kept.reshape(mine, group))
    weighted = [normed_grads[s] * gains[s] for s in range(STREAMS)]
    means_back = sum_features(jnp.stack(alongs, axis=0)) / width
    gain_parts = [jnp.sum(g * u, axis=1) for g, u in zip(normed_grads, units)]
    stream_grads = [
        (weighted[s] - means_back[2 * s] - units[s] * means_back[2 * s + 1]) * inv_scales[s]
        for s in range(STREAMS)
    ]
    stream_grads[3] = stream_grads[3] + output_grad
    smalls = jnp.concatenate([mixer_grad_part, jnp.stack(gain_parts, axis=0)], axis=0)

    split = jnp.stack([v.astype(low).reshape(places, piece, group) for v in stream_grads], axis=1)
    attended, split, smalls = lax.optimization_barrier((attended, split, smalls))
    split = exchange(split)
    split = jnp.concatenate([split[p] for p in range(places)], axis=-1).astype(full)
    mix_layers = mix_all.reshape(STREAMS, HIST, total_tokens)
    history_grad = sum(mix_layers[s][:, None] * split[s][None] for s in range(STREAMS))
    history_grad = history_grad.swapaxes(1, 2)
    mix_parts = jnp.concatenate(
        [jnp.sum(split[s][None] * stored.astype(full), axis=1) for s in range(STREAMS)], axis=0
    )
    mix_parts = mix_parts.reshape(n_mix, dp * hid, block).transpose(1, 0, 2)

    wide = w_query.shape[1] // ways
    operands = [rights[3]] + rights[:3] + [output_low, normed[3]] + normed[:3] + [attended]
    blocks = [(feats, [(5, 0, 0, i, wide)]) for i in range(0, rights[3].shape[0], wide)]
    blocks += [(feats, [(6 + s, 0, 1 + s, 0, wide)]) for s in range(3)]
    blocks += [(n_head, [(9, 0, 4, i, wide)]) for i in range(0, width, wide)]
    late_sum = chain_sums(operands, blocks, 1)
    late_sum, mix_parts, smalls = lax.optimization_barrier((late_sum, mix_parts, smalls))
    smalls = sum_tokens(smalls)
    smalls = gather_ways(smalls.reshape(-1, places, piece), 2).reshape(-1, feats)
    w_mixer_grad = smalls[:n_inner].T
    norm_gains_grad = smalls[n_inner:].T
    mix_parts = lax.all_to_all(mix_parts, ("dp", "hid"), split_axis=0, concat_axis=0, tiled=True)
    mix_grad = jnp.sum(mix_parts, axis=0).T
    w_down_grad = unturn(branch_sum.reshape(w_down.shape))
    late_sum = late_sum.reshape(ways, -1, feats, wide)
    w_up_grad, w_query_grad, w_key_grad, w_value_grad, w_out_grad = assemble(late_sum, w_up)

    return (
        block_output,
        mix_next,
        history_grad,
        mix_grad,
        norm_gains_grad,
        w_query_grad,
        w_key_grad,
        w_value_grad,
        w_out_grad,
        w_up_grad,
        w_down_grad,
        w_mixer_grad,
        mixer_out_grad,
        sum_grad,
    )


def solution(mesh):
    everywhere = ("dp", "hid")
    placed = (
        P(None, None, everywhere),
        P(everywhere, None),
        P(everywhere),
        P("dp", None),
        P("dp", None),
        P("dp", None),
        P("dp", None),
        P("dp", None),
        P("dp", None),
        P("dp", None),
        P("dp", None),
        P(),
        P(),
        P(None, everywhere),
        P(everywhere, None),
    )
    return jax.shard_map(
        local,
        mesh=mesh,
        in_specs=placed,
        out_specs=(
            P(None, everywhere),
            P(everywhere, None),
            P(None, None, everywhere),
            P(everywhere, None),
            P("dp", None),
            P("dp", None),
            P("dp", None),
            P("dp", None),
            P("dp", None),
            P("dp", None),
            P("dp", None),
            P("dp", None),
            P(),
            P(),
        ),
        check_vma=False,
    )
```

```python
import functools
import math

import jax
import jax.numpy as jnp
from jax import lax
from jax.experimental import pallas as pl
from jax.experimental.pallas import tpu as pltpu
from jax.sharding import PartitionSpec as P

HEADS = 16
HEAD = 128
ROT = 32
HIST = 8
STREAMS = 4
CORES = 2
CHUNK = 1 << 15
SLACK = 6
TILE = 128
LATE_TILE = 256
SPAN = 256
VMEM = 52 << 20
PULL_START = 4
PULL_GAP = 8
GRAD_GAP = 5

highest = lax.Precision.HIGHEST
rope_base = 10000.0
low = jnp.bfloat16
full = jnp.float32


def contract(left, right, left_dim, right_dim):
    return lax.dot_general(
        left, right, (((left_dim,), (right_dim,)), ((), ())), preferred_element_type=full
    )


def contract_high(left, right, left_dim, right_dim):
    return lax.dot_general(
        left,
        right,
        (((left_dim,), (right_dim,)), ((), ())),
        precision=highest,
        preferred_element_type=full,
    )


def batched(left, right, left_dim, right_dim):
    return lax.dot_general(
        left, right, (((left_dim,), (right_dim,)), ((0,), (0,))), preferred_element_type=full
    )


def gelu_exact(values_in):
    return jax.nn.gelu(values_in, approximate=False)


def core_swap(values_in):
    size = lax.axis_size("dp")
    return lax.ppermute(values_in, "dp", [(i, i ^ 1) for i in range(size)])


def outer_shift(values_in, step):
    size = lax.axis_size("dp")
    outer = size // CORES
    pairs = [
        (o * CORES + c, ((o + step) % outer) * CORES + c) for o in range(outer) for c in range(CORES)
    ]
    return lax.ppermute(values_in, "dp", pairs)


def hid_swap(values_in, bit):
    size = lax.axis_size("hid")
    return lax.ppermute(values_in, "hid", [(i, i ^ bit) for i in range(size)])


def ordered(first, values_in, other, axis):
    return jnp.stack(
        [jnp.where(first, values_in, other), jnp.where(first, other, values_in)], axis=axis
    )


def take(values_in, index):
    return lax.dynamic_index_in_dim(values_in, index, 0, keepdims=False)


def put(target, values_in, index):
    return lax.dynamic_update_index_in_dim(target, values_in, index, 0)


def split_ways():
    return 2 if HEADS // lax.axis_size("dp") >= 2 else 1


def gather_ways(values_in, axis):
    if split_ways() == 1:
        return jnp.expand_dims(values_in, axis)
    return ordered(lax.axis_index("hid") % 2 == 0, values_in, hid_swap(values_in, 1), axis)


def gather_dp(values_in):
    size = lax.axis_size("dp")
    outer = size // CORES
    me = lax.axis_index("dp")
    mine, core = me // CORES, me % CORES
    if outer == 2:
        held = ordered(mine == 0, values_in, outer_shift(values_in, 1), 0)
    else:
        held = jnp.zeros((outer,) + values_in.shape, values_in.dtype)
        held = put(held, values_in, mine)
        for step in range(1, outer):
            held = put(held, outer_shift(values_in, step), (mine - step) % outer)
    pair = ordered(core == 0, held, core_swap(held), 1)
    return pair.reshape((size,) + values_in.shape)


def gather_outer(values_in):
    steps = range(1, lax.axis_size("dp") // CORES)
    return [values_in] + [outer_shift(values_in, step) for step in steps]


def gather_cores(held):
    return [v for h in held for v in (h, core_swap(h))]


def gather_turns(values_in):
    return gather_cores(gather_outer(values_in))


def turn_source(turn):
    outer, me = lax.axis_size("dp") // CORES, lax.axis_index("dp")
    there = (me // CORES + outer - turn // CORES) % outer
    return there * CORES + (me + turn) % CORES


def turn_of(index):
    outer, me = lax.axis_size("dp") // CORES, lax.axis_index("dp")
    step = (me // CORES + outer - index // CORES) % outer
    return step * CORES + (me + index) % CORES


def sum_features(values_in):
    if split_ways() == 2:
        values_in = values_in + hid_swap(values_in, 1)
    parts = gather_dp(values_in)
    total = parts[0]
    for i in range(1, parts.shape[0]):
        total = total + parts[i]
    return total


def sum_tokens(values_in):
    size = lax.axis_size("hid")
    bit = split_ways()
    while bit < size:
        values_in = values_in + hid_swap(values_in, bit)
        bit *= 2
    return values_in


def gather_all(values_in):
    count = lax.axis_size("dp") * lax.axis_size("hid")
    copies = jnp.broadcast_to(values_in[None], (count,) + values_in.shape)
    held = lax.all_to_all(copies, ("dp", "hid"), split_axis=0, concat_axis=0, tiled=True)
    return held.transpose(1, 0, 2).reshape(values_in.shape[0], -1)


def scatter_dp(make):
    size = lax.axis_size("dp")
    outer = size // CORES
    me = lax.axis_index("dp")
    mine, core = me // CORES, me % CORES
    total = None
    for step in list(range(1, outer)) + [0]:
        there = (mine + step) % outer
        away = core_swap(make(there * CORES + 1 - core).astype(low))
        block = make(there * CORES + core) + away.astype(full)
        if step:
            block = outer_shift(block.astype(low), step).astype(full)
        total = block if total is None else total + block
    return total


def exchange(values_in):
    ways, size = split_ways(), lax.axis_size("hid")
    groups = None
    if ways > 1:
        groups = [[t * ways + w for t in range(size // ways)] for w in range(ways)]
    return lax.all_to_all(
        values_in, "hid", split_axis=0, concat_axis=0, tiled=True, axis_index_groups=groups
    )


def turn_heads(values_in, cosine, sine):
    half = ROT // 2
    front, back = values_in[:half], values_in[half:ROT]
    return jnp.concatenate(
        [front * cosine - back * sine, back * cosine + front * sine, values_in[ROT:]], axis=0
    )


def across(left, right, left_dim, right_dim):
    return lax.dot_general(
        left, right, (((left_dim,), (right_dim,)), ((), ())), preferred_element_type=full
    )


def attend_kernel(
    products_ref, cosine_ref, sine_ref, start_ref, heads_ref, attended_ref, tops_ref
):
    tokens = products_ref.shape[2]
    for s in range(2):
        turned = turn_heads(products_ref[s], cosine_ref[...], sine_ref[...])
        heads_ref[s] = turned.astype(low)
    heads_ref[2] = products_ref[2].astype(low)
    for first in range(0, tokens, SPAN):
        stop = first + SPAN
        span = slice(first, stop)
        scores, top = masked_scores(heads_ref, start_ref, first)
        weights = jnp.exp(scores - top)
        total = jnp.sum(weights, axis=0, keepdims=True)
        weights = (weights / total).astype(low)
        mixed = across(heads_ref[2, :, :stop], weights, 1, 0)
        attended_ref[:, span] = mixed.astype(low)
        tops_ref[0, 0:1, span] = top
        tops_ref[0, 1:2, span] = total


def masked_scores(heads_ref, start_ref, first):
    stop = first + SPAN
    span = slice(first, stop)
    scores = across(heads_ref[1, :, :stop], heads_ref[0, :, span], 0, 0) / math.sqrt(HEAD)
    key = lax.broadcasted_iota(jnp.int32, scores.shape, 0)
    query = lax.broadcasted_iota(jnp.int32, scores.shape, 1) + first
    seen = (key >= start_ref[:, span]) & (key <= query)
    scores = jnp.where(seen, scores, -1e30)
    return scores, jnp.max(scores, axis=0, keepdims=True)


def attend_back_kernel(
    heads_ref, gradient_ref, cosine_ref, sine_ref, start_ref, tops_ref, lows_ref, key_sum, value_sum
):
    tokens = heads_ref.shape[2]
    cosine, sine = cosine_ref[...], sine_ref[...]
    scale = 1.0 / math.sqrt(HEAD)
    key_sum[...] = jnp.zeros_like(key_sum)
    value_sum[...] = jnp.zeros_like(value_sum)
    for first in range(0, tokens, SPAN):
        stop = first + SPAN
        span = slice(first, stop)
        scores, _ = masked_scores(heads_ref, start_ref, first)
        probs = jnp.exp(scores - tops_ref[0, 0:1, span]) / tops_ref[0, 1:2, span]
        gradient = gradient_ref[:, span]
        change = across(heads_ref[2, :, :stop], gradient, 0, 0)
        row_total = jnp.sum(probs * change, axis=0, keepdims=True)
        change = (probs * (change - row_total)).astype(low)
        query = across(heads_ref[1, :, :stop], change, 1, 0) * scale
        lows_ref[0, :, span] = turn_heads(query, cosine[:, span], -sine[:, span]).astype(low)
        key_sum[:, :stop] = key_sum[:, :stop] + across(heads_ref[0, :, span], change, 1, 1) * scale
        value_sum[:, :stop] = value_sum[:, :stop] + across(gradient, probs.astype(low), 1, 1)
    lows_ref[1] = turn_heads(key_sum[...], cosine, -sine).astype(low)
    lows_ref[2] = value_sum[...].astype(low)


def attend(products, cosine, sine, start):
    _, n_heads, head, tokens = products.shape
    per_head = pl.BlockSpec((3, None, head, tokens), lambda h: (0, h, 0, 0))
    table = pl.BlockSpec(cosine.shape, lambda h: (0, 0))
    return pl.pallas_call(
        attend_kernel,
        grid=(n_heads,),
        out_shape=[
            jax.ShapeDtypeStruct(products.shape, low),
            jax.ShapeDtypeStruct((n_heads, head, tokens), low),
            jax.ShapeDtypeStruct((n_heads, 2, tokens), full),
        ],
        in_specs=[per_head, table, table, pl.BlockSpec(start.shape, lambda h: (0, 0))],
        out_specs=[
            per_head,
            pl.BlockSpec((None, head, tokens), lambda h: (h, 0, 0)),
            pl.BlockSpec((1, 2, tokens), lambda h: (h, 0, 0)),
        ],
        compiler_params=pltpu.CompilerParams(vmem_limit_bytes=40 << 20),
        cost_estimate=pl.CostEstimate(
            flops=4 * n_heads * head * tokens * tokens,
            bytes_accessed=10 * products.size,
            transcendentals=n_heads * tokens * tokens,
        ),
    )(products, cosine, sine, start)


def attend_back(heads, gradient, cosine, sine, start, tops):
    _, n_heads, head, tokens = heads.shape
    per_head = pl.BlockSpec((3, None, head, tokens), lambda h: (0, h, 0, 0))
    table = pl.BlockSpec(cosine.shape, lambda h: (0, 0))
    return pl.pallas_call(
        attend_back_kernel,
        grid=(n_heads,),
        out_shape=jax.ShapeDtypeStruct(heads.shape, low),
        in_specs=[
            per_head,
            pl.BlockSpec((None, head, tokens), lambda h: (h, 0, 0)),
            table,
            table,
            pl.BlockSpec(start.shape, lambda h: (0, 0)),
            pl.BlockSpec((1, 2, tokens), lambda h: (h, 0, 0)),
        ],
        out_specs=per_head,
        scratch_shapes=[pltpu.VMEM((head, tokens), full)] * 2,
        compiler_params=pltpu.CompilerParams(vmem_limit_bytes=40 << 20),
        cost_estimate=pl.CostEstimate(
            flops=10 * n_heads * head * tokens * tokens,
            bytes_accessed=6 * heads.size,
            transcendentals=n_heads * tokens * tokens,
        ),
    )(heads, gradient, cosine, sine, start, tops)


def forward_kernel(dims, *refs):
    places, piece, group, n_head, n_units = dims
    (send_ref, mom_ref, gains_ref, query_ref, key_ref, value_ref, up_ref), refs = refs[:7], refs[7:]
    (
        normed_ref,
        own_ref,
        shift_ref,
        active_ref,
        slope_ref,
        heads_ref,
        turned_ref,
        turned_up_ref,
    ), refs = refs[:8], refs[8:]
    (
        devs,
        moms,
        joins,
        weights,
        core_out,
        core_in,
        outer_out,
        outer_in,
        mom_send,
        mom_recv,
        dev_send,
        dev_recv,
        way_send,
        way_recv,
        pair_send,
        pair_recv,
        join_send,
        join_recv,
        weight_sem,
        turned_sem,
        core_send,
        core_recv,
        outer_send,
        outer_recv,
    ) = refs
    count = weights.shape[0]
    ups = n_units // n_head
    index, hid = lax.axis_index("dp"), lax.axis_index("hid")
    outer, core = index // 2, index % 2
    place, way = hid // 2, hid % 2
    me = index * 2 + way
    partner = {"hid": hid + 1 - 2 * way}
    core_peer = {"dp": index + 1 - 2 * core}
    outer_peer = {"dp": (index + 2) % 4}

    def peer(k):
        return (place + k) % places

    def z_device(k):
        return {"hid": peer(k) * 2 + way}

    others = [(i, j) for i in range(4) for j in range(2) if i or j]

    def join_device(i, j):
        return {"dp": (index + i) % 4, "hid": place * 2 + (way + j) % 2}

    def weight_copy(unit, t):
        there = (1 - outer if t < 2 else outer) * 2 + (core if t % 2 else 1 - core)
        block = there * 2 + way
        if unit < ups:
            source, start = up_ref, block * n_units + unit * n_head
        else:
            source, start = (query_ref, key_ref, value_ref)[unit - ups], block * n_head
        start = pl.multiple_of(start, n_head)
        return pltpu.make_async_copy(
            source.at[:, pl.ds(start, n_head)], weights.at[unit, t], weight_sem.at[unit]
        )

    for unit in range(count):
        for t in range(4):
            weight_copy(unit, t).start()

    barrier = pltpu.get_barrier_semaphore()

    for k in range(1, places):
        greet(z_device(k))
    for i, j in others:
        greet(join_device(i, j))
    pl.semaphore_wait(barrier, places - 1 + len(others))

    def mom_copy(k, sender, target):
        return remote(
            mom_ref.at[target], moms.at[way, sender], mom_send, mom_recv.at[sender], z_device(k)
        )

    def dev_copy(s, k, sender, target):
        return remote(
            send_ref.at[target, s],
            devs.at[s, way, sender],
            dev_send,
            dev_recv.at[s, sender],
            z_device(k),
        )

    for k in range(1, places):
        mom_copy(k, place, peer(k)).start()
    for s in (3, 0, 1, 2):
        for k in range(1, places):
            dev_copy(s, k, place, peer(k)).start()
    moms[way, place] = mom_ref[place]
    for s in range(STREAMS):
        devs[s, way, place] = send_ref[place, s]

    def way_copy(source, s, q):
        return remote(source, devs.at[s, way, q], way_send, way_recv.at[s], partner)

    def forward(s):
        way_copy(send_ref.at[place, s], s, place).start()
        for k in range(1, places):
            q = peer(k)
            dev_copy(s, k, q, q).wait_recv()
            way_copy(devs.at[s, way, q], s, q).start()

    def join_parts(means, parts, size):
        mean = means[0]
        for m in means[1:]:
            mean = mean + m
        mean = mean / len(means)
        total = parts[0]
        for v in parts[1:]:
            total = total + v
        for m in means:
            total = total + size * (m - mean) * (m - mean)
        return mean, total

    for k in range(1, places):
        mom_copy(k, peer(k), place).wait_recv()
    remote(moms.at[way], moms.at[way], pair_send, pair_recv, partner).start()
    mean, total = join_parts(
        [moms[way, q, :STREAMS, :] for q in range(places)],
        [moms[way, q, STREAMS:, :] for q in range(places)],
        piece,
    )
    joins[me, :STREAMS, :] = mean
    joins[me, STREAMS:, :] = total
    for i, j in others:
        remote(joins.at[me], joins.at[me], join_send, join_recv, join_device(i, j)).start()
    forward(3)
    n_others = len(others)
    remote(
        joins.at[pl.ds(0, n_others)], joins.at[pl.ds(0, n_others)], join_send, join_recv, partner
    ).wait_recv()
    remote(moms.at[way], moms.at[1 - way], pair_send, pair_recv, partner).wait_recv()
    mean, total = join_parts(
        [joins[i, :STREAMS, :] for i in range(n_others + 1)],
        [joins[i, STREAMS:, :] for i in range(n_others + 1)],
        piece * places,
    )
    scale = lax.rsqrt(total / (piece * places * (n_others + 1)) + 1e-05)
    for s in range(STREAMS):
        for q in range(places):
            for w in range(2):
                off = moms[w, q, s : s + 1, :] - mean[s : s + 1]
                shift_ref[s, 2 * q + w : 2 * q + w + 1, :] = off * scale[s : s + 1]
        shift_ref[s, 2 * places : 2 * places + 1, :] = scale[s : s + 1]
        shift_ref[s, 2 * places + 1 : 2 * places + 2, :] = mean[s : s + 1]

    def normalize(s):
        remote(devs.at[s, 1 - way], devs.at[s, 1 - way], way_send, way_recv.at[s], partner).wait_recv()
        size = shift_ref[s, 2 * places : 2 * places + 1, :]
        for q in range(places):
            for w in range(2):
                block = 2 * q + w
                rows = slice(block * piece, (block + 1) * piece)
                unit = devs[s, w, q].astype(full) * size + shift_ref[s, block : block + 1, :]
                normed_ref[s, rows, :] = (unit * gains_ref[s, rows, :]).astype(low)

    def core_copy(unit, half):
        return remote(
            core_out.at[unit, half],
            core_in.at[unit, half],
            core_send,
            core_recv.at[unit, half],
            core_peer,
        )

    def outer_copy(unit):
        return remote(
            outer_out.at[unit], outer_in.at[unit], outer_send, outer_recv.at[unit], outer_peer
        )

    def project(unit, carry):
        @pl.when(unit == 0)
        def _():
            normalize(3)
            forward(0)

        for s in (1, 2):

            @pl.when(unit == s)
            def _(s=s):
                forward(s)

        @pl.when(unit >= ups)
        def _():
            normalize(unit - ups)

        stream = jnp.where(unit < ups, 3, unit - ups)
        pltpu.make_async_copy(weights.at[unit], weights.at[unit], weight_sem.at[unit]).wait()

        def product(t):
            return lax.dot_general(
                weights[unit, t],
                normed_ref[stream],
                (((0,), (0,)), ((), ())),
                preferred_element_type=full,
            )

        core_out[unit, 0] = product(0).astype(low)
        core_copy(unit, 0).start()
        passing = product(1)
        core_out[unit, 1] = product(2).astype(low)
        core_copy(unit, 1).start()
        core_copy(unit, 0).wait_recv()
        outer_out[unit] = (passing + core_in[unit, 0].astype(full)).astype(low)
        outer_copy(unit).start()
        kept = product(3)
        core_copy(unit, 1).wait_recv()
        kept = kept + core_in[unit, 1].astype(full)

        @pl.when(unit < ups)
        def _():
            slope_ref[pl.ds(pl.multiple_of(unit * n_head, n_head), n_head), :] = kept

        @pl.when(unit >= ups)
        def _():
            heads_ref[unit - ups] = kept

        return carry

    lax.fori_loop(0, count, project, 0)

    def turned_copies():
        for unit in range(count):
            for t in range(4):
                turn = 3 - t
                if unit < ups:
                    start = turn * n_units + unit * n_head
                    target = turned_up_ref.at[:, start : start + n_head]
                else:
                    target = turned_ref.at[unit - ups, :, turn * n_head : (turn + 1) * n_head]
                yield pltpu.make_async_copy(weights.at[unit, t], target, turned_sem)

    for copy in turned_copies():
        copy.start()
    for s in range(STREAMS):
        own_ref[s] = devs[s, way]

    step = 32

    def finish_up(unit, carry):
        outer_copy(unit).wait_recv()

        def part(i, carry):
            inner = pl.ds(pl.multiple_of(i * step, step), step)
            rows = pl.ds(pl.multiple_of(unit * n_head + i * step, step), step)
            hidden = slope_ref[rows, :] + outer_in[unit, inner, :].astype(full)
            half = 0.5 + 0.5 * lax.erf(hidden * math.sqrt(0.5))
            active_ref[rows, :] = (hidden * half).astype(low)
            bell = jnp.exp(-0.5 * hidden * hidden) * (1.0 / math.sqrt(2.0 * math.pi))
            slope_ref[rows, :] = half + hidden * bell
            return carry

        return lax.fori_loop(0, n_head // step, part, carry)

    lax.fori_loop(0, ups, finish_up, 0)

    def finish_head(unit, carry):
        outer_copy(unit).wait_recv()
        heads_ref[unit - ups] = heads_ref[unit - ups] + outer_in[unit].astype(full)
        return carry

    lax.fori_loop(ups, count, finish_head, 0)

    def sent(ref, sem):
        remote(ref, ref, sem, join_recv, partner).wait_send()

    sent(moms.at[0, pl.ds(0, places - 1)], mom_send)
    sent(send_ref.at[pl.ds(0, places - 1)], dev_send)
    sent(send_ref, way_send)
    sent(moms.at[0], pair_send)
    sent(joins.at[pl.ds(0, n_others)], join_send)
    sent(core_out, core_send)
    sent(outer_out, outer_send)
    pltpu.make_async_copy(weights, weights, turned_sem).wait()


def forward_projections(deviations, moments, norm_gains, w_query, w_key, w_value, w_up):
    places, _, piece, group = deviations.shape
    feats = norm_gains.shape[0]
    n_head = w_query.shape[1] // 8
    n_units = w_up.shape[1] // 8
    count = n_units // n_head + 3
    vmem, dma = pltpu.VMEM, pltpu.SemaphoreType.DMA
    out_types = [
        ((STREAMS, feats, group), low),
        ((STREAMS, places, piece, group), low),
        ((STREAMS, 2 * places + 8, group), full),
        ((n_units, group), low),
        ((n_units, group), full),
        ((3, n_head, group), full),
        ((3, feats, 4 * n_head), low),
        ((feats, 4 * n_units), low),
    ]
    spaces = [vmem] * 6 + [pl.ANY] * 2
    return pl.pallas_call(
        functools.partial(forward_kernel, (places, piece, group, n_head, n_units)),
        out_shape=[jax.ShapeDtypeStruct(*t) for t in out_types],
        in_specs=[pl.BlockSpec(memory_space=vmem)] * 3 + [pl.BlockSpec(memory_space=pl.ANY)] * 4,
        out_specs=[pl.BlockSpec(memory_space=m) for m in spaces],
        scratch_shapes=[
            vmem((STREAMS, 2, places, piece, group), low),
            vmem((2, places, 2 * STREAMS, group), full),
            vmem((8, 2 * STREAMS, group), full),
            vmem((count, 4, feats, n_head), low),
            vmem((count, 2, n_head, group), low),
            vmem((count, 2, n_head, group), low),
            vmem((count, n_head, group), low),
            vmem((count, n_head, group), low),
            dma,
            dma((places,)),
            dma,
            dma((STREAMS, places)),
            dma,
            dma((STREAMS,)),
            dma,
            dma,
            dma,
            dma,
            dma((count,)),
            dma,
            dma,
            dma((count, 2)),
            dma,
            dma((count,)),
        ],
        compiler_params=pltpu.CompilerParams(
            collective_id=7, has_side_effects=True, vmem_limit_bytes=62 << 20
        ),
        cost_estimate=pl.CostEstimate(
            flops=8 * count * n_head * feats * group,
            bytes_accessed=300 << 20,
            transcendentals=2 * n_units * group,
        ),
    )(
        deviations,
        moments,
        norm_gains.T.astype(full)[:, :, None],
        w_query,
        w_key,
        w_value,
        w_up,
    )


def remote(source, target, send, recv, device):
    return pltpu.make_async_remote_copy(
        src_ref=source,
        dst_ref=target,
        send_sem=send,
        recv_sem=recv,
        device_id=device,
        device_id_type=pl.DeviceIdType.MESH,
    )


def greet(device):
    pl.semaphore_signal(
        pltpu.get_barrier_semaphore(),
        inc=1,
        device_id=device,
        device_id_type=pl.DeviceIdType.MESH,
    )


def chain_place(ways, places):
    last = places - 1
    me = lax.axis_index("hid")
    if ways == 2:
        place, way = me // 2, me % 2
        return place, way, me + 2, me - 2, me + 1 - 2 * way
    odd, half = me % 2, places // 2
    place = (1 - odd) * (me // 2) + odd * (last - me // 2)
    turn_up = (place + 1) // half
    turn_down = (place - 1 + places) // half - 2
    above = (1 - turn_up) * 2 * (place + 1) + turn_up * (2 * (last - place - 1) + 1)
    below = (1 - turn_down) * 2 * (place - 1) + turn_down * (2 * (last - place + 1) + 1)
    return place, 0, above, below, me


def chain_semaphores(count):
    dma = pltpu.SemaphoreType.DMA
    return [dma, dma((count,)), dma, dma((count,)), dma, dma, dma]


def chain_loop(ways, places, out_ref, own, landed, semaphores, compute, hook=None):
    up_send, up_recv, down_send, down_recv, side_send, side_recv, kept = semaphores
    count, depth = landed.shape[:2]
    per_tile = own.shape[0] // depth
    last = places - 1
    place, way, above, below, beside = chain_place(ways, places)

    def up_copy(i):
        return remote(landed.at[i], landed.at[i], up_send, up_recv.at[i], {"hid": above})

    def down_copy(source, i):
        return remote(source, out_ref.at[way, i], down_send, down_recv.at[i], {"hid": below})

    def side_copy(source, i):
        return remote(source, out_ref.at[way, i], side_send, side_recv, {"hid": beside})

    def upward(i):
        @pl.when(i % per_tile == 0)
        def _():
            compute(i // per_tile)

        mine = own[pl.ds(pl.multiple_of(i % per_tile * depth, depth), depth), :]

        @pl.when(place == 0)
        def _():
            landed[i] = mine.astype(low)
            up_copy(i).start()

        @pl.when(place > 0)
        def _():
            up_copy(i).wait_recv()
            landed[i] = (landed[i].astype(full) + mine).astype(low)

            @pl.when(place < last)
            def _():
                up_copy(i).start()

            @pl.when(place == last)
            def _():
                down_copy(landed.at[i], i).start()
                if ways == 2:
                    side_copy(landed.at[i], i).start()
                pltpu.make_async_copy(landed.at[i], out_ref.at[way, i], kept).start()

    def downward(i):
        down_copy(landed.at[i], i).wait_recv()

        @pl.when(place > 0)
        def _():
            down_copy(out_ref.at[way, i], i).start()

        if ways == 2:
            side_copy(out_ref.at[way, i], i).start()

    lag = SLACK * (last - place) + 2

    def step(i, carry):
        @pl.when(i < count)
        def _():
            upward(i)

        behind = i - lag

        @pl.when((behind >= 0) & (behind < count) & (place < last))
        def _():
            downward(behind)

        if hook is not None:
            hook(i)
        return carry

    lax.fori_loop(0, count + SLACK * last + 2, step, 0)

    @pl.when(place < last)
    def _():
        remote(landed, landed, up_send, kept, {"hid": above}).wait_send()

    @pl.when(place > 0)
    def _():
        remote(landed, out_ref.at[way], down_send, kept, {"hid": below}).wait_send()

    @pl.when(place == last)
    def _():
        pltpu.make_async_copy(landed, out_ref.at[way], kept).wait()

    if ways == 2:
        remote(landed, out_ref.at[way], side_send, kept, {"hid": beside}).wait_send()
        remote(landed, out_ref.at[1 - way], kept, side_recv, {"hid": beside}).wait_recv()


def chain_kernel(ways, places, blocks, n_operands, *refs):
    operand_refs, out_ref, refs = refs[:n_operands], refs[n_operands], refs[n_operands + 1 :]
    operands, (own, landed, fetched, *semaphores) = refs[:n_operands], refs[n_operands:]
    last = places - 1
    place, way, above, below, beside = chain_place(ways, places)

    def fetch(n):
        return pltpu.make_async_copy(operand_refs[n], operands[n], fetched.at[n])

    for n in range(n_operands):
        fetch(n).start()

    barrier = pltpu.get_barrier_semaphore()

    @pl.when(place > 0)
    def _():
        greet({"hid": below})

    @pl.when(place < last)
    def _():
        greet({"hid": above})

    if ways == 2:
        greet({"hid": beside})
    met = jnp.where(place > 0, 1, 0) + jnp.where(place < last, 1, 0) + (ways - 1)
    pl.semaphore_wait(barrier, met)

    def compute(tile):
        seen, first = set(), 0
        for rows, segments in blocks:
            start = first
            first = first + rows // TILE
            fresh = [n for seg in segments for n in (seg[0], seg[2])]
            fresh = [n for n in dict.fromkeys(fresh) if n not in seen]
            seen.update(fresh)

            @pl.when(tile == start)
            def _(fresh=fresh):
                for n in fresh:
                    fetch(n).wait()

            @pl.when((tile >= start) & (tile < first))
            def _(start=start, segments=segments):
                column = 0
                for left, left_row, right, right_row, size in segments:
                    row = pl.multiple_of(left_row + (tile - start) * TILE, TILE)
                    own[:, column : column + size] = lax.dot_general(
                        operands[left][pl.ds(row, TILE), :],
                        operands[right][right_row : right_row + size, :],
                        (((1,), (1,)), ((), ())),
                        preferred_element_type=full,
                    )
                    column += size

    chain_loop(ways, places, out_ref, own, landed, semaphores, compute)


def chain_sum(operands, blocks, collective_id):
    ways, size = split_ways(), lax.axis_size("hid")
    columns = sum(seg[4] for seg in blocks[0][1])
    rows = sum(block[0] for block in blocks)
    depth = max(16, CHUNK // columns)
    count = rows // depth
    tokens = operands[0].shape[1]
    return pl.pallas_call(
        functools.partial(chain_kernel, ways, size // ways, blocks, len(operands)),
        out_shape=jax.ShapeDtypeStruct((ways, count, depth, columns), low),
        in_specs=[pl.BlockSpec(memory_space=pl.ANY)] * len(operands),
        out_specs=pl.BlockSpec(memory_space=pl.ANY),
        scratch_shapes=[pltpu.VMEM(v.shape, low) for v in operands]
        + [
            pltpu.VMEM((TILE, columns), full),
            pltpu.VMEM((count, depth, columns), low),
            pltpu.SemaphoreType.DMA((len(operands),)),
        ]
        + chain_semaphores(count),
        compiler_params=pltpu.CompilerParams(
            collective_id=collective_id, has_side_effects=True, vmem_limit_bytes=60 << 20
        ),
        cost_estimate=pl.CostEstimate(
            flops=2 * rows * columns * tokens,
            bytes_accessed=300 * rows * columns,
            transcendentals=0,
        ),
    )(*operands)


def late_kernel(dims, *refs):
    places, piece, group, n_head, n_units = dims
    (
        hidden_ref,
        hidden_far_ref,
        lows_ref,
        lows_far_ref,
        output_low_ref,
        attended_ref,
        normed_ref,
        turned_ref,
        turned_up_ref,
        devs_ref,
        output_grad_ref,
        shifts,
        scales,
        gains,
        all_gains,
    ), refs = refs[:15], refs[15:]
    (out_ref, split_ref, gain_ref), refs = refs[:3], refs[3:]
    (
        hidden,
        lows,
        output_low,
        attended,
        normed,
        turned,
        turned_up,
        devs,
        output_grad,
        kept,
        given,
        taken,
        grads,
        joins,
        totals,
        own,
        landed,
        fetched,
        core_send,
        core_recv,
        side_send,
        side_recv,
        join_send,
        join_recv,
        place_send,
        place_recv,
        own_copy,
        *semaphores,
    ) = refs
    index, hid = lax.axis_index("dp"), lax.axis_index("hid")
    core = index % 2
    place, way = hid // 2, hid % 2
    me = index * 2 + way
    partner = {"hid": hid + 1 - 2 * way}
    core_peer = {"dp": index + 1 - 2 * core}
    others = [(i, j) for i in range(4) for j in range(2) if i or j]
    wide = own.shape[1]
    feats = normed.shape[1]

    def join_device(i, j):
        return {"dp": (index + i) % 4, "hid": place * 2 + (way + j) % 2}

    def head_rows(turn):
        return slice(turn * n_head, (turn + 1) * n_head)

    def unit_rows(turn):
        return slice(turn * n_units, (turn + 1) * n_units)

    fetches = [
        [(output_low_ref, output_low), (attended_ref, attended), (normed_ref, normed)],
        [(hidden_ref, hidden.at[unit_rows(0)])],
        [
            (hidden_far_ref, hidden.at[unit_rows(2)]),
            (turned_ref, turned),
            (turned_up_ref, turned_up),
            (devs_ref, devs),
            (output_grad_ref, output_grad),
        ]
        + [
            (source.at[head_rows(s)], lows.at[s, head_rows(turn)])
            for s in range(3)
            for turn, source in ((0, lows_ref), (2, lows_far_ref))
        ],
    ]

    def fetch(stage):
        return [pltpu.make_async_copy(a, b, fetched.at[stage, n]) for n, (a, b) in enumerate(fetches[stage])]

    for stage in range(len(fetches)):
        for copy in fetch(stage):
            copy.start()

    for k in range(1, places):
        greet({"hid": (place + k) % places * 2 + way})
    for i, j in others:
        greet(join_device(i, j))
    pl.semaphore_wait(pltpu.get_barrier_semaphore(), places - 1 + len(others))

    def core_copies(far):
        source, heads = (hidden_far_ref, lows_far_ref) if far else (hidden_ref, lows_ref)
        turn = 3 if far else 1
        yield remote(source, hidden.at[unit_rows(turn)], core_send.at[far], core_recv.at[far], core_peer)
        for s in range(3):
            yield remote(
                heads.at[head_rows(s)],
                lows.at[s, head_rows(turn)],
                core_send.at[2 + far],
                core_recv.at[2 + far],
                core_peer,
            )

    for far in range(2):
        for copy in core_copies(far):
            copy.start()

    def wait_cores():
        for far in range(2):
            remote(hidden_ref, hidden_ref, core_send.at[far], core_recv.at[far], core_peer).wait_recv()
            remote(lows_ref, lows_ref, core_send.at[2 + far], core_recv.at[2 + far], core_peer).wait_recv()

    per_block = feats // LATE_TILE
    per_out = n_head // LATE_TILE

    def compute(tile):
        @pl.when(tile == 0)
        def _():
            for copy in fetch(0):
                copy.wait()

        @pl.when(tile == per_block)
        def _():
            for copy in fetch(1):
                copy.wait()

        inner = tile % per_block

        def product(left, right):
            own[...] = lax.dot_general(
                left, right, (((1,), (1,)), ((), ())), preferred_element_type=full
            )

        def rows(n):
            return pl.ds(pl.multiple_of(n * LATE_TILE, LATE_TILE), LATE_TILE)

        @pl.when(tile < per_block)
        def _():
            half = pl.ds(pl.multiple_of(inner // per_out * wide, wide), wide)
            product(attended[rows(inner % per_out), :], output_low[half, :])

        block = tile // per_block

        @pl.when((block >= 1) & (block < 5))
        def _():
            turn = (block - 1) // 2 + (block - 1) % 2 * 2
            units = pl.ds(pl.multiple_of(turn * n_units, n_units), n_units)
            product(normed[3, rows(inner), :], hidden[units, :])

        @pl.when(block >= 5)
        def _():
            product(normed[block - 5, rows(inner), :], lows[block - 5])

    totals[...] = jnp.zeros_like(totals)

    def side_copy(s, r):
        return remote(given.at[s, r], taken.at[s, r], side_send, side_recv.at[s], partner)

    def pull(s):
        def use(part):
            for r in range(places):
                rows = slice(2 * piece * r, 2 * piece * (r + 1))
                here = part[rows]
                totals[s, 0:1, :] = totals[s, 0:1, :] + jnp.sum(
                    here * all_gains[s, r], axis=0, keepdims=True
                )
                totals[s, 1:2, :] = totals[s, 1:2, :] + jnp.sum(
                    here * normed[s, rows, :].astype(full), axis=0, keepdims=True
                )
                first = way == 0
                kept[s, r] = jnp.where(first, here[:piece], here[piece:])
                given[s, r] = jnp.where(first, here[piece:], here[:piece]).astype(low)
                side_copy(s, r).start()

        @pl.when(s < 3)
        def _():
            use(jnp.dot(turned[s], lows[s], preferred_element_type=full))

        @pl.when(s == 3)
        def _():
            use(jnp.dot(turned_up[...], hidden[...], preferred_element_type=full))

    def share_totals():
        joins[me] = totals[...]
        for i, j in others:
            remote(joins.at[me], joins.at[me], join_send, join_recv, join_device(i, j)).start()

    def sum_totals():
        some = joins.at[pl.ds(0, len(others))]
        remote(some, some, join_send, join_recv, partner).wait_recv()
        total = joins[0]
        for i in range(1, len(others) + 1):
            total = total + joins[i]
        totals[...] = total / (feats * 4)

    def stream_grad(s, r):
        @pl.when(r == 0)
        def _():
            remote(given.at[s], taken.at[s], side_send, side_recv.at[s], partner).wait_recv()

        gradient = kept[s, r] + taken[s, r].astype(full)
        unit = devs[s, r].astype(full) * scales[s] + shifts[s, r]
        gain_ref[s, r] = jnp.sum(gradient * unit, axis=1, keepdims=True)
        result = gradient * gains[s, r] - totals[s, 0:1, :] - unit * totals[s, 1:2, :]
        extra = output_grad[r] * jnp.where(s == 3, 1.0, 0.0)
        grads[s, r] = (result * scales[s] + extra).astype(low)

        @pl.when(r == place)
        def _():
            pltpu.make_async_copy(grads.at[s, r], split_ref.at[s, place], own_copy).start()

        @pl.when(r != place)
        def _():
            remote(
                grads.at[s, r],
                split_ref.at[s, place],
                place_send,
                place_recv,
                {"hid": r * 2 + way},
            ).start()

    n_pulls = STREAMS * places
    middle = PULL_START + PULL_GAP * STREAMS
    resume = middle + 8

    def hook(i):
        @pl.when(i == PULL_START)
        def _():
            for copy in fetch(2):
                copy.wait()
            wait_cores()

        k = (i - PULL_START) // PULL_GAP

        @pl.when((i >= PULL_START) & (i < middle) & ((i - PULL_START) % PULL_GAP == 0))
        def _():
            pull(k)

        @pl.when(i == middle)
        def _():
            share_totals()

        @pl.when(i == resume)
        def _():
            sum_totals()

        n = (i - resume) // GRAD_GAP

        @pl.when((i >= resume) & (n < n_pulls) & ((i - resume) % GRAD_GAP == 0))
        def _():
            stream_grad(n // places, n % places)

    chain_loop(2, places, out_ref, own, landed, semaphores, compute, hook)

    def sent(ref, sem):
        remote(ref, ref, sem, join_recv, partner).wait_send()

    for far in range(2):
        sent(hidden_ref, core_send.at[far])
        sent(lows_ref, core_send.at[2 + far])
    sent(given, side_send)
    sent(joins.at[pl.ds(0, len(others))], join_send)
    moved = grads.at[pl.ds(0, places - 1)]
    sent(moved, place_send)
    remote(moved, moved, place_send, place_recv, partner).wait_recv()
    mine = grads.at[0]
    pltpu.make_async_copy(mine, mine, own_copy).wait()


def late_sums(operands, tables, collective_id):
    hidden, _, lows, _, output_low, attended, normed = operands[:7]
    _, places, piece, group = operands[9].shape
    feats = normed.shape[1]
    n_units, n_head = hidden.shape[0], attended.shape[0]
    wide = n_units
    rows = 8 * feats
    depth = max(16, CHUNK // wide)
    count = rows // depth
    vmem, dma = pltpu.VMEM, pltpu.SemaphoreType.DMA
    block = (STREAMS, places, piece, group)
    outs = [
        jax.ShapeDtypeStruct((2, count, depth, wide), low),
        jax.ShapeDtypeStruct(block, low),
        jax.ShapeDtypeStruct((STREAMS, places, piece, 1), full),
    ]
    any_space, vmem_space = pl.BlockSpec(memory_space=pl.ANY), pl.BlockSpec(memory_space=vmem)
    total, split, gain_parts = pl.pallas_call(
        functools.partial(late_kernel, (places, piece, group, n_head, n_units)),
        out_shape=outs,
        in_specs=[any_space] * len(operands) + [vmem_space] * len(tables),
        out_specs=[any_space, any_space, vmem_space],
        scratch_shapes=[
            vmem((4 * n_units, group), low),
            vmem((3, 4 * n_head, group), low),
            vmem(output_low.shape, low),
            vmem(attended.shape, low),
            vmem(normed.shape, low),
            vmem(operands[7].shape, low),
            vmem(operands[8].shape, low),
            vmem(block, low),
            vmem(block[1:], full),
            vmem(block, full),
            vmem(block, low),
            vmem(block, low),
            vmem(block, low),
            vmem((8, STREAMS, 2, group), full),
            vmem((STREAMS, 2, group), full),
            vmem((LATE_TILE, wide), full),
            vmem((count, depth, wide), low),
            dma((3, 11)),
            dma((4,)),
            dma((4,)),
            dma,
            dma((STREAMS,)),
            dma,
            dma,
            dma,
            dma,
            dma,
        ]
        + chain_semaphores(count),
        compiler_params=pltpu.CompilerParams(
            collective_id=collective_id, has_side_effects=True, vmem_limit_bytes=63 << 20
        ),
        cost_estimate=pl.CostEstimate(
            flops=4 * rows * wide * group, bytes_accessed=900 << 20, transcendentals=0
        ),
    )(*operands, *tables)
    return total.reshape(2, 8, feats, wide), split, gain_parts


def chain_sums(operands, blocks, collective_id):
    groups, held, size = [[]], set(), 0
    for rows, segments in blocks:
        used = {n for seg in segments for n in (seg[0], seg[2])}
        more = sum(2 * operands[n].size for n in used - held)
        more += 2 * rows * sum(seg[4] for seg in segments)
        if groups[-1] and size + more > VMEM:
            groups.append([])
            held, size = set(), 0
            more = sum(2 * operands[n].size for n in used)
            more += 2 * rows * sum(seg[4] for seg in segments)
        groups[-1].append((rows, segments))
        held |= used
        size += more
    totals = []
    for i, group in enumerate(groups):
        used = sorted({n for _, segments in group for seg in segments for n in (seg[0], seg[2])})
        place = {n: k for k, n in enumerate(used)}
        own = [
            (rows, [(place[a], b, place[c], d, e) for a, b, c, d, e in segments])
            for rows, segments in group
        ]
        total = chain_sum([operands[n] for n in used], own, collective_id + i)
        totals.append(total.reshape(total.shape[0], -1, total.shape[3]))
    return totals[0] if len(totals) == 1 else jnp.concatenate(totals, axis=1)


def assemble_kernel(ways, dp, fused, own_ref, *refs):
    halves, (up_ref, *head_refs, out_ref) = refs[:ways], refs[ways:]
    rows, wide = own_ref.shape[2:]
    size = up_ref.shape[1] // dp // ways
    blocks = dp * size // wide
    own = wide // dp
    feats = out_ref.shape[1] // dp
    for d in range(dp):
        turn = turn_of(d)
        for w in range(ways):
            start = turn * size
            lanes = pl.ds(pl.multiple_of(start % wide, size), size)
            place = (d * ways + w) * size
            up_block = 1 + turn // 2 + turn % 2 * 2 if fused else start // wide
            up_ref[:, place : place + size] = own_ref[w, up_block, :, lanes].astype(full)
            for s, ref in enumerate(head_refs):
                lanes = pl.ds(pl.multiple_of(turn * own, own), own)
                place = (d * ways + w) * own
                ref[:, place : place + own] = own_ref[w, blocks + s + fused, :, lanes].astype(full)
        start = turn * feats
        lanes = pl.ds(pl.multiple_of(start % wide, feats), feats)
        for w in range(ways):

            @pl.when(start // wide == w)
            def _(w=w, d=d, lanes=lanes):
                out_ref[:, d * feats : (d + 1) * feats] = halves[w][0, 0, :, lanes].astype(full)


def assemble(total, w_up, fused):
    ways, dp = split_ways(), lax.axis_size("dp")
    blocks, rows, wide = total.shape[1:]
    depth = min(64, rows // ways)
    share = rows // ways // depth

    def half_map(half):
        return lambda i: (i // share, 0 if fused else blocks - 1, half * share + i % share, 0)

    widths = [w_up.shape[1]] + [ways * wide] * 4
    return pl.pallas_call(
        functools.partial(assemble_kernel, ways, dp, int(fused)),
        grid=(rows // depth,),
        out_shape=[jax.ShapeDtypeStruct((rows, n), full) for n in widths],
        in_specs=[pl.BlockSpec((ways, blocks, depth, wide), lambda i: (0, 0, i, 0))]
        + [pl.BlockSpec((1, 1, depth, wide), half_map(half)) for half in range(ways)],
        out_specs=[pl.BlockSpec((depth, n), lambda i: (i, 0)) for n in widths],
        compiler_params=pltpu.CompilerParams(vmem_limit_bytes=48 << 20),
        cost_estimate=pl.CostEstimate(
            flops=0, bytes_accessed=6 * total.size, transcendentals=0
        ),
    )(total, *[total] * ways)


def unturn_kernel(dp, own_ref, out_ref):
    size = out_ref.shape[1] // dp
    for d in range(dp):
        lanes = pl.ds(pl.multiple_of(turn_of(d) * size, size), size)
        out_ref[:, d * size : (d + 1) * size] = own_ref[:, lanes].astype(full)


def unturn(total):
    rows, columns = total.shape
    depth = 256
    return pl.pallas_call(
        functools.partial(unturn_kernel, lax.axis_size("dp")),
        grid=(rows // depth,),
        out_shape=jax.ShapeDtypeStruct((rows, columns), full),
        in_specs=[pl.BlockSpec((depth, columns), lambda i: (i, 0))],
        out_specs=pl.BlockSpec((depth, columns), lambda i: (i, 0)),
        cost_estimate=pl.CostEstimate(
            flops=0, bytes_accessed=6 * total.size, transcendentals=0
        ),
    )(total)


def to_owner(values_in):
    dp, hid, ways = lax.axis_size("dp"), lax.axis_size("hid"), split_ways()
    index = lax.axis_index("dp") * ways + lax.axis_index("hid") % ways
    mine = lax.dynamic_index_in_dim(values_in, index, 1, keepdims=False)
    pairs = [
        (d * hid + t * ways + w, (t * dp + d) * ways + w)
        for d in range(dp)
        for t in range(hid // ways)
        for w in range(ways)
    ]
    return lax.ppermute(mine, ("dp", "hid"), pairs)


def rotate(values_in, cosine, sine):
    half = cosine.shape[1]
    front, back = values_in[:, :half], values_in[:, half : 2 * half]
    return jnp.concatenate(
        [
            front * cosine - back * sine,
            back * cosine + front * sine,
            values_in[:, 2 * half :],
        ],
        axis=1,
    )


def local(
    history,
    mix,
    segment_ids,
    norm_gains,
    w_query,
    w_key,
    w_value,
    w_out,
    w_up,
    w_down,
    w_mixer,
    mixer_out,
    mix_static,
    out_cotangent,
    mix_cotangent,
):
    dp, hid, ways = lax.axis_size("dp"), lax.axis_size("hid"), split_ways()
    places = hid // ways
    my_hid = lax.axis_index("hid")
    place, way = my_hid // ways, my_hid % ways
    block = segment_ids.shape[0]
    total_tokens = block * dp * hid
    row = total_tokens // dp
    group = total_tokens // places
    rows = group // row
    piece = history.shape[2]
    mine = piece * places
    feats = piece * hid
    width = feats * dp
    heads = HEADS // dp // ways
    n_mix = mix.shape[1]
    n_cot = mix_cotangent.shape[1]

    def by_place(values_in):
        return jnp.stack(
            [values_in[..., p * group : (p + 1) * group] for p in range(places)], axis=0
        )

    stored = history.swapaxes(1, 2)
    mix_all = gather_all(mix.T)
    own_means, own_devs, deviations = [], [], []
    for s in range(STREAMS):
        total = mix_all[s * HIST] * stored[0].astype(full)
        for j in range(1, HIST):
            total = total + mix_all[s * HIST + j] * stored[j].astype(full)
        own_means.append(jnp.mean(total, axis=0))
        off = total - own_means[s]
        own_devs.append(jnp.sum(off * off, axis=0))
        deviations.append(off.astype(low))
    moments = by_place(jnp.stack(own_means + own_devs, axis=0))
    deviations = by_place(jnp.stack(deviations, axis=0))
    fused = dp == 4 and ways == 2 and rows == 1

    table = jnp.concatenate([mix_cotangent.T, segment_ids.astype(full)[None]], axis=0)
    table = lax.dynamic_slice_in_dim(gather_all(table), place * group, group, 1)
    cot_t = table[:n_cot]
    ids = table[-1].reshape(rows, row)

    there = jnp.arange(row, dtype=jnp.int32)
    same_doc = ids[:, :, None] == ids[:, None, :]
    doc_start = jnp.min(jnp.where(same_doc, there[None, None], row), axis=2)
    position = (there[None] - doc_start).astype(full).reshape(group)
    visible = same_doc & (there[None, None] <= there[None, :, None])
    frequency = rope_base ** (-jnp.arange(ROT // 2, dtype=full) * 2.0 / ROT)
    angle = frequency[:, None] * position[None, :]
    cosine, sine = jnp.cos(angle)[None], jnp.sin(angle)[None]

    def own_rows(values_in):
        parts = values_in.reshape((places, ways, piece) + values_in.shape[1:])
        part = lax.dynamic_index_in_dim(parts, way, 1, keepdims=False)
        return part.reshape((mine,) + values_in.shape[1:])

    def all_rows(values_in):
        parts = values_in.reshape((places, piece) + values_in.shape[1:])
        return gather_ways(parts, 1).reshape((feats,) + values_in.shape[1:])

    own_gains = own_rows(norm_gains).astype(full)
    gains = [own_gains[:, s][:, None] for s in range(STREAMS)]
    all_gains = norm_gains.astype(full)

    def project(weight, left):
        columns = weight.shape[1] // dp // ways

        def make(index):
            start = (index * ways + way) * columns
            part = lax.dynamic_slice_in_dim(weight, start, columns, 1)
            return contract(part, left, 0, 0)

        return scatter_dp(make)

    def way_columns(weight):
        if ways == 1:
            return weight
        size = weight.shape[1] // dp // ways
        parts = [weight[:, i * size : (i + 1) * size] for i in range(dp * ways)]
        pairs = zip(parts[::2], parts[1::2])
        return jnp.concatenate([jnp.where(way == 0, a, b) for a, b in pairs], axis=1)

    def way_rows(weight):
        size = weight.shape[0] // ways
        return lax.dynamic_slice_in_dim(weight, way * size, size, 0)

    def by_head(values_in):
        return values_in.reshape(heads, HEAD, group)

    def turned(weight, stride, offset, size):
        starts = [turn_source(turn) * stride + offset for turn in range(dp)]
        parts = [lax.dynamic_slice_in_dim(weight, start, size, 1) for start in starts]
        return jnp.concatenate(parts, axis=1)

    n_head = heads * HEAD
    n_units = w_up.shape[1] // dp // ways
    if fused:
        normed, deviations, shifts, active, slope, products, turned_heads, turned_up = (
            forward_projections(deviations, moments, norm_gains, w_query, w_key, w_value, w_up)
        )
        inv_scales = shifts[:, 2 * places]
        own_shifts = shifts[:, : 2 * places].reshape(STREAMS, places, ways, group)
        own_shifts = lax.dynamic_index_in_dim(own_shifts, way, 2, keepdims=False)
        offset = own_shifts[3] / inv_scales[3] + shifts[3, 2 * places + 1]
        residual = (deviations[3].astype(full) + offset[:, None]).reshape(mine, group)
        units = [
            (deviations[s].astype(full) * inv_scales[s] + own_shifts[s][:, None]).reshape(mine, group)
            for s in range(STREAMS)
        ]
        normed_all = normed
        normed = [normed[s] for s in range(STREAMS)]
        products = products.reshape(3, heads, HEAD, group)
        turned_weights = [turned_heads[s] for s in range(3)] + [turned_up]
    else:
        moments = exchange(moments)
        deviations = exchange(deviations)
        deviations = [deviations[:, s] for s in range(STREAMS)]
        def join_moments(mean_parts, dev_parts, size):
            mean = jnp.mean(mean_parts, axis=0)
            spread = size * jnp.sum(jnp.square(mean_parts - mean), axis=0)
            return mean, jnp.sum(dev_parts, axis=0) + spread

        block_means = moments[:, :STREAMS]
        joined = join_moments(block_means, moments[:, STREAMS:], piece)
        joined = gather_dp(gather_ways(jnp.concatenate(joined, axis=0), 0))
        joined = joined.reshape((dp * ways,) + joined.shape[2:])
        means, variance = join_moments(joined[:, :STREAMS], joined[:, STREAMS:], mine)
        inv_scales = lax.rsqrt(variance / width + 1e-05)
        all_means = gather_ways(block_means, 1)

        def unit(values_in, block_mean, s):
            return (values_in.astype(full) + (block_mean - means[s])[..., None, :]) * inv_scales[s]

        units = [
            unit(deviations[s], block_means[:, s], s).reshape(mine, group) for s in range(STREAMS)
        ]
        normed = []
        for s in range(STREAMS):
            both = unit(gather_ways(deviations[s], 1), all_means[:, :, s], s).reshape(feats, group)
            normed.append((both * all_gains[:, s][:, None]).astype(low))
        residual = (deviations[3].astype(full) + block_means[:, 3][:, None]).reshape(mine, group)
        products = [
            by_head(project(w, normed[s])) for s, w in enumerate((w_query, w_key, w_value))
        ]
        hidden = project(w_up, normed[3])
        active, hidden_pull = jax.vjp(gelu_exact, hidden)
        active = active.astype(low)
        (slope,) = hidden_pull(jnp.ones_like(hidden))
        turned_weights = [
            turned(w, ways * n_head, way * n_head, n_head) for w in (w_query, w_key, w_value)
        ] + [turned(w_up, ways * n_units, way * n_units, n_units)]
    out_rows, down_rows = way_rows(w_out), way_rows(w_down)
    turned_weights += [turned(out_rows, feats, 0, feats), turned(down_rows, feats, 0, feats)]

    def by_row(values_in):
        if rows == 1:
            return values_in
        return (
            values_in.reshape(heads, HEAD, rows, row)
            .transpose(0, 2, 1, 3)
            .reshape(heads * rows, HEAD, row)
        )

    def from_row(values_in):
        if rows == 1:
            return values_in
        return (
            values_in.reshape(heads, rows, HEAD, row)
            .transpose(0, 2, 1, 3)
            .reshape(heads, HEAD, group)
        )

    if fused:
        starts = doc_start.reshape(1, group)
        turned_values, attended, tops = attend(products, cosine[0], sine[0], starts)
        attended = attended.reshape(n_head, group)
    else:
        queries = rotate(products[0], cosine, sine).astype(low)
        keys = rotate(products[1], cosine, sine).astype(low)
        values = products[2].astype(low)
        q_rows, k_rows, v_rows = by_row(queries), by_row(keys), by_row(values)
        score_scale = 1.0 / math.sqrt(HEAD)
        scores = batched(q_rows, k_rows, 1, 1) * score_scale
        mask = jnp.broadcast_to(visible[None], (heads, rows, row, row)).reshape(scores.shape)
        scores = jnp.where(mask, scores, -1e30)
        probs = jax.nn.softmax(scores, axis=-1)
        probs_low = probs.astype(low)
        attended = from_row(batched(v_rows, probs_low, 2, 2).astype(low)).reshape(heads * HEAD, group)

    cotangent, attended = lax.optimization_barrier((out_cotangent, attended))
    upstream = exchange(by_place(cotangent.T)).reshape(mine, group)

    def make_out(index):
        start = index * feats
        left = lax.dynamic_slice_in_dim(out_rows, start, feats, 1)
        other = lax.dynamic_slice_in_dim(down_rows, start, feats, 1)
        return contract(left, attended, 0, 0) + contract(other, active, 0, 0)

    branches = scatter_dp(make_out).reshape(places, ways, piece, group)
    kept = lax.dynamic_index_in_dim(branches, way, 1, keepdims=False)
    if ways == 2:
        given = lax.dynamic_index_in_dim(branches, 1 - way, 1, keepdims=False).astype(low)
        kept = kept + hid_swap(given, 1).astype(full)
    output = residual + kept.reshape(mine, group)
    output, upstream, turned_weights = lax.optimization_barrier(
        (output, upstream, turned_weights)
    )
    upstream = upstream.astype(full)
    output_rounded = output.astype(low)

    block_output = exchange(output_rounded.reshape(places, piece, group))

    square = jnp.sum(output * output, axis=0, keepdims=True)
    mixer_rows = own_rows(w_mixer)
    mixer_part = contract(mixer_rows, output_rounded, 0, 0)
    sums = sum_features(jnp.concatenate([mixer_part, square], axis=0))
    inv_rms = lax.rsqrt(sums[-1] / width + 1e-06)
    inner_raw = sums[:-1]
    inner_pre = inner_raw * inv_rms
    inner_act, inner_pull = jax.vjp(gelu_exact, inner_pre)
    raw_mix = contract_high(mixer_out, inner_act, 0, 0)
    column = jnp.stack(
        [
            jnp.sum(raw_mix, axis=1),
            jnp.sum(raw_mix * raw_mix, axis=1),
            jnp.sum(cot_t, axis=1),
            jnp.sum(cot_t * raw_mix, axis=1),
        ],
        axis=0,
    )
    act_total = jnp.sum(inner_act, axis=1)
    act_cot = contract_high(inner_act, cot_t, 1, 1)
    act_raw = contract_high(inner_act, raw_mix, 1, 1)
    n_inner = act_total.shape[0]
    flat = sum_tokens(
        jnp.concatenate([column.reshape(-1), act_total, act_cot.reshape(-1), act_raw.reshape(-1)])
    )
    sum_raw, sum_square, sum_grad, sum_grad_raw = flat[: 4 * n_cot].reshape(4, n_cot)
    start = 4 * n_cot
    act_total = flat[start : start + n_inner]
    start += n_inner
    act_cot = flat[start : start + n_inner * n_cot].reshape(n_inner, n_cot)
    start += n_inner * n_cot
    act_raw = flat[start:].reshape(n_inner, n_cot)
    average = sum_raw / total_tokens
    variance_mix = sum_square / total_tokens - average * average
    inv_spread = lax.rsqrt(variance_mix + 1e-05)
    unit_mix = (raw_mix - average[:, None]) * inv_spread[:, None]
    mix_next = mix_static[:, None] + unit_mix
    mix_next = to_owner(mix_next.reshape(n_cot, dp * ways, block)).T
    mean_grad = sum_grad / total_tokens
    sum_grad_unit = inv_spread * (sum_grad_raw - average * sum_grad)
    mean_grad_unit = sum_grad_unit / total_tokens
    raw_grad = inv_spread[:, None] * (
        cot_t - mean_grad[:, None] - unit_mix * mean_grad_unit[:, None]
    )
    act_unit = inv_spread[None, :] * (act_raw - act_total[:, None] * average[None, :])
    mixer_out_grad = inv_spread[None, :] * (
        act_cot - act_total[:, None] * mean_grad[None, :] - act_unit * mean_grad_unit[None, :]
    )
    act_grad = contract_high(mixer_out, raw_grad, 1, 0)
    inner_low = inner_pull(act_grad)[0].astype(low)
    scaled = (output * inv_rms).astype(low)
    mixer_grad_part = contract(inner_low, scaled, 1, 1)
    scaled_grad = contract(mixer_rows, inner_low, 1, 0)
    along = jnp.sum(inner_low.astype(full) * inner_raw, axis=0) / width
    output_grad = upstream + inv_rms * scaled_grad - output * (inv_rms * inv_rms * inv_rms) * along
    output_lows = gather_turns(all_rows(output_grad.astype(low)))

    output_low = jnp.concatenate(output_lows, axis=0)

    hidden_low = (contract(turned_weights[5], output_low, 1, 0) * slope).astype(low)

    attended_grad = contract(turned_weights[4], output_low, 1, 0).astype(low)
    if fused:
        lows_mine = attend_back(
            turned_values, by_head(attended_grad), cosine[0], sine[0], starts, tops
        ).reshape(3 * n_head, group)
    else:
        a_rows = by_row(by_head(attended_grad))
        prob_grad = batched(a_rows, v_rows, 1, 1)
        row_total = jnp.sum(probs * prob_grad, axis=-1, keepdims=True)
        score_grad = (probs * (prob_grad - row_total)).astype(low)
        query_grad = from_row(batched(k_rows, score_grad, 2, 2) * score_scale)
        key_grad = from_row(batched(q_rows, score_grad, 2, 1) * score_scale)
        value_grad = from_row(batched(a_rows, probs_low, 2, 1))
        query_low = rotate(query_grad, cosine, -sine).astype(low).reshape(heads * HEAD, group)
        key_low = rotate(key_grad, cosine, -sine).astype(low).reshape(heads * HEAD, group)
        value_low = value_grad.astype(low).reshape(heads * HEAD, group)

        lows_mine = jnp.concatenate([query_low, key_low, value_low], axis=0)
    active_kept, hidden_low, lows_mine = lax.optimization_barrier((active, hidden_low, lows_mine))
    hidden_lows, lows = gather_outer(hidden_low), gather_outer(lows_mine)
    blocks = [(active.shape[0], [(0, 0, 1, 0, width)])]
    branch_sum = chain_sum([active_kept, output_low], blocks, 0)
    branch_sum, block_output, hidden_lows, lows = lax.optimization_barrier(
        (branch_sum, block_output, hidden_lows, lows)
    )
    block_output = block_output.transpose(1, 0, 2).reshape(piece, total_tokens).T

    if fused:
        operands = [hidden_lows[0], hidden_lows[1], lows[0], lows[1], output_low, attended]
        operands += [normed_all, turned_heads, turned_up, deviations]
        operands.append(output_grad.reshape(places, piece, group))
        tables = [
            own_shifts[:, :, None],
            inv_scales[:, None],
            own_gains.T.reshape(STREAMS, places, piece, 1),
            all_gains.T.reshape(STREAMS, places, 2 * piece, 1),
        ]
        late_sum, split, gain_parts = late_sums(operands, tables, 1)
        split = split.swapaxes(0, 1)
        gain_parts = gain_parts.reshape(STREAMS, mine)
    else:
        hidden_lows, lows = gather_cores(hidden_lows), gather_cores(lows)

        normed_grads, alongs, rights = [], [], []
        for s in range(STREAMS):
            if s < 3:
                right = jnp.concatenate([v[s * n_head : (s + 1) * n_head] for v in lows], axis=0)
            else:
                right = jnp.concatenate(hidden_lows, axis=0)
            rights.append(right)
            part = contract(turned_weights[s], right, 1, 0)
            alongs.append(jnp.sum(part * all_gains[:, s][:, None], axis=0))
            alongs.append(jnp.sum(part * normed[s].astype(full), axis=0))
            part = part.reshape(places, ways, piece, group)
            kept = lax.dynamic_index_in_dim(part, way, 1, keepdims=False)
            if ways == 2:
                given = lax.dynamic_index_in_dim(part, 1 - way, 1, keepdims=False).astype(low)
                kept = kept + hid_swap(given, 1).astype(full)
            normed_grads.append(kept.reshape(mine, group))
        weighted = [normed_grads[s] * gains[s] for s in range(STREAMS)]
        means_back = sum_features(jnp.stack(alongs, axis=0)) / width
        gain_parts = [jnp.sum(g * u, axis=1) for g, u in zip(normed_grads, units)]
        stream_grads = [
            (weighted[s] - means_back[2 * s] - units[s] * means_back[2 * s + 1]) * inv_scales[s]
            for s in range(STREAMS)
        ]
        stream_grads[3] = stream_grads[3] + output_grad
        gain_parts = jnp.stack(gain_parts, axis=0)

        split = jnp.stack([v.astype(low).reshape(places, piece, group) for v in stream_grads], axis=1)
        attended, split = lax.optimization_barrier((attended, split))
        split = exchange(split)
        wide = w_query.shape[1] // ways
        operands = [rights[3]] + rights[:3] + [output_low, normed[3]] + normed[:3] + [attended]
        blocks = [(feats, [(5, 0, 0, i, wide)]) for i in range(0, rights[3].shape[0], wide)]
        blocks += [(feats, [(6 + s, 0, 1 + s, 0, wide)]) for s in range(3)]
        blocks += [(n_head, [(9, 0, 4, i, wide)]) for i in range(0, width, wide)]
        late_sum = chain_sums(operands, blocks, 1).reshape(ways, -1, feats, wide)

    smalls = jnp.concatenate([mixer_grad_part, gain_parts], axis=0)
    split = jnp.concatenate([split[p] for p in range(places)], axis=-1).astype(full)
    mix_layers = mix_all.reshape(STREAMS, HIST, total_tokens)
    history_grad = sum(mix_layers[s][:, None] * split[s][None] for s in range(STREAMS))
    history_grad = history_grad.swapaxes(1, 2)
    mix_parts = jnp.concatenate(
        [jnp.sum(split[s][None] * stored.astype(full), axis=1) for s in range(STREAMS)], axis=0
    )
    mix_parts = mix_parts.reshape(n_mix, dp * hid, block).transpose(1, 0, 2)

    late_sum, mix_parts, smalls = lax.optimization_barrier((late_sum, mix_parts, smalls))
    smalls = sum_tokens(smalls)
    smalls = gather_ways(smalls.reshape(-1, places, piece), 2).reshape(-1, feats)
    w_mixer_grad = smalls[:n_inner].T
    norm_gains_grad = smalls[n_inner:].T
    mix_parts = lax.all_to_all(mix_parts, ("dp", "hid"), split_axis=0, concat_axis=0, tiled=True)
    mix_grad = jnp.sum(mix_parts, axis=0).T
    w_down_grad = unturn(branch_sum.reshape(w_down.shape))
    w_up_grad, w_query_grad, w_key_grad, w_value_grad, w_out_grad = assemble(late_sum, w_up, fused)

    return (
        block_output,
        mix_next,
        history_grad,
        mix_grad,
        norm_gains_grad,
        w_query_grad,
        w_key_grad,
        w_value_grad,
        w_out_grad,
        w_up_grad,
        w_down_grad,
        w_mixer_grad,
        mixer_out_grad,
        sum_grad,
    )


def solution(mesh):
    everywhere = ("dp", "hid")
    placed = (
        P(None, None, everywhere),
        P(everywhere, None),
        P(everywhere),
        P("dp", None),
        P("dp", None),
        P("dp", None),
        P("dp", None),
        P("dp", None),
        P("dp", None),
        P("dp", None),
        P("dp", None),
        P(),
        P(),
        P(None, everywhere),
        P(everywhere, None),
    )
    return jax.shard_map(
        local,
        mesh=mesh,
        in_specs=placed,
        out_specs=(
            P(None, everywhere),
            P(everywhere, None),
            P(None, None, everywhere),
            P(everywhere, None),
            P("dp", None),
            P("dp", None),
            P("dp", None),
            P("dp", None),
            P("dp", None),
            P("dp", None),
            P("dp", None),
            P("dp", None),
            P(),
            P(),
        ),
        check_vma=False,
    )
```

```python
import functools
import math

import jax
import jax.numpy as jnp
from jax import lax
from jax.experimental import pallas as pl
from jax.experimental.pallas import tpu as pltpu
from jax.sharding import PartitionSpec as P

HEADS = 16
HEAD = 128
ROT = 32
HIST = 8
STREAMS = 4
CORES = 2
CHUNK = 1 << 15
SLACK = 6
TILE = 128
LATE_TILE = 256
SPAN = 256
VMEM = 52 << 20
PULL_START = 4
PULL_GAP = 8
GRAD_GAP = 5

highest = lax.Precision.HIGHEST
rope_base = 10000.0
low = jnp.bfloat16
full = jnp.float32


def contract(left, right, left_dim, right_dim):
    return lax.dot_general(
        left, right, (((left_dim,), (right_dim,)), ((), ())), preferred_element_type=full
    )


def contract_high(left, right, left_dim, right_dim):
    return lax.dot_general(
        left,
        right,
        (((left_dim,), (right_dim,)), ((), ())),
        precision=highest,
        preferred_element_type=full,
    )


def batched(left, right, left_dim, right_dim):
    return lax.dot_general(
        left, right, (((left_dim,), (right_dim,)), ((0,), (0,))), preferred_element_type=full
    )


def gelu_exact(values_in):
    return jax.nn.gelu(values_in, approximate=False)


def core_swap(values_in):
    size = lax.axis_size("dp")
    return lax.ppermute(values_in, "dp", [(i, i ^ 1) for i in range(size)])


def outer_shift(values_in, step):
    size = lax.axis_size("dp")
    outer = size // CORES
    pairs = [
        (o * CORES + c, ((o + step) % outer) * CORES + c) for o in range(outer) for c in range(CORES)
    ]
    return lax.ppermute(values_in, "dp", pairs)


def hid_swap(values_in, bit):
    size = lax.axis_size("hid")
    return lax.ppermute(values_in, "hid", [(i, i ^ bit) for i in range(size)])


def ordered(first, values_in, other, axis):
    return jnp.stack(
        [jnp.where(first, values_in, other), jnp.where(first, other, values_in)], axis=axis
    )


def take(values_in, index):
    return lax.dynamic_index_in_dim(values_in, index, 0, keepdims=False)


def put(target, values_in, index):
    return lax.dynamic_update_index_in_dim(target, values_in, index, 0)


def split_ways():
    return 2 if HEADS // lax.axis_size("dp") >= 2 else 1


def gather_ways(values_in, axis):
    if split_ways() == 1:
        return jnp.expand_dims(values_in, axis)
    return ordered(lax.axis_index("hid") % 2 == 0, values_in, hid_swap(values_in, 1), axis)


def gather_dp(values_in):
    size = lax.axis_size("dp")
    outer = size // CORES
    me = lax.axis_index("dp")
    mine, core = me // CORES, me % CORES
    if outer == 2:
        held = ordered(mine == 0, values_in, outer_shift(values_in, 1), 0)
    else:
        held = jnp.zeros((outer,) + values_in.shape, values_in.dtype)
        held = put(held, values_in, mine)
        for step in range(1, outer):
            held = put(held, outer_shift(values_in, step), (mine - step) % outer)
    pair = ordered(core == 0, held, core_swap(held), 1)
    return pair.reshape((size,) + values_in.shape)


def gather_outer(values_in):
    steps = range(1, lax.axis_size("dp") // CORES)
    return [values_in] + [outer_shift(values_in, step) for step in steps]


def gather_cores(held):
    return [v for h in held for v in (h, core_swap(h))]


def gather_turns(values_in):
    return gather_cores(gather_outer(values_in))


def turn_source(turn):
    outer, me = lax.axis_size("dp") // CORES, lax.axis_index("dp")
    there = (me // CORES + outer - turn // CORES) % outer
    return there * CORES + (me + turn) % CORES


def turn_of(index):
    outer, me = lax.axis_size("dp") // CORES, lax.axis_index("dp")
    step = (me // CORES + outer - index // CORES) % outer
    return step * CORES + (me + index) % CORES


def sum_features(values_in):
    if split_ways() == 2:
        values_in = values_in + hid_swap(values_in, 1)
    parts = gather_dp(values_in)
    total = parts[0]
    for i in range(1, parts.shape[0]):
        total = total + parts[i]
    return total


def sum_tokens(values_in):
    size = lax.axis_size("hid")
    bit = split_ways()
    while bit < size:
        values_in = values_in + hid_swap(values_in, bit)
        bit *= 2
    return values_in


def gather_all(values_in):
    count = lax.axis_size("dp") * lax.axis_size("hid")
    copies = jnp.broadcast_to(values_in[None], (count,) + values_in.shape)
    held = lax.all_to_all(copies, ("dp", "hid"), split_axis=0, concat_axis=0, tiled=True)
    return held.transpose(1, 0, 2).reshape(values_in.shape[0], -1)


def scatter_dp(make):
    size = lax.axis_size("dp")
    outer = size // CORES
    me = lax.axis_index("dp")
    mine, core = me // CORES, me % CORES
    total = None
    for step in list(range(1, outer)) + [0]:
        there = (mine + step) % outer
        away = core_swap(make(there * CORES + 1 - core).astype(low))
        block = make(there * CORES + core) + away.astype(full)
        if step:
            block = outer_shift(block.astype(low), step).astype(full)
        total = block if total is None else total + block
    return total


def exchange(values_in):
    ways, size = split_ways(), lax.axis_size("hid")
    groups = None
    if ways > 1:
        groups = [[t * ways + w for t in range(size // ways)] for w in range(ways)]
    return lax.all_to_all(
        values_in, "hid", split_axis=0, concat_axis=0, tiled=True, axis_index_groups=groups
    )


def turn_heads(values_in, cosine, sine):
    half = ROT // 2
    front, back = values_in[:half], values_in[half:ROT]
    return jnp.concatenate(
        [front * cosine - back * sine, back * cosine + front * sine, values_in[ROT:]], axis=0
    )


def across(left, right, left_dim, right_dim):
    return lax.dot_general(
        left, right, (((left_dim,), (right_dim,)), ((), ())), preferred_element_type=full
    )


def attend_kernel(
    products_ref, cosine_ref, sine_ref, start_ref, heads_ref, attended_ref, tops_ref
):
    tokens = products_ref.shape[2]
    for s in range(2):
        turned = turn_heads(products_ref[s], cosine_ref[...], sine_ref[...])
        heads_ref[s] = turned.astype(low)
    heads_ref[2] = products_ref[2].astype(low)
    for first in range(0, tokens, SPAN):
        stop = first + SPAN
        span = slice(first, stop)
        scores, top = masked_scores(heads_ref, start_ref, first)
        weights = jnp.exp(scores - top)
        total = jnp.sum(weights, axis=0, keepdims=True)
        weights = (weights / total).astype(low)
        mixed = across(heads_ref[2, :, :stop], weights, 1, 0)
        attended_ref[:, span] = mixed.astype(low)
        tops_ref[0, 0:1, span] = top
        tops_ref[0, 1:2, span] = total


def masked_scores(heads_ref, start_ref, first):
    stop = first + SPAN
    span = slice(first, stop)
    scores = across(heads_ref[1, :, :stop], heads_ref[0, :, span], 0, 0) / math.sqrt(HEAD)
    key = lax.broadcasted_iota(jnp.int32, scores.shape, 0)
    query = lax.broadcasted_iota(jnp.int32, scores.shape, 1) + first
    seen = (key >= start_ref[:, span]) & (key <= query)
    scores = jnp.where(seen, scores, -1e30)
    return scores, jnp.max(scores, axis=0, keepdims=True)


def attend_back_kernel(
    heads_ref, gradient_ref, cosine_ref, sine_ref, start_ref, tops_ref, lows_ref, key_sum, value_sum
):
    tokens = heads_ref.shape[2]
    cosine, sine = cosine_ref[...], sine_ref[...]
    scale = 1.0 / math.sqrt(HEAD)
    key_sum[...] = jnp.zeros_like(key_sum)
    value_sum[...] = jnp.zeros_like(value_sum)
    for first in range(0, tokens, SPAN):
        stop = first + SPAN
        span = slice(first, stop)
        scores, _ = masked_scores(heads_ref, start_ref, first)
        probs = jnp.exp(scores - tops_ref[0, 0:1, span]) / tops_ref[0, 1:2, span]
        gradient = gradient_ref[:, span]
        change = across(heads_ref[2, :, :stop], gradient, 0, 0)
        row_total = jnp.sum(probs * change, axis=0, keepdims=True)
        change = (probs * (change - row_total)).astype(low)
        query = across(heads_ref[1, :, :stop], change, 1, 0) * scale
        lows_ref[0, :, span] = turn_heads(query, cosine[:, span], -sine[:, span]).astype(low)
        key_sum[:, :stop] = key_sum[:, :stop] + across(heads_ref[0, :, span], change, 1, 1) * scale
        value_sum[:, :stop] = value_sum[:, :stop] + across(gradient, probs.astype(low), 1, 1)
    lows_ref[1] = turn_heads(key_sum[...], cosine, -sine).astype(low)
    lows_ref[2] = value_sum[...].astype(low)


def attend(products, cosine, sine, start):
    _, n_heads, head, tokens = products.shape
    per_head = pl.BlockSpec((3, None, head, tokens), lambda h: (0, h, 0, 0))
    table = pl.BlockSpec(cosine.shape, lambda h: (0, 0))
    return pl.pallas_call(
        attend_kernel,
        grid=(n_heads,),
        out_shape=[
            jax.ShapeDtypeStruct(products.shape, low),
            jax.ShapeDtypeStruct((n_heads, head, tokens), low),
            jax.ShapeDtypeStruct((n_heads, 2, tokens), full),
        ],
        in_specs=[per_head, table, table, pl.BlockSpec(start.shape, lambda h: (0, 0))],
        out_specs=[
            per_head,
            pl.BlockSpec((None, head, tokens), lambda h: (h, 0, 0)),
            pl.BlockSpec((1, 2, tokens), lambda h: (h, 0, 0)),
        ],
        compiler_params=pltpu.CompilerParams(vmem_limit_bytes=40 << 20),
        cost_estimate=pl.CostEstimate(
            flops=4 * n_heads * head * tokens * tokens,
            bytes_accessed=10 * products.size,
            transcendentals=n_heads * tokens * tokens,
        ),
    )(products, cosine, sine, start)


def attend_back(heads, gradient, cosine, sine, start, tops):
    _, n_heads, head, tokens = heads.shape
    per_head = pl.BlockSpec((3, None, head, tokens), lambda h: (0, h, 0, 0))
    table = pl.BlockSpec(cosine.shape, lambda h: (0, 0))
    return pl.pallas_call(
        attend_back_kernel,
        grid=(n_heads,),
        out_shape=jax.ShapeDtypeStruct(heads.shape, low),
        in_specs=[
            per_head,
            pl.BlockSpec((None, head, tokens), lambda h: (h, 0, 0)),
            table,
            table,
            pl.BlockSpec(start.shape, lambda h: (0, 0)),
            pl.BlockSpec((1, 2, tokens), lambda h: (h, 0, 0)),
        ],
        out_specs=per_head,
        scratch_shapes=[pltpu.VMEM((head, tokens), full)] * 2,
        compiler_params=pltpu.CompilerParams(vmem_limit_bytes=40 << 20),
        cost_estimate=pl.CostEstimate(
            flops=10 * n_heads * head * tokens * tokens,
            bytes_accessed=6 * heads.size,
            transcendentals=n_heads * tokens * tokens,
        ),
    )(heads, gradient, cosine, sine, start, tops)


def forward_kernel(dims, *refs):
    places, piece, group, n_head, n_units = dims
    (send_ref, mom_ref, gains_ref, query_ref, key_ref, value_ref, up_ref), refs = refs[:7], refs[7:]
    cot_ref, refs = refs[0], refs[1:]
    (
        normed_ref,
        own_ref,
        shift_ref,
        active_ref,
        slope_ref,
        heads_ref,
        turned_ref,
        turned_up_ref,
        cot_out,
    ), refs = refs[:9], refs[9:]
    (
        devs,
        moms,
        joins,
        weights,
        core_out,
        core_in,
        outer_out,
        outer_in,
        mom_send,
        mom_recv,
        dev_send,
        dev_recv,
        way_send,
        way_recv,
        pair_send,
        pair_recv,
        join_send,
        join_recv,
        weight_sem,
        turned_sem,
        core_send,
        core_recv,
        outer_send,
        outer_recv,
        cot_send,
        cot_recv,
        cot_own,
    ) = refs
    count = weights.shape[0]
    ups = n_units // n_head
    index, hid = lax.axis_index("dp"), lax.axis_index("hid")
    outer, core = index // 2, index % 2
    place, way = hid // 2, hid % 2
    me = index * 2 + way
    partner = {"hid": hid + 1 - 2 * way}
    core_peer = {"dp": index + 1 - 2 * core}
    outer_peer = {"dp": (index + 2) % 4}

    def peer(k):
        return (place + k) % places

    def z_device(k):
        return {"hid": peer(k) * 2 + way}

    others = [(i, j) for i in range(4) for j in range(2) if i or j]

    def join_device(i, j):
        return {"dp": (index + i) % 4, "hid": place * 2 + (way + j) % 2}

    def weight_copy(unit, t):
        there = (1 - outer if t < 2 else outer) * 2 + (core if t % 2 else 1 - core)
        block = there * 2 + way
        if unit < ups:
            source, start = up_ref, block * n_units + unit * n_head
        else:
            source, start = (query_ref, key_ref, value_ref)[unit - ups], block * n_head
        start = pl.multiple_of(start, n_head)
        return pltpu.make_async_copy(
            source.at[:, pl.ds(start, n_head)], weights.at[unit, t], weight_sem.at[unit]
        )

    for unit in range(count):
        for t in range(4):
            weight_copy(unit, t).start()

    barrier = pltpu.get_barrier_semaphore()

    for k in range(1, places):
        greet(z_device(k))
    for i, j in others:
        greet(join_device(i, j))
    pl.semaphore_wait(barrier, places - 1 + len(others))

    def mom_copy(k, sender, target):
        return remote(
            mom_ref.at[target], moms.at[way, sender], mom_send, mom_recv.at[sender], z_device(k)
        )

    def dev_copy(s, k, sender, target):
        return remote(
            send_ref.at[target, s],
            devs.at[s, way, sender],
            dev_send,
            dev_recv.at[s, sender],
            z_device(k),
        )

    for k in range(1, places):
        mom_copy(k, place, peer(k)).start()
    for s in (3, 0, 1, 2):
        for k in range(1, places):
            dev_copy(s, k, place, peer(k)).start()
    for k in range(1, places):
        remote(cot_ref.at[peer(k)], cot_out.at[place], cot_send, cot_recv, z_device(k)).start()
    pltpu.make_async_copy(cot_ref.at[place], cot_out.at[place], cot_own).start()
    moms[way, place] = mom_ref[place]
    for s in range(STREAMS):
        devs[s, way, place] = send_ref[place, s]

    def way_copy(source, s, q):
        return remote(source, devs.at[s, way, q], way_send, way_recv.at[s], partner)

    def forward(s):
        way_copy(send_ref.at[place, s], s, place).start()
        for k in range(1, places):
            q = peer(k)
            dev_copy(s, k, q, q).wait_recv()
            way_copy(devs.at[s, way, q], s, q).start()

    def join_parts(means, parts, size):
        mean = means[0]
        for m in means[1:]:
            mean = mean + m
        mean = mean / len(means)
        total = parts[0]
        for v in parts[1:]:
            total = total + v
        for m in means:
            total = total + size * (m - mean) * (m - mean)
        return mean, total

    for k in range(1, places):
        mom_copy(k, peer(k), place).wait_recv()
    remote(moms.at[way], moms.at[way], pair_send, pair_recv, partner).start()
    mean, total = join_parts(
        [moms[way, q, :STREAMS, :] for q in range(places)],
        [moms[way, q, STREAMS:, :] for q in range(places)],
        piece,
    )
    joins[me, :STREAMS, :] = mean
    joins[me, STREAMS:, :] = total
    for i, j in others:
        remote(joins.at[me], joins.at[me], join_send, join_recv, join_device(i, j)).start()
    forward(3)
    n_others = len(others)
    remote(
        joins.at[pl.ds(0, n_others)], joins.at[pl.ds(0, n_others)], join_send, join_recv, partner
    ).wait_recv()
    remote(moms.at[way], moms.at[1 - way], pair_send, pair_recv, partner).wait_recv()
    mean, total = join_parts(
        [joins[i, :STREAMS, :] for i in range(n_others + 1)],
        [joins[i, STREAMS:, :] for i in range(n_others + 1)],
        piece * places,
    )
    scale = lax.rsqrt(total / (piece * places * (n_others + 1)) + 1e-05)
    for s in range(STREAMS):
        for q in range(places):
            for w in range(2):
                off = moms[w, q, s : s + 1, :] - mean[s : s + 1]
                shift_ref[s, 2 * q + w : 2 * q + w + 1, :] = off * scale[s : s + 1]
        shift_ref[s, 2 * places : 2 * places + 1, :] = scale[s : s + 1]
        shift_ref[s, 2 * places + 1 : 2 * places + 2, :] = mean[s : s + 1]

    def normalize(s):
        remote(devs.at[s, 1 - way], devs.at[s, 1 - way], way_send, way_recv.at[s], partner).wait_recv()
        size = shift_ref[s, 2 * places : 2 * places + 1, :]
        for q in range(places):
            for w in range(2):
                block = 2 * q + w
                rows = slice(block * piece, (block + 1) * piece)
                unit = devs[s, w, q].astype(full) * size + shift_ref[s, block : block + 1, :]
                normed_ref[s, rows, :] = (unit * gains_ref[s, rows, :]).astype(low)

    def core_copy(unit, half):
        return remote(
            core_out.at[unit, half],
            core_in.at[unit, half],
            core_send,
            core_recv.at[unit, half],
            core_peer,
        )

    def outer_copy(unit):
        return remote(
            outer_out.at[unit], outer_in.at[unit], outer_send, outer_recv.at[unit], outer_peer
        )

    def project(unit, carry):
        @pl.when(unit == 0)
        def _():
            normalize(3)
            forward(0)

        for s in (1, 2):

            @pl.when(unit == s)
            def _(s=s):
                forward(s)

        @pl.when(unit >= ups)
        def _():
            normalize(unit - ups)

        stream = jnp.where(unit < ups, 3, unit - ups)
        pltpu.make_async_copy(weights.at[unit], weights.at[unit], weight_sem.at[unit]).wait()

        def product(t):
            return lax.dot_general(
                weights[unit, t],
                normed_ref[stream],
                (((0,), (0,)), ((), ())),
                preferred_element_type=full,
            )

        core_out[unit, 0] = product(0).astype(low)
        core_copy(unit, 0).start()
        passing = product(1)
        core_out[unit, 1] = product(2).astype(low)
        core_copy(unit, 1).start()
        core_copy(unit, 0).wait_recv()
        outer_out[unit] = (passing + core_in[unit, 0].astype(full)).astype(low)
        outer_copy(unit).start()
        kept = product(3)
        core_copy(unit, 1).wait_recv()
        kept = kept + core_in[unit, 1].astype(full)

        @pl.when(unit < ups)
        def _():
            slope_ref[pl.ds(pl.multiple_of(unit * n_head, n_head), n_head), :] = kept

        @pl.when(unit >= ups)
        def _():
            heads_ref[unit - ups] = kept

        return carry

    lax.fori_loop(0, count, project, 0)

    def turned_copies():
        for unit in range(count):
            for t in range(4):
                turn = 3 - t
                if unit < ups:
                    start = turn * n_units + unit * n_head
                    target = turned_up_ref.at[:, start : start + n_head]
                else:
                    target = turned_ref.at[unit - ups, :, turn * n_head : (turn + 1) * n_head]
                yield pltpu.make_async_copy(weights.at[unit, t], target, turned_sem)

    for copy in turned_copies():
        copy.start()
    for s in range(STREAMS):
        own_ref[s] = devs[s, way]

    step = 32

    def finish_up(unit, carry):
        outer_copy(unit).wait_recv()

        def part(i, carry):
            inner = pl.ds(pl.multiple_of(i * step, step), step)
            rows = pl.ds(pl.multiple_of(unit * n_head + i * step, step), step)
            hidden = slope_ref[rows, :] + outer_in[unit, inner, :].astype(full)
            half = 0.5 + 0.5 * lax.erf(hidden * math.sqrt(0.5))
            active_ref[rows, :] = (hidden * half).astype(low)
            bell = jnp.exp(-0.5 * hidden * hidden) * (1.0 / math.sqrt(2.0 * math.pi))
            slope_ref[rows, :] = half + hidden * bell
            return carry

        return lax.fori_loop(0, n_head // step, part, carry)

    lax.fori_loop(0, ups, finish_up, 0)

    def finish_head(unit, carry):
        outer_copy(unit).wait_recv()
        heads_ref[unit - ups] = heads_ref[unit - ups] + outer_in[unit].astype(full)
        return carry

    lax.fori_loop(ups, count, finish_head, 0)

    def sent(ref, sem):
        remote(ref, ref, sem, join_recv, partner).wait_send()

    sent(moms.at[0, pl.ds(0, places - 1)], mom_send)
    sent(send_ref.at[pl.ds(0, places - 1)], dev_send)
    sent(send_ref, way_send)
    sent(moms.at[0], pair_send)
    sent(joins.at[pl.ds(0, n_others)], join_send)
    sent(core_out, core_send)
    sent(outer_out, outer_send)
    moved = cot_ref.at[pl.ds(0, places - 1)]
    sent(moved, cot_send)
    remote(moved, moved, cot_send, cot_recv, partner).wait_recv()
    pltpu.make_async_copy(cot_ref.at[0], cot_out.at[0], cot_own).wait()
    pltpu.make_async_copy(weights, weights, turned_sem).wait()


def forward_projections(deviations, moments, norm_gains, w_query, w_key, w_value, w_up, cotangent):
    places, _, piece, group = deviations.shape
    feats = norm_gains.shape[0]
    n_head = w_query.shape[1] // 8
    n_units = w_up.shape[1] // 8
    count = n_units // n_head + 3
    vmem, dma = pltpu.VMEM, pltpu.SemaphoreType.DMA
    out_types = [
        ((STREAMS, feats, group), low),
        ((STREAMS, places, piece, group), low),
        ((STREAMS, 2 * places + 8, group), full),
        ((n_units, group), low),
        ((n_units, group), full),
        ((3, n_head, group), full),
        ((3, feats, 4 * n_head), low),
        ((feats, 4 * n_units), low),
        (cotangent.shape, low),
    ]
    spaces = [vmem] * 6 + [pl.ANY] * 3
    return pl.pallas_call(
        functools.partial(forward_kernel, (places, piece, group, n_head, n_units)),
        out_shape=[jax.ShapeDtypeStruct(*t) for t in out_types],
        in_specs=[pl.BlockSpec(memory_space=vmem)] * 3 + [pl.BlockSpec(memory_space=pl.ANY)] * 5,
        out_specs=[pl.BlockSpec(memory_space=m) for m in spaces],
        scratch_shapes=[
            vmem((STREAMS, 2, places, piece, group), low),
            vmem((2, places, 2 * STREAMS, group), full),
            vmem((8, 2 * STREAMS, group), full),
            vmem((count, 4, feats, n_head), low),
            vmem((count, 2, n_head, group), low),
            vmem((count, 2, n_head, group), low),
            vmem((count, n_head, group), low),
            vmem((count, n_head, group), low),
            dma,
            dma((places,)),
            dma,
            dma((STREAMS, places)),
            dma,
            dma((STREAMS,)),
            dma,
            dma,
            dma,
            dma,
            dma((count,)),
            dma,
            dma,
            dma((count, 2)),
            dma,
            dma((count,)),
            dma,
            dma,
            dma,
        ],
        compiler_params=pltpu.CompilerParams(
            collective_id=7, has_side_effects=True, vmem_limit_bytes=62 << 20
        ),
        cost_estimate=pl.CostEstimate(
            flops=8 * count * n_head * feats * group,
            bytes_accessed=300 << 20,
            transcendentals=2 * n_units * group,
        ),
    )(
        deviations,
        moments,
        norm_gains.T.astype(full)[:, :, None],
        w_query,
        w_key,
        w_value,
        w_up,
        cotangent,
    )


def remote(source, target, send, recv, device):
    return pltpu.make_async_remote_copy(
        src_ref=source,
        dst_ref=target,
        send_sem=send,
        recv_sem=recv,
        device_id=device,
        device_id_type=pl.DeviceIdType.MESH,
    )


def greet(device):
    pl.semaphore_signal(
        pltpu.get_barrier_semaphore(),
        inc=1,
        device_id=device,
        device_id_type=pl.DeviceIdType.MESH,
    )


def chain_place(ways, places):
    last = places - 1
    me = lax.axis_index("hid")
    if ways == 2:
        place, way = me // 2, me % 2
        return place, way, me + 2, me - 2, me + 1 - 2 * way
    odd, half = me % 2, places // 2
    place = (1 - odd) * (me // 2) + odd * (last - me // 2)
    turn_up = (place + 1) // half
    turn_down = (place - 1 + places) // half - 2
    above = (1 - turn_up) * 2 * (place + 1) + turn_up * (2 * (last - place - 1) + 1)
    below = (1 - turn_down) * 2 * (place - 1) + turn_down * (2 * (last - place + 1) + 1)
    return place, 0, above, below, me


def chain_semaphores(count):
    dma = pltpu.SemaphoreType.DMA
    return [dma, dma((count,)), dma, dma((count,)), dma, dma, dma, dma, dma((count,))]


def chain_loop(ways, places, out_ref, own, landed, semaphores, compute, hook=None, far=None):
    (
        up_send,
        up_recv,
        down_send,
        down_recv,
        side_send,
        side_recv,
        kept,
        far_send,
        far_recv,
    ) = semaphores
    count, depth = landed.shape[:2]
    per_tile = own.shape[0] // depth
    last = places - 1
    root = last if far is None else places // 2
    place, way, above, below, beside = chain_place(ways, places)
    above, below, beside = {"hid": above}, {"hid": below}, {"hid": beside}

    def send_in(i):
        @pl.when(place < root)
        def _():
            remote(landed.at[i], landed.at[i], up_send, up_recv.at[i], above).start()

        if far is not None:

            @pl.when(place == root + 1)
            def _():
                remote(landed.at[i], far.at[i], up_send, far_recv.at[i], below).start()

            @pl.when(place > root + 1)
            def _():
                remote(landed.at[i], landed.at[i], up_send, up_recv.at[i], below).start()

    def send_out(source, i):
        def to(device, send):
            remote(source, out_ref.at[way, i], send, down_recv.at[i], device).start()

        @pl.when((place <= root) & (place > 0))
        def _():
            to(below, down_send)

        if far is not None:

            @pl.when((place >= root) & (place < last))
            def _():
                to(above, far_send)

        if ways == 2:
            remote(source, out_ref.at[way, i], side_send, side_recv, beside).start()

    def upward(i):
        @pl.when(i % per_tile == 0)
        def _():
            compute(i // per_tile)

        mine = own[pl.ds(pl.multiple_of(i % per_tile * depth, depth), depth), :]
        ends = place == 0 if far is None else (place == 0) | (place == last)

        @pl.when(ends)
        def _():
            landed[i] = mine.astype(low)

        @pl.when(jnp.logical_not(ends))
        def _():
            remote(landed.at[i], landed.at[i], up_send, up_recv.at[i], above).wait_recv()
            total = landed[i].astype(full) + mine
            if far is None:
                landed[i] = total.astype(low)
            else:

                @pl.when(place != root)
                def _():
                    landed[i] = total.astype(low)

                @pl.when(place == root)
                def _():
                    remote(far.at[i], far.at[i], up_send, far_recv.at[i], above).wait_recv()
                    landed[i] = (total + far[i].astype(full)).astype(low)

        @pl.when(place != root)
        def _():
            send_in(i)

        @pl.when(place == root)
        def _():
            send_out(landed.at[i], i)
            pltpu.make_async_copy(landed.at[i], out_ref.at[way, i], kept).start()

    def downward(i):
        done = out_ref.at[way, i]
        remote(done, done, down_send, down_recv.at[i], below).wait_recv()
        send_out(done, i)

    away = root - place if far is None else jnp.where(place < root, root - place, place - root)
    lag = SLACK * away + 2

    def step(i, carry):
        @pl.when(i < count)
        def _():
            upward(i)

        behind = i - lag

        @pl.when((behind >= 0) & (behind < count) & (place != root))
        def _():
            downward(behind)

        if hook is not None:
            hook(i)
        return carry

    lax.fori_loop(0, count + SLACK * root + 2, step, 0)

    def sent(sem):
        remote(landed, landed, sem, side_recv, beside).wait_send()

    @pl.when(place != root)
    def _():
        sent(up_send)

    @pl.when((place <= root) & (place > 0))
    def _():
        sent(down_send)

    if far is not None:

        @pl.when((place >= root) & (place < last))
        def _():
            sent(far_send)

    @pl.when(place == root)
    def _():
        pltpu.make_async_copy(landed, out_ref.at[way], kept).wait()

    if ways == 2:
        sent(side_send)
        remote(landed, landed, side_send, side_recv, beside).wait_recv()


def chain_kernel(ways, places, blocks, n_operands, *refs):
    operand_refs, out_ref, refs = refs[:n_operands], refs[n_operands], refs[n_operands + 1 :]
    operands, (own, landed, far, fetched, *semaphores) = refs[:n_operands], refs[n_operands:]
    last = places - 1
    place, way, above, below, beside = chain_place(ways, places)

    def fetch(n):
        return pltpu.make_async_copy(operand_refs[n], operands[n], fetched.at[n])

    for n in range(n_operands):
        fetch(n).start()

    barrier = pltpu.get_barrier_semaphore()

    @pl.when(place > 0)
    def _():
        greet({"hid": below})

    @pl.when(place < last)
    def _():
        greet({"hid": above})

    if ways == 2:
        greet({"hid": beside})
    met = jnp.where(place > 0, 1, 0) + jnp.where(place < last, 1, 0) + (ways - 1)
    pl.semaphore_wait(barrier, met)

    def compute(tile):
        seen, first = set(), 0
        for rows, segments in blocks:
            start = first
            first = first + rows // TILE
            fresh = [n for seg in segments for n in (seg[0], seg[2])]
            fresh = [n for n in dict.fromkeys(fresh) if n not in seen]
            seen.update(fresh)

            @pl.when(tile == start)
            def _(fresh=fresh):
                for n in fresh:
                    fetch(n).wait()

            @pl.when((tile >= start) & (tile < first))
            def _(start=start, segments=segments):
                column = 0
                for left, left_row, right, right_row, size in segments:
                    row = pl.multiple_of(left_row + (tile - start) * TILE, TILE)
                    own[:, column : column + size] = lax.dot_general(
                        operands[left][pl.ds(row, TILE), :],
                        operands[right][right_row : right_row + size, :],
                        (((1,), (1,)), ((), ())),
                        preferred_element_type=full,
                    )
                    column += size

    chain_loop(ways, places, out_ref, own, landed, semaphores, compute, far=far)


def chain_sum(operands, blocks, collective_id):
    ways, size = split_ways(), lax.axis_size("hid")
    columns = sum(seg[4] for seg in blocks[0][1])
    rows = sum(block[0] for block in blocks)
    depth = max(16, CHUNK // columns)
    count = rows // depth
    tokens = operands[0].shape[1]
    return pl.pallas_call(
        functools.partial(chain_kernel, ways, size // ways, blocks, len(operands)),
        out_shape=jax.ShapeDtypeStruct((ways, count, depth, columns), low),
        in_specs=[pl.BlockSpec(memory_space=pl.ANY)] * len(operands),
        out_specs=pl.BlockSpec(memory_space=pl.ANY),
        scratch_shapes=[pltpu.VMEM(v.shape, low) for v in operands]
        + [
            pltpu.VMEM((TILE, columns), full),
            pltpu.VMEM((count, depth, columns), low),
            pltpu.VMEM((count, depth, columns), low),
            pltpu.SemaphoreType.DMA((len(operands),)),
        ]
        + chain_semaphores(count),
        compiler_params=pltpu.CompilerParams(
            collective_id=collective_id, has_side_effects=True, vmem_limit_bytes=60 << 20
        ),
        cost_estimate=pl.CostEstimate(
            flops=2 * rows * columns * tokens,
            bytes_accessed=300 * rows * columns,
            transcendentals=0,
        ),
    )(*operands)


def branch_kernel(dims, *refs):
    places, piece, group = dims
    (attended_ref, active_ref, residual_ref, mixer_ref, out_w_ref, down_w_ref), refs = refs[:6], refs[6:]
    (output_ref, rounded_ref, sums_ref, turned_out_ref, turned_down_ref), refs = refs[:5], refs[5:]
    (
        weights,
        passing,
        kept,
        core_out,
        core_in,
        outer_out,
        outer_in,
        side_out,
        side_in,
        parts_out,
        parts_in,
        totals,
        weight_sem,
        turned_sem,
        core_send,
        core_recv,
        outer_send,
        outer_recv,
        side_send,
        side_recv,
        part_send,
        part_recv,
        total_send,
        total_recv,
    ) = refs
    index, hid = lax.axis_index("dp"), lax.axis_index("hid")
    outer, core = index // 2, index % 2
    place, way = hid // 2, hid % 2
    me = index * 2 + way
    partner = {"hid": hid + 1 - 2 * way}
    core_peer = {"dp": index + 1 - 2 * core}
    outer_peer = {"dp": (index + 2) % 4}
    others = [(i, j) for i in range(4) for j in range(2) if i or j]
    n_head, n_units = attended_ref.shape[0], active_ref.shape[0]
    feats = weights.shape[2]
    wide = group // 8

    def peer(i, j):
        there, other = (index + i) % 4, (way + j) % 2
        return there * 2 + other, {"dp": there, "hid": place * 2 + other}

    def weight_copies(t):
        there = (1 - outer if t < 2 else outer) * 2 + (core if t % 2 else 1 - core)
        columns = pl.ds(pl.multiple_of(there * feats, feats), feats)
        for ref, first, size in ((out_w_ref, 0, n_head), (down_w_ref, n_head, n_units)):
            rows = pl.ds(pl.multiple_of(way * size, size), size)
            yield pltpu.make_async_copy(
                ref.at[rows, columns], weights.at[t, first : first + size], weight_sem.at[t]
            )

    def turned_copies(t):
        columns = slice((3 - t) * feats, (4 - t) * feats)
        for ref, first, size in ((turned_out_ref, 0, n_head), (turned_down_ref, n_head, n_units)):
            yield pltpu.make_async_copy(
                weights.at[t, first : first + size], ref.at[:, columns], turned_sem
            )

    for t in range(4):
        for copy in weight_copies(t):
            copy.start()
    for i, j in others:
        greet(peer(i, j)[1])
    pl.semaphore_wait(pltpu.get_barrier_semaphore(), len(others))

    def halves(t, target, kind):
        pltpu.make_async_copy(weights.at[t], weights.at[t], weight_sem.at[t]).wait()
        product = across(weights[t, :n_head, :], attended_ref[...], 0, 0)
        product = product + across(weights[t, n_head:, :], active_ref[...], 0, 0)
        for q in range(places):
            first = product[2 * q * piece : (2 * q + 1) * piece]
            second = product[(2 * q + 1) * piece : (2 * q + 2) * piece]
            rows = slice(q * piece, (q + 1) * piece)
            target[0, rows, :] = jnp.where(way == 0, second, first).astype(kind)
            target[1, rows, :] = jnp.where(way == 0, first, second).astype(kind)
        for copy in turned_copies(t):
            copy.start()

    def core_copy(stage, half):
        return remote(
            core_out.at[stage, half],
            core_in.at[stage, half],
            core_send,
            core_recv.at[stage, half],
            core_peer,
        )

    def outer_copy(half):
        return remote(
            outer_out.at[half], outer_in.at[half], outer_send, outer_recv.at[half], outer_peer
        )

    halves(0, core_out.at[0], low)
    for half in range(2):
        core_copy(0, half).start()
    halves(1, passing, full)
    for half in range(2):
        core_copy(0, half).wait_recv()
        outer_out[half] = (passing[half] + core_in[0, half].astype(full)).astype(low)
        outer_copy(half).start()
    halves(2, core_out.at[1], low)
    for half in range(2):
        core_copy(1, half).start()
    halves(3, kept, full)
    for half in range(2):
        core_copy(1, half).wait_recv()
        kept[half] = kept[half] + core_in[1, half].astype(full)
    kept[1] = kept[1] + residual_ref[...]
    side = remote(side_out, side_in, side_send, side_recv, partner)
    outer_copy(0).wait_recv()
    side_out[...] = (kept[0] + outer_in[0].astype(full)).astype(low)
    side.start()
    outer_copy(1).wait_recv()
    kept[1] = kept[1] + outer_in[1].astype(full)
    side.wait_recv()
    output = kept[1] + side_in[...].astype(full)
    output_ref[...] = output
    rounded = output.astype(low)
    rounded_ref[...] = rounded

    mixed = jnp.dot(mixer_ref[...], rounded, preferred_element_type=full)
    square = jnp.sum(output * output, axis=0, keepdims=True)
    row = lax.broadcasted_iota(jnp.int32, mixed.shape, 0)
    mixed = jnp.where(row == mixed.shape[0] - 1, square, mixed)
    for b in range(8):
        parts_out[b] = mixed[:, b * wide : (b + 1) * wide]
    parts_in[me] = parts_out[me]
    for i, j in others:
        slot, device = peer(i, j)
        remote(parts_out.at[slot], parts_in.at[me], part_send, part_recv, device).start()
    some = pl.ds(0, len(others))

    def whole(ref, send, recv):
        return remote(ref.at[some], ref.at[some], send, recv, partner)

    whole(parts_in, part_send, part_recv).wait_recv()
    total = parts_in[0]
    for b in range(1, 8):
        total = total + parts_in[b]
    totals[me] = total
    for i, j in others:
        remote(totals.at[me], totals.at[me], total_send, total_recv, peer(i, j)[1]).start()
    whole(totals, total_send, total_recv).wait_recv()
    for b in range(8):
        sums_ref[:, b * wide : (b + 1) * wide] = totals[b]

    whole(parts_out, part_send, part_recv).wait_send()
    whole(totals, total_send, total_recv).wait_send()
    remote(core_out, core_out, core_send, side_recv, partner).wait_send()
    remote(outer_out, outer_out, outer_send, side_recv, partner).wait_send()
    side.wait_send()
    pltpu.make_async_copy(weights, weights, turned_sem).wait()


def add_branches(places, attended, active, residual, mixer_rows, w_out, w_down):
    mine, group = residual.shape
    n_head, n_units = attended.shape[0], active.shape[0]
    feats = w_out.shape[0]
    n_sums = 48
    table = jnp.zeros((n_sums, mine), low).at[: mixer_rows.shape[1]].set(mixer_rows.T)
    vmem, dma = pltpu.VMEM, pltpu.SemaphoreType.DMA
    out_types = [
        ((mine, group), full),
        ((mine, group), low),
        ((n_sums, group), full),
        ((n_head, w_out.shape[1]), low),
        ((n_units, w_down.shape[1]), low),
    ]
    spaces = [vmem] * 3 + [pl.ANY] * 2
    block = (2, mine, group)
    slots = (8, n_sums, group // 8)
    return pl.pallas_call(
        functools.partial(branch_kernel, (places, mine // places, group)),
        out_shape=[jax.ShapeDtypeStruct(*t) for t in out_types],
        in_specs=[pl.BlockSpec(memory_space=vmem)] * 4 + [pl.BlockSpec(memory_space=pl.ANY)] * 2,
        out_specs=[pl.BlockSpec(memory_space=m) for m in spaces],
        scratch_shapes=[
            vmem((4, n_head + n_units, feats), low),
            vmem(block, full),
            vmem(block, full),
            vmem((2,) + block, low),
            vmem((2,) + block, low),
            vmem(block, low),
            vmem(block, low),
            vmem(block[1:], low),
            vmem(block[1:], low),
            vmem(slots, full),
            vmem(slots, full),
            vmem(slots, full),
            dma((4,)),
            dma,
            dma,
            dma((2, 2)),
            dma,
            dma((2,)),
            dma,
            dma,
            dma,
            dma,
            dma,
            dma,
        ],
        compiler_params=pltpu.CompilerParams(
            collective_id=8, has_side_effects=True, vmem_limit_bytes=56 << 20
        ),
        cost_estimate=pl.CostEstimate(
            flops=8 * (n_head + n_units) * feats * group, bytes_accessed=100 << 20, transcendentals=0
        ),
    )(attended, active, residual, table, w_out, w_down)


def late_kernel(dims, *refs):
    places, piece, group, n_head, n_units = dims
    (
        hidden_ref,
        hidden_far_ref,
        lows_ref,
        lows_far_ref,
        output_low_ref,
        attended_ref,
        normed_ref,
        turned_ref,
        turned_up_ref,
        devs_ref,
        output_grad_ref,
        shifts,
        scales,
        gains,
        all_gains,
    ), refs = refs[:15], refs[15:]
    (out_ref, split_ref, gain_ref), refs = refs[:3], refs[3:]
    (
        hidden,
        lows,
        output_low,
        attended,
        normed,
        turned,
        turned_up,
        devs,
        output_grad,
        kept,
        given,
        taken,
        grads,
        joins,
        totals,
        own,
        landed,
        fetched,
        core_send,
        core_recv,
        side_send,
        side_recv,
        join_send,
        join_recv,
        place_send,
        place_recv,
        own_copy,
        *semaphores,
    ) = refs
    index, hid = lax.axis_index("dp"), lax.axis_index("hid")
    core = index % 2
    place, way = hid // 2, hid % 2
    me = index * 2 + way
    partner = {"hid": hid + 1 - 2 * way}
    core_peer = {"dp": index + 1 - 2 * core}
    others = [(i, j) for i in range(4) for j in range(2) if i or j]
    wide = own.shape[1]
    feats = normed.shape[1]

    def join_device(i, j):
        return {"dp": (index + i) % 4, "hid": place * 2 + (way + j) % 2}

    def head_rows(turn):
        return slice(turn * n_head, (turn + 1) * n_head)

    def unit_rows(turn):
        return slice(turn * n_units, (turn + 1) * n_units)

    fetches = [
        [(output_low_ref, output_low), (attended_ref, attended), (normed_ref, normed)],
        [(hidden_ref, hidden.at[unit_rows(0)])],
        [
            (hidden_far_ref, hidden.at[unit_rows(2)]),
            (turned_ref, turned),
            (turned_up_ref, turned_up),
            (devs_ref, devs),
            (output_grad_ref, output_grad),
        ]
        + [
            (source.at[head_rows(s)], lows.at[s, head_rows(turn)])
            for s in range(3)
            for turn, source in ((0, lows_ref), (2, lows_far_ref))
        ],
    ]

    def fetch(stage):
        return [pltpu.make_async_copy(a, b, fetched.at[stage, n]) for n, (a, b) in enumerate(fetches[stage])]

    for stage in range(len(fetches)):
        for copy in fetch(stage):
            copy.start()

    for k in range(1, places):
        greet({"hid": (place + k) % places * 2 + way})
    for i, j in others:
        greet(join_device(i, j))
    pl.semaphore_wait(pltpu.get_barrier_semaphore(), places - 1 + len(others))

    def core_copies(far):
        source, heads = (hidden_far_ref, lows_far_ref) if far else (hidden_ref, lows_ref)
        turn = 3 if far else 1
        yield remote(source, hidden.at[unit_rows(turn)], core_send.at[far], core_recv.at[far], core_peer)
        for s in range(3):
            yield remote(
                heads.at[head_rows(s)],
                lows.at[s, head_rows(turn)],
                core_send.at[2 + far],
                core_recv.at[2 + far],
                core_peer,
            )

    for far in range(2):
        for copy in core_copies(far):
            copy.start()

    def wait_cores():
        for far in range(2):
            remote(hidden_ref, hidden_ref, core_send.at[far], core_recv.at[far], core_peer).wait_recv()
            remote(lows_ref, lows_ref, core_send.at[2 + far], core_recv.at[2 + far], core_peer).wait_recv()

    per_block = feats // LATE_TILE
    per_out = n_head // LATE_TILE

    def compute(tile):
        @pl.when(tile == 0)
        def _():
            for copy in fetch(0):
                copy.wait()

        @pl.when(tile == per_block)
        def _():
            for copy in fetch(1):
                copy.wait()

        inner = tile % per_block

        def product(left, right):
            own[...] = lax.dot_general(
                left, right, (((1,), (1,)), ((), ())), preferred_element_type=full
            )

        def rows(n):
            return pl.ds(pl.multiple_of(n * LATE_TILE, LATE_TILE), LATE_TILE)

        @pl.when(tile < per_block)
        def _():
            half = pl.ds(pl.multiple_of(inner // per_out * wide, wide), wide)
            product(attended[rows(inner % per_out), :], output_low[half, :])

        block = tile // per_block

        @pl.when((block >= 1) & (block < 5))
        def _():
            turn = (block - 1) // 2 + (block - 1) % 2 * 2
            units = pl.ds(pl.multiple_of(turn * n_units, n_units), n_units)
            product(normed[3, rows(inner), :], hidden[units, :])

        @pl.when(block >= 5)
        def _():
            product(normed[block - 5, rows(inner), :], lows[block - 5])

    totals[...] = jnp.zeros_like(totals)

    def side_copy(s, r):
        return remote(given.at[s, r], taken.at[s, r], side_send, side_recv.at[s], partner)

    def pull(s):
        def use(part):
            for r in range(places):
                rows = slice(2 * piece * r, 2 * piece * (r + 1))
                here = part[rows]
                totals[s, 0:1, :] = totals[s, 0:1, :] + jnp.sum(
                    here * all_gains[s, r], axis=0, keepdims=True
                )
                totals[s, 1:2, :] = totals[s, 1:2, :] + jnp.sum(
                    here * normed[s, rows, :].astype(full), axis=0, keepdims=True
                )
                first = way == 0
                kept[s, r] = jnp.where(first, here[:piece], here[piece:])
                given[s, r] = jnp.where(first, here[piece:], here[:piece]).astype(low)
                side_copy(s, r).start()

        @pl.when(s < 3)
        def _():
            use(jnp.dot(turned[s], lows[s], preferred_element_type=full))

        @pl.when(s == 3)
        def _():
            use(jnp.dot(turned_up[...], hidden[...], preferred_element_type=full))

    def share_totals():
        joins[me] = totals[...]
        for i, j in others:
            remote(joins.at[me], joins.at[me], join_send, join_recv, join_device(i, j)).start()

    def sum_totals():
        some = joins.at[pl.ds(0, len(others))]
        remote(some, some, join_send, join_recv, partner).wait_recv()
        total = joins[0]
        for i in range(1, len(others) + 1):
            total = total + joins[i]
        totals[...] = total / (feats * 4)

    def stream_grad(s, r):
        @pl.when(r == 0)
        def _():
            remote(given.at[s], taken.at[s], side_send, side_recv.at[s], partner).wait_recv()

        gradient = kept[s, r] + taken[s, r].astype(full)
        unit = devs[s, r].astype(full) * scales[s] + shifts[s, r]
        gain_ref[s, r] = jnp.sum(gradient * unit, axis=1, keepdims=True)
        result = gradient * gains[s, r] - totals[s, 0:1, :] - unit * totals[s, 1:2, :]
        extra = output_grad[r] * jnp.where(s == 3, 1.0, 0.0)
        grads[s, r] = (result * scales[s] + extra).astype(low)

        @pl.when(r == place)
        def _():
            pltpu.make_async_copy(grads.at[s, r], split_ref.at[s, place], own_copy).start()

        @pl.when(r != place)
        def _():
            remote(
                grads.at[s, r],
                split_ref.at[s, place],
                place_send,
                place_recv,
                {"hid": r * 2 + way},
            ).start()

    n_pulls = STREAMS * places
    middle = PULL_START + PULL_GAP * STREAMS
    resume = middle + 8

    def hook(i):
        @pl.when(i == PULL_START)
        def _():
            for copy in fetch(2):
                copy.wait()
            wait_cores()

        k = (i - PULL_START) // PULL_GAP

        @pl.when((i >= PULL_START) & (i < middle) & ((i - PULL_START) % PULL_GAP == 0))
        def _():
            pull(k)

        @pl.when(i == middle)
        def _():
            share_totals()

        @pl.when(i == resume)
        def _():
            sum_totals()

        n = (i - resume) // GRAD_GAP

        @pl.when((i >= resume) & (n < n_pulls) & ((i - resume) % GRAD_GAP == 0))
        def _():
            stream_grad(n // places, n % places)

    chain_loop(2, places, out_ref, own, landed, semaphores, compute, hook)

    def sent(ref, sem):
        remote(ref, ref, sem, join_recv, partner).wait_send()

    for far in range(2):
        sent(hidden_ref, core_send.at[far])
        sent(lows_ref, core_send.at[2 + far])
    sent(given, side_send)
    sent(joins.at[pl.ds(0, len(others))], join_send)
    moved = grads.at[pl.ds(0, places - 1)]
    sent(moved, place_send)
    remote(moved, moved, place_send, place_recv, partner).wait_recv()
    mine = grads.at[0]
    pltpu.make_async_copy(mine, mine, own_copy).wait()


def late_sums(operands, tables, collective_id):
    hidden, _, lows, _, output_low, attended, normed = operands[:7]
    _, places, piece, group = operands[9].shape
    feats = normed.shape[1]
    n_units, n_head = hidden.shape[0], attended.shape[0]
    wide = n_units
    rows = 8 * feats
    depth = max(16, CHUNK // wide)
    count = rows // depth
    vmem, dma = pltpu.VMEM, pltpu.SemaphoreType.DMA
    block = (STREAMS, places, piece, group)
    outs = [
        jax.ShapeDtypeStruct((2, count, depth, wide), low),
        jax.ShapeDtypeStruct(block, low),
        jax.ShapeDtypeStruct((STREAMS, places, piece, 1), full),
    ]
    any_space, vmem_space = pl.BlockSpec(memory_space=pl.ANY), pl.BlockSpec(memory_space=vmem)
    total, split, gain_parts = pl.pallas_call(
        functools.partial(late_kernel, (places, piece, group, n_head, n_units)),
        out_shape=outs,
        in_specs=[any_space] * len(operands) + [vmem_space] * len(tables),
        out_specs=[any_space, any_space, vmem_space],
        scratch_shapes=[
            vmem((4 * n_units, group), low),
            vmem((3, 4 * n_head, group), low),
            vmem(output_low.shape, low),
            vmem(attended.shape, low),
            vmem(normed.shape, low),
            vmem(operands[7].shape, low),
            vmem(operands[8].shape, low),
            vmem(block, low),
            vmem(block[1:], full),
            vmem(block, full),
            vmem(block, low),
            vmem(block, low),
            vmem(block, low),
            vmem((8, STREAMS, 2, group), full),
            vmem((STREAMS, 2, group), full),
            vmem((LATE_TILE, wide), full),
            vmem((count, depth, wide), low),
            dma((3, 11)),
            dma((4,)),
            dma((4,)),
            dma,
            dma((STREAMS,)),
            dma,
            dma,
            dma,
            dma,
            dma,
        ]
        + chain_semaphores(count),
        compiler_params=pltpu.CompilerParams(
            collective_id=collective_id, has_side_effects=True, vmem_limit_bytes=63 << 20
        ),
        cost_estimate=pl.CostEstimate(
            flops=4 * rows * wide * group, bytes_accessed=900 << 20, transcendentals=0
        ),
    )(*operands, *tables)
    return total.reshape(2, 8, feats, wide), split, gain_parts


def chain_sums(operands, blocks, collective_id):
    groups, held, size = [[]], set(), 0
    for rows, segments in blocks:
        used = {n for seg in segments for n in (seg[0], seg[2])}
        more = sum(2 * operands[n].size for n in used - held)
        more += 4 * rows * sum(seg[4] for seg in segments)
        if groups[-1] and size + more > VMEM:
            groups.append([])
            held, size = set(), 0
            more = sum(2 * operands[n].size for n in used)
            more += 4 * rows * sum(seg[4] for seg in segments)
        groups[-1].append((rows, segments))
        held |= used
        size += more
    totals = []
    for i, group in enumerate(groups):
        used = sorted({n for _, segments in group for seg in segments for n in (seg[0], seg[2])})
        place = {n: k for k, n in enumerate(used)}
        own = [
            (rows, [(place[a], b, place[c], d, e) for a, b, c, d, e in segments])
            for rows, segments in group
        ]
        total = chain_sum([operands[n] for n in used], own, collective_id + i)
        totals.append(total.reshape(total.shape[0], -1, total.shape[3]))
    return totals[0] if len(totals) == 1 else jnp.concatenate(totals, axis=1)


def assemble_kernel(ways, dp, fused, own_ref, *refs):
    halves, (up_ref, *head_refs, out_ref) = refs[:ways], refs[ways:]
    rows, wide = own_ref.shape[2:]
    size = up_ref.shape[1] // dp // ways
    blocks = dp * size // wide
    own = wide // dp
    feats = out_ref.shape[1] // dp
    for d in range(dp):
        turn = turn_of(d)
        for w in range(ways):
            start = turn * size
            lanes = pl.ds(pl.multiple_of(start % wide, size), size)
            place = (d * ways + w) * size
            up_block = 1 + turn // 2 + turn % 2 * 2 if fused else start // wide
            up_ref[:, place : place + size] = own_ref[w, up_block, :, lanes].astype(full)
            for s, ref in enumerate(head_refs):
                lanes = pl.ds(pl.multiple_of(turn * own, own), own)
                place = (d * ways + w) * own
                ref[:, place : place + own] = own_ref[w, blocks + s + fused, :, lanes].astype(full)
        start = turn * feats
        lanes = pl.ds(pl.multiple_of(start % wide, feats), feats)
        for w in range(ways):

            @pl.when(start // wide == w)
            def _(w=w, d=d, lanes=lanes):
                out_ref[:, d * feats : (d + 1) * feats] = halves[w][0, 0, :, lanes].astype(full)


def assemble(total, w_up, fused):
    ways, dp = split_ways(), lax.axis_size("dp")
    blocks, rows, wide = total.shape[1:]
    depth = min(64, rows // ways)
    share = rows // ways // depth

    def half_map(half):
        return lambda i: (i // share, 0 if fused else blocks - 1, half * share + i % share, 0)

    widths = [w_up.shape[1]] + [ways * wide] * 4
    return pl.pallas_call(
        functools.partial(assemble_kernel, ways, dp, int(fused)),
        grid=(rows // depth,),
        out_shape=[jax.ShapeDtypeStruct((rows, n), full) for n in widths],
        in_specs=[pl.BlockSpec((ways, blocks, depth, wide), lambda i: (0, 0, i, 0))]
        + [pl.BlockSpec((1, 1, depth, wide), half_map(half)) for half in range(ways)],
        out_specs=[pl.BlockSpec((depth, n), lambda i: (i, 0)) for n in widths],
        compiler_params=pltpu.CompilerParams(vmem_limit_bytes=48 << 20),
        cost_estimate=pl.CostEstimate(
            flops=0, bytes_accessed=6 * total.size, transcendentals=0
        ),
    )(total, *[total] * ways)


def unturn_kernel(dp, own_ref, out_ref):
    size = out_ref.shape[1] // dp
    for d in range(dp):
        lanes = pl.ds(pl.multiple_of(turn_of(d) * size, size), size)
        out_ref[:, d * size : (d + 1) * size] = own_ref[:, lanes].astype(full)


def unturn(total):
    rows, columns = total.shape
    depth = 256
    return pl.pallas_call(
        functools.partial(unturn_kernel, lax.axis_size("dp")),
        grid=(rows // depth,),
        out_shape=jax.ShapeDtypeStruct((rows, columns), full),
        in_specs=[pl.BlockSpec((depth, columns), lambda i: (i, 0))],
        out_specs=pl.BlockSpec((depth, columns), lambda i: (i, 0)),
        cost_estimate=pl.CostEstimate(
            flops=0, bytes_accessed=6 * total.size, transcendentals=0
        ),
    )(total)


def history_kernel(split_ref, stored_ref, mix_ref, grad_ref, parts_ref):
    streams = [split_ref[s, 0].astype(full) for s in range(STREAMS)]
    rows = [None] * (STREAMS * HIST)
    for j in range(HIST):
        layer = stored_ref[j].astype(full)
        total = mix_ref[j : j + 1, :] * streams[0]
        for s in range(1, STREAMS):
            total = total + mix_ref[s * HIST + j : s * HIST + j + 1, :] * streams[s]
        grad_ref[j] = total
        for s in range(STREAMS):
            rows[s * HIST + j] = jnp.sum(streams[s] * layer, axis=0, keepdims=True)
    parts = jnp.concatenate(rows, axis=0)
    block = parts_ref.shape[2]
    for b in range(parts_ref.shape[0]):
        parts_ref[b] = parts[:, b * block : (b + 1) * block]


def history_gradients(split, stored, mix_all, block):
    _, places, piece, group = split.shape
    n_mix, tokens = mix_all.shape
    wide = min(512, group)
    per_place = group // wide
    return pl.pallas_call(
        history_kernel,
        grid=(tokens // wide,),
        out_shape=[
            jax.ShapeDtypeStruct((HIST, piece, tokens), full),
            jax.ShapeDtypeStruct((tokens // block, n_mix, block), full),
        ],
        in_specs=[
            pl.BlockSpec((STREAMS, 1, piece, wide), lambda i: (0, i // per_place, 0, i % per_place)),
            pl.BlockSpec((HIST, piece, wide), lambda i: (0, 0, i)),
            pl.BlockSpec((n_mix, wide), lambda i: (0, i)),
        ],
        out_specs=[
            pl.BlockSpec((HIST, piece, wide), lambda i: (0, 0, i)),
            pl.BlockSpec((wide // block, n_mix, block), lambda i: (i, 0, 0)),
        ],
        compiler_params=pltpu.CompilerParams(vmem_limit_bytes=40 << 20),
        cost_estimate=pl.CostEstimate(
            flops=4 * STREAMS * HIST * piece * tokens,
            bytes_accessed=6 * HIST * piece * tokens + 2 * split.size,
            transcendentals=0,
        ),
    )(split, stored, mix_all)


def to_owner(values_in):
    dp, hid, ways = lax.axis_size("dp"), lax.axis_size("hid"), split_ways()
    index = lax.axis_index("dp") * ways + lax.axis_index("hid") % ways
    mine = lax.dynamic_index_in_dim(values_in, index, 1, keepdims=False)
    pairs = [
        (d * hid + t * ways + w, (t * dp + d) * ways + w)
        for d in range(dp)
        for t in range(hid // ways)
        for w in range(ways)
    ]
    return lax.ppermute(mine, ("dp", "hid"), pairs)


def rotate(values_in, cosine, sine):
    half = cosine.shape[1]
    front, back = values_in[:, :half], values_in[:, half : 2 * half]
    return jnp.concatenate(
        [
            front * cosine - back * sine,
            back * cosine + front * sine,
            values_in[:, 2 * half :],
        ],
        axis=1,
    )


def local(
    history,
    mix,
    segment_ids,
    norm_gains,
    w_query,
    w_key,
    w_value,
    w_out,
    w_up,
    w_down,
    w_mixer,
    mixer_out,
    mix_static,
    out_cotangent,
    mix_cotangent,
):
    dp, hid, ways = lax.axis_size("dp"), lax.axis_size("hid"), split_ways()
    places = hid // ways
    my_hid = lax.axis_index("hid")
    place, way = my_hid // ways, my_hid % ways
    block = segment_ids.shape[0]
    total_tokens = block * dp * hid
    row = total_tokens // dp
    group = total_tokens // places
    rows = group // row
    piece = history.shape[2]
    mine = piece * places
    feats = piece * hid
    width = feats * dp
    heads = HEADS // dp // ways
    n_mix = mix.shape[1]
    n_cot = mix_cotangent.shape[1]

    def by_place(values_in):
        return jnp.stack(
            [values_in[..., p * group : (p + 1) * group] for p in range(places)], axis=0
        )

    stored = history.swapaxes(1, 2)
    mix_all = gather_all(mix.T)
    own_means, own_devs, deviations = [], [], []
    for s in range(STREAMS):
        total = mix_all[s * HIST] * stored[0].astype(full)
        for j in range(1, HIST):
            total = total + mix_all[s * HIST + j] * stored[j].astype(full)
        own_means.append(jnp.mean(total, axis=0))
        off = total - own_means[s]
        own_devs.append(jnp.sum(off * off, axis=0))
        deviations.append(off.astype(low))
    moments = by_place(jnp.stack(own_means + own_devs, axis=0))
    deviations = by_place(jnp.stack(deviations, axis=0))
    fused = dp == 4 and ways == 2 and rows == 1

    table = jnp.concatenate([mix_cotangent.T, segment_ids.astype(full)[None]], axis=0)
    table = lax.dynamic_slice_in_dim(gather_all(table), place * group, group, 1)
    cot_t = table[:n_cot]
    ids = table[-1].reshape(rows, row)

    there = jnp.arange(row, dtype=jnp.int32)
    same_doc = ids[:, :, None] == ids[:, None, :]
    doc_start = jnp.min(jnp.where(same_doc, there[None, None], row), axis=2)
    position = (there[None] - doc_start).astype(full).reshape(group)
    visible = same_doc & (there[None, None] <= there[None, :, None])
    frequency = rope_base ** (-jnp.arange(ROT // 2, dtype=full) * 2.0 / ROT)
    angle = frequency[:, None] * position[None, :]
    cosine, sine = jnp.cos(angle)[None], jnp.sin(angle)[None]

    def own_rows(values_in):
        parts = values_in.reshape((places, ways, piece) + values_in.shape[1:])
        part = lax.dynamic_index_in_dim(parts, way, 1, keepdims=False)
        return part.reshape((mine,) + values_in.shape[1:])

    def all_rows(values_in):
        parts = values_in.reshape((places, piece) + values_in.shape[1:])
        return gather_ways(parts, 1).reshape((feats,) + values_in.shape[1:])

    own_gains = own_rows(norm_gains).astype(full)
    gains = [own_gains[:, s][:, None] for s in range(STREAMS)]
    all_gains = norm_gains.astype(full)

    def project(weight, left):
        columns = weight.shape[1] // dp // ways

        def make(index):
            start = (index * ways + way) * columns
            part = lax.dynamic_slice_in_dim(weight, start, columns, 1)
            return contract(part, left, 0, 0)

        return scatter_dp(make)

    def way_columns(weight):
        if ways == 1:
            return weight
        size = weight.shape[1] // dp // ways
        parts = [weight[:, i * size : (i + 1) * size] for i in range(dp * ways)]
        pairs = zip(parts[::2], parts[1::2])
        return jnp.concatenate([jnp.where(way == 0, a, b) for a, b in pairs], axis=1)

    def way_rows(weight):
        size = weight.shape[0] // ways
        return lax.dynamic_slice_in_dim(weight, way * size, size, 0)

    def by_head(values_in):
        return values_in.reshape(heads, HEAD, group)

    def turned(weight, stride, offset, size):
        starts = [turn_source(turn) * stride + offset for turn in range(dp)]
        parts = [lax.dynamic_slice_in_dim(weight, start, size, 1) for start in starts]
        return jnp.concatenate(parts, axis=1)

    n_head = heads * HEAD
    n_units = w_up.shape[1] // dp // ways
    if fused:
        normed, deviations, shifts, active, slope, products, turned_heads, turned_up, upstream = (
            forward_projections(
                deviations,
                moments,
                norm_gains,
                w_query,
                w_key,
                w_value,
                w_up,
                by_place(out_cotangent.T),
            )
        )
        upstream = upstream.reshape(mine, group)
        inv_scales = shifts[:, 2 * places]
        own_shifts = shifts[:, : 2 * places].reshape(STREAMS, places, ways, group)
        own_shifts = lax.dynamic_index_in_dim(own_shifts, way, 2, keepdims=False)
        offset = own_shifts[3] / inv_scales[3] + shifts[3, 2 * places + 1]
        residual = (deviations[3].astype(full) + offset[:, None]).reshape(mine, group)
        units = [
            (deviations[s].astype(full) * inv_scales[s] + own_shifts[s][:, None]).reshape(mine, group)
            for s in range(STREAMS)
        ]
        normed_all = normed
        normed = [normed[s] for s in range(STREAMS)]
        products = products.reshape(3, heads, HEAD, group)
        turned_weights = [turned_heads[s] for s in range(3)] + [turned_up]
    else:
        moments = exchange(moments)
        deviations = exchange(deviations)
        deviations = [deviations[:, s] for s in range(STREAMS)]
        def join_moments(mean_parts, dev_parts, size):
            mean = jnp.mean(mean_parts, axis=0)
            spread = size * jnp.sum(jnp.square(mean_parts - mean), axis=0)
            return mean, jnp.sum(dev_parts, axis=0) + spread

        block_means = moments[:, :STREAMS]
        joined = join_moments(block_means, moments[:, STREAMS:], piece)
        joined = gather_dp(gather_ways(jnp.concatenate(joined, axis=0), 0))
        joined = joined.reshape((dp * ways,) + joined.shape[2:])
        means, variance = join_moments(joined[:, :STREAMS], joined[:, STREAMS:], mine)
        inv_scales = lax.rsqrt(variance / width + 1e-05)
        all_means = gather_ways(block_means, 1)

        def unit(values_in, block_mean, s):
            return (values_in.astype(full) + (block_mean - means[s])[..., None, :]) * inv_scales[s]

        units = [
            unit(deviations[s], block_means[:, s], s).reshape(mine, group) for s in range(STREAMS)
        ]
        normed = []
        for s in range(STREAMS):
            both = unit(gather_ways(deviations[s], 1), all_means[:, :, s], s).reshape(feats, group)
            normed.append((both * all_gains[:, s][:, None]).astype(low))
        residual = (deviations[3].astype(full) + block_means[:, 3][:, None]).reshape(mine, group)
        products = [
            by_head(project(w, normed[s])) for s, w in enumerate((w_query, w_key, w_value))
        ]
        hidden = project(w_up, normed[3])
        active, hidden_pull = jax.vjp(gelu_exact, hidden)
        active = active.astype(low)
        (slope,) = hidden_pull(jnp.ones_like(hidden))
        turned_weights = [
            turned(w, ways * n_head, way * n_head, n_head) for w in (w_query, w_key, w_value)
        ] + [turned(w_up, ways * n_units, way * n_units, n_units)]

    def by_row(values_in):
        if rows == 1:
            return values_in
        return (
            values_in.reshape(heads, HEAD, rows, row)
            .transpose(0, 2, 1, 3)
            .reshape(heads * rows, HEAD, row)
        )

    def from_row(values_in):
        if rows == 1:
            return values_in
        return (
            values_in.reshape(heads, rows, HEAD, row)
            .transpose(0, 2, 1, 3)
            .reshape(heads, HEAD, group)
        )

    if fused:
        starts = doc_start.reshape(1, group)
        turned_values, attended, tops = attend(products, cosine[0], sine[0], starts)
        attended = attended.reshape(n_head, group)
    else:
        queries = rotate(products[0], cosine, sine).astype(low)
        keys = rotate(products[1], cosine, sine).astype(low)
        values = products[2].astype(low)
        q_rows, k_rows, v_rows = by_row(queries), by_row(keys), by_row(values)
        score_scale = 1.0 / math.sqrt(HEAD)
        scores = batched(q_rows, k_rows, 1, 1) * score_scale
        mask = jnp.broadcast_to(visible[None], (heads, rows, row, row)).reshape(scores.shape)
        scores = jnp.where(mask, scores, -1e30)
        probs = jax.nn.softmax(scores, axis=-1)
        probs_low = probs.astype(low)
        attended = from_row(batched(v_rows, probs_low, 2, 2).astype(low)).reshape(heads * HEAD, group)

        cotangent, attended = lax.optimization_barrier((out_cotangent, attended))
        upstream = exchange(by_place(cotangent.T)).reshape(mine, group)

    mixer_rows = own_rows(w_mixer)
    if fused:
        output, output_rounded, sums, *turned_ends = add_branches(
            places, attended, active, residual, mixer_rows, w_out, w_down
        )
        sums = jnp.concatenate([sums[: mixer_rows.shape[1]], sums[-1:]], axis=0)
        turned_weights += turned_ends
    else:
        out_rows, down_rows = way_rows(w_out), way_rows(w_down)
        turned_weights += [turned(out_rows, feats, 0, feats), turned(down_rows, feats, 0, feats)]
        def make_out(index):
            start = index * feats
            left = lax.dynamic_slice_in_dim(out_rows, start, feats, 1)
            other = lax.dynamic_slice_in_dim(down_rows, start, feats, 1)
            return contract(left, attended, 0, 0) + contract(other, active, 0, 0)

        branches = scatter_dp(make_out).reshape(places, ways, piece, group)
        kept = lax.dynamic_index_in_dim(branches, way, 1, keepdims=False)
        if ways == 2:
            given = lax.dynamic_index_in_dim(branches, 1 - way, 1, keepdims=False).astype(low)
            kept = kept + hid_swap(given, 1).astype(full)
        output = residual + kept.reshape(mine, group)
        output, upstream, turned_weights = lax.optimization_barrier(
            (output, upstream, turned_weights)
        )
        output_rounded = output.astype(low)
        square = jnp.sum(output * output, axis=0, keepdims=True)
        mixer_part = contract(mixer_rows, output_rounded, 0, 0)
        sums = sum_features(jnp.concatenate([mixer_part, square], axis=0))
    upstream = upstream.astype(full)

    block_output = exchange(output_rounded.reshape(places, piece, group))

    inv_rms = lax.rsqrt(sums[-1] / width + 1e-06)
    inner_raw = sums[:-1]
    inner_pre = inner_raw * inv_rms
    inner_act, inner_pull = jax.vjp(gelu_exact, inner_pre)
    raw_mix = contract_high(mixer_out, inner_act, 0, 0)
    column = jnp.stack(
        [
            jnp.sum(raw_mix, axis=1),
            jnp.sum(raw_mix * raw_mix, axis=1),
            jnp.sum(cot_t, axis=1),
            jnp.sum(cot_t * raw_mix, axis=1),
        ],
        axis=0,
    )
    act_total = jnp.sum(inner_act, axis=1)
    act_cot = contract_high(inner_act, cot_t, 1, 1)
    act_raw = contract_high(inner_act, raw_mix, 1, 1)
    n_inner = act_total.shape[0]
    flat = sum_tokens(
        jnp.concatenate([column.reshape(-1), act_total, act_cot.reshape(-1), act_raw.reshape(-1)])
    )
    sum_raw, sum_square, sum_grad, sum_grad_raw = flat[: 4 * n_cot].reshape(4, n_cot)
    start = 4 * n_cot
    act_total = flat[start : start + n_inner]
    start += n_inner
    act_cot = flat[start : start + n_inner * n_cot].reshape(n_inner, n_cot)
    start += n_inner * n_cot
    act_raw = flat[start:].reshape(n_inner, n_cot)
    average = sum_raw / total_tokens
    variance_mix = sum_square / total_tokens - average * average
    inv_spread = lax.rsqrt(variance_mix + 1e-05)
    unit_mix = (raw_mix - average[:, None]) * inv_spread[:, None]
    mix_next = mix_static[:, None] + unit_mix
    mix_next = to_owner(mix_next.reshape(n_cot, dp * ways, block)).T
    mean_grad = sum_grad / total_tokens
    sum_grad_unit = inv_spread * (sum_grad_raw - average * sum_grad)
    mean_grad_unit = sum_grad_unit / total_tokens
    raw_grad = inv_spread[:, None] * (
        cot_t - mean_grad[:, None] - unit_mix * mean_grad_unit[:, None]
    )
    act_unit = inv_spread[None, :] * (act_raw - act_total[:, None] * average[None, :])
    mixer_out_grad = inv_spread[None, :] * (
        act_cot - act_total[:, None] * mean_grad[None, :] - act_unit * mean_grad_unit[None, :]
    )
    act_grad = contract_high(mixer_out, raw_grad, 1, 0)
    inner_low = inner_pull(act_grad)[0].astype(low)
    scaled = (output * inv_rms).astype(low)
    mixer_grad_part = contract(inner_low, scaled, 1, 1)
    scaled_grad = contract(mixer_rows, inner_low, 1, 0)
    along = jnp.sum(inner_low.astype(full) * inner_raw, axis=0) / width
    output_grad = upstream + inv_rms * scaled_grad - output * (inv_rms * inv_rms * inv_rms) * along
    if fused:
        near = output_grad.astype(low)
        far = outer_shift(near, 1)
        beside = hid_swap(near, 1)
        far_beside = outer_shift(beside, 1)

        def interleave(values_in, other):
            values_in, other = [v.reshape(places, piece, group) for v in (values_in, other)]
            return ordered(way == 0, values_in, other, 1).reshape(feats, group)

        output_lows = gather_cores([interleave(near, beside), interleave(far, far_beside)])
    else:
        output_lows = gather_turns(all_rows(output_grad.astype(low)))

    output_low = jnp.concatenate(output_lows, axis=0)

    hidden_low = (contract(turned_weights[5], output_low, 1, 0) * slope).astype(low)

    attended_grad = contract(turned_weights[4], output_low, 1, 0).astype(low)
    if fused:
        lows_mine = attend_back(
            turned_values, by_head(attended_grad), cosine[0], sine[0], starts, tops
        ).reshape(3 * n_head, group)
    else:
        a_rows = by_row(by_head(attended_grad))
        prob_grad = batched(a_rows, v_rows, 1, 1)
        row_total = jnp.sum(probs * prob_grad, axis=-1, keepdims=True)
        score_grad = (probs * (prob_grad - row_total)).astype(low)
        query_grad = from_row(batched(k_rows, score_grad, 2, 2) * score_scale)
        key_grad = from_row(batched(q_rows, score_grad, 2, 1) * score_scale)
        value_grad = from_row(batched(a_rows, probs_low, 2, 1))
        query_low = rotate(query_grad, cosine, -sine).astype(low).reshape(heads * HEAD, group)
        key_low = rotate(key_grad, cosine, -sine).astype(low).reshape(heads * HEAD, group)
        value_low = value_grad.astype(low).reshape(heads * HEAD, group)

        lows_mine = jnp.concatenate([query_low, key_low, value_low], axis=0)
    active_kept, hidden_low, lows_mine = lax.optimization_barrier((active, hidden_low, lows_mine))
    hidden_lows, lows = gather_outer(hidden_low), gather_outer(lows_mine)
    blocks = [(active.shape[0], [(0, 0, 1, 0, width)])]
    branch_sum = chain_sum([active_kept, output_low], blocks, 0)
    branch_sum, block_output, hidden_lows, lows = lax.optimization_barrier(
        (branch_sum, block_output, hidden_lows, lows)
    )
    block_output = block_output.transpose(1, 0, 2).reshape(piece, total_tokens).T

    if fused:
        operands = [hidden_lows[0], hidden_lows[1], lows[0], lows[1], output_low, attended]
        operands += [normed_all, turned_heads, turned_up, deviations]
        operands.append(output_grad.reshape(places, piece, group))
        tables = [
            own_shifts[:, :, None],
            inv_scales[:, None],
            own_gains.T.reshape(STREAMS, places, piece, 1),
            all_gains.T.reshape(STREAMS, places, 2 * piece, 1),
        ]
        late_sum, split, gain_parts = late_sums(operands, tables, 1)
        gain_parts = gain_parts.reshape(STREAMS, mine)
        history_grad, mix_parts = history_gradients(split, stored, mix_all, block)
    else:
        hidden_lows, lows = gather_cores(hidden_lows), gather_cores(lows)

        normed_grads, alongs, rights = [], [], []
        for s in range(STREAMS):
            if s < 3:
                right = jnp.concatenate([v[s * n_head : (s + 1) * n_head] for v in lows], axis=0)
            else:
                right = jnp.concatenate(hidden_lows, axis=0)
            rights.append(right)
            part = contract(turned_weights[s], right, 1, 0)
            alongs.append(jnp.sum(part * all_gains[:, s][:, None], axis=0))
            alongs.append(jnp.sum(part * normed[s].astype(full), axis=0))
            part = part.reshape(places, ways, piece, group)
            kept = lax.dynamic_index_in_dim(part, way, 1, keepdims=False)
            if ways == 2:
                given = lax.dynamic_index_in_dim(part, 1 - way, 1, keepdims=False).astype(low)
                kept = kept + hid_swap(given, 1).astype(full)
            normed_grads.append(kept.reshape(mine, group))
        weighted = [normed_grads[s] * gains[s] for s in range(STREAMS)]
        means_back = sum_features(jnp.stack(alongs, axis=0)) / width
        gain_parts = [jnp.sum(g * u, axis=1) for g, u in zip(normed_grads, units)]
        stream_grads = [
            (weighted[s] - means_back[2 * s] - units[s] * means_back[2 * s + 1]) * inv_scales[s]
            for s in range(STREAMS)
        ]
        stream_grads[3] = stream_grads[3] + output_grad
        gain_parts = jnp.stack(gain_parts, axis=0)

        split = jnp.stack([v.astype(low).reshape(places, piece, group) for v in stream_grads], axis=1)
        attended, split = lax.optimization_barrier((attended, split))
        split = exchange(split)
        wide = w_query.shape[1] // ways
        operands = [rights[3]] + rights[:3] + [output_low, normed[3]] + normed[:3] + [attended]
        blocks = [(feats, [(5, 0, 0, i, wide)]) for i in range(0, rights[3].shape[0], wide)]
        blocks += [(feats, [(6 + s, 0, 1 + s, 0, wide)]) for s in range(3)]
        blocks += [(n_head, [(9, 0, 4, i, wide)]) for i in range(0, width, wide)]
        late_sum = chain_sums(operands, blocks, 1).reshape(ways, -1, feats, wide)
        split = jnp.concatenate([split[p] for p in range(places)], axis=-1).astype(full)
        mix_layers = mix_all.reshape(STREAMS, HIST, total_tokens)
        history_grad = sum(mix_layers[s][:, None] * split[s][None] for s in range(STREAMS))
        mix_parts = jnp.concatenate(
            [jnp.sum(split[s][None] * stored.astype(full), axis=1) for s in range(STREAMS)], axis=0
        )
        mix_parts = mix_parts.reshape(n_mix, dp * hid, block).transpose(1, 0, 2)

    history_grad = history_grad.swapaxes(1, 2)
    smalls = jnp.concatenate([mixer_grad_part, gain_parts], axis=0)
    late_sum, mix_parts, smalls = lax.optimization_barrier((late_sum, mix_parts, smalls))
    mix_parts = lax.all_to_all(mix_parts, ("dp", "hid"), split_axis=0, concat_axis=0, tiled=True)
    late_grads = assemble(late_sum, w_up, fused)
    w_down_grad = unturn(branch_sum.reshape(w_down.shape))
    bit = ways
    while bit < hid:
        smalls = smalls + hid_swap(smalls, bit)
        if bit == ways:
            late_grads, smalls = lax.optimization_barrier((late_grads, smalls))
        else:
            w_down_grad, smalls = lax.optimization_barrier((w_down_grad, smalls))
        bit *= 2
    w_up_grad, w_query_grad, w_key_grad, w_value_grad, w_out_grad = late_grads
    smalls = gather_ways(smalls.reshape(-1, places, piece), 2).reshape(-1, feats)
    w_mixer_grad = smalls[:n_inner].T
    norm_gains_grad = smalls[n_inner:].T
    mix_grad = jnp.sum(mix_parts, axis=0).T

    return (
        block_output,
        mix_next,
        history_grad,
        mix_grad,
        norm_gains_grad,
        w_query_grad,
        w_key_grad,
        w_value_grad,
        w_out_grad,
        w_up_grad,
        w_down_grad,
        w_mixer_grad,
        mixer_out_grad,
        sum_grad,
    )


def solution(mesh):
    everywhere = ("dp", "hid")
    placed = (
        P(None, None, everywhere),
        P(everywhere, None),
        P(everywhere),
        P("dp", None),
        P("dp", None),
        P("dp", None),
        P("dp", None),
        P("dp", None),
        P("dp", None),
        P("dp", None),
        P("dp", None),
        P(),
        P(),
        P(None, everywhere),
        P(everywhere, None),
    )
    return jax.shard_map(
        local,
        mesh=mesh,
        in_specs=placed,
        out_specs=(
            P(None, everywhere),
            P(everywhere, None),
            P(None, None, everywhere),
            P(everywhere, None),
            P("dp", None),
            P("dp", None),
            P("dp", None),
            P("dp", None),
            P("dp", None),
            P("dp", None),
            P("dp", None),
            P("dp", None),
            P(),
            P(),
        ),
        check_vma=False,
    )
```

```python
import functools
import math

import jax
import jax.numpy as jnp
from jax import lax
from jax.experimental import pallas as pl
from jax.experimental.pallas import tpu as pltpu
from jax.sharding import PartitionSpec as P

HEADS = 16
HEAD = 128
ROT = 32
HIST = 8
STREAMS = 4
CORES = 2
CHUNK = 1 << 15
SLACK = 6
TILE = 128
LATE_TILE = 256
LATE_CHUNK = 1 << 16
LATE_SLACK = 4
SPAN = 256
VMEM = 52 << 20
PULL_START = 2
PULL_GAP = 4
GRAD_GAP = 2

highest = lax.Precision.HIGHEST
rope_base = 10000.0
low = jnp.bfloat16
full = jnp.float32


def contract(left, right, left_dim, right_dim):
    return lax.dot_general(
        left, right, (((left_dim,), (right_dim,)), ((), ())), preferred_element_type=full
    )


def contract_high(left, right, left_dim, right_dim):
    return lax.dot_general(
        left,
        right,
        (((left_dim,), (right_dim,)), ((), ())),
        precision=highest,
        preferred_element_type=full,
    )


def batched(left, right, left_dim, right_dim):
    return lax.dot_general(
        left, right, (((left_dim,), (right_dim,)), ((0,), (0,))), preferred_element_type=full
    )


def gelu_exact(values_in):
    return jax.nn.gelu(values_in, approximate=False)


def core_swap(values_in):
    size = lax.axis_size("dp")
    return lax.ppermute(values_in, "dp", [(i, i ^ 1) for i in range(size)])


def outer_shift(values_in, step):
    size = lax.axis_size("dp")
    outer = size // CORES
    pairs = [
        (o * CORES + c, ((o + step) % outer) * CORES + c) for o in range(outer) for c in range(CORES)
    ]
    return lax.ppermute(values_in, "dp", pairs)


def hid_swap(values_in, bit):
    size = lax.axis_size("hid")
    return lax.ppermute(values_in, "hid", [(i, i ^ bit) for i in range(size)])


def ordered(first, values_in, other, axis):
    return jnp.stack(
        [jnp.where(first, values_in, other), jnp.where(first, other, values_in)], axis=axis
    )


def take(values_in, index):
    return lax.dynamic_index_in_dim(values_in, index, 0, keepdims=False)


def put(target, values_in, index):
    return lax.dynamic_update_index_in_dim(target, values_in, index, 0)


def split_ways():
    return 2 if HEADS // lax.axis_size("dp") >= 2 else 1


def gather_ways(values_in, axis):
    if split_ways() == 1:
        return jnp.expand_dims(values_in, axis)
    return ordered(lax.axis_index("hid") % 2 == 0, values_in, hid_swap(values_in, 1), axis)


def gather_dp(values_in):
    size = lax.axis_size("dp")
    outer = size // CORES
    me = lax.axis_index("dp")
    mine, core = me // CORES, me % CORES
    if outer == 2:
        held = ordered(mine == 0, values_in, outer_shift(values_in, 1), 0)
    else:
        held = jnp.zeros((outer,) + values_in.shape, values_in.dtype)
        held = put(held, values_in, mine)
        for step in range(1, outer):
            held = put(held, outer_shift(values_in, step), (mine - step) % outer)
    pair = ordered(core == 0, held, core_swap(held), 1)
    return pair.reshape((size,) + values_in.shape)


def gather_outer(values_in):
    steps = range(1, lax.axis_size("dp") // CORES)
    return [values_in] + [outer_shift(values_in, step) for step in steps]


def gather_cores(held):
    return [v for h in held for v in (h, core_swap(h))]


def gather_turns(values_in):
    return gather_cores(gather_outer(values_in))


def turn_source(turn):
    outer, me = lax.axis_size("dp") // CORES, lax.axis_index("dp")
    there = (me // CORES + outer - turn // CORES) % outer
    return there * CORES + (me + turn) % CORES


def turn_of(index):
    outer, me = lax.axis_size("dp") // CORES, lax.axis_index("dp")
    step = (me // CORES + outer - index // CORES) % outer
    return step * CORES + (me + index) % CORES


def sum_features(values_in):
    if split_ways() == 2:
        values_in = values_in + hid_swap(values_in, 1)
    parts = gather_dp(values_in)
    total = parts[0]
    for i in range(1, parts.shape[0]):
        total = total + parts[i]
    return total


def sum_tokens(values_in):
    size = lax.axis_size("hid")
    ways = split_ways()
    places = size // ways
    mine = lax.axis_index("hid") // ways
    held = put(jnp.zeros((places,) + values_in.shape, values_in.dtype), values_in, mine)
    for step in range(1, places):
        pairs = [(i, (i + step * ways) % size) for i in range(size)]
        held = put(held, lax.ppermute(values_in, "hid", pairs), (mine + places - step) % places)
    return jnp.sum(held, axis=0)


def gather_all(values_in):
    count = lax.axis_size("dp") * lax.axis_size("hid")
    copies = jnp.broadcast_to(values_in[None], (count,) + values_in.shape)
    held = lax.all_to_all(copies, ("dp", "hid"), split_axis=0, concat_axis=0, tiled=True)
    return held.transpose(1, 0, 2).reshape(values_in.shape[0], -1)


def scatter_dp(make):
    size = lax.axis_size("dp")
    outer = size // CORES
    me = lax.axis_index("dp")
    mine, core = me // CORES, me % CORES
    total = None
    for step in list(range(1, outer)) + [0]:
        there = (mine + step) % outer
        away = core_swap(make(there * CORES + 1 - core).astype(low))
        block = make(there * CORES + core) + away.astype(full)
        if step:
            block = outer_shift(block.astype(low), step).astype(full)
        total = block if total is None else total + block
    return total


def exchange(values_in):
    ways, size = split_ways(), lax.axis_size("hid")
    groups = None
    if ways > 1:
        groups = [[t * ways + w for t in range(size // ways)] for w in range(ways)]
    return lax.all_to_all(
        values_in, "hid", split_axis=0, concat_axis=0, tiled=True, axis_index_groups=groups
    )


def turn_heads(values_in, cosine, sine):
    half = ROT // 2
    front, back = values_in[:half], values_in[half:ROT]
    return jnp.concatenate(
        [front * cosine - back * sine, back * cosine + front * sine, values_in[ROT:]], axis=0
    )


def across(left, right, left_dim, right_dim):
    return lax.dot_general(
        left, right, (((left_dim,), (right_dim,)), ((), ())), preferred_element_type=full
    )


def attend_kernel(
    products_ref, cosine_ref, sine_ref, start_ref, heads_ref, attended_ref, tops_ref
):
    tokens = products_ref.shape[2]
    for s in range(2):
        turned = turn_heads(products_ref[s], cosine_ref[...], sine_ref[...])
        heads_ref[s] = turned.astype(low)
    heads_ref[2] = products_ref[2].astype(low)
    for first in range(0, tokens, SPAN):
        stop = first + SPAN
        span = slice(first, stop)
        scores, top = masked_scores(heads_ref, start_ref, first)
        weights = jnp.exp(scores - top)
        total = jnp.sum(weights, axis=0, keepdims=True)
        weights = (weights / total).astype(low)
        mixed = across(heads_ref[2, :, :stop], weights, 1, 0)
        attended_ref[:, span] = mixed.astype(low)
        tops_ref[0, 0:1, span] = top
        tops_ref[0, 1:2, span] = total


def masked_scores(heads_ref, start_ref, first):
    stop = first + SPAN
    span = slice(first, stop)
    scores = across(heads_ref[1, :, :stop], heads_ref[0, :, span], 0, 0) / math.sqrt(HEAD)
    key = lax.broadcasted_iota(jnp.int32, scores.shape, 0)
    query = lax.broadcasted_iota(jnp.int32, scores.shape, 1) + first
    seen = (key >= start_ref[:, span]) & (key <= query)
    scores = jnp.where(seen, scores, -1e30)
    return scores, jnp.max(scores, axis=0, keepdims=True)


def attend_back_kernel(
    heads_ref, gradient_ref, cosine_ref, sine_ref, start_ref, tops_ref, lows_ref, key_sum, value_sum
):
    tokens = heads_ref.shape[2]
    cosine, sine = cosine_ref[...], sine_ref[...]
    scale = 1.0 / math.sqrt(HEAD)
    key_sum[...] = jnp.zeros_like(key_sum)
    value_sum[...] = jnp.zeros_like(value_sum)
    for first in range(0, tokens, SPAN):
        stop = first + SPAN
        span = slice(first, stop)
        scores, _ = masked_scores(heads_ref, start_ref, first)
        probs = jnp.exp(scores - tops_ref[0, 0:1, span]) / tops_ref[0, 1:2, span]
        gradient = gradient_ref[:, span]
        change = across(heads_ref[2, :, :stop], gradient, 0, 0)
        row_total = jnp.sum(probs * change, axis=0, keepdims=True)
        change = (probs * (change - row_total)).astype(low)
        query = across(heads_ref[1, :, :stop], change, 1, 0) * scale
        lows_ref[0, :, span] = turn_heads(query, cosine[:, span], -sine[:, span]).astype(low)
        key_sum[:, :stop] = key_sum[:, :stop] + across(heads_ref[0, :, span], change, 1, 1) * scale
        value_sum[:, :stop] = value_sum[:, :stop] + across(gradient, probs.astype(low), 1, 1)
    lows_ref[1] = turn_heads(key_sum[...], cosine, -sine).astype(low)
    lows_ref[2] = value_sum[...].astype(low)


def attend(products, cosine, sine, start):
    _, n_heads, head, tokens = products.shape
    per_head = pl.BlockSpec((3, None, head, tokens), lambda h: (0, h, 0, 0))
    table = pl.BlockSpec(cosine.shape, lambda h: (0, 0))
    return pl.pallas_call(
        attend_kernel,
        grid=(n_heads,),
        out_shape=[
            jax.ShapeDtypeStruct(products.shape, low),
            jax.ShapeDtypeStruct((n_heads, head, tokens), low),
            jax.ShapeDtypeStruct((n_heads, 2, tokens), full),
        ],
        in_specs=[per_head, table, table, pl.BlockSpec(start.shape, lambda h: (0, 0))],
        out_specs=[
            per_head,
            pl.BlockSpec((None, head, tokens), lambda h: (h, 0, 0)),
            pl.BlockSpec((1, 2, tokens), lambda h: (h, 0, 0)),
        ],
        compiler_params=pltpu.CompilerParams(vmem_limit_bytes=40 << 20),
        cost_estimate=pl.CostEstimate(
            flops=4 * n_heads * head * tokens * tokens,
            bytes_accessed=10 * products.size,
            transcendentals=n_heads * tokens * tokens,
        ),
    )(products, cosine, sine, start)


def attend_back(heads, gradient, cosine, sine, start, tops):
    _, n_heads, head, tokens = heads.shape
    per_head = pl.BlockSpec((3, None, head, tokens), lambda h: (0, h, 0, 0))
    table = pl.BlockSpec(cosine.shape, lambda h: (0, 0))
    return pl.pallas_call(
        attend_back_kernel,
        grid=(n_heads,),
        out_shape=jax.ShapeDtypeStruct(heads.shape, low),
        in_specs=[
            per_head,
            pl.BlockSpec((None, head, tokens), lambda h: (h, 0, 0)),
            table,
            table,
            pl.BlockSpec(start.shape, lambda h: (0, 0)),
            pl.BlockSpec((1, 2, tokens), lambda h: (h, 0, 0)),
        ],
        out_specs=per_head,
        scratch_shapes=[pltpu.VMEM((head, tokens), full)] * 2,
        compiler_params=pltpu.CompilerParams(vmem_limit_bytes=40 << 20),
        cost_estimate=pl.CostEstimate(
            flops=10 * n_heads * head * tokens * tokens,
            bytes_accessed=6 * heads.size,
            transcendentals=n_heads * tokens * tokens,
        ),
    )(heads, gradient, cosine, sine, start, tops)


def forward_kernel(dims, *refs):
    places, piece, group, n_head, n_units = dims
    (send_ref, mom_ref, gains_ref, query_ref, key_ref, value_ref, up_ref), refs = refs[:7], refs[7:]
    cot_ref, refs = refs[0], refs[1:]
    (
        normed_ref,
        own_ref,
        residual_ref,
        own_shift_ref,
        scale_ref,
        active_ref,
        slope_ref,
        heads_ref,
        turned_ref,
        turned_up_ref,
        cot_out,
    ), refs = refs[:11], refs[11:]
    (
        devs,
        shift_ref,
        moms,
        joins,
        weights,
        core_out,
        core_in,
        outer_out,
        outer_in,
        mom_send,
        mom_recv,
        dev_send,
        dev_recv,
        way_send,
        way_recv,
        pair_send,
        pair_recv,
        join_send,
        join_recv,
        weight_sem,
        turned_sem,
        core_send,
        core_recv,
        outer_send,
        outer_recv,
        cot_send,
        cot_recv,
        cot_own,
    ) = refs
    count = weights.shape[0]
    ups = n_units // n_head
    index, hid = lax.axis_index("dp"), lax.axis_index("hid")
    outer, core = index // 2, index % 2
    place, way = hid // 2, hid % 2
    me = index * 2 + way
    partner = {"hid": hid + 1 - 2 * way}
    core_peer = {"dp": index + 1 - 2 * core}
    outer_peer = {"dp": (index + 2) % 4}

    def peer(k):
        return (place + k) % places

    def z_device(k):
        return {"hid": peer(k) * 2 + way}

    others = [(i, j) for i in range(4) for j in range(2) if i or j]

    def join_device(i, j):
        return {"dp": (index + i) % 4, "hid": place * 2 + (way + j) % 2}

    def weight_copy(unit, t):
        there = (1 - outer if t < 2 else outer) * 2 + (core if t % 2 else 1 - core)
        block = there * 2 + way
        if unit < ups:
            source, start = up_ref, block * n_units + unit * n_head
        else:
            source, start = (query_ref, key_ref, value_ref)[unit - ups], block * n_head
        start = pl.multiple_of(start, n_head)
        return pltpu.make_async_copy(
            source.at[:, pl.ds(start, n_head)], weights.at[unit, t], weight_sem.at[unit]
        )

    for unit in range(count):
        for t in range(4):
            weight_copy(unit, t).start()

    barrier = pltpu.get_barrier_semaphore()

    for k in range(1, places):
        greet(z_device(k))
    for i, j in others:
        greet(join_device(i, j))
    pl.semaphore_wait(barrier, places - 1 + len(others))

    def mom_copy(k, sender, target):
        return remote(
            mom_ref.at[target], moms.at[way, sender], mom_send, mom_recv.at[sender], z_device(k)
        )

    def dev_copy(s, k, sender, target):
        return remote(
            send_ref.at[target, s],
            devs.at[s, way, sender],
            dev_send,
            dev_recv.at[s, sender],
            z_device(k),
        )

    for k in range(1, places):
        mom_copy(k, place, peer(k)).start()
    for s in (3, 0, 1, 2):
        for k in range(1, places):
            dev_copy(s, k, place, peer(k)).start()
    for k in range(1, places):
        remote(cot_ref.at[peer(k)], cot_out.at[place], cot_send, cot_recv, z_device(k)).start()
    pltpu.make_async_copy(cot_ref.at[place], cot_out.at[place], cot_own).start()
    moms[way, place] = mom_ref[place]
    for s in range(STREAMS):
        devs[s, way, place] = send_ref[place, s]

    def way_copy(source, s, q):
        return remote(source, devs.at[s, way, q], way_send, way_recv.at[s], partner)

    def forward(s):
        way_copy(send_ref.at[place, s], s, place).start()
        for k in range(1, places):
            q = peer(k)
            dev_copy(s, k, q, q).wait_recv()
            way_copy(devs.at[s, way, q], s, q).start()

    def join_parts(means, parts, size):
        mean = means[0]
        for m in means[1:]:
            mean = mean + m
        mean = mean / len(means)
        total = parts[0]
        for v in parts[1:]:
            total = total + v
        for m in means:
            total = total + size * (m - mean) * (m - mean)
        return mean, total

    for k in range(1, places):
        mom_copy(k, peer(k), place).wait_recv()
    remote(moms.at[way], moms.at[way], pair_send, pair_recv, partner).start()
    mean, total = join_parts(
        [moms[way, q, :STREAMS, :] for q in range(places)],
        [moms[way, q, STREAMS:, :] for q in range(places)],
        piece,
    )
    joins[me, :STREAMS, :] = mean
    joins[me, STREAMS:, :] = total
    for i, j in others:
        remote(joins.at[me], joins.at[me], join_send, join_recv, join_device(i, j)).start()
    forward(3)
    n_others = len(others)
    remote(
        joins.at[pl.ds(0, n_others)], joins.at[pl.ds(0, n_others)], join_send, join_recv, partner
    ).wait_recv()
    remote(moms.at[way], moms.at[1 - way], pair_send, pair_recv, partner).wait_recv()
    mean, total = join_parts(
        [joins[i, :STREAMS, :] for i in range(n_others + 1)],
        [joins[i, STREAMS:, :] for i in range(n_others + 1)],
        piece * places,
    )
    scale = lax.rsqrt(total / (piece * places * (n_others + 1)) + 1e-05)
    for s in range(STREAMS):
        for q in range(places):
            for w in range(2):
                off = moms[w, q, s : s + 1, :] - mean[s : s + 1]
                shift_ref[s, 2 * q + w : 2 * q + w + 1, :] = off * scale[s : s + 1]
        shift_ref[s, 2 * places : 2 * places + 1, :] = scale[s : s + 1]
        scale_ref[s] = scale[s : s + 1]
        for q in range(places):
            first, second = [shift_ref[s, 2 * q + w : 2 * q + w + 1, :] for w in range(2)]
            own_shift_ref[s, q] = jnp.where(way == 0, first, second)

    def normalize(s):
        remote(devs.at[s, 1 - way], devs.at[s, 1 - way], way_send, way_recv.at[s], partner).wait_recv()
        size = shift_ref[s, 2 * places : 2 * places + 1, :]
        for q in range(places):
            for w in range(2):
                block = 2 * q + w
                rows = slice(block * piece, (block + 1) * piece)
                unit = devs[s, w, q].astype(full) * size + shift_ref[s, block : block + 1, :]
                normed_ref[s, rows, :] = (unit * gains_ref[s, rows, :]).astype(low)

    def core_copy(unit, half):
        return remote(
            core_out.at[unit, half],
            core_in.at[unit, half],
            core_send,
            core_recv.at[unit, half],
            core_peer,
        )

    def outer_copy(unit):
        return remote(
            outer_out.at[unit], outer_in.at[unit], outer_send, outer_recv.at[unit], outer_peer
        )

    def project(unit, carry):
        @pl.when(unit == 0)
        def _():
            normalize(3)
            forward(0)

        for s in (1, 2):

            @pl.when(unit == s)
            def _(s=s):
                forward(s)

        @pl.when(unit >= ups)
        def _():
            normalize(unit - ups)

        stream = jnp.where(unit < ups, 3, unit - ups)
        pltpu.make_async_copy(weights.at[unit], weights.at[unit], weight_sem.at[unit]).wait()

        def product(t):
            return lax.dot_general(
                weights[unit, t],
                normed_ref[stream],
                (((0,), (0,)), ((), ())),
                preferred_element_type=full,
            )

        core_out[unit, 0] = product(0).astype(low)
        core_copy(unit, 0).start()
        passing = product(1)
        core_out[unit, 1] = product(2).astype(low)
        core_copy(unit, 1).start()
        core_copy(unit, 0).wait_recv()
        outer_out[unit] = (passing + core_in[unit, 0].astype(full)).astype(low)
        outer_copy(unit).start()
        kept = product(3)
        core_copy(unit, 1).wait_recv()
        kept = kept + core_in[unit, 1].astype(full)

        @pl.when(unit < ups)
        def _():
            slope_ref[pl.ds(pl.multiple_of(unit * n_head, n_head), n_head), :] = kept

        @pl.when(unit >= ups)
        def _():
            heads_ref[unit - ups] = kept

        return carry

    lax.fori_loop(0, count, project, 0)

    def turned_copies():
        for unit in range(count):
            for t in range(4):
                turn = 3 - t
                if unit < ups:
                    start = turn * n_units + unit * n_head
                    target = turned_up_ref.at[:, start : start + n_head]
                else:
                    target = turned_ref.at[unit - ups, :, turn * n_head : (turn + 1) * n_head]
                yield pltpu.make_async_copy(weights.at[unit, t], target, turned_sem)

    for copy in turned_copies():
        copy.start()
    for s in range(STREAMS):
        own_ref[s] = devs[s, way]
    for q in range(places):
        offset = moms[way, q, 3:4, :]
        residual_ref[q * piece : (q + 1) * piece, :] = devs[3, way, q].astype(full) + offset

    step = 32

    def finish_up(unit, carry):
        outer_copy(unit).wait_recv()

        def part(i, carry):
            inner = pl.ds(pl.multiple_of(i * step, step), step)
            rows = pl.ds(pl.multiple_of(unit * n_head + i * step, step), step)
            hidden = slope_ref[rows, :] + outer_in[unit, inner, :].astype(full)
            half = 0.5 + 0.5 * lax.erf(hidden * math.sqrt(0.5))
            active_ref[rows, :] = (hidden * half).astype(low)
            bell = jnp.exp(-0.5 * hidden * hidden) * (1.0 / math.sqrt(2.0 * math.pi))
            slope_ref[rows, :] = half + hidden * bell
            return carry

        return lax.fori_loop(0, n_head // step, part, carry)

    lax.fori_loop(0, ups, finish_up, 0)

    def finish_head(unit, carry):
        outer_copy(unit).wait_recv()
        heads_ref[unit - ups] = heads_ref[unit - ups] + outer_in[unit].astype(full)
        return carry

    lax.fori_loop(ups, count, finish_head, 0)

    def sent(ref, sem):
        remote(ref, ref, sem, join_recv, partner).wait_send()

    sent(moms.at[0, pl.ds(0, places - 1)], mom_send)
    sent(send_ref.at[pl.ds(0, places - 1)], dev_send)
    sent(send_ref, way_send)
    sent(moms.at[0], pair_send)
    sent(joins.at[pl.ds(0, n_others)], join_send)
    sent(core_out, core_send)
    sent(outer_out, outer_send)
    moved = cot_ref.at[pl.ds(0, places - 1)]
    sent(moved, cot_send)
    remote(moved, moved, cot_send, cot_recv, partner).wait_recv()
    pltpu.make_async_copy(cot_ref.at[0], cot_out.at[0], cot_own).wait()
    pltpu.make_async_copy(weights, weights, turned_sem).wait()


def forward_projections(deviations, moments, norm_gains, w_query, w_key, w_value, w_up, cotangent):
    places, _, piece, group = deviations.shape
    feats = norm_gains.shape[0]
    n_head = w_query.shape[1] // 8
    n_units = w_up.shape[1] // 8
    count = n_units // n_head + 3
    vmem, dma = pltpu.VMEM, pltpu.SemaphoreType.DMA
    out_types = [
        ((STREAMS, feats, group), low),
        ((STREAMS, places, piece, group), low),
        ((places * piece, group), full),
        ((STREAMS, places, 1, group), full),
        ((STREAMS, 1, group), full),
        ((n_units, group), low),
        ((n_units, group), full),
        ((3, n_head, group), full),
        ((3, feats, 4 * n_head), low),
        ((feats, 4 * n_units), low),
        (cotangent.shape, low),
    ]
    spaces = [vmem] * 8 + [pl.ANY] * 3
    return pl.pallas_call(
        functools.partial(forward_kernel, (places, piece, group, n_head, n_units)),
        out_shape=[jax.ShapeDtypeStruct(*t) for t in out_types],
        in_specs=[pl.BlockSpec(memory_space=vmem)] * 3 + [pl.BlockSpec(memory_space=pl.ANY)] * 5,
        out_specs=[pl.BlockSpec(memory_space=m) for m in spaces],
        scratch_shapes=[
            vmem((STREAMS, 2, places, piece, group), low),
            vmem((STREAMS, 2 * places + 8, group), full),
            vmem((2, places, 2 * STREAMS, group), full),
            vmem((8, 2 * STREAMS, group), full),
            vmem((count, 4, feats, n_head), low),
            vmem((count, 2, n_head, group), low),
            vmem((count, 2, n_head, group), low),
            vmem((count, n_head, group), low),
            vmem((count, n_head, group), low),
            dma,
            dma((places,)),
            dma,
            dma((STREAMS, places)),
            dma,
            dma((STREAMS,)),
            dma,
            dma,
            dma,
            dma,
            dma((count,)),
            dma,
            dma,
            dma((count, 2)),
            dma,
            dma((count,)),
            dma,
            dma,
            dma,
        ],
        compiler_params=pltpu.CompilerParams(
            collective_id=7, has_side_effects=True, vmem_limit_bytes=62 << 20
        ),
        cost_estimate=pl.CostEstimate(
            flops=8 * count * n_head * feats * group,
            bytes_accessed=300 << 20,
            transcendentals=2 * n_units * group,
        ),
    )(
        deviations,
        moments,
        norm_gains.T.astype(full)[:, :, None],
        w_query,
        w_key,
        w_value,
        w_up,
        cotangent,
    )


def remote(source, target, send, recv, device):
    return pltpu.make_async_remote_copy(
        src_ref=source,
        dst_ref=target,
        send_sem=send,
        recv_sem=recv,
        device_id=device,
        device_id_type=pl.DeviceIdType.MESH,
    )


def greet(device):
    pl.semaphore_signal(
        pltpu.get_barrier_semaphore(),
        inc=1,
        device_id=device,
        device_id_type=pl.DeviceIdType.MESH,
    )


def chain_place(ways, places):
    last = places - 1
    me = lax.axis_index("hid")
    if ways == 2:
        place, way = me // 2, me % 2
        return place, way, me + 2, me - 2, me + 1 - 2 * way
    odd, half = me % 2, places // 2
    place = (1 - odd) * (me // 2) + odd * (last - me // 2)
    turn_up = (place + 1) // half
    turn_down = (place - 1 + places) // half - 2
    above = (1 - turn_up) * 2 * (place + 1) + turn_up * (2 * (last - place - 1) + 1)
    below = (1 - turn_down) * 2 * (place - 1) + turn_down * (2 * (last - place + 1) + 1)
    return place, 0, above, below, me


def chain_semaphores(count):
    dma = pltpu.SemaphoreType.DMA
    return [dma, dma((count,)), dma, dma((count,)), dma, dma, dma, dma, dma((count,))]


def chain_loop(ways, places, out_ref, own, landed, semaphores, compute, slack, hook=None, far=None):
    (
        up_send,
        up_recv,
        down_send,
        down_recv,
        side_send,
        side_recv,
        kept,
        far_send,
        far_recv,
    ) = semaphores
    count, depth = landed.shape[:2]
    per_tile = own.shape[0] // depth
    last = places - 1
    root = last if far is None else places // 2
    place, way, above, below, beside = chain_place(ways, places)
    above, below, beside = {"hid": above}, {"hid": below}, {"hid": beside}

    def send_in(i):
        @pl.when(place < root)
        def _():
            remote(landed.at[i], landed.at[i], up_send, up_recv.at[i], above).start()

        if far is not None:

            @pl.when(place == root + 1)
            def _():
                remote(landed.at[i], far.at[i], up_send, far_recv.at[i], below).start()

            @pl.when(place > root + 1)
            def _():
                remote(landed.at[i], landed.at[i], up_send, up_recv.at[i], below).start()

    def send_out(source, i):
        def to(device, send):
            remote(source, out_ref.at[way, i], send, down_recv.at[i], device).start()

        @pl.when((place <= root) & (place > 0))
        def _():
            to(below, down_send)

        if far is not None:

            @pl.when((place >= root) & (place < last))
            def _():
                to(above, far_send)

        if ways == 2:
            remote(source, out_ref.at[way, i], side_send, side_recv, beside).start()

    def upward(i):
        @pl.when(i % per_tile == 0)
        def _():
            compute(i // per_tile)

        mine = own[pl.ds(pl.multiple_of(i % per_tile * depth, depth), depth), :]
        ends = place == 0 if far is None else (place == 0) | (place == last)

        @pl.when(ends)
        def _():
            landed[i] = mine.astype(low)

        @pl.when(jnp.logical_not(ends))
        def _():
            remote(landed.at[i], landed.at[i], up_send, up_recv.at[i], above).wait_recv()
            total = landed[i].astype(full) + mine
            if far is None:
                landed[i] = total.astype(low)
            else:

                @pl.when(place != root)
                def _():
                    landed[i] = total.astype(low)

                @pl.when(place == root)
                def _():
                    remote(far.at[i], far.at[i], up_send, far_recv.at[i], above).wait_recv()
                    landed[i] = (total + far[i].astype(full)).astype(low)

        @pl.when(place != root)
        def _():
            send_in(i)

        @pl.when(place == root)
        def _():
            send_out(landed.at[i], i)
            pltpu.make_async_copy(landed.at[i], out_ref.at[way, i], kept).start()

    def downward(i):
        done = out_ref.at[way, i]
        remote(done, done, down_send, down_recv.at[i], below).wait_recv()
        send_out(done, i)

    away = root - place if far is None else jnp.where(place < root, root - place, place - root)
    lag = slack * away + 2

    def step(i, carry):
        @pl.when(i < count)
        def _():
            upward(i)

        behind = i - lag

        @pl.when((behind >= 0) & (behind < count) & (place != root))
        def _():
            downward(behind)

        if hook is not None:
            hook(i)
        return carry

    lax.fori_loop(0, count + slack * root + 2, step, 0)

    def sent(sem):
        remote(landed, landed, sem, side_recv, beside).wait_send()

    @pl.when(place != root)
    def _():
        sent(up_send)

    @pl.when((place <= root) & (place > 0))
    def _():
        sent(down_send)

    if far is not None:

        @pl.when((place >= root) & (place < last))
        def _():
            sent(far_send)

    @pl.when(place == root)
    def _():
        pltpu.make_async_copy(landed, out_ref.at[way], kept).wait()

    if ways == 2:
        sent(side_send)
        remote(landed, landed, side_send, side_recv, beside).wait_recv()


def chain_kernel(ways, places, blocks, n_operands, *refs):
    operand_refs, out_ref, refs = refs[:n_operands], refs[n_operands], refs[n_operands + 1 :]
    operands, (own, landed, far, fetched, *semaphores) = refs[:n_operands], refs[n_operands:]
    last = places - 1
    place, way, above, below, beside = chain_place(ways, places)

    def fetch(n):
        return pltpu.make_async_copy(operand_refs[n], operands[n], fetched.at[n])

    for n in range(n_operands):
        fetch(n).start()

    barrier = pltpu.get_barrier_semaphore()

    @pl.when(place > 0)
    def _():
        greet({"hid": below})

    @pl.when(place < last)
    def _():
        greet({"hid": above})

    if ways == 2:
        greet({"hid": beside})
    met = jnp.where(place > 0, 1, 0) + jnp.where(place < last, 1, 0) + (ways - 1)
    pl.semaphore_wait(barrier, met)

    def compute(tile):
        seen, first = set(), 0
        for rows, segments in blocks:
            start = first
            first = first + rows // TILE
            fresh = [n for seg in segments for n in (seg[0], seg[2])]
            fresh = [n for n in dict.fromkeys(fresh) if n not in seen]
            seen.update(fresh)

            @pl.when(tile == start)
            def _(fresh=fresh):
                for n in fresh:
                    fetch(n).wait()

            @pl.when((tile >= start) & (tile < first))
            def _(start=start, segments=segments):
                column = 0
                for left, left_row, right, right_row, size in segments:
                    row = pl.multiple_of(left_row + (tile - start) * TILE, TILE)
                    own[:, column : column + size] = lax.dot_general(
                        operands[left][pl.ds(row, TILE), :],
                        operands[right][right_row : right_row + size, :],
                        (((1,), (1,)), ((), ())),
                        preferred_element_type=full,
                    )
                    column += size

    chain_loop(ways, places, out_ref, own, landed, semaphores, compute, SLACK, far=far)


def chain_sum(operands, blocks, collective_id):
    ways, size = split_ways(), lax.axis_size("hid")
    columns = sum(seg[4] for seg in blocks[0][1])
    rows = sum(block[0] for block in blocks)
    depth = max(16, CHUNK // columns)
    count = rows // depth
    tokens = operands[0].shape[1]
    return pl.pallas_call(
        functools.partial(chain_kernel, ways, size // ways, blocks, len(operands)),
        out_shape=jax.ShapeDtypeStruct((ways, count, depth, columns), low),
        in_specs=[pl.BlockSpec(memory_space=pl.ANY)] * len(operands),
        out_specs=pl.BlockSpec(memory_space=pl.ANY),
        scratch_shapes=[pltpu.VMEM(v.shape, low) for v in operands]
        + [
            pltpu.VMEM((TILE, columns), full),
            pltpu.VMEM((count, depth, columns), low),
            pltpu.VMEM((count, depth, columns), low),
            pltpu.SemaphoreType.DMA((len(operands),)),
        ]
        + chain_semaphores(count),
        compiler_params=pltpu.CompilerParams(
            collective_id=collective_id, has_side_effects=True, vmem_limit_bytes=60 << 20
        ),
        cost_estimate=pl.CostEstimate(
            flops=2 * rows * columns * tokens,
            bytes_accessed=300 * rows * columns,
            transcendentals=0,
        ),
    )(*operands)


def branch_kernel(dims, *refs):
    places, piece, group = dims
    (attended_ref, active_ref, residual_ref, mixer_ref, out_w_ref, down_w_ref), refs = refs[:6], refs[6:]
    (output_ref, rounded_ref, sums_ref, turned_out_ref, turned_down_ref), refs = refs[:5], refs[5:]
    (
        weights,
        sums,
        core_out,
        core_in,
        outer_out,
        outer_in,
        side_out,
        side_in,
        parts_out,
        parts_in,
        totals,
        weight_sem,
        turned_sem,
        core_send,
        core_recv,
        outer_send,
        outer_recv,
        side_send,
        side_recv,
        part_send,
        part_recv,
        total_send,
        total_recv,
    ) = refs
    index, hid = lax.axis_index("dp"), lax.axis_index("hid")
    outer, core = index // 2, index % 2
    place, way = hid // 2, hid % 2
    me = index * 2 + way
    partner = {"hid": hid + 1 - 2 * way}
    core_peer = {"dp": index + 1 - 2 * core}
    outer_peer = {"dp": (index + 2) % 4}
    others = [(i, j) for i in range(4) for j in range(2) if i or j]
    n_head, n_units = attended_ref.shape[0], active_ref.shape[0]
    feats = weights.shape[2]
    wide = group // 8

    def peer(i, j):
        there, other = (index + i) % 4, (way + j) % 2
        return there * 2 + other, {"dp": there, "hid": place * 2 + other}

    def weight_copies(t):
        there = (1 - outer if t < 2 else outer) * 2 + (core if t % 2 else 1 - core)
        columns = pl.ds(pl.multiple_of(there * feats, feats), feats)
        for ref, first, size in ((out_w_ref, 0, n_head), (down_w_ref, n_head, n_units)):
            rows = pl.ds(pl.multiple_of(way * size, size), size)
            yield pltpu.make_async_copy(
                ref.at[rows, columns], weights.at[t, first : first + size], weight_sem.at[t]
            )

    def turned_copies(t):
        columns = pl.ds(pl.multiple_of((3 - t) * feats, feats), feats)
        for ref, first, size in ((turned_out_ref, 0, n_head), (turned_down_ref, n_head, n_units)):
            yield pltpu.make_async_copy(
                weights.at[t, first : first + size], ref.at[:, columns], turned_sem
            )

    for t in range(4):
        for copy in weight_copies(t):
            copy.start()
    for i, j in others:
        greet(peer(i, j)[1])
    pl.semaphore_wait(pltpu.get_barrier_semaphore(), len(others))

    def halves(t, target, kind):
        pltpu.make_async_copy(weights.at[t], weights.at[t], weight_sem.at[t]).wait()
        product = across(weights[t, :n_head, :], attended_ref[...], 0, 0)
        product = product + across(weights[t, n_head:, :], active_ref[...], 0, 0)
        for q in range(places):
            first = product[2 * q * piece : (2 * q + 1) * piece]
            second = product[(2 * q + 1) * piece : (2 * q + 2) * piece]
            rows = slice(q * piece, (q + 1) * piece)
            target[0, rows, :] = jnp.where(way == 0, second, first).astype(kind)
            target[1, rows, :] = jnp.where(way == 0, first, second).astype(kind)
        for copy in turned_copies(t):
            copy.start()

    def core_copy(stage, half):
        return remote(
            core_out.at[stage, half],
            core_in.at[stage, half],
            core_send,
            core_recv.at[stage, half],
            core_peer,
        )

    def outer_copy(half):
        return remote(
            outer_out.at[half], outer_in.at[half], outer_send, outer_recv.at[half], outer_peer
        )

    def stage(k, carry):
        halves(2 * k, core_out.at[k], low)
        for half in range(2):
            core_copy(k, half).start()
        halves(2 * k + 1, sums.at[k], full)
        for half in range(2):
            core_copy(k, half).wait_recv()
            sums[k, half] = sums[k, half] + core_in[k, half].astype(full)

            @pl.when(k == 0)
            def _(half=half):
                outer_out[half] = sums[0, half].astype(low)
                outer_copy(half).start()

        return carry

    lax.fori_loop(0, 2, stage, 0)
    kept = sums.at[1]
    kept[1] = kept[1] + residual_ref[...]
    side = remote(side_out, side_in, side_send, side_recv, partner)
    outer_copy(0).wait_recv()
    side_out[...] = (kept[0] + outer_in[0].astype(full)).astype(low)
    side.start()
    outer_copy(1).wait_recv()
    kept[1] = kept[1] + outer_in[1].astype(full)
    side.wait_recv()
    output = kept[1] + side_in[...].astype(full)
    output_ref[...] = output
    rounded = output.astype(low)
    rounded_ref[...] = rounded

    mixed = jnp.dot(mixer_ref[...], rounded, preferred_element_type=full)
    square = jnp.sum(output * output, axis=0, keepdims=True)
    row = lax.broadcasted_iota(jnp.int32, mixed.shape, 0)
    mixed = jnp.where(row == mixed.shape[0] - 1, square, mixed)
    for b in range(8):
        parts_out[b] = mixed[:, b * wide : (b + 1) * wide]
    parts_in[me] = parts_out[me]
    for i, j in others:
        slot, device = peer(i, j)
        remote(parts_out.at[slot], parts_in.at[me], part_send, part_recv, device).start()
    some = pl.ds(0, len(others))

    def whole(ref, send, recv):
        return remote(ref.at[some], ref.at[some], send, recv, partner)

    whole(parts_in, part_send, part_recv).wait_recv()
    total = parts_in[0]
    for b in range(1, 8):
        total = total + parts_in[b]
    totals[me] = total
    for i, j in others:
        remote(totals.at[me], totals.at[me], total_send, total_recv, peer(i, j)[1]).start()
    whole(totals, total_send, total_recv).wait_recv()
    for b in range(8):
        sums_ref[:, b * wide : (b + 1) * wide] = totals[b]

    whole(parts_out, part_send, part_recv).wait_send()
    whole(totals, total_send, total_recv).wait_send()
    remote(core_out, core_out, core_send, side_recv, partner).wait_send()
    remote(outer_out, outer_out, outer_send, side_recv, partner).wait_send()
    side.wait_send()
    pltpu.make_async_copy(weights, weights, turned_sem).wait()


def add_branches(places, attended, active, residual, mixer_rows, w_out, w_down):
    mine, group = residual.shape
    n_head, n_units = attended.shape[0], active.shape[0]
    feats = w_out.shape[0]
    n_sums = 48
    table = jnp.zeros((n_sums, mine), low).at[: mixer_rows.shape[1]].set(mixer_rows.T)
    vmem, dma = pltpu.VMEM, pltpu.SemaphoreType.DMA
    out_types = [
        ((mine, group), full),
        ((mine, group), low),
        ((n_sums, group), full),
        ((n_head, w_out.shape[1]), low),
        ((n_units, w_down.shape[1]), low),
    ]
    spaces = [vmem] * 3 + [pl.ANY] * 2
    block = (2, mine, group)
    slots = (8, n_sums, group // 8)
    return pl.pallas_call(
        functools.partial(branch_kernel, (places, mine // places, group)),
        out_shape=[jax.ShapeDtypeStruct(*t) for t in out_types],
        in_specs=[pl.BlockSpec(memory_space=vmem)] * 4 + [pl.BlockSpec(memory_space=pl.ANY)] * 2,
        out_specs=[pl.BlockSpec(memory_space=m) for m in spaces],
        scratch_shapes=[
            vmem((4, n_head + n_units, feats), low),
            vmem((2,) + block, full),
            vmem((2,) + block, low),
            vmem((2,) + block, low),
            vmem(block, low),
            vmem(block, low),
            vmem(block[1:], low),
            vmem(block[1:], low),
            vmem(slots, full),
            vmem(slots, full),
            vmem(slots, full),
            dma((4,)),
            dma,
            dma,
            dma((2, 2)),
            dma,
            dma((2,)),
            dma,
            dma,
            dma,
            dma,
            dma,
            dma,
        ],
        compiler_params=pltpu.CompilerParams(
            collective_id=8, has_side_effects=True, vmem_limit_bytes=56 << 20
        ),
        cost_estimate=pl.CostEstimate(
            flops=8 * (n_head + n_units) * feats * group, bytes_accessed=100 << 20, transcendentals=0
        ),
    )(attended, active, residual, table, w_out, w_down)


def late_kernel(dims, *refs):
    places, piece, group, n_head, n_units = dims
    (
        hidden_ref,
        hidden_far_ref,
        lows_ref,
        lows_far_ref,
        output_low_ref,
        attended_ref,
        normed_ref,
        turned_ref,
        turned_up_ref,
        devs_ref,
        output_grad_ref,
        shifts,
        scales,
        gains,
        all_gains,
    ), refs = refs[:15], refs[15:]
    (out_ref, split_ref, gain_ref), refs = refs[:3], refs[3:]
    (
        hidden,
        lows,
        output_low,
        attended,
        normed,
        turned,
        turned_up,
        devs,
        output_grad,
        kept,
        given,
        taken,
        grads,
        joins,
        totals,
        own,
        pulled,
        landed,
        fetched,
        core_send,
        core_recv,
        side_send,
        side_recv,
        join_send,
        join_recv,
        place_send,
        place_recv,
        own_copy,
        *semaphores,
    ) = refs
    index, hid = lax.axis_index("dp"), lax.axis_index("hid")
    core = index % 2
    place, way = hid // 2, hid % 2
    me = index * 2 + way
    partner = {"hid": hid + 1 - 2 * way}
    core_peer = {"dp": index + 1 - 2 * core}
    others = [(i, j) for i in range(4) for j in range(2) if i or j]
    wide = own.shape[1]
    feats = normed.shape[1]

    def join_device(i, j):
        return {"dp": (index + i) % 4, "hid": place * 2 + (way + j) % 2}

    def head_rows(turn):
        return slice(turn * n_head, (turn + 1) * n_head)

    def unit_rows(turn):
        return slice(turn * n_units, (turn + 1) * n_units)

    fetches = [
        [(output_low_ref, output_low), (attended_ref, attended), (normed_ref, normed)],
        [(hidden_ref, hidden.at[unit_rows(0)])],
        [
            (hidden_far_ref, hidden.at[unit_rows(2)]),
            (turned_ref, turned),
            (turned_up_ref, turned_up),
            (devs_ref, devs),
            (output_grad_ref, output_grad),
        ]
        + [
            (source.at[head_rows(s)], lows.at[s, head_rows(turn)])
            for s in range(3)
            for turn, source in ((0, lows_ref), (2, lows_far_ref))
        ],
    ]

    def fetch(stage):
        return [pltpu.make_async_copy(a, b, fetched.at[stage, n]) for n, (a, b) in enumerate(fetches[stage])]

    for stage in range(len(fetches)):
        for copy in fetch(stage):
            copy.start()

    for k in range(1, places):
        greet({"hid": (place + k) % places * 2 + way})
    for i, j in others:
        greet(join_device(i, j))
    pl.semaphore_wait(pltpu.get_barrier_semaphore(), places - 1 + len(others))

    def core_copies(far):
        source, heads = (hidden_far_ref, lows_far_ref) if far else (hidden_ref, lows_ref)
        turn = 3 if far else 1
        yield remote(source, hidden.at[unit_rows(turn)], core_send.at[far], core_recv.at[far], core_peer)
        for s in range(3):
            yield remote(
                heads.at[head_rows(s)],
                lows.at[s, head_rows(turn)],
                core_send.at[2 + far],
                core_recv.at[2 + far],
                core_peer,
            )

    for far in range(2):
        for copy in core_copies(far):
            copy.start()

    def wait_cores():
        for far in range(2):
            remote(hidden_ref, hidden_ref, core_send.at[far], core_recv.at[far], core_peer).wait_recv()
            remote(lows_ref, lows_ref, core_send.at[2 + far], core_recv.at[2 + far], core_peer).wait_recv()

    per_block = feats // LATE_TILE
    per_out = n_head // LATE_TILE

    def compute(tile):
        @pl.when(tile == 0)
        def _():
            for copy in fetch(0):
                copy.wait()

        @pl.when(tile == per_block)
        def _():
            for copy in fetch(1):
                copy.wait()

        inner = tile % per_block

        def product(left, right):
            own[...] = lax.dot_general(
                left, right, (((1,), (1,)), ((), ())), preferred_element_type=full
            )

        def rows(n):
            return pl.ds(pl.multiple_of(n * LATE_TILE, LATE_TILE), LATE_TILE)

        @pl.when(tile < per_block)
        def _():
            half = pl.ds(pl.multiple_of(inner // per_out * wide, wide), wide)
            product(attended[rows(inner % per_out), :], output_low[half, :])

        block = tile // per_block

        @pl.when((block >= 1) & (block < 5))
        def _():
            turn = (block - 1) // 2 + (block - 1) % 2 * 2
            units = pl.ds(pl.multiple_of(turn * n_units, n_units), n_units)
            product(normed[3, rows(inner), :], hidden[units, :])

        @pl.when(block >= 5)
        def _():
            product(normed[block - 5, rows(inner), :], lows[block - 5])

    totals[...] = jnp.zeros_like(totals)

    def side_copy(s, r):
        return remote(given.at[s, r], taken.at[s, r], side_send, side_recv.at[s], partner)

    def pull(s):
        @pl.when(s < 3)
        def _():
            pulled[...] = jnp.dot(turned[s], lows[s], preferred_element_type=full)

        @pl.when(s == 3)
        def _():
            pulled[...] = jnp.dot(turned_up[...], hidden[...], preferred_element_type=full)

        def use(r, carry):
            rows = pl.ds(pl.multiple_of(2 * piece * r, 2 * piece), 2 * piece)
            here = pulled[rows, :]
            totals[s, 0:1, :] = totals[s, 0:1, :] + jnp.sum(
                here * all_gains[s, r], axis=0, keepdims=True
            )
            totals[s, 1:2, :] = totals[s, 1:2, :] + jnp.sum(
                here * normed[s, rows, :].astype(full), axis=0, keepdims=True
            )
            first = way == 0
            kept[s, r] = jnp.where(first, here[:piece], here[piece:])
            given[s, r] = jnp.where(first, here[piece:], here[:piece]).astype(low)
            side_copy(s, r).start()
            return carry

        lax.fori_loop(0, places, use, 0)

    def share_totals():
        joins[me] = totals[...]
        for i, j in others:
            remote(joins.at[me], joins.at[me], join_send, join_recv, join_device(i, j)).start()

    def sum_totals():
        some = joins.at[pl.ds(0, len(others))]
        remote(some, some, join_send, join_recv, partner).wait_recv()
        total = joins[0]
        for i in range(1, len(others) + 1):
            total = total + joins[i]
        totals[...] = total / (feats * 4)

    def stream_grad(s, r):
        @pl.when(r == 0)
        def _():
            remote(given.at[s], taken.at[s], side_send, side_recv.at[s], partner).wait_recv()

        gradient = kept[s, r] + taken[s, r].astype(full)
        unit = devs[s, r].astype(full) * scales[s] + shifts[s, r]
        gain_ref[s, r] = jnp.sum(gradient * unit, axis=1, keepdims=True)
        result = gradient * gains[s, r] - totals[s, 0:1, :] - unit * totals[s, 1:2, :]
        extra = output_grad[r] * jnp.where(s == 3, 1.0, 0.0)
        grads[s, r] = (result * scales[s] + extra).astype(low)

        @pl.when(r == place)
        def _():
            pltpu.make_async_copy(grads.at[s, r], split_ref.at[s, place], own_copy).start()

        @pl.when(r != place)
        def _():
            remote(
                grads.at[s, r],
                split_ref.at[s, place],
                place_send,
                place_recv,
                {"hid": r * 2 + way},
            ).start()

    n_pulls = STREAMS * places
    middle = PULL_START + PULL_GAP * STREAMS
    resume = middle + 8

    def hook(i):
        @pl.when(i == PULL_START)
        def _():
            for copy in fetch(2):
                copy.wait()
            wait_cores()

        k = (i - PULL_START) // PULL_GAP

        @pl.when((i >= PULL_START) & (i < middle) & ((i - PULL_START) % PULL_GAP == 0))
        def _():
            pull(k)

        @pl.when(i == middle)
        def _():
            share_totals()

        @pl.when(i == resume)
        def _():
            sum_totals()

        n = (i - resume) // GRAD_GAP

        @pl.when((i >= resume) & (n < n_pulls) & ((i - resume) % GRAD_GAP == 0))
        def _():
            stream_grad(n // places, n % places)

    chain_loop(2, places, out_ref, own, landed, semaphores, compute, LATE_SLACK, hook)

    def sent(ref, sem):
        remote(ref, ref, sem, join_recv, partner).wait_send()

    for far in range(2):
        sent(hidden_ref, core_send.at[far])
        sent(lows_ref, core_send.at[2 + far])
    sent(given, side_send)
    sent(joins.at[pl.ds(0, len(others))], join_send)
    moved = grads.at[pl.ds(0, places - 1)]
    sent(moved, place_send)
    remote(moved, moved, place_send, place_recv, partner).wait_recv()
    mine = grads.at[0]
    pltpu.make_async_copy(mine, mine, own_copy).wait()


def late_sums(operands, tables, collective_id):
    hidden, _, lows, _, output_low, attended, normed = operands[:7]
    _, places, piece, group = operands[9].shape
    feats = normed.shape[1]
    n_units, n_head = hidden.shape[0], attended.shape[0]
    wide = n_units
    rows = 8 * feats
    depth = max(16, LATE_CHUNK // wide)
    count = rows // depth
    vmem, dma = pltpu.VMEM, pltpu.SemaphoreType.DMA
    block = (STREAMS, places, piece, group)
    outs = [
        jax.ShapeDtypeStruct((2, count, depth, wide), low),
        jax.ShapeDtypeStruct(block, low),
        jax.ShapeDtypeStruct((STREAMS, places, piece, 1), full),
    ]
    any_space, vmem_space = pl.BlockSpec(memory_space=pl.ANY), pl.BlockSpec(memory_space=vmem)
    total, split, gain_parts = pl.pallas_call(
        functools.partial(late_kernel, (places, piece, group, n_head, n_units)),
        out_shape=outs,
        in_specs=[any_space] * len(operands) + [vmem_space] * len(tables),
        out_specs=[any_space, any_space, vmem_space],
        scratch_shapes=[
            vmem((4 * n_units, group), low),
            vmem((3, 4 * n_head, group), low),
            vmem(output_low.shape, low),
            vmem(attended.shape, low),
            vmem(normed.shape, low),
            vmem(operands[7].shape, low),
            vmem(operands[8].shape, low),
            vmem(block, low),
            vmem(block[1:], full),
            vmem(block, full),
            vmem(block, low),
            vmem(block, low),
            vmem(block, low),
            vmem((8, STREAMS, 2, group), full),
            vmem((STREAMS, 2, group), full),
            vmem((LATE_TILE, wide), full),
            vmem((feats, group), full),
            vmem((count, depth, wide), low),
            dma((3, 11)),
            dma((4,)),
            dma((4,)),
            dma,
            dma((STREAMS,)),
            dma,
            dma,
            dma,
            dma,
            dma,
        ]
        + chain_semaphores(count),
        compiler_params=pltpu.CompilerParams(
            collective_id=collective_id, has_side_effects=True, vmem_limit_bytes=63 << 20
        ),
        cost_estimate=pl.CostEstimate(
            flops=4 * rows * wide * group, bytes_accessed=900 << 20, transcendentals=0
        ),
    )(*operands, *tables)
    return total.reshape(2, 8, feats, wide), split, gain_parts


def chain_sums(operands, blocks, collective_id):
    groups, held, size = [[]], set(), 0
    for rows, segments in blocks:
        used = {n for seg in segments for n in (seg[0], seg[2])}
        more = sum(2 * operands[n].size for n in used - held)
        more += 4 * rows * sum(seg[4] for seg in segments)
        if groups[-1] and size + more > VMEM:
            groups.append([])
            held, size = set(), 0
            more = sum(2 * operands[n].size for n in used)
            more += 4 * rows * sum(seg[4] for seg in segments)
        groups[-1].append((rows, segments))
        held |= used
        size += more
    totals = []
    for i, group in enumerate(groups):
        used = sorted({n for _, segments in group for seg in segments for n in (seg[0], seg[2])})
        place = {n: k for k, n in enumerate(used)}
        own = [
            (rows, [(place[a], b, place[c], d, e) for a, b, c, d, e in segments])
            for rows, segments in group
        ]
        total = chain_sum([operands[n] for n in used], own, collective_id + i)
        totals.append(total.reshape(total.shape[0], -1, total.shape[3]))
    return totals[0] if len(totals) == 1 else jnp.concatenate(totals, axis=1)


def assemble_kernel(ways, dp, fused, own_ref, *refs):
    halves, (up_ref, *head_refs, out_ref) = refs[:ways], refs[ways:]
    rows, wide = own_ref.shape[2:]
    size = up_ref.shape[1] // dp // ways
    blocks = dp * size // wide
    own = wide // dp
    feats = out_ref.shape[1] // dp
    for d in range(dp):
        turn = turn_of(d)
        for w in range(ways):
            start = turn * size
            lanes = pl.ds(pl.multiple_of(start % wide, size), size)
            place = (d * ways + w) * size
            up_block = 1 + turn // 2 + turn % 2 * 2 if fused else start // wide
            up_ref[:, place : place + size] = own_ref[w, up_block, :, lanes].astype(full)
            for s, ref in enumerate(head_refs):
                lanes = pl.ds(pl.multiple_of(turn * own, own), own)
                place = (d * ways + w) * own
                ref[:, place : place + own] = own_ref[w, blocks + s + fused, :, lanes].astype(full)
        start = turn * feats
        lanes = pl.ds(pl.multiple_of(start % wide, feats), feats)
        for w in range(ways):

            @pl.when(start // wide == w)
            def _(w=w, d=d, lanes=lanes):
                out_ref[:, d * feats : (d + 1) * feats] = halves[w][0, 0, :, lanes].astype(full)


def assemble(total, w_up, fused):
    ways, dp = split_ways(), lax.axis_size("dp")
    blocks, rows, wide = total.shape[1:]
    depth = min(64, rows // ways)
    share = rows // ways // depth

    def half_map(half):
        return lambda i: (i // share, 0 if fused else blocks - 1, half * share + i % share, 0)

    widths = [w_up.shape[1]] + [ways * wide] * 4
    return pl.pallas_call(
        functools.partial(assemble_kernel, ways, dp, int(fused)),
        grid=(rows // depth,),
        out_shape=[jax.ShapeDtypeStruct((rows, n), full) for n in widths],
        in_specs=[pl.BlockSpec((ways, blocks, depth, wide), lambda i: (0, 0, i, 0))]
        + [pl.BlockSpec((1, 1, depth, wide), half_map(half)) for half in range(ways)],
        out_specs=[pl.BlockSpec((depth, n), lambda i: (i, 0)) for n in widths],
        compiler_params=pltpu.CompilerParams(vmem_limit_bytes=48 << 20),
        cost_estimate=pl.CostEstimate(
            flops=0, bytes_accessed=6 * total.size, transcendentals=0
        ),
    )(total, *[total] * ways)


def unturn_kernel(dp, own_ref, out_ref):
    size = out_ref.shape[1] // dp
    for d in range(dp):
        lanes = pl.ds(pl.multiple_of(turn_of(d) * size, size), size)
        out_ref[:, d * size : (d + 1) * size] = own_ref[:, lanes].astype(full)


def unturn(total):
    rows, columns = total.shape
    depth = 256
    return pl.pallas_call(
        functools.partial(unturn_kernel, lax.axis_size("dp")),
        grid=(rows // depth,),
        out_shape=jax.ShapeDtypeStruct((rows, columns), full),
        in_specs=[pl.BlockSpec((depth, columns), lambda i: (i, 0))],
        out_specs=pl.BlockSpec((depth, columns), lambda i: (i, 0)),
        cost_estimate=pl.CostEstimate(
            flops=0, bytes_accessed=6 * total.size, transcendentals=0
        ),
    )(total)


def history_kernel(split_ref, stored_ref, mix_ref, grad_ref, parts_ref):
    streams = [split_ref[s, 0].astype(full) for s in range(STREAMS)]
    rows = [None] * (STREAMS * HIST)
    for j in range(HIST):
        layer = stored_ref[j].astype(full)
        total = mix_ref[j : j + 1, :] * streams[0]
        for s in range(1, STREAMS):
            total = total + mix_ref[s * HIST + j : s * HIST + j + 1, :] * streams[s]
        grad_ref[j] = total
        for s in range(STREAMS):
            rows[s * HIST + j] = jnp.sum(streams[s] * layer, axis=0, keepdims=True)
    parts = jnp.concatenate(rows, axis=0)
    block = parts_ref.shape[2]
    for b in range(parts_ref.shape[0]):
        parts_ref[b] = parts[:, b * block : (b + 1) * block]


def history_gradients(split, stored, mix_all, block):
    _, places, piece, group = split.shape
    n_mix, tokens = mix_all.shape
    wide = min(512, group)
    per_place = group // wide
    return pl.pallas_call(
        history_kernel,
        grid=(tokens // wide,),
        out_shape=[
            jax.ShapeDtypeStruct((HIST, piece, tokens), full),
            jax.ShapeDtypeStruct((tokens // block, n_mix, block), full),
        ],
        in_specs=[
            pl.BlockSpec((STREAMS, 1, piece, wide), lambda i: (0, i // per_place, 0, i % per_place)),
            pl.BlockSpec((HIST, piece, wide), lambda i: (0, 0, i)),
            pl.BlockSpec((n_mix, wide), lambda i: (0, i)),
        ],
        out_specs=[
            pl.BlockSpec((HIST, piece, wide), lambda i: (0, 0, i)),
            pl.BlockSpec((wide // block, n_mix, block), lambda i: (i, 0, 0)),
        ],
        compiler_params=pltpu.CompilerParams(vmem_limit_bytes=40 << 20),
        cost_estimate=pl.CostEstimate(
            flops=4 * STREAMS * HIST * piece * tokens,
            bytes_accessed=6 * HIST * piece * tokens + 2 * split.size,
            transcendentals=0,
        ),
    )(split, stored, mix_all)


def to_owner(values_in):
    dp, hid, ways = lax.axis_size("dp"), lax.axis_size("hid"), split_ways()
    index = lax.axis_index("dp") * ways + lax.axis_index("hid") % ways
    mine = lax.dynamic_index_in_dim(values_in, index, 1, keepdims=False)
    pairs = [
        (d * hid + t * ways + w, (t * dp + d) * ways + w)
        for d in range(dp)
        for t in range(hid // ways)
        for w in range(ways)
    ]
    return lax.ppermute(mine, ("dp", "hid"), pairs)


def rotate(values_in, cosine, sine):
    half = cosine.shape[1]
    front, back = values_in[:, :half], values_in[:, half : 2 * half]
    return jnp.concatenate(
        [
            front * cosine - back * sine,
            back * cosine + front * sine,
            values_in[:, 2 * half :],
        ],
        axis=1,
    )


def local(
    history,
    mix,
    segment_ids,
    norm_gains,
    w_query,
    w_key,
    w_value,
    w_out,
    w_up,
    w_down,
    w_mixer,
    mixer_out,
    mix_static,
    out_cotangent,
    mix_cotangent,
):
    dp, hid, ways = lax.axis_size("dp"), lax.axis_size("hid"), split_ways()
    places = hid // ways
    my_hid = lax.axis_index("hid")
    place, way = my_hid // ways, my_hid % ways
    block = segment_ids.shape[0]
    total_tokens = block * dp * hid
    row = total_tokens // dp
    group = total_tokens // places
    rows = group // row
    piece = history.shape[2]
    mine = piece * places
    feats = piece * hid
    width = feats * dp
    heads = HEADS // dp // ways
    n_mix = mix.shape[1]
    n_cot = mix_cotangent.shape[1]

    def by_place(values_in):
        return jnp.stack(
            [values_in[..., p * group : (p + 1) * group] for p in range(places)], axis=0
        )

    stored = history.swapaxes(1, 2)
    mix_all = gather_all(mix.T)
    fused = dp == 4 and ways == 2 and rows == 1
    if fused:
        parts = norm_gains.astype(full).T.reshape(STREAMS, places, ways, piece)
        gain_tables = (
            lax.dynamic_index_in_dim(parts, way, 2, keepdims=False)[..., None],
            parts.reshape(STREAMS, places, ways * piece, 1),
        )
        mix_all, gain_tables = lax.optimization_barrier((mix_all, gain_tables))
    own_means, own_devs, deviations = [], [], []
    for s in range(STREAMS):
        total = mix_all[s * HIST] * stored[0].astype(full)
        for j in range(1, HIST):
            total = total + mix_all[s * HIST + j] * stored[j].astype(full)
        own_means.append(jnp.mean(total, axis=0))
        off = total - own_means[s]
        own_devs.append(jnp.sum(off * off, axis=0))
        deviations.append(off.astype(low))
    moments = by_place(jnp.stack(own_means + own_devs, axis=0))
    deviations = by_place(jnp.stack(deviations, axis=0))

    table = jnp.concatenate([mix_cotangent.T, segment_ids.astype(full)[None]], axis=0)
    table = lax.dynamic_slice_in_dim(gather_all(table), place * group, group, 1)
    cot_t = table[:n_cot]
    ids = table[-1].reshape(rows, row)

    there = jnp.arange(row, dtype=jnp.int32)
    same_doc = ids[:, :, None] == ids[:, None, :]
    doc_start = jnp.min(jnp.where(same_doc, there[None, None], row), axis=2)
    position = (there[None] - doc_start).astype(full).reshape(group)
    visible = same_doc & (there[None, None] <= there[None, :, None])
    frequency = rope_base ** (-jnp.arange(ROT // 2, dtype=full) * 2.0 / ROT)
    angle = frequency[:, None] * position[None, :]
    cosine, sine = jnp.cos(angle)[None], jnp.sin(angle)[None]

    def own_rows(values_in):
        parts = values_in.reshape((places, ways, piece) + values_in.shape[1:])
        part = lax.dynamic_index_in_dim(parts, way, 1, keepdims=False)
        return part.reshape((mine,) + values_in.shape[1:])

    def all_rows(values_in):
        parts = values_in.reshape((places, piece) + values_in.shape[1:])
        return gather_ways(parts, 1).reshape((feats,) + values_in.shape[1:])

    own_gains = own_rows(norm_gains).astype(full)
    gains = [own_gains[:, s][:, None] for s in range(STREAMS)]
    all_gains = norm_gains.astype(full)

    def project(weight, left):
        columns = weight.shape[1] // dp // ways

        def make(index):
            start = (index * ways + way) * columns
            part = lax.dynamic_slice_in_dim(weight, start, columns, 1)
            return contract(part, left, 0, 0)

        return scatter_dp(make)

    def way_columns(weight):
        if ways == 1:
            return weight
        size = weight.shape[1] // dp // ways
        parts = [weight[:, i * size : (i + 1) * size] for i in range(dp * ways)]
        pairs = zip(parts[::2], parts[1::2])
        return jnp.concatenate([jnp.where(way == 0, a, b) for a, b in pairs], axis=1)

    def way_rows(weight):
        size = weight.shape[0] // ways
        return lax.dynamic_slice_in_dim(weight, way * size, size, 0)

    def by_head(values_in):
        return values_in.reshape(heads, HEAD, group)

    def turned(weight, stride, offset, size):
        starts = [turn_source(turn) * stride + offset for turn in range(dp)]
        parts = [lax.dynamic_slice_in_dim(weight, start, size, 1) for start in starts]
        return jnp.concatenate(parts, axis=1)

    n_head = heads * HEAD
    n_units = w_up.shape[1] // dp // ways
    if fused:
        normed, deviations, residual, own_shifts, inv_scales, active, slope, products, *ends = (
            forward_projections(
                deviations,
                moments,
                norm_gains,
                w_query,
                w_key,
                w_value,
                w_up,
                by_place(out_cotangent.T),
            )
        )
        turned_heads, turned_up, upstream = ends
        upstream = upstream.reshape(mine, group)
        normed_all = normed
        normed = [normed[s] for s in range(STREAMS)]
        products = products.reshape(3, heads, HEAD, group)
        turned_weights = [turned_heads[s] for s in range(3)] + [turned_up]
    else:
        moments = exchange(moments)
        deviations = exchange(deviations)
        deviations = [deviations[:, s] for s in range(STREAMS)]
        def join_moments(mean_parts, dev_parts, size):
            mean = jnp.mean(mean_parts, axis=0)
            spread = size * jnp.sum(jnp.square(mean_parts - mean), axis=0)
            return mean, jnp.sum(dev_parts, axis=0) + spread

        block_means = moments[:, :STREAMS]
        joined = join_moments(block_means, moments[:, STREAMS:], piece)
        joined = gather_dp(gather_ways(jnp.concatenate(joined, axis=0), 0))
        joined = joined.reshape((dp * ways,) + joined.shape[2:])
        means, variance = join_moments(joined[:, :STREAMS], joined[:, STREAMS:], mine)
        inv_scales = lax.rsqrt(variance / width + 1e-05)
        all_means = gather_ways(block_means, 1)

        def unit(values_in, block_mean, s):
            return (values_in.astype(full) + (block_mean - means[s])[..., None, :]) * inv_scales[s]

        units = [
            unit(deviations[s], block_means[:, s], s).reshape(mine, group) for s in range(STREAMS)
        ]
        normed = []
        for s in range(STREAMS):
            both = unit(gather_ways(deviations[s], 1), all_means[:, :, s], s).reshape(feats, group)
            normed.append((both * all_gains[:, s][:, None]).astype(low))
        residual = (deviations[3].astype(full) + block_means[:, 3][:, None]).reshape(mine, group)
        products = [
            by_head(project(w, normed[s])) for s, w in enumerate((w_query, w_key, w_value))
        ]
        hidden = project(w_up, normed[3])
        active, hidden_pull = jax.vjp(gelu_exact, hidden)
        active = active.astype(low)
        (slope,) = hidden_pull(jnp.ones_like(hidden))
        turned_weights = [
            turned(w, ways * n_head, way * n_head, n_head) for w in (w_query, w_key, w_value)
        ] + [turned(w_up, ways * n_units, way * n_units, n_units)]

    def by_row(values_in):
        if rows == 1:
            return values_in
        return (
            values_in.reshape(heads, HEAD, rows, row)
            .transpose(0, 2, 1, 3)
            .reshape(heads * rows, HEAD, row)
        )

    def from_row(values_in):
        if rows == 1:
            return values_in
        return (
            values_in.reshape(heads, rows, HEAD, row)
            .transpose(0, 2, 1, 3)
            .reshape(heads, HEAD, group)
        )

    if fused:
        starts = doc_start.reshape(1, group)
        turned_values, attended, tops = attend(products, cosine[0], sine[0], starts)
        attended = attended.reshape(n_head, group)
    else:
        queries = rotate(products[0], cosine, sine).astype(low)
        keys = rotate(products[1], cosine, sine).astype(low)
        values = products[2].astype(low)
        q_rows, k_rows, v_rows = by_row(queries), by_row(keys), by_row(values)
        score_scale = 1.0 / math.sqrt(HEAD)
        scores = batched(q_rows, k_rows, 1, 1) * score_scale
        mask = jnp.broadcast_to(visible[None], (heads, rows, row, row)).reshape(scores.shape)
        scores = jnp.where(mask, scores, -1e30)
        probs = jax.nn.softmax(scores, axis=-1)
        probs_low = probs.astype(low)
        attended = from_row(batched(v_rows, probs_low, 2, 2).astype(low)).reshape(heads * HEAD, group)

        cotangent, attended = lax.optimization_barrier((out_cotangent, attended))
        upstream = exchange(by_place(cotangent.T)).reshape(mine, group)

    mixer_rows = own_rows(w_mixer)
    if fused:
        output, output_rounded, sums, *turned_ends = add_branches(
            places, attended, active, residual, mixer_rows, w_out, w_down
        )
        sums = jnp.concatenate([sums[: mixer_rows.shape[1]], sums[-1:]], axis=0)
        turned_weights += turned_ends
    else:
        out_rows, down_rows = way_rows(w_out), way_rows(w_down)
        turned_weights += [turned(out_rows, feats, 0, feats), turned(down_rows, feats, 0, feats)]
        def make_out(index):
            start = index * feats
            left = lax.dynamic_slice_in_dim(out_rows, start, feats, 1)
            other = lax.dynamic_slice_in_dim(down_rows, start, feats, 1)
            return contract(left, attended, 0, 0) + contract(other, active, 0, 0)

        branches = scatter_dp(make_out).reshape(places, ways, piece, group)
        kept = lax.dynamic_index_in_dim(branches, way, 1, keepdims=False)
        if ways == 2:
            given = lax.dynamic_index_in_dim(branches, 1 - way, 1, keepdims=False).astype(low)
            kept = kept + hid_swap(given, 1).astype(full)
        output = residual + kept.reshape(mine, group)
        output, upstream, turned_weights = lax.optimization_barrier(
            (output, upstream, turned_weights)
        )
        output_rounded = output.astype(low)
        square = jnp.sum(output * output, axis=0, keepdims=True)
        mixer_part = contract(mixer_rows, output_rounded, 0, 0)
        sums = sum_features(jnp.concatenate([mixer_part, square], axis=0))
    upstream = upstream.astype(full)

    block_output = exchange(output_rounded.reshape(places, piece, group))

    inv_rms = lax.rsqrt(sums[-1] / width + 1e-06)
    inner_raw = sums[:-1]
    inner_pre = inner_raw * inv_rms
    inner_act, inner_pull = jax.vjp(gelu_exact, inner_pre)
    raw_mix = contract_high(mixer_out, inner_act, 0, 0)
    column = jnp.stack(
        [
            jnp.sum(raw_mix, axis=1),
            jnp.sum(raw_mix * raw_mix, axis=1),
            jnp.sum(cot_t, axis=1),
            jnp.sum(cot_t * raw_mix, axis=1),
        ],
        axis=0,
    )
    act_total = jnp.sum(inner_act, axis=1)
    act_cot = contract_high(inner_act, cot_t, 1, 1)
    act_raw = contract_high(inner_act, raw_mix, 1, 1)
    n_inner = act_total.shape[0]
    flat = sum_tokens(
        jnp.concatenate([column.reshape(-1), act_total, act_cot.reshape(-1), act_raw.reshape(-1)])
    )
    sum_raw, sum_square, sum_grad, sum_grad_raw = flat[: 4 * n_cot].reshape(4, n_cot)
    start = 4 * n_cot
    act_total = flat[start : start + n_inner]
    start += n_inner
    act_cot = flat[start : start + n_inner * n_cot].reshape(n_inner, n_cot)
    start += n_inner * n_cot
    act_raw = flat[start:].reshape(n_inner, n_cot)
    average = sum_raw / total_tokens
    variance_mix = sum_square / total_tokens - average * average
    inv_spread = lax.rsqrt(variance_mix + 1e-05)
    unit_mix = (raw_mix - average[:, None]) * inv_spread[:, None]
    mix_next = mix_static[:, None] + unit_mix
    mix_next = to_owner(mix_next.reshape(n_cot, dp * ways, block)).T
    mean_grad = sum_grad / total_tokens
    sum_grad_unit = inv_spread * (sum_grad_raw - average * sum_grad)
    mean_grad_unit = sum_grad_unit / total_tokens
    raw_grad = inv_spread[:, None] * (
        cot_t - mean_grad[:, None] - unit_mix * mean_grad_unit[:, None]
    )
    act_unit = inv_spread[None, :] * (act_raw - act_total[:, None] * average[None, :])
    mixer_out_grad = inv_spread[None, :] * (
        act_cot - act_total[:, None] * mean_grad[None, :] - act_unit * mean_grad_unit[None, :]
    )
    act_grad = contract_high(mixer_out, raw_grad, 1, 0)
    inner_low = inner_pull(act_grad)[0].astype(low)
    scaled = (output * inv_rms).astype(low)
    mixer_grad_part = contract(inner_low, scaled, 1, 1)
    scaled_grad = contract(mixer_rows, inner_low, 1, 0)
    along = jnp.sum(inner_low.astype(full) * inner_raw, axis=0) / width
    output_grad = upstream + inv_rms * scaled_grad - output * (inv_rms * inv_rms * inv_rms) * along
    if fused:
        near = output_grad.astype(low)
        far = outer_shift(near, 1)
        beside = hid_swap(near, 1)
        far_beside = outer_shift(beside, 1)

        def interleave(values_in, other):
            values_in, other = [v.reshape(places, piece, group) for v in (values_in, other)]
            return ordered(way == 0, values_in, other, 1).reshape(feats, group)

        output_lows = gather_cores([interleave(near, beside), interleave(far, far_beside)])
    else:
        output_lows = gather_turns(all_rows(output_grad.astype(low)))

    output_low = jnp.concatenate(output_lows, axis=0)

    hidden_low = (contract(turned_weights[5], output_low, 1, 0) * slope).astype(low)

    attended_grad = contract(turned_weights[4], output_low, 1, 0).astype(low)
    if fused:
        lows_mine = attend_back(
            turned_values, by_head(attended_grad), cosine[0], sine[0], starts, tops
        ).reshape(3 * n_head, group)
    else:
        a_rows = by_row(by_head(attended_grad))
        prob_grad = batched(a_rows, v_rows, 1, 1)
        row_total = jnp.sum(probs * prob_grad, axis=-1, keepdims=True)
        score_grad = (probs * (prob_grad - row_total)).astype(low)
        query_grad = from_row(batched(k_rows, score_grad, 2, 2) * score_scale)
        key_grad = from_row(batched(q_rows, score_grad, 2, 1) * score_scale)
        value_grad = from_row(batched(a_rows, probs_low, 2, 1))
        query_low = rotate(query_grad, cosine, -sine).astype(low).reshape(heads * HEAD, group)
        key_low = rotate(key_grad, cosine, -sine).astype(low).reshape(heads * HEAD, group)
        value_low = value_grad.astype(low).reshape(heads * HEAD, group)

        lows_mine = jnp.concatenate([query_low, key_low, value_low], axis=0)
    active_kept, hidden_low, lows_mine = lax.optimization_barrier((active, hidden_low, lows_mine))
    hidden_lows, lows = gather_outer(hidden_low), gather_outer(lows_mine)
    blocks = [(active.shape[0], [(0, 0, 1, 0, width)])]
    branch_sum = chain_sum([active_kept, output_low], blocks, 0)
    branch_sum, block_output, hidden_lows, lows = lax.optimization_barrier(
        (branch_sum, block_output, hidden_lows, lows)
    )
    block_output = block_output.transpose(1, 0, 2).reshape(piece, total_tokens).T

    if fused:
        operands = [hidden_lows[0], hidden_lows[1], lows[0], lows[1], output_low, attended]
        operands += [normed_all, turned_heads, turned_up, deviations]
        operands.append(output_grad.reshape(places, piece, group))
        tables = [
            own_shifts,
            inv_scales,
            *gain_tables,
        ]
        late_sum, split, gain_parts = late_sums(operands, tables, 1)
        gain_parts = gain_parts.reshape(STREAMS, mine)
        history_grad, mix_parts = history_gradients(split, stored, mix_all, block)
    else:
        hidden_lows, lows = gather_cores(hidden_lows), gather_cores(lows)

        normed_grads, alongs, rights = [], [], []
        for s in range(STREAMS):
            if s < 3:
                right = jnp.concatenate([v[s * n_head : (s + 1) * n_head] for v in lows], axis=0)
            else:
                right = jnp.concatenate(hidden_lows, axis=0)
            rights.append(right)
            part = contract(turned_weights[s], right, 1, 0)
            alongs.append(jnp.sum(part * all_gains[:, s][:, None], axis=0))
            alongs.append(jnp.sum(part * normed[s].astype(full), axis=0))
            part = part.reshape(places, ways, piece, group)
            kept = lax.dynamic_index_in_dim(part, way, 1, keepdims=False)
            if ways == 2:
                given = lax.dynamic_index_in_dim(part, 1 - way, 1, keepdims=False).astype(low)
                kept = kept + hid_swap(given, 1).astype(full)
            normed_grads.append(kept.reshape(mine, group))
        weighted = [normed_grads[s] * gains[s] for s in range(STREAMS)]
        means_back = sum_features(jnp.stack(alongs, axis=0)) / width
        gain_parts = [jnp.sum(g * u, axis=1) for g, u in zip(normed_grads, units)]
        stream_grads = [
            (weighted[s] - means_back[2 * s] - units[s] * means_back[2 * s + 1]) * inv_scales[s]
            for s in range(STREAMS)
        ]
        stream_grads[3] = stream_grads[3] + output_grad
        gain_parts = jnp.stack(gain_parts, axis=0)

        split = jnp.stack([v.astype(low).reshape(places, piece, group) for v in stream_grads], axis=1)
        attended, split = lax.optimization_barrier((attended, split))
        split = exchange(split)
        wide = w_query.shape[1] // ways
        operands = [rights[3]] + rights[:3] + [output_low, normed[3]] + normed[:3] + [attended]
        blocks = [(feats, [(5, 0, 0, i, wide)]) for i in range(0, rights[3].shape[0], wide)]
        blocks += [(feats, [(6 + s, 0, 1 + s, 0, wide)]) for s in range(3)]
        blocks += [(n_head, [(9, 0, 4, i, wide)]) for i in range(0, width, wide)]
        late_sum = chain_sums(operands, blocks, 1).reshape(ways, -1, feats, wide)
        split = jnp.concatenate([split[p] for p in range(places)], axis=-1).astype(full)
        mix_layers = mix_all.reshape(STREAMS, HIST, total_tokens)
        history_grad = sum(mix_layers[s][:, None] * split[s][None] for s in range(STREAMS))
        mix_parts = jnp.concatenate(
            [jnp.sum(split[s][None] * stored.astype(full), axis=1) for s in range(STREAMS)], axis=0
        )
        mix_parts = mix_parts.reshape(n_mix, dp * hid, block).transpose(1, 0, 2)

    history_grad = history_grad.swapaxes(1, 2)
    smalls = jnp.concatenate([mixer_grad_part, gain_parts], axis=0)
    late_sum, mix_parts, smalls = lax.optimization_barrier((late_sum, mix_parts, smalls))
    mix_parts = lax.all_to_all(mix_parts, ("dp", "hid"), split_axis=0, concat_axis=0, tiled=True)
    late_grads = assemble(late_sum, w_up, fused)
    w_down_grad = unturn(branch_sum.reshape(w_down.shape))
    bit = ways
    while bit < hid:
        smalls = smalls + hid_swap(smalls, bit)
        if bit == ways:
            late_grads, smalls = lax.optimization_barrier((late_grads, smalls))
        else:
            w_down_grad, smalls = lax.optimization_barrier((w_down_grad, smalls))
        bit *= 2
    w_up_grad, w_query_grad, w_key_grad, w_value_grad, w_out_grad = late_grads
    smalls = gather_ways(smalls.reshape(-1, places, piece), 2).reshape(-1, feats)
    w_mixer_grad = smalls[:n_inner].T
    norm_gains_grad = smalls[n_inner:].T
    mix_grad = jnp.sum(mix_parts, axis=0).T

    return (
        block_output,
        mix_next,
        history_grad,
        mix_grad,
        norm_gains_grad,
        w_query_grad,
        w_key_grad,
        w_value_grad,
        w_out_grad,
        w_up_grad,
        w_down_grad,
        w_mixer_grad,
        mixer_out_grad,
        sum_grad,
    )


def solution(mesh):
    everywhere = ("dp", "hid")
    placed = (
        P(None, None, everywhere),
        P(everywhere, None),
        P(everywhere),
        P("dp", None),
        P("dp", None),
        P("dp", None),
        P("dp", None),
        P("dp", None),
        P("dp", None),
        P("dp", None),
        P("dp", None),
        P(),
        P(),
        P(None, everywhere),
        P(everywhere, None),
    )
    return jax.shard_map(
        local,
        mesh=mesh,
        in_specs=placed,
        out_specs=(
            P(None, everywhere),
            P(everywhere, None),
            P(None, None, everywhere),
            P(everywhere, None),
            P("dp", None),
            P("dp", None),
            P("dp", None),
            P("dp", None),
            P("dp", None),
            P("dp", None),
            P("dp", None),
            P("dp", None),
            P(),
            P(),
        ),
        check_vma=False,
    )
```

```python
import functools
import math

import jax
import jax.numpy as jnp
from jax import lax
from jax.experimental import pallas as pl
from jax.experimental.pallas import tpu as pltpu
from jax.sharding import PartitionSpec as P

HEADS = 16
HEAD = 128
ROT = 32
HIST = 8
STREAMS = 4
CORES = 2
CHUNK = 1 << 15
SLACK = 6
TILE = 128
LATE_TILE = 256
LATE_CHUNK = 1 << 16
LATE_SLACK = 4
SPAN = 256
VMEM = 52 << 20
PULL_START = 2
PULL_GAP = 4
GRAD_GAP = 2

highest = lax.Precision.HIGHEST
rope_base = 10000.0
low = jnp.bfloat16
full = jnp.float32


def contract(left, right, left_dim, right_dim):
    return lax.dot_general(
        left, right, (((left_dim,), (right_dim,)), ((), ())), preferred_element_type=full
    )


def contract_high(left, right, left_dim, right_dim):
    return lax.dot_general(
        left,
        right,
        (((left_dim,), (right_dim,)), ((), ())),
        precision=highest,
        preferred_element_type=full,
    )


def batched(left, right, left_dim, right_dim):
    return lax.dot_general(
        left, right, (((left_dim,), (right_dim,)), ((0,), (0,))), preferred_element_type=full
    )


def gelu_exact(values_in):
    return jax.nn.gelu(values_in, approximate=False)


def core_swap(values_in):
    size = lax.axis_size("dp")
    return lax.ppermute(values_in, "dp", [(i, i ^ 1) for i in range(size)])


def outer_shift(values_in, step):
    size = lax.axis_size("dp")
    outer = size // CORES
    pairs = [
        (o * CORES + c, ((o + step) % outer) * CORES + c) for o in range(outer) for c in range(CORES)
    ]
    return lax.ppermute(values_in, "dp", pairs)


def hid_swap(values_in, bit):
    size = lax.axis_size("hid")
    return lax.ppermute(values_in, "hid", [(i, i ^ bit) for i in range(size)])


def ordered(first, values_in, other, axis):
    return jnp.stack(
        [jnp.where(first, values_in, other), jnp.where(first, other, values_in)], axis=axis
    )


def take(values_in, index):
    return lax.dynamic_index_in_dim(values_in, index, 0, keepdims=False)


def put(target, values_in, index):
    return lax.dynamic_update_index_in_dim(target, values_in, index, 0)


def split_ways():
    return 2 if HEADS // lax.axis_size("dp") >= 2 else 1


def gather_ways(values_in, axis):
    if split_ways() == 1:
        return jnp.expand_dims(values_in, axis)
    return ordered(lax.axis_index("hid") % 2 == 0, values_in, hid_swap(values_in, 1), axis)


def gather_dp(values_in):
    size = lax.axis_size("dp")
    outer = size // CORES
    me = lax.axis_index("dp")
    mine, core = me // CORES, me % CORES
    if outer == 2:
        held = ordered(mine == 0, values_in, outer_shift(values_in, 1), 0)
    else:
        held = jnp.zeros((outer,) + values_in.shape, values_in.dtype)
        held = put(held, values_in, mine)
        for step in range(1, outer):
            held = put(held, outer_shift(values_in, step), (mine - step) % outer)
    pair = ordered(core == 0, held, core_swap(held), 1)
    return pair.reshape((size,) + values_in.shape)


def gather_outer(values_in):
    steps = range(1, lax.axis_size("dp") // CORES)
    return [values_in] + [outer_shift(values_in, step) for step in steps]


def gather_cores(held):
    return [v for h in held for v in (h, core_swap(h))]


def gather_turns(values_in):
    return gather_cores(gather_outer(values_in))


def turn_source(turn):
    outer, me = lax.axis_size("dp") // CORES, lax.axis_index("dp")
    there = (me // CORES + outer - turn // CORES) % outer
    return there * CORES + (me + turn) % CORES


def turn_of(index):
    outer, me = lax.axis_size("dp") // CORES, lax.axis_index("dp")
    step = (me // CORES + outer - index // CORES) % outer
    return step * CORES + (me + index) % CORES


def sum_features(values_in):
    if split_ways() == 2:
        values_in = values_in + hid_swap(values_in, 1)
    parts = gather_dp(values_in)
    total = parts[0]
    for i in range(1, parts.shape[0]):
        total = total + parts[i]
    return total


def sum_tokens(values_in):
    size = lax.axis_size("hid")
    ways = split_ways()
    places = size // ways
    mine = lax.axis_index("hid") // ways
    held = put(jnp.zeros((places,) + values_in.shape, values_in.dtype), values_in, mine)
    for step in range(1, places):
        pairs = [(i, (i + step * ways) % size) for i in range(size)]
        held = put(held, lax.ppermute(values_in, "hid", pairs), (mine + places - step) % places)
    return jnp.sum(held, axis=0)


def gather_all(values_in):
    count = lax.axis_size("dp") * lax.axis_size("hid")
    copies = jnp.broadcast_to(values_in[None], (count,) + values_in.shape)
    held = lax.all_to_all(copies, ("dp", "hid"), split_axis=0, concat_axis=0, tiled=True)
    return held.transpose(1, 0, 2).reshape(values_in.shape[0], -1)


def scatter_dp(make):
    size = lax.axis_size("dp")
    outer = size // CORES
    me = lax.axis_index("dp")
    mine, core = me // CORES, me % CORES
    total = None
    for step in list(range(1, outer)) + [0]:
        there = (mine + step) % outer
        away = core_swap(make(there * CORES + 1 - core).astype(low))
        block = make(there * CORES + core) + away.astype(full)
        if step:
            block = outer_shift(block.astype(low), step).astype(full)
        total = block if total is None else total + block
    return total


def exchange(values_in):
    ways, size = split_ways(), lax.axis_size("hid")
    groups = None
    if ways > 1:
        groups = [[t * ways + w for t in range(size // ways)] for w in range(ways)]
    return lax.all_to_all(
        values_in, "hid", split_axis=0, concat_axis=0, tiled=True, axis_index_groups=groups
    )


def turn_heads(values_in, cosine, sine):
    half = ROT // 2
    front, back = values_in[:half], values_in[half:ROT]
    return jnp.concatenate(
        [front * cosine - back * sine, back * cosine + front * sine, values_in[ROT:]], axis=0
    )


def across(left, right, left_dim, right_dim):
    return lax.dot_general(
        left, right, (((left_dim,), (right_dim,)), ((), ())), preferred_element_type=full
    )


def attend_kernel(
    products_ref, cosine_ref, sine_ref, start_ref, heads_ref, attended_ref, tops_ref
):
    tokens = products_ref.shape[2]
    for s in range(2):
        turned = turn_heads(products_ref[s], cosine_ref[...], sine_ref[...])
        heads_ref[s] = turned.astype(low)
    heads_ref[2] = products_ref[2].astype(low)
    for first in range(0, tokens, SPAN):
        stop = first + SPAN
        span = slice(first, stop)
        scores, top = masked_scores(heads_ref, start_ref, first)
        weights = jnp.exp(scores - top)
        total = jnp.sum(weights, axis=0, keepdims=True)
        weights = (weights / total).astype(low)
        mixed = across(heads_ref[2, :, :stop], weights, 1, 0)
        attended_ref[:, span] = mixed.astype(low)
        tops_ref[0, 0:1, span] = top
        tops_ref[0, 1:2, span] = total


def masked_scores(heads_ref, start_ref, first):
    stop = first + SPAN
    span = slice(first, stop)
    scores = across(heads_ref[1, :, :stop], heads_ref[0, :, span], 0, 0) / math.sqrt(HEAD)
    key = lax.broadcasted_iota(jnp.int32, scores.shape, 0)
    query = lax.broadcasted_iota(jnp.int32, scores.shape, 1) + first
    seen = (key >= start_ref[:, span]) & (key <= query)
    scores = jnp.where(seen, scores, -1e30)
    return scores, jnp.max(scores, axis=0, keepdims=True)


def attend_back_kernel(
    heads_ref, gradient_ref, cosine_ref, sine_ref, start_ref, tops_ref, lows_ref, key_sum, value_sum
):
    tokens = heads_ref.shape[2]
    cosine, sine = cosine_ref[...], sine_ref[...]
    scale = 1.0 / math.sqrt(HEAD)
    key_sum[...] = jnp.zeros_like(key_sum)
    value_sum[...] = jnp.zeros_like(value_sum)
    for first in range(0, tokens, SPAN):
        stop = first + SPAN
        span = slice(first, stop)
        scores, _ = masked_scores(heads_ref, start_ref, first)
        probs = jnp.exp(scores - tops_ref[0, 0:1, span]) / tops_ref[0, 1:2, span]
        gradient = gradient_ref[:, span]
        change = across(heads_ref[2, :, :stop], gradient, 0, 0)
        row_total = jnp.sum(probs * change, axis=0, keepdims=True)
        change = (probs * (change - row_total)).astype(low)
        query = across(heads_ref[1, :, :stop], change, 1, 0) * scale
        lows_ref[0, :, span] = turn_heads(query, cosine[:, span], -sine[:, span]).astype(low)
        key_sum[:, :stop] = key_sum[:, :stop] + across(heads_ref[0, :, span], change, 1, 1) * scale
        value_sum[:, :stop] = value_sum[:, :stop] + across(gradient, probs.astype(low), 1, 1)
    lows_ref[1] = turn_heads(key_sum[...], cosine, -sine).astype(low)
    lows_ref[2] = value_sum[...].astype(low)


def attend(products, cosine, sine, start):
    _, n_heads, head, tokens = products.shape
    per_head = pl.BlockSpec((3, None, head, tokens), lambda h: (0, h, 0, 0))
    table = pl.BlockSpec(cosine.shape, lambda h: (0, 0))
    return pl.pallas_call(
        attend_kernel,
        grid=(n_heads,),
        out_shape=[
            jax.ShapeDtypeStruct(products.shape, low),
            jax.ShapeDtypeStruct((n_heads, head, tokens), low),
            jax.ShapeDtypeStruct((n_heads, 2, tokens), full),
        ],
        in_specs=[per_head, table, table, pl.BlockSpec(start.shape, lambda h: (0, 0))],
        out_specs=[
            per_head,
            pl.BlockSpec((None, head, tokens), lambda h: (h, 0, 0)),
            pl.BlockSpec((1, 2, tokens), lambda h: (h, 0, 0)),
        ],
        compiler_params=pltpu.CompilerParams(vmem_limit_bytes=40 << 20),
        cost_estimate=pl.CostEstimate(
            flops=4 * n_heads * head * tokens * tokens,
            bytes_accessed=10 * products.size,
            transcendentals=n_heads * tokens * tokens,
        ),
    )(products, cosine, sine, start)


def attend_back(heads, gradient, cosine, sine, start, tops):
    _, n_heads, head, tokens = heads.shape
    per_head = pl.BlockSpec((3, None, head, tokens), lambda h: (0, h, 0, 0))
    table = pl.BlockSpec(cosine.shape, lambda h: (0, 0))
    return pl.pallas_call(
        attend_back_kernel,
        grid=(n_heads,),
        out_shape=jax.ShapeDtypeStruct(heads.shape, low),
        in_specs=[
            per_head,
            pl.BlockSpec((None, head, tokens), lambda h: (h, 0, 0)),
            table,
            table,
            pl.BlockSpec(start.shape, lambda h: (0, 0)),
            pl.BlockSpec((1, 2, tokens), lambda h: (h, 0, 0)),
        ],
        out_specs=per_head,
        scratch_shapes=[pltpu.VMEM((head, tokens), full)] * 2,
        compiler_params=pltpu.CompilerParams(vmem_limit_bytes=40 << 20),
        cost_estimate=pl.CostEstimate(
            flops=10 * n_heads * head * tokens * tokens,
            bytes_accessed=6 * heads.size,
            transcendentals=n_heads * tokens * tokens,
        ),
    )(heads, gradient, cosine, sine, start, tops)


def forward_kernel(dims, *refs):
    places, piece, group, n_head, n_units = dims
    (send_ref, mom_ref, gains_ref, query_ref, key_ref, value_ref, up_ref), refs = refs[:7], refs[7:]
    cot_ref, refs = refs[0], refs[1:]
    (
        normed_ref,
        own_ref,
        residual_ref,
        own_shift_ref,
        scale_ref,
        active_ref,
        slope_ref,
        heads_ref,
        turned_ref,
        turned_up_ref,
        cot_out,
    ), refs = refs[:11], refs[11:]
    (
        devs,
        shift_ref,
        moms,
        joins,
        weights,
        core_out,
        core_in,
        outer_out,
        outer_in,
        mom_send,
        mom_recv,
        dev_send,
        dev_recv,
        way_send,
        way_recv,
        pair_send,
        pair_recv,
        join_send,
        join_recv,
        weight_sem,
        turned_sem,
        core_send,
        core_recv,
        outer_send,
        outer_recv,
        cot_send,
        cot_recv,
        cot_own,
    ) = refs
    count = weights.shape[0]
    ups = n_units // n_head
    index, hid = lax.axis_index("dp"), lax.axis_index("hid")
    outer, core = index // 2, index % 2
    place, way = hid // 2, hid % 2
    me = index * 2 + way
    partner = {"hid": hid + 1 - 2 * way}
    core_peer = {"dp": index + 1 - 2 * core}
    outer_peer = {"dp": (index + 2) % 4}

    def peer(k):
        return (place + k) % places

    def z_device(k):
        return {"hid": peer(k) * 2 + way}

    others = [(i, j) for i in range(4) for j in range(2) if i or j]

    def join_device(i, j):
        return {"dp": (index + i) % 4, "hid": place * 2 + (way + j) % 2}

    def weight_copy(unit, t):
        there = (1 - outer if t < 2 else outer) * 2 + (core if t % 2 else 1 - core)
        block = there * 2 + way
        if unit < ups:
            source, start = up_ref, block * n_units + unit * n_head
        else:
            source, start = (query_ref, key_ref, value_ref)[unit - ups], block * n_head
        start = pl.multiple_of(start, n_head)
        return pltpu.make_async_copy(
            source.at[:, pl.ds(start, n_head)], weights.at[unit, t], weight_sem.at[unit]
        )

    for unit in range(count):
        for t in range(4):
            weight_copy(unit, t).start()

    barrier = pltpu.get_barrier_semaphore()

    for k in range(1, places):
        greet(z_device(k))
    for i, j in others:
        greet(join_device(i, j))
    pl.semaphore_wait(barrier, places - 1 + len(others))

    def mom_copy(k, sender, target):
        return remote(
            mom_ref.at[target], moms.at[way, sender], mom_send, mom_recv.at[sender], z_device(k)
        )

    def dev_copy(s, k, sender, target):
        return remote(
            send_ref.at[target, s],
            devs.at[s, way, sender],
            dev_send,
            dev_recv.at[s, sender],
            z_device(k),
        )

    for k in range(1, places):
        mom_copy(k, place, peer(k)).start()
    for s in (3, 0, 1, 2):
        for k in range(1, places):
            dev_copy(s, k, place, peer(k)).start()
    for k in range(1, places):
        remote(cot_ref.at[peer(k)], cot_out.at[place], cot_send, cot_recv, z_device(k)).start()
    pltpu.make_async_copy(cot_ref.at[place], cot_out.at[place], cot_own).start()
    moms[way, place] = mom_ref[place]
    for s in range(STREAMS):
        devs[s, way, place] = send_ref[place, s]

    def way_copy(source, s, q):
        return remote(source, devs.at[s, way, q], way_send, way_recv.at[s], partner)

    def forward(s):
        way_copy(send_ref.at[place, s], s, place).start()
        for k in range(1, places):
            q = peer(k)
            dev_copy(s, k, q, q).wait_recv()
            way_copy(devs.at[s, way, q], s, q).start()

    def join_parts(means, parts, size):
        mean = means[0]
        for m in means[1:]:
            mean = mean + m
        mean = mean / len(means)
        total = parts[0]
        for v in parts[1:]:
            total = total + v
        for m in means:
            total = total + size * (m - mean) * (m - mean)
        return mean, total

    for k in range(1, places):
        mom_copy(k, peer(k), place).wait_recv()
    remote(moms.at[way], moms.at[way], pair_send, pair_recv, partner).start()
    mean, total = join_parts(
        [moms[way, q, :STREAMS, :] for q in range(places)],
        [moms[way, q, STREAMS:, :] for q in range(places)],
        piece,
    )
    joins[me, :STREAMS, :] = mean
    joins[me, STREAMS:, :] = total
    for i, j in others:
        remote(joins.at[me], joins.at[me], join_send, join_recv, join_device(i, j)).start()
    forward(3)
    n_others = len(others)
    remote(
        joins.at[pl.ds(0, n_others)], joins.at[pl.ds(0, n_others)], join_send, join_recv, partner
    ).wait_recv()
    remote(moms.at[way], moms.at[1 - way], pair_send, pair_recv, partner).wait_recv()
    mean, total = join_parts(
        [joins[i, :STREAMS, :] for i in range(n_others + 1)],
        [joins[i, STREAMS:, :] for i in range(n_others + 1)],
        piece * places,
    )
    scale = lax.rsqrt(total / (piece * places * (n_others + 1)) + 1e-05)
    for s in range(STREAMS):
        for q in range(places):
            for w in range(2):
                off = moms[w, q, s : s + 1, :] - mean[s : s + 1]
                shift_ref[s, 2 * q + w : 2 * q + w + 1, :] = off * scale[s : s + 1]
        shift_ref[s, 2 * places : 2 * places + 1, :] = scale[s : s + 1]
        scale_ref[s] = scale[s : s + 1]
        for q in range(places):
            first, second = [shift_ref[s, 2 * q + w : 2 * q + w + 1, :] for w in range(2)]
            own_shift_ref[s, q] = jnp.where(way == 0, first, second)

    def normalize(s):
        remote(devs.at[s, 1 - way], devs.at[s, 1 - way], way_send, way_recv.at[s], partner).wait_recv()
        size = shift_ref[s, 2 * places : 2 * places + 1, :]
        for q in range(places):
            for w in range(2):
                block = 2 * q + w
                rows = slice(block * piece, (block + 1) * piece)
                unit = devs[s, w, q].astype(full) * size + shift_ref[s, block : block + 1, :]
                normed_ref[s, rows, :] = (unit * gains_ref[s, rows, :]).astype(low)

    def core_copy(unit, half):
        return remote(
            core_out.at[unit, half],
            core_in.at[unit, half],
            core_send,
            core_recv.at[unit, half],
            core_peer,
        )

    def outer_copy(unit):
        return remote(
            outer_out.at[unit], outer_in.at[unit], outer_send, outer_recv.at[unit], outer_peer
        )

    def project(unit, carry):
        @pl.when(unit == 0)
        def _():
            normalize(3)
            forward(0)

        for s in (1, 2):

            @pl.when(unit == s)
            def _(s=s):
                forward(s)

        @pl.when(unit >= ups)
        def _():
            normalize(unit - ups)

        stream = jnp.where(unit < ups, 3, unit - ups)
        pltpu.make_async_copy(weights.at[unit], weights.at[unit], weight_sem.at[unit]).wait()

        def product(t):
            return lax.dot_general(
                weights[unit, t],
                normed_ref[stream],
                (((0,), (0,)), ((), ())),
                preferred_element_type=full,
            )

        def stage(k, carry):
            core_out[unit, k] = product(2 * k).astype(low)
            core_copy(unit, k).start()
            kept = product(2 * k + 1)
            core_copy(unit, k).wait_recv()
            kept = kept + core_in[unit, k].astype(full)

            @pl.when(k == 0)
            def _():
                outer_out[unit] = kept.astype(low)
                outer_copy(unit).start()

            @pl.when((k == 1) & (unit < ups))
            def _():
                slope_ref[pl.ds(pl.multiple_of(unit * n_head, n_head), n_head), :] = kept

            @pl.when((k == 1) & (unit >= ups))
            def _():
                heads_ref[unit - ups] = kept

            return carry

        lax.fori_loop(0, 2, stage, 0)
        return carry

    lax.fori_loop(0, count, project, 0)

    def turned_copies():
        for unit in range(count):
            for t in range(4):
                turn = 3 - t
                if unit < ups:
                    start = turn * n_units + unit * n_head
                    target = turned_up_ref.at[:, start : start + n_head]
                else:
                    target = turned_ref.at[unit - ups, :, turn * n_head : (turn + 1) * n_head]
                yield pltpu.make_async_copy(weights.at[unit, t], target, turned_sem)

    for copy in turned_copies():
        copy.start()
    for s in range(STREAMS):
        own_ref[s] = devs[s, way]
    for q in range(places):
        offset = moms[way, q, 3:4, :]
        residual_ref[q * piece : (q + 1) * piece, :] = devs[3, way, q].astype(full) + offset

    step = 32

    def finish_up(unit, carry):
        outer_copy(unit).wait_recv()

        def part(i, carry):
            inner = pl.ds(pl.multiple_of(i * step, step), step)
            rows = pl.ds(pl.multiple_of(unit * n_head + i * step, step), step)
            hidden = slope_ref[rows, :] + outer_in[unit, inner, :].astype(full)
            half = 0.5 + 0.5 * lax.erf(hidden * math.sqrt(0.5))
            active_ref[rows, :] = (hidden * half).astype(low)
            bell = jnp.exp(-0.5 * hidden * hidden) * (1.0 / math.sqrt(2.0 * math.pi))
            slope_ref[rows, :] = half + hidden * bell
            return carry

        return lax.fori_loop(0, n_head // step, part, carry)

    lax.fori_loop(0, ups, finish_up, 0)

    def finish_head(unit, carry):
        outer_copy(unit).wait_recv()
        heads_ref[unit - ups] = heads_ref[unit - ups] + outer_in[unit].astype(full)
        return carry

    lax.fori_loop(ups, count, finish_head, 0)

    def sent(ref, sem):
        remote(ref, ref, sem, join_recv, partner).wait_send()

    sent(moms.at[0, pl.ds(0, places - 1)], mom_send)
    sent(send_ref.at[pl.ds(0, places - 1)], dev_send)
    sent(send_ref, way_send)
    sent(moms.at[0], pair_send)
    sent(joins.at[pl.ds(0, n_others)], join_send)
    sent(core_out, core_send)
    sent(outer_out, outer_send)
    moved = cot_ref.at[pl.ds(0, places - 1)]
    sent(moved, cot_send)
    remote(moved, moved, cot_send, cot_recv, partner).wait_recv()
    pltpu.make_async_copy(cot_ref.at[0], cot_out.at[0], cot_own).wait()
    pltpu.make_async_copy(weights, weights, turned_sem).wait()


def forward_projections(deviations, moments, norm_gains, w_query, w_key, w_value, w_up, cotangent):
    places, _, piece, group = deviations.shape
    feats = norm_gains.shape[0]
    n_head = w_query.shape[1] // 8
    n_units = w_up.shape[1] // 8
    count = n_units // n_head + 3
    vmem, dma = pltpu.VMEM, pltpu.SemaphoreType.DMA
    out_types = [
        ((STREAMS, feats, group), low),
        ((STREAMS, places, piece, group), low),
        ((places * piece, group), full),
        ((STREAMS, places, 1, group), full),
        ((STREAMS, 1, group), full),
        ((n_units, group), low),
        ((n_units, group), full),
        ((3, n_head, group), full),
        ((3, feats, 4 * n_head), low),
        ((feats, 4 * n_units), low),
        (cotangent.shape, low),
    ]
    spaces = [vmem] * 8 + [pl.ANY] * 3
    return pl.pallas_call(
        functools.partial(forward_kernel, (places, piece, group, n_head, n_units)),
        out_shape=[jax.ShapeDtypeStruct(*t) for t in out_types],
        in_specs=[pl.BlockSpec(memory_space=vmem)] * 3 + [pl.BlockSpec(memory_space=pl.ANY)] * 5,
        out_specs=[pl.BlockSpec(memory_space=m) for m in spaces],
        scratch_shapes=[
            vmem((STREAMS, 2, places, piece, group), low),
            vmem((STREAMS, 2 * places + 8, group), full),
            vmem((2, places, 2 * STREAMS, group), full),
            vmem((8, 2 * STREAMS, group), full),
            vmem((count, 4, feats, n_head), low),
            vmem((count, 2, n_head, group), low),
            vmem((count, 2, n_head, group), low),
            vmem((count, n_head, group), low),
            vmem((count, n_head, group), low),
            dma,
            dma((places,)),
            dma,
            dma((STREAMS, places)),
            dma,
            dma((STREAMS,)),
            dma,
            dma,
            dma,
            dma,
            dma((count,)),
            dma,
            dma,
            dma((count, 2)),
            dma,
            dma((count,)),
            dma,
            dma,
            dma,
        ],
        compiler_params=pltpu.CompilerParams(
            collective_id=7, has_side_effects=True, vmem_limit_bytes=62 << 20
        ),
        cost_estimate=pl.CostEstimate(
            flops=8 * count * n_head * feats * group,
            bytes_accessed=300 << 20,
            transcendentals=2 * n_units * group,
        ),
    )(
        deviations,
        moments,
        norm_gains.T.astype(full)[:, :, None],
        w_query,
        w_key,
        w_value,
        w_up,
        cotangent,
    )


def remote(source, target, send, recv, device):
    return pltpu.make_async_remote_copy(
        src_ref=source,
        dst_ref=target,
        send_sem=send,
        recv_sem=recv,
        device_id=device,
        device_id_type=pl.DeviceIdType.MESH,
    )


def greet(device):
    pl.semaphore_signal(
        pltpu.get_barrier_semaphore(),
        inc=1,
        device_id=device,
        device_id_type=pl.DeviceIdType.MESH,
    )


def chain_place(ways, places):
    last = places - 1
    me = lax.axis_index("hid")
    if ways == 2:
        place, way = me // 2, me % 2
        return place, way, me + 2, me - 2, me + 1 - 2 * way
    odd, half = me % 2, places // 2
    place = (1 - odd) * (me // 2) + odd * (last - me // 2)
    turn_up = (place + 1) // half
    turn_down = (place - 1 + places) // half - 2
    above = (1 - turn_up) * 2 * (place + 1) + turn_up * (2 * (last - place - 1) + 1)
    below = (1 - turn_down) * 2 * (place - 1) + turn_down * (2 * (last - place + 1) + 1)
    return place, 0, above, below, me


def chain_semaphores(count):
    dma = pltpu.SemaphoreType.DMA
    return [dma, dma((count,)), dma, dma((count,)), dma, dma, dma, dma, dma((count,))]


def chain_loop(ways, places, out_ref, own, landed, semaphores, compute, slack, hook=None, far=None):
    (
        up_send,
        up_recv,
        down_send,
        down_recv,
        side_send,
        side_recv,
        kept,
        far_send,
        far_recv,
    ) = semaphores
    count, depth = landed.shape[:2]
    per_tile = own.shape[0] // depth
    last = places - 1
    root = last if far is None else places // 2
    place, way, above, below, beside = chain_place(ways, places)
    above, below, beside = {"hid": above}, {"hid": below}, {"hid": beside}

    def send_in(i):
        @pl.when(place < root)
        def _():
            remote(landed.at[i], landed.at[i], up_send, up_recv.at[i], above).start()

        if far is not None:

            @pl.when(place == root + 1)
            def _():
                remote(landed.at[i], far.at[i], up_send, far_recv.at[i], below).start()

            @pl.when(place > root + 1)
            def _():
                remote(landed.at[i], landed.at[i], up_send, up_recv.at[i], below).start()

    def send_out(source, i):
        def to(device, send):
            remote(source, out_ref.at[way, i], send, down_recv.at[i], device).start()

        @pl.when((place <= root) & (place > 0))
        def _():
            to(below, down_send)

        if far is not None:

            @pl.when((place >= root) & (place < last))
            def _():
                to(above, far_send)

        if ways == 2:
            remote(source, out_ref.at[way, i], side_send, side_recv, beside).start()

    def upward(i):
        @pl.when(i % per_tile == 0)
        def _():
            compute(i // per_tile)

        mine = own[pl.ds(pl.multiple_of(i % per_tile * depth, depth), depth), :]
        ends = place == 0 if far is None else (place == 0) | (place == last)

        @pl.when(ends)
        def _():
            landed[i] = mine.astype(low)

        @pl.when(jnp.logical_not(ends))
        def _():
            remote(landed.at[i], landed.at[i], up_send, up_recv.at[i], above).wait_recv()
            total = landed[i].astype(full) + mine
            if far is None:
                landed[i] = total.astype(low)
            else:

                @pl.when(place != root)
                def _():
                    landed[i] = total.astype(low)

                @pl.when(place == root)
                def _():
                    remote(far.at[i], far.at[i], up_send, far_recv.at[i], above).wait_recv()
                    landed[i] = (total + far[i].astype(full)).astype(low)

        @pl.when(place != root)
        def _():
            send_in(i)

        @pl.when(place == root)
        def _():
            send_out(landed.at[i], i)
            pltpu.make_async_copy(landed.at[i], out_ref.at[way, i], kept).start()

    def downward(i):
        done = out_ref.at[way, i]
        remote(done, done, down_send, down_recv.at[i], below).wait_recv()
        send_out(done, i)

    away = root - place if far is None else jnp.where(place < root, root - place, place - root)
    lag = slack * away + 2

    def step(i, carry):
        @pl.when(i < count)
        def _():
            upward(i)

        behind = i - lag

        @pl.when((behind >= 0) & (behind < count) & (place != root))
        def _():
            downward(behind)

        if hook is not None:
            hook(i)
        return carry

    lax.fori_loop(0, count + slack * root + 2, step, 0)

    def sent(sem):
        remote(landed, landed, sem, side_recv, beside).wait_send()

    @pl.when(place != root)
    def _():
        sent(up_send)

    @pl.when((place <= root) & (place > 0))
    def _():
        sent(down_send)

    if far is not None:

        @pl.when((place >= root) & (place < last))
        def _():
            sent(far_send)

    @pl.when(place == root)
    def _():
        pltpu.make_async_copy(landed, out_ref.at[way], kept).wait()

    if ways == 2:
        sent(side_send)
        remote(landed, landed, side_send, side_recv, beside).wait_recv()


def chain_kernel(ways, places, blocks, n_operands, *refs):
    operand_refs, out_ref, refs = refs[:n_operands], refs[n_operands], refs[n_operands + 1 :]
    operands, (own, landed, far, fetched, *semaphores) = refs[:n_operands], refs[n_operands:]
    last = places - 1
    place, way, above, below, beside = chain_place(ways, places)

    def fetch(n):
        return pltpu.make_async_copy(operand_refs[n], operands[n], fetched.at[n])

    for n in range(n_operands):
        fetch(n).start()

    barrier = pltpu.get_barrier_semaphore()

    @pl.when(place > 0)
    def _():
        greet({"hid": below})

    @pl.when(place < last)
    def _():
        greet({"hid": above})

    if ways == 2:
        greet({"hid": beside})
    met = jnp.where(place > 0, 1, 0) + jnp.where(place < last, 1, 0) + (ways - 1)
    pl.semaphore_wait(barrier, met)

    def compute(tile):
        seen, first = set(), 0
        for rows, segments in blocks:
            start = first
            first = first + rows // TILE
            fresh = [n for seg in segments for n in (seg[0], seg[2])]
            fresh = [n for n in dict.fromkeys(fresh) if n not in seen]
            seen.update(fresh)

            @pl.when(tile == start)
            def _(fresh=fresh):
                for n in fresh:
                    fetch(n).wait()

            @pl.when((tile >= start) & (tile < first))
            def _(start=start, segments=segments):
                column = 0
                for left, left_row, right, right_row, size in segments:
                    row = pl.multiple_of(left_row + (tile - start) * TILE, TILE)
                    own[:, column : column + size] = lax.dot_general(
                        operands[left][pl.ds(row, TILE), :],
                        operands[right][right_row : right_row + size, :],
                        (((1,), (1,)), ((), ())),
                        preferred_element_type=full,
                    )
                    column += size

    chain_loop(ways, places, out_ref, own, landed, semaphores, compute, SLACK, far=far)


def chain_sum(operands, blocks, collective_id):
    ways, size = split_ways(), lax.axis_size("hid")
    columns = sum(seg[4] for seg in blocks[0][1])
    rows = sum(block[0] for block in blocks)
    depth = max(16, CHUNK // columns)
    count = rows // depth
    tokens = operands[0].shape[1]
    return pl.pallas_call(
        functools.partial(chain_kernel, ways, size // ways, blocks, len(operands)),
        out_shape=jax.ShapeDtypeStruct((ways, count, depth, columns), low),
        in_specs=[pl.BlockSpec(memory_space=pl.ANY)] * len(operands),
        out_specs=pl.BlockSpec(memory_space=pl.ANY),
        scratch_shapes=[pltpu.VMEM(v.shape, low) for v in operands]
        + [
            pltpu.VMEM((TILE, columns), full),
            pltpu.VMEM((count, depth, columns), low),
            pltpu.VMEM((count, depth, columns), low),
            pltpu.SemaphoreType.DMA((len(operands),)),
        ]
        + chain_semaphores(count),
        compiler_params=pltpu.CompilerParams(
            collective_id=collective_id, has_side_effects=True, vmem_limit_bytes=60 << 20
        ),
        cost_estimate=pl.CostEstimate(
            flops=2 * rows * columns * tokens,
            bytes_accessed=300 * rows * columns,
            transcendentals=0,
        ),
    )(*operands)


def branch_kernel(dims, *refs):
    places, piece, group = dims
    (attended_ref, active_ref, residual_ref, mixer_ref, out_w_ref, down_w_ref), refs = refs[:6], refs[6:]
    (output_ref, rounded_ref, sums_ref, turned_out_ref, turned_down_ref), refs = refs[:5], refs[5:]
    (
        weights,
        sums,
        core_out,
        core_in,
        outer_out,
        outer_in,
        side_out,
        side_in,
        parts_out,
        parts_in,
        totals,
        weight_sem,
        turned_sem,
        core_send,
        core_recv,
        outer_send,
        outer_recv,
        side_send,
        side_recv,
        part_send,
        part_recv,
        total_send,
        total_recv,
    ) = refs
    index, hid = lax.axis_index("dp"), lax.axis_index("hid")
    outer, core = index // 2, index % 2
    place, way = hid // 2, hid % 2
    me = index * 2 + way
    partner = {"hid": hid + 1 - 2 * way}
    core_peer = {"dp": index + 1 - 2 * core}
    outer_peer = {"dp": (index + 2) % 4}
    others = [(i, j) for i in range(4) for j in range(2) if i or j]
    n_head, n_units = attended_ref.shape[0], active_ref.shape[0]
    feats = weights.shape[2]
    wide = group // 8

    def peer(i, j):
        there, other = (index + i) % 4, (way + j) % 2
        return there * 2 + other, {"dp": there, "hid": place * 2 + other}

    def weight_copies(t):
        there = (1 - outer if t < 2 else outer) * 2 + (core if t % 2 else 1 - core)
        columns = pl.ds(pl.multiple_of(there * feats, feats), feats)
        for ref, first, size in ((out_w_ref, 0, n_head), (down_w_ref, n_head, n_units)):
            rows = pl.ds(pl.multiple_of(way * size, size), size)
            yield pltpu.make_async_copy(
                ref.at[rows, columns], weights.at[t, first : first + size], weight_sem.at[t]
            )

    def turned_copies(t):
        columns = pl.ds(pl.multiple_of((3 - t) * feats, feats), feats)
        for ref, first, size in ((turned_out_ref, 0, n_head), (turned_down_ref, n_head, n_units)):
            yield pltpu.make_async_copy(
                weights.at[t, first : first + size], ref.at[:, columns], turned_sem
            )

    for t in range(4):
        for copy in weight_copies(t):
            copy.start()
    for i, j in others:
        greet(peer(i, j)[1])
    pl.semaphore_wait(pltpu.get_barrier_semaphore(), len(others))

    def halves(t, target, kind):
        pltpu.make_async_copy(weights.at[t], weights.at[t], weight_sem.at[t]).wait()
        product = across(weights[t, :n_head, :], attended_ref[...], 0, 0)
        product = product + across(weights[t, n_head:, :], active_ref[...], 0, 0)
        for q in range(places):
            first = product[2 * q * piece : (2 * q + 1) * piece]
            second = product[(2 * q + 1) * piece : (2 * q + 2) * piece]
            rows = slice(q * piece, (q + 1) * piece)
            target[0, rows, :] = jnp.where(way == 0, second, first).astype(kind)
            target[1, rows, :] = jnp.where(way == 0, first, second).astype(kind)
        for copy in turned_copies(t):
            copy.start()

    def core_copy(stage, half):
        return remote(
            core_out.at[stage, half],
            core_in.at[stage, half],
            core_send,
            core_recv.at[stage, half],
            core_peer,
        )

    def outer_copy(half):
        return remote(
            outer_out.at[half], outer_in.at[half], outer_send, outer_recv.at[half], outer_peer
        )

    def stage(k, carry):
        halves(2 * k, core_out.at[k], low)
        for half in range(2):
            core_copy(k, half).start()
        halves(2 * k + 1, sums.at[k], full)
        for half in range(2):
            core_copy(k, half).wait_recv()
            sums[k, half] = sums[k, half] + core_in[k, half].astype(full)

            @pl.when(k == 0)
            def _(half=half):
                outer_out[half] = sums[0, half].astype(low)
                outer_copy(half).start()

        return carry

    lax.fori_loop(0, 2, stage, 0)
    kept = sums.at[1]
    kept[1] = kept[1] + residual_ref[...]
    side = remote(side_out, side_in, side_send, side_recv, partner)
    outer_copy(0).wait_recv()
    side_out[...] = (kept[0] + outer_in[0].astype(full)).astype(low)
    side.start()
    outer_copy(1).wait_recv()
    kept[1] = kept[1] + outer_in[1].astype(full)
    side.wait_recv()
    output = kept[1] + side_in[...].astype(full)
    output_ref[...] = output
    rounded = output.astype(low)
    rounded_ref[...] = rounded

    mixed = jnp.dot(mixer_ref[...], rounded, preferred_element_type=full)
    square = jnp.sum(output * output, axis=0, keepdims=True)
    row = lax.broadcasted_iota(jnp.int32, mixed.shape, 0)
    mixed = jnp.where(row == mixed.shape[0] - 1, square, mixed)
    for b in range(8):
        parts_out[b] = mixed[:, b * wide : (b + 1) * wide]
    parts_in[me] = parts_out[me]
    for i, j in others:
        slot, device = peer(i, j)
        remote(parts_out.at[slot], parts_in.at[me], part_send, part_recv, device).start()
    some = pl.ds(0, len(others))

    def whole(ref, send, recv):
        return remote(ref.at[some], ref.at[some], send, recv, partner)

    whole(parts_in, part_send, part_recv).wait_recv()
    total = parts_in[0]
    for b in range(1, 8):
        total = total + parts_in[b]
    totals[me] = total
    for i, j in others:
        remote(totals.at[me], totals.at[me], total_send, total_recv, peer(i, j)[1]).start()
    whole(totals, total_send, total_recv).wait_recv()
    for b in range(8):
        sums_ref[:, b * wide : (b + 1) * wide] = totals[b]

    whole(parts_out, part_send, part_recv).wait_send()
    whole(totals, total_send, total_recv).wait_send()
    remote(core_out, core_out, core_send, side_recv, partner).wait_send()
    remote(outer_out, outer_out, outer_send, side_recv, partner).wait_send()
    side.wait_send()
    pltpu.make_async_copy(weights, weights, turned_sem).wait()


def add_branches(places, attended, active, residual, mixer_rows, w_out, w_down):
    mine, group = residual.shape
    n_head, n_units = attended.shape[0], active.shape[0]
    feats = w_out.shape[0]
    n_sums = 48
    table = jnp.zeros((n_sums, mine), low).at[: mixer_rows.shape[1]].set(mixer_rows.T)
    vmem, dma = pltpu.VMEM, pltpu.SemaphoreType.DMA
    out_types = [
        ((mine, group), full),
        ((mine, group), low),
        ((n_sums, group), full),
        ((n_head, w_out.shape[1]), low),
        ((n_units, w_down.shape[1]), low),
    ]
    spaces = [vmem] * 3 + [pl.ANY] * 2
    block = (2, mine, group)
    slots = (8, n_sums, group // 8)
    return pl.pallas_call(
        functools.partial(branch_kernel, (places, mine // places, group)),
        out_shape=[jax.ShapeDtypeStruct(*t) for t in out_types],
        in_specs=[pl.BlockSpec(memory_space=vmem)] * 4 + [pl.BlockSpec(memory_space=pl.ANY)] * 2,
        out_specs=[pl.BlockSpec(memory_space=m) for m in spaces],
        scratch_shapes=[
            vmem((4, n_head + n_units, feats), low),
            vmem((2,) + block, full),
            vmem((2,) + block, low),
            vmem((2,) + block, low),
            vmem(block, low),
            vmem(block, low),
            vmem(block[1:], low),
            vmem(block[1:], low),
            vmem(slots, full),
            vmem(slots, full),
            vmem(slots, full),
            dma((4,)),
            dma,
            dma,
            dma((2, 2)),
            dma,
            dma((2,)),
            dma,
            dma,
            dma,
            dma,
            dma,
            dma,
        ],
        compiler_params=pltpu.CompilerParams(
            collective_id=8, has_side_effects=True, vmem_limit_bytes=56 << 20
        ),
        cost_estimate=pl.CostEstimate(
            flops=8 * (n_head + n_units) * feats * group, bytes_accessed=100 << 20, transcendentals=0
        ),
    )(attended, active, residual, table, w_out, w_down)


def late_kernel(dims, *refs):
    places, piece, group, n_head, n_units = dims
    (
        hidden_ref,
        hidden_far_ref,
        lows_ref,
        lows_far_ref,
        output_low_ref,
        attended_ref,
        normed_ref,
        turned_ref,
        turned_up_ref,
        devs_ref,
        output_grad_ref,
        shifts,
        scales,
        gains,
        all_gains,
    ), refs = refs[:15], refs[15:]
    (out_ref, split_ref, gain_ref), refs = refs[:3], refs[3:]
    (
        hidden,
        lows,
        output_low,
        attended,
        normed,
        turned,
        turned_up,
        devs,
        output_grad,
        kept,
        given,
        taken,
        grads,
        joins,
        totals,
        own,
        pulled,
        landed,
        fetched,
        core_send,
        core_recv,
        side_send,
        side_recv,
        join_send,
        join_recv,
        place_send,
        place_recv,
        own_copy,
        *semaphores,
    ) = refs
    index, hid = lax.axis_index("dp"), lax.axis_index("hid")
    core = index % 2
    place, way = hid // 2, hid % 2
    me = index * 2 + way
    partner = {"hid": hid + 1 - 2 * way}
    core_peer = {"dp": index + 1 - 2 * core}
    others = [(i, j) for i in range(4) for j in range(2) if i or j]
    wide = own.shape[1]
    feats = normed.shape[1]

    def join_device(i, j):
        return {"dp": (index + i) % 4, "hid": place * 2 + (way + j) % 2}

    def head_rows(turn):
        return slice(turn * n_head, (turn + 1) * n_head)

    def unit_rows(turn):
        return slice(turn * n_units, (turn + 1) * n_units)

    fetches = [
        [(output_low_ref, output_low), (attended_ref, attended), (normed_ref, normed)],
        [(hidden_ref, hidden.at[unit_rows(0)])],
        [
            (hidden_far_ref, hidden.at[unit_rows(2)]),
            (turned_ref, turned),
            (turned_up_ref, turned_up),
            (devs_ref, devs),
            (output_grad_ref, output_grad),
        ]
        + [
            (source.at[head_rows(s)], lows.at[s, head_rows(turn)])
            for s in range(3)
            for turn, source in ((0, lows_ref), (2, lows_far_ref))
        ],
    ]

    def fetch(stage):
        return [pltpu.make_async_copy(a, b, fetched.at[stage, n]) for n, (a, b) in enumerate(fetches[stage])]

    for stage in range(len(fetches)):
        for copy in fetch(stage):
            copy.start()

    for k in range(1, places):
        greet({"hid": (place + k) % places * 2 + way})
    for i, j in others:
        greet(join_device(i, j))
    pl.semaphore_wait(pltpu.get_barrier_semaphore(), places - 1 + len(others))

    def core_copies(far):
        source, heads = (hidden_far_ref, lows_far_ref) if far else (hidden_ref, lows_ref)
        turn = 3 if far else 1
        yield remote(source, hidden.at[unit_rows(turn)], core_send.at[far], core_recv.at[far], core_peer)
        for s in range(3):
            yield remote(
                heads.at[head_rows(s)],
                lows.at[s, head_rows(turn)],
                core_send.at[2 + far],
                core_recv.at[2 + far],
                core_peer,
            )

    for far in range(2):
        for copy in core_copies(far):
            copy.start()

    def wait_cores():
        for far in range(2):
            remote(hidden_ref, hidden_ref, core_send.at[far], core_recv.at[far], core_peer).wait_recv()
            remote(lows_ref, lows_ref, core_send.at[2 + far], core_recv.at[2 + far], core_peer).wait_recv()

    per_block = feats // LATE_TILE
    per_out = n_head // LATE_TILE

    def compute(tile):
        @pl.when(tile == 0)
        def _():
            for copy in fetch(0):
                copy.wait()

        @pl.when(tile == per_block)
        def _():
            for copy in fetch(1):
                copy.wait()

        inner = tile % per_block

        def product(left, right):
            own[...] = lax.dot_general(
                left, right, (((1,), (1,)), ((), ())), preferred_element_type=full
            )

        def rows(n):
            return pl.ds(pl.multiple_of(n * LATE_TILE, LATE_TILE), LATE_TILE)

        @pl.when(tile < per_block)
        def _():
            half = pl.ds(pl.multiple_of(inner // per_out * wide, wide), wide)
            product(attended[rows(inner % per_out), :], output_low[half, :])

        block = tile // per_block

        @pl.when((block >= 1) & (block < 5))
        def _():
            turn = (block - 1) // 2 + (block - 1) % 2 * 2
            units = pl.ds(pl.multiple_of(turn * n_units, n_units), n_units)
            product(normed[3, rows(inner), :], hidden[units, :])

        @pl.when(block >= 5)
        def _():
            product(normed[block - 5, rows(inner), :], lows[block - 5])

    totals[...] = jnp.zeros_like(totals)

    def side_copy(s, r):
        return remote(given.at[s, r], taken.at[s, r], side_send, side_recv.at[s], partner)

    def pull(s):
        @pl.when(s < 3)
        def _():
            pulled[...] = jnp.dot(turned[s], lows[s], preferred_element_type=full)

        @pl.when(s == 3)
        def _():
            pulled[...] = jnp.zeros_like(pulled)

            def add_turn(turn, carry):
                units = pl.ds(pl.multiple_of(turn * n_units, n_units), n_units)
                pulled[...] += jnp.dot(
                    turned_up[:, units], hidden[units, :], preferred_element_type=full
                )
                return carry

            lax.fori_loop(0, 4, add_turn, 0)

        def use(r, carry):
            rows = pl.ds(pl.multiple_of(2 * piece * r, 2 * piece), 2 * piece)
            here = pulled[rows, :]
            totals[s, 0:1, :] = totals[s, 0:1, :] + jnp.sum(
                here * all_gains[s, r], axis=0, keepdims=True
            )
            totals[s, 1:2, :] = totals[s, 1:2, :] + jnp.sum(
                here * normed[s, rows, :].astype(full), axis=0, keepdims=True
            )
            first = way == 0
            kept[s, r] = jnp.where(first, here[:piece], here[piece:])
            given[s, r] = jnp.where(first, here[piece:], here[:piece]).astype(low)
            side_copy(s, r).start()
            return carry

        lax.fori_loop(0, places, use, 0)

    def share_totals():
        joins[me] = totals[...]
        for i, j in others:
            remote(joins.at[me], joins.at[me], join_send, join_recv, join_device(i, j)).start()

    def sum_totals():
        some = joins.at[pl.ds(0, len(others))]
        remote(some, some, join_send, join_recv, partner).wait_recv()
        total = joins[0]
        for i in range(1, len(others) + 1):
            total = total + joins[i]
        totals[...] = total / (feats * 4)

    def stream_grad(s, r):
        @pl.when(r == 0)
        def _():
            remote(given.at[s], taken.at[s], side_send, side_recv.at[s], partner).wait_recv()

        gradient = kept[s, r] + taken[s, r].astype(full)
        unit = devs[s, r].astype(full) * scales[s] + shifts[s, r]
        gain_ref[s, r] = jnp.sum(gradient * unit, axis=1, keepdims=True)
        result = gradient * gains[s, r] - totals[s, 0:1, :] - unit * totals[s, 1:2, :]
        extra = output_grad[r] * jnp.where(s == 3, 1.0, 0.0)
        grads[s, r] = (result * scales[s] + extra).astype(low)

        @pl.when(r == place)
        def _():
            pltpu.make_async_copy(grads.at[s, r], split_ref.at[s, place], own_copy).start()

        @pl.when(r != place)
        def _():
            remote(
                grads.at[s, r],
                split_ref.at[s, place],
                place_send,
                place_recv,
                {"hid": r * 2 + way},
            ).start()

    n_pulls = STREAMS * places
    middle = PULL_START + PULL_GAP * STREAMS
    resume = middle + 8

    def hook(i):
        @pl.when(i == PULL_START)
        def _():
            for copy in fetch(2):
                copy.wait()
            wait_cores()

        k = (i - PULL_START) // PULL_GAP

        @pl.when((i >= PULL_START) & (i < middle) & ((i - PULL_START) % PULL_GAP == 0))
        def _():
            pull(k)

        @pl.when(i == middle)
        def _():
            share_totals()

        @pl.when(i == resume)
        def _():
            sum_totals()

        n = (i - resume) // GRAD_GAP

        @pl.when((i >= resume) & (n < n_pulls) & ((i - resume) % GRAD_GAP == 0))
        def _():
            stream_grad(n // places, n % places)

    chain_loop(2, places, out_ref, own, landed, semaphores, compute, LATE_SLACK, hook)

    def sent(ref, sem):
        remote(ref, ref, sem, join_recv, partner).wait_send()

    for far in range(2):
        sent(hidden_ref, core_send.at[far])
        sent(lows_ref, core_send.at[2 + far])
    sent(given, side_send)
    sent(joins.at[pl.ds(0, len(others))], join_send)
    moved = grads.at[pl.ds(0, places - 1)]
    sent(moved, place_send)
    remote(moved, moved, place_send, place_recv, partner).wait_recv()
    mine = grads.at[0]
    pltpu.make_async_copy(mine, mine, own_copy).wait()


def late_sums(operands, tables, collective_id):
    hidden, _, lows, _, output_low, attended, normed = operands[:7]
    _, places, piece, group = operands[9].shape
    feats = normed.shape[1]
    n_units, n_head = hidden.shape[0], attended.shape[0]
    wide = n_units
    rows = 8 * feats
    depth = max(16, LATE_CHUNK // wide)
    count = rows // depth
    vmem, dma = pltpu.VMEM, pltpu.SemaphoreType.DMA
    block = (STREAMS, places, piece, group)
    outs = [
        jax.ShapeDtypeStruct((2, count, depth, wide), low),
        jax.ShapeDtypeStruct(block, low),
        jax.ShapeDtypeStruct((STREAMS, places, piece, 1), full),
    ]
    any_space, vmem_space = pl.BlockSpec(memory_space=pl.ANY), pl.BlockSpec(memory_space=vmem)
    total, split, gain_parts = pl.pallas_call(
        functools.partial(late_kernel, (places, piece, group, n_head, n_units)),
        out_shape=outs,
        in_specs=[any_space] * len(operands) + [vmem_space] * len(tables),
        out_specs=[any_space, any_space, vmem_space],
        scratch_shapes=[
            vmem((4 * n_units, group), low),
            vmem((3, 4 * n_head, group), low),
            vmem(output_low.shape, low),
            vmem(attended.shape, low),
            vmem(normed.shape, low),
            vmem(operands[7].shape, low),
            vmem(operands[8].shape, low),
            vmem(block, low),
            vmem(block[1:], full),
            vmem(block, full),
            vmem(block, low),
            vmem(block, low),
            vmem(block, low),
            vmem((8, STREAMS, 2, group), full),
            vmem((STREAMS, 2, group), full),
            vmem((LATE_TILE, wide), full),
            vmem((feats, group), full),
            vmem((count, depth, wide), low),
            dma((3, 11)),
            dma((4,)),
            dma((4,)),
            dma,
            dma((STREAMS,)),
            dma,
            dma,
            dma,
            dma,
            dma,
        ]
        + chain_semaphores(count),
        compiler_params=pltpu.CompilerParams(
            collective_id=collective_id, has_side_effects=True, vmem_limit_bytes=63 << 20
        ),
        cost_estimate=pl.CostEstimate(
            flops=4 * rows * wide * group, bytes_accessed=900 << 20, transcendentals=0
        ),
    )(*operands, *tables)
    return total.reshape(2, 8, feats, wide), split, gain_parts


def chain_sums(operands, blocks, collective_id):
    groups, held, size = [[]], set(), 0
    for rows, segments in blocks:
        used = {n for seg in segments for n in (seg[0], seg[2])}
        more = sum(2 * operands[n].size for n in used - held)
        more += 4 * rows * sum(seg[4] for seg in segments)
        if groups[-1] and size + more > VMEM:
            groups.append([])
            held, size = set(), 0
            more = sum(2 * operands[n].size for n in used)
            more += 4 * rows * sum(seg[4] for seg in segments)
        groups[-1].append((rows, segments))
        held |= used
        size += more
    totals = []
    for i, group in enumerate(groups):
        used = sorted({n for _, segments in group for seg in segments for n in (seg[0], seg[2])})
        place = {n: k for k, n in enumerate(used)}
        own = [
            (rows, [(place[a], b, place[c], d, e) for a, b, c, d, e in segments])
            for rows, segments in group
        ]
        total = chain_sum([operands[n] for n in used], own, collective_id + i)
        totals.append(total.reshape(total.shape[0], -1, total.shape[3]))
    return totals[0] if len(totals) == 1 else jnp.concatenate(totals, axis=1)


def assemble_kernel(ways, dp, fused, own_ref, *refs):
    halves, (up_ref, *head_refs, out_ref) = refs[:ways], refs[ways:]
    rows, wide = own_ref.shape[2:]
    size = up_ref.shape[1] // dp // ways
    blocks = dp * size // wide
    own = wide // dp
    feats = out_ref.shape[1] // dp
    for d in range(dp):
        turn = turn_of(d)
        for w in range(ways):
            start = turn * size
            lanes = pl.ds(pl.multiple_of(start % wide, size), size)
            place = (d * ways + w) * size
            up_block = 1 + turn // 2 + turn % 2 * 2 if fused else start // wide
            up_ref[:, place : place + size] = own_ref[w, up_block, :, lanes].astype(full)
            for s, ref in enumerate(head_refs):
                lanes = pl.ds(pl.multiple_of(turn * own, own), own)
                place = (d * ways + w) * own
                ref[:, place : place + own] = own_ref[w, blocks + s + fused, :, lanes].astype(full)
        start = turn * feats
        lanes = pl.ds(pl.multiple_of(start % wide, feats), feats)
        for w in range(ways):

            @pl.when(start // wide == w)
            def _(w=w, d=d, lanes=lanes):
                out_ref[:, d * feats : (d + 1) * feats] = halves[w][0, 0, :, lanes].astype(full)


def assemble(total, w_up, fused):
    ways, dp = split_ways(), lax.axis_size("dp")
    blocks, rows, wide = total.shape[1:]
    depth = min(64, rows // ways)
    share = rows // ways // depth

    def half_map(half):
        return lambda i: (i // share, 0 if fused else blocks - 1, half * share + i % share, 0)

    widths = [w_up.shape[1]] + [ways * wide] * 4
    return pl.pallas_call(
        functools.partial(assemble_kernel, ways, dp, int(fused)),
        grid=(rows // depth,),
        out_shape=[jax.ShapeDtypeStruct((rows, n), full) for n in widths],
        in_specs=[pl.BlockSpec((ways, blocks, depth, wide), lambda i: (0, 0, i, 0))]
        + [pl.BlockSpec((1, 1, depth, wide), half_map(half)) for half in range(ways)],
        out_specs=[pl.BlockSpec((depth, n), lambda i: (i, 0)) for n in widths],
        compiler_params=pltpu.CompilerParams(vmem_limit_bytes=48 << 20),
        cost_estimate=pl.CostEstimate(
            flops=0, bytes_accessed=6 * total.size, transcendentals=0
        ),
    )(total, *[total] * ways)


def unturn_kernel(dp, own_ref, out_ref):
    size = out_ref.shape[1] // dp
    for d in range(dp):
        lanes = pl.ds(pl.multiple_of(turn_of(d) * size, size), size)
        out_ref[:, d * size : (d + 1) * size] = own_ref[:, lanes].astype(full)


def unturn(total):
    rows, columns = total.shape
    depth = 256
    return pl.pallas_call(
        functools.partial(unturn_kernel, lax.axis_size("dp")),
        grid=(rows // depth,),
        out_shape=jax.ShapeDtypeStruct((rows, columns), full),
        in_specs=[pl.BlockSpec((depth, columns), lambda i: (i, 0))],
        out_specs=pl.BlockSpec((depth, columns), lambda i: (i, 0)),
        cost_estimate=pl.CostEstimate(
            flops=0, bytes_accessed=6 * total.size, transcendentals=0
        ),
    )(total)


def stream_kernel(stored_ref, mix_ref, deviations_ref, moments_ref):
    means, spreads = [], []
    for s in range(STREAMS):
        total = mix_ref[s * HIST : s * HIST + 1, :] * stored_ref[0].astype(full)
        for j in range(1, HIST):
            row = s * HIST + j
            total = total + mix_ref[row : row + 1, :] * stored_ref[j].astype(full)
        mean = jnp.mean(total, axis=0, keepdims=True)
        off = total - mean
        deviations_ref[0, s] = off.astype(low)
        means.append(mean)
        spreads.append(jnp.sum(off * off, axis=0, keepdims=True))
    moments_ref[0] = jnp.concatenate(means + spreads, axis=0)


def mix_streams(stored, mix_all, places):
    _, piece, tokens = stored.shape
    group = tokens // places
    wide = min(512, group)
    per_place = group // wide
    return pl.pallas_call(
        stream_kernel,
        grid=(tokens // wide,),
        out_shape=[
            jax.ShapeDtypeStruct((places, STREAMS, piece, group), low),
            jax.ShapeDtypeStruct((places, 2 * STREAMS, group), full),
        ],
        in_specs=[
            pl.BlockSpec((HIST, piece, wide), lambda i: (0, 0, i)),
            pl.BlockSpec((mix_all.shape[0], wide), lambda i: (0, i)),
        ],
        out_specs=[
            pl.BlockSpec((1, STREAMS, piece, wide), lambda i: (i // per_place, 0, 0, i % per_place)),
            pl.BlockSpec((1, 2 * STREAMS, wide), lambda i: (i // per_place, 0, i % per_place)),
        ],
        compiler_params=pltpu.CompilerParams(vmem_limit_bytes=40 << 20),
        cost_estimate=pl.CostEstimate(
            flops=2 * STREAMS * HIST * piece * tokens,
            bytes_accessed=4 * HIST * piece * tokens,
            transcendentals=0,
        ),
    )(stored, mix_all)


def history_kernel(split_ref, stored_ref, mix_ref, grad_ref, parts_ref):
    streams = [split_ref[s, 0].astype(full) for s in range(STREAMS)]
    rows = [None] * (STREAMS * HIST)
    for j in range(HIST):
        layer = stored_ref[j].astype(full)
        total = mix_ref[j : j + 1, :] * streams[0]
        for s in range(1, STREAMS):
            total = total + mix_ref[s * HIST + j : s * HIST + j + 1, :] * streams[s]
        grad_ref[j] = total
        for s in range(STREAMS):
            rows[s * HIST + j] = jnp.sum(streams[s] * layer, axis=0, keepdims=True)
    parts = jnp.concatenate(rows, axis=0)
    block = parts_ref.shape[2]
    for b in range(parts_ref.shape[0]):
        parts_ref[b] = parts[:, b * block : (b + 1) * block]


def history_gradients(split, stored, mix_all, block):
    _, places, piece, group = split.shape
    n_mix, tokens = mix_all.shape
    wide = min(512, group)
    per_place = group // wide
    return pl.pallas_call(
        history_kernel,
        grid=(tokens // wide,),
        out_shape=[
            jax.ShapeDtypeStruct((HIST, piece, tokens), full),
            jax.ShapeDtypeStruct((tokens // block, n_mix, block), full),
        ],
        in_specs=[
            pl.BlockSpec((STREAMS, 1, piece, wide), lambda i: (0, i // per_place, 0, i % per_place)),
            pl.BlockSpec((HIST, piece, wide), lambda i: (0, 0, i)),
            pl.BlockSpec((n_mix, wide), lambda i: (0, i)),
        ],
        out_specs=[
            pl.BlockSpec((HIST, piece, wide), lambda i: (0, 0, i)),
            pl.BlockSpec((wide // block, n_mix, block), lambda i: (i, 0, 0)),
        ],
        compiler_params=pltpu.CompilerParams(vmem_limit_bytes=40 << 20),
        cost_estimate=pl.CostEstimate(
            flops=4 * STREAMS * HIST * piece * tokens,
            bytes_accessed=6 * HIST * piece * tokens + 2 * split.size,
            transcendentals=0,
        ),
    )(split, stored, mix_all)


def to_owner(values_in):
    dp, hid, ways = lax.axis_size("dp"), lax.axis_size("hid"), split_ways()
    index = lax.axis_index("dp") * ways + lax.axis_index("hid") % ways
    mine = lax.dynamic_index_in_dim(values_in, index, 1, keepdims=False)
    pairs = [
        (d * hid + t * ways + w, (t * dp + d) * ways + w)
        for d in range(dp)
        for t in range(hid // ways)
        for w in range(ways)
    ]
    return lax.ppermute(mine, ("dp", "hid"), pairs)


def rotate(values_in, cosine, sine):
    half = cosine.shape[1]
    front, back = values_in[:, :half], values_in[:, half : 2 * half]
    return jnp.concatenate(
        [
            front * cosine - back * sine,
            back * cosine + front * sine,
            values_in[:, 2 * half :],
        ],
        axis=1,
    )


def local(
    history,
    mix,
    segment_ids,
    norm_gains,
    w_query,
    w_key,
    w_value,
    w_out,
    w_up,
    w_down,
    w_mixer,
    mixer_out,
    mix_static,
    out_cotangent,
    mix_cotangent,
):
    dp, hid, ways = lax.axis_size("dp"), lax.axis_size("hid"), split_ways()
    places = hid // ways
    my_hid = lax.axis_index("hid")
    place, way = my_hid // ways, my_hid % ways
    block = segment_ids.shape[0]
    total_tokens = block * dp * hid
    row = total_tokens // dp
    group = total_tokens // places
    rows = group // row
    piece = history.shape[2]
    mine = piece * places
    feats = piece * hid
    width = feats * dp
    heads = HEADS // dp // ways
    n_mix = mix.shape[1]
    n_cot = mix_cotangent.shape[1]

    def by_place(values_in):
        return jnp.stack(
            [values_in[..., p * group : (p + 1) * group] for p in range(places)], axis=0
        )

    stored = history.swapaxes(1, 2)
    mix_all = gather_all(mix.T)
    fused = dp == 4 and ways == 2 and rows == 1
    if fused:
        parts = norm_gains.astype(full).T.reshape(STREAMS, places, ways, piece)
        gain_tables = (
            lax.dynamic_index_in_dim(parts, way, 2, keepdims=False)[..., None],
            parts.reshape(STREAMS, places, ways * piece, 1),
        )
        mix_all, gain_tables = lax.optimization_barrier((mix_all, gain_tables))
    deviations, moments = mix_streams(stored, mix_all, places)

    table = jnp.concatenate([mix_cotangent.T, segment_ids.astype(full)[None]], axis=0)
    table = lax.dynamic_slice_in_dim(gather_all(table), place * group, group, 1)
    cot_t = table[:n_cot]
    ids = table[-1].reshape(rows, row)

    there = jnp.arange(row, dtype=jnp.int32)
    same_doc = ids[:, :, None] == ids[:, None, :]
    doc_start = jnp.min(jnp.where(same_doc, there[None, None], row), axis=2)
    position = (there[None] - doc_start).astype(full).reshape(group)
    visible = same_doc & (there[None, None] <= there[None, :, None])
    frequency = rope_base ** (-jnp.arange(ROT // 2, dtype=full) * 2.0 / ROT)
    angle = frequency[:, None] * position[None, :]
    cosine, sine = jnp.cos(angle)[None], jnp.sin(angle)[None]

    def own_rows(values_in):
        parts = values_in.reshape((places, ways, piece) + values_in.shape[1:])
        part = lax.dynamic_index_in_dim(parts, way, 1, keepdims=False)
        return part.reshape((mine,) + values_in.shape[1:])

    def all_rows(values_in):
        parts = values_in.reshape((places, piece) + values_in.shape[1:])
        return gather_ways(parts, 1).reshape((feats,) + values_in.shape[1:])

    own_gains = own_rows(norm_gains).astype(full)
    gains = [own_gains[:, s][:, None] for s in range(STREAMS)]
    all_gains = norm_gains.astype(full)

    def project(weight, left):
        columns = weight.shape[1] // dp // ways

        def make(index):
            start = (index * ways + way) * columns
            part = lax.dynamic_slice_in_dim(weight, start, columns, 1)
            return contract(part, left, 0, 0)

        return scatter_dp(make)

    def way_columns(weight):
        if ways == 1:
            return weight
        size = weight.shape[1] // dp // ways
        parts = [weight[:, i * size : (i + 1) * size] for i in range(dp * ways)]
        pairs = zip(parts[::2], parts[1::2])
        return jnp.concatenate([jnp.where(way == 0, a, b) for a, b in pairs], axis=1)

    def way_rows(weight):
        size = weight.shape[0] // ways
        return lax.dynamic_slice_in_dim(weight, way * size, size, 0)

    def by_head(values_in):
        return values_in.reshape(heads, HEAD, group)

    def turned(weight, stride, offset, size):
        starts = [turn_source(turn) * stride + offset for turn in range(dp)]
        parts = [lax.dynamic_slice_in_dim(weight, start, size, 1) for start in starts]
        return jnp.concatenate(parts, axis=1)

    n_head = heads * HEAD
    n_units = w_up.shape[1] // dp // ways
    if fused:
        normed, deviations, residual, own_shifts, inv_scales, active, slope, products, *ends = (
            forward_projections(
                deviations,
                moments,
                norm_gains,
                w_query,
                w_key,
                w_value,
                w_up,
                by_place(out_cotangent.T),
            )
        )
        turned_heads, turned_up, upstream = ends
        upstream = upstream.reshape(mine, group)
        normed_all = normed
        normed = [normed[s] for s in range(STREAMS)]
        products = products.reshape(3, heads, HEAD, group)
        turned_weights = [turned_heads[s] for s in range(3)] + [turned_up]
    else:
        moments = exchange(moments)
        deviations = exchange(deviations)
        deviations = [deviations[:, s] for s in range(STREAMS)]
        def join_moments(mean_parts, dev_parts, size):
            mean = jnp.mean(mean_parts, axis=0)
            spread = size * jnp.sum(jnp.square(mean_parts - mean), axis=0)
            return mean, jnp.sum(dev_parts, axis=0) + spread

        block_means = moments[:, :STREAMS]
        joined = join_moments(block_means, moments[:, STREAMS:], piece)
        joined = gather_dp(gather_ways(jnp.concatenate(joined, axis=0), 0))
        joined = joined.reshape((dp * ways,) + joined.shape[2:])
        means, variance = join_moments(joined[:, :STREAMS], joined[:, STREAMS:], mine)
        inv_scales = lax.rsqrt(variance / width + 1e-05)
        all_means = gather_ways(block_means, 1)

        def unit(values_in, block_mean, s):
            return (values_in.astype(full) + (block_mean - means[s])[..., None, :]) * inv_scales[s]

        units = [
            unit(deviations[s], block_means[:, s], s).reshape(mine, group) for s in range(STREAMS)
        ]
        normed = []
        for s in range(STREAMS):
            both = unit(gather_ways(deviations[s], 1), all_means[:, :, s], s).reshape(feats, group)
            normed.append((both * all_gains[:, s][:, None]).astype(low))
        residual = (deviations[3].astype(full) + block_means[:, 3][:, None]).reshape(mine, group)
        products = [
            by_head(project(w, normed[s])) for s, w in enumerate((w_query, w_key, w_value))
        ]
        hidden = project(w_up, normed[3])
        active, hidden_pull = jax.vjp(gelu_exact, hidden)
        active = active.astype(low)
        (slope,) = hidden_pull(jnp.ones_like(hidden))
        turned_weights = [
            turned(w, ways * n_head, way * n_head, n_head) for w in (w_query, w_key, w_value)
        ] + [turned(w_up, ways * n_units, way * n_units, n_units)]

    def by_row(values_in):
        if rows == 1:
            return values_in
        return (
            values_in.reshape(heads, HEAD, rows, row)
            .transpose(0, 2, 1, 3)
            .reshape(heads * rows, HEAD, row)
        )

    def from_row(values_in):
        if rows == 1:
            return values_in
        return (
            values_in.reshape(heads, rows, HEAD, row)
            .transpose(0, 2, 1, 3)
            .reshape(heads, HEAD, group)
        )

    if fused:
        starts = doc_start.reshape(1, group)
        turned_values, attended, tops = attend(products, cosine[0], sine[0], starts)
        attended = attended.reshape(n_head, group)
    else:
        queries = rotate(products[0], cosine, sine).astype(low)
        keys = rotate(products[1], cosine, sine).astype(low)
        values = products[2].astype(low)
        q_rows, k_rows, v_rows = by_row(queries), by_row(keys), by_row(values)
        score_scale = 1.0 / math.sqrt(HEAD)
        scores = batched(q_rows, k_rows, 1, 1) * score_scale
        mask = jnp.broadcast_to(visible[None], (heads, rows, row, row)).reshape(scores.shape)
        scores = jnp.where(mask, scores, -1e30)
        probs = jax.nn.softmax(scores, axis=-1)
        probs_low = probs.astype(low)
        attended = from_row(batched(v_rows, probs_low, 2, 2).astype(low)).reshape(heads * HEAD, group)

        cotangent, attended = lax.optimization_barrier((out_cotangent, attended))
        upstream = exchange(by_place(cotangent.T)).reshape(mine, group)

    mixer_rows = own_rows(w_mixer)
    if fused:
        output, output_rounded, sums, *turned_ends = add_branches(
            places, attended, active, residual, mixer_rows, w_out, w_down
        )
        sums = jnp.concatenate([sums[: mixer_rows.shape[1]], sums[-1:]], axis=0)
        turned_weights += turned_ends
    else:
        out_rows, down_rows = way_rows(w_out), way_rows(w_down)
        turned_weights += [turned(out_rows, feats, 0, feats), turned(down_rows, feats, 0, feats)]
        def make_out(index):
            start = index * feats
            left = lax.dynamic_slice_in_dim(out_rows, start, feats, 1)
            other = lax.dynamic_slice_in_dim(down_rows, start, feats, 1)
            return contract(left, attended, 0, 0) + contract(other, active, 0, 0)

        branches = scatter_dp(make_out).reshape(places, ways, piece, group)
        kept = lax.dynamic_index_in_dim(branches, way, 1, keepdims=False)
        if ways == 2:
            given = lax.dynamic_index_in_dim(branches, 1 - way, 1, keepdims=False).astype(low)
            kept = kept + hid_swap(given, 1).astype(full)
        output = residual + kept.reshape(mine, group)
        output, upstream, turned_weights = lax.optimization_barrier(
            (output, upstream, turned_weights)
        )
        output_rounded = output.astype(low)
        square = jnp.sum(output * output, axis=0, keepdims=True)
        mixer_part = contract(mixer_rows, output_rounded, 0, 0)
        sums = sum_features(jnp.concatenate([mixer_part, square], axis=0))
    upstream = upstream.astype(full)

    block_output = exchange(output_rounded.reshape(places, piece, group))

    inv_rms = lax.rsqrt(sums[-1] / width + 1e-06)
    inner_raw = sums[:-1]
    inner_pre = inner_raw * inv_rms
    inner_act, inner_pull = jax.vjp(gelu_exact, inner_pre)
    raw_mix = contract_high(mixer_out, inner_act, 0, 0)
    column = jnp.stack(
        [
            jnp.sum(raw_mix, axis=1),
            jnp.sum(raw_mix * raw_mix, axis=1),
            jnp.sum(cot_t, axis=1),
            jnp.sum(cot_t * raw_mix, axis=1),
        ],
        axis=0,
    )
    act_total = jnp.sum(inner_act, axis=1)
    act_cot = contract_high(inner_act, cot_t, 1, 1)
    act_raw = contract_high(inner_act, raw_mix, 1, 1)
    n_inner = act_total.shape[0]
    flat = sum_tokens(
        jnp.concatenate([column.reshape(-1), act_total, act_cot.reshape(-1), act_raw.reshape(-1)])
    )
    sum_raw, sum_square, sum_grad, sum_grad_raw = flat[: 4 * n_cot].reshape(4, n_cot)
    start = 4 * n_cot
    act_total = flat[start : start + n_inner]
    start += n_inner
    act_cot = flat[start : start + n_inner * n_cot].reshape(n_inner, n_cot)
    start += n_inner * n_cot
    act_raw = flat[start:].reshape(n_inner, n_cot)
    average = sum_raw / total_tokens
    variance_mix = sum_square / total_tokens - average * average
    inv_spread = lax.rsqrt(variance_mix + 1e-05)
    unit_mix = (raw_mix - average[:, None]) * inv_spread[:, None]
    mix_next = mix_static[:, None] + unit_mix
    mix_next = to_owner(mix_next.reshape(n_cot, dp * ways, block)).T
    mean_grad = sum_grad / total_tokens
    sum_grad_unit = inv_spread * (sum_grad_raw - average * sum_grad)
    mean_grad_unit = sum_grad_unit / total_tokens
    raw_grad = inv_spread[:, None] * (
        cot_t - mean_grad[:, None] - unit_mix * mean_grad_unit[:, None]
    )
    act_unit = inv_spread[None, :] * (act_raw - act_total[:, None] * average[None, :])
    mixer_out_grad = inv_spread[None, :] * (
        act_cot - act_total[:, None] * mean_grad[None, :] - act_unit * mean_grad_unit[None, :]
    )
    act_grad = contract_high(mixer_out, raw_grad, 1, 0)
    inner_low = inner_pull(act_grad)[0].astype(low)
    scaled = (output * inv_rms).astype(low)
    mixer_grad_part = contract(inner_low, scaled, 1, 1)
    scaled_grad = contract(mixer_rows, inner_low, 1, 0)
    along = jnp.sum(inner_low.astype(full) * inner_raw, axis=0) / width
    output_grad = upstream + inv_rms * scaled_grad - output * (inv_rms * inv_rms * inv_rms) * along
    if fused:
        near = output_grad.astype(low)
        far = outer_shift(near, 1)
        beside = hid_swap(near, 1)
        far_beside = outer_shift(beside, 1)

        def interleave(values_in, other):
            values_in, other = [v.reshape(places, piece, group) for v in (values_in, other)]
            return ordered(way == 0, values_in, other, 1).reshape(feats, group)

        output_lows = gather_cores([interleave(near, beside), interleave(far, far_beside)])
    else:
        output_lows = gather_turns(all_rows(output_grad.astype(low)))

    output_low = jnp.concatenate(output_lows, axis=0)

    hidden_low = (contract(turned_weights[5], output_low, 1, 0) * slope).astype(low)

    attended_grad = contract(turned_weights[4], output_low, 1, 0).astype(low)
    if fused:
        lows_mine = attend_back(
            turned_values, by_head(attended_grad), cosine[0], sine[0], starts, tops
        ).reshape(3 * n_head, group)
    else:
        a_rows = by_row(by_head(attended_grad))
        prob_grad = batched(a_rows, v_rows, 1, 1)
        row_total = jnp.sum(probs * prob_grad, axis=-1, keepdims=True)
        score_grad = (probs * (prob_grad - row_total)).astype(low)
        query_grad = from_row(batched(k_rows, score_grad, 2, 2) * score_scale)
        key_grad = from_row(batched(q_rows, score_grad, 2, 1) * score_scale)
        value_grad = from_row(batched(a_rows, probs_low, 2, 1))
        query_low = rotate(query_grad, cosine, -sine).astype(low).reshape(heads * HEAD, group)
        key_low = rotate(key_grad, cosine, -sine).astype(low).reshape(heads * HEAD, group)
        value_low = value_grad.astype(low).reshape(heads * HEAD, group)

        lows_mine = jnp.concatenate([query_low, key_low, value_low], axis=0)
    active_kept, hidden_low, lows_mine = lax.optimization_barrier((active, hidden_low, lows_mine))
    hidden_lows, lows = gather_outer(hidden_low), gather_outer(lows_mine)
    blocks = [(active.shape[0], [(0, 0, 1, 0, width)])]
    branch_sum = chain_sum([active_kept, output_low], blocks, 0)
    branch_sum, block_output, hidden_lows, lows = lax.optimization_barrier(
        (branch_sum, block_output, hidden_lows, lows)
    )
    block_output = block_output.transpose(1, 0, 2).reshape(piece, total_tokens).T

    if fused:
        operands = [hidden_lows[0], hidden_lows[1], lows[0], lows[1], output_low, attended]
        operands += [normed_all, turned_heads, turned_up, deviations]
        operands.append(output_grad.reshape(places, piece, group))
        tables = [
            own_shifts,
            inv_scales,
            *gain_tables,
        ]
        late_sum, split, gain_parts = late_sums(operands, tables, 1)
        gain_parts = gain_parts.reshape(STREAMS, mine)
        history_grad, mix_parts = history_gradients(split, stored, mix_all, block)
    else:
        hidden_lows, lows = gather_cores(hidden_lows), gather_cores(lows)

        normed_grads, alongs, rights = [], [], []
        for s in range(STREAMS):
            if s < 3:
                right = jnp.concatenate([v[s * n_head : (s + 1) * n_head] for v in lows], axis=0)
            else:
                right = jnp.concatenate(hidden_lows, axis=0)
            rights.append(right)
            part = contract(turned_weights[s], right, 1, 0)
            alongs.append(jnp.sum(part * all_gains[:, s][:, None], axis=0))
            alongs.append(jnp.sum(part * normed[s].astype(full), axis=0))
            part = part.reshape(places, ways, piece, group)
            kept = lax.dynamic_index_in_dim(part, way, 1, keepdims=False)
            if ways == 2:
                given = lax.dynamic_index_in_dim(part, 1 - way, 1, keepdims=False).astype(low)
                kept = kept + hid_swap(given, 1).astype(full)
            normed_grads.append(kept.reshape(mine, group))
        weighted = [normed_grads[s] * gains[s] for s in range(STREAMS)]
        means_back = sum_features(jnp.stack(alongs, axis=0)) / width
        gain_parts = [jnp.sum(g * u, axis=1) for g, u in zip(normed_grads, units)]
        stream_grads = [
            (weighted[s] - means_back[2 * s] - units[s] * means_back[2 * s + 1]) * inv_scales[s]
            for s in range(STREAMS)
        ]
        stream_grads[3] = stream_grads[3] + output_grad
        gain_parts = jnp.stack(gain_parts, axis=0)

        split = jnp.stack([v.astype(low).reshape(places, piece, group) for v in stream_grads], axis=1)
        attended, split = lax.optimization_barrier((attended, split))
        split = exchange(split)
        wide = w_query.shape[1] // ways
        operands = [rights[3]] + rights[:3] + [output_low, normed[3]] + normed[:3] + [attended]
        blocks = [(feats, [(5, 0, 0, i, wide)]) for i in range(0, rights[3].shape[0], wide)]
        blocks += [(feats, [(6 + s, 0, 1 + s, 0, wide)]) for s in range(3)]
        blocks += [(n_head, [(9, 0, 4, i, wide)]) for i in range(0, width, wide)]
        late_sum = chain_sums(operands, blocks, 1).reshape(ways, -1, feats, wide)
        split = jnp.concatenate([split[p] for p in range(places)], axis=-1).astype(full)
        mix_layers = mix_all.reshape(STREAMS, HIST, total_tokens)
        history_grad = sum(mix_layers[s][:, None] * split[s][None] for s in range(STREAMS))
        mix_parts = jnp.concatenate(
            [jnp.sum(split[s][None] * stored.astype(full), axis=1) for s in range(STREAMS)], axis=0
        )
        mix_parts = mix_parts.reshape(n_mix, dp * hid, block).transpose(1, 0, 2)

    history_grad = history_grad.swapaxes(1, 2)
    smalls = jnp.concatenate([mixer_grad_part, gain_parts], axis=0)
    late_sum, mix_parts, smalls = lax.optimization_barrier((late_sum, mix_parts, smalls))
    mix_parts = lax.all_to_all(mix_parts, ("dp", "hid"), split_axis=0, concat_axis=0, tiled=True)
    late_grads = assemble(late_sum, w_up, fused)
    w_down_grad = unturn(branch_sum.reshape(w_down.shape))
    bit = ways
    while bit < hid:
        smalls = smalls + hid_swap(smalls, bit)
        if bit == ways:
            late_grads, smalls = lax.optimization_barrier((late_grads, smalls))
        else:
            w_down_grad, smalls = lax.optimization_barrier((w_down_grad, smalls))
        bit *= 2
    w_up_grad, w_query_grad, w_key_grad, w_value_grad, w_out_grad = late_grads
    smalls = gather_ways(smalls.reshape(-1, places, piece), 2).reshape(-1, feats)
    w_mixer_grad = smalls[:n_inner].T
    norm_gains_grad = smalls[n_inner:].T
    mix_grad = jnp.sum(mix_parts, axis=0).T

    return (
        block_output,
        mix_next,
        history_grad,
        mix_grad,
        norm_gains_grad,
        w_query_grad,
        w_key_grad,
        w_value_grad,
        w_out_grad,
        w_up_grad,
        w_down_grad,
        w_mixer_grad,
        mixer_out_grad,
        sum_grad,
    )


def solution(mesh):
    everywhere = ("dp", "hid")
    placed = (
        P(None, None, everywhere),
        P(everywhere, None),
        P(everywhere),
        P("dp", None),
        P("dp", None),
        P("dp", None),
        P("dp", None),
        P("dp", None),
        P("dp", None),
        P("dp", None),
        P("dp", None),
        P(),
        P(),
        P(None, everywhere),
        P(everywhere, None),
    )
    return jax.shard_map(
        local,
        mesh=mesh,
        in_specs=placed,
        out_specs=(
            P(None, everywhere),
            P(everywhere, None),
            P(None, None, everywhere),
            P(everywhere, None),
            P("dp", None),
            P("dp", None),
            P("dp", None),
            P("dp", None),
            P("dp", None),
            P("dp", None),
            P("dp", None),
            P("dp", None),
            P(),
            P(),
        ),
        check_vma=False,
    )
```

```python
import functools
import math

import jax
import jax.numpy as jnp
from jax import lax
from jax.experimental import pallas as pl
from jax.experimental.pallas import tpu as pltpu
from jax.sharding import PartitionSpec as P

HEADS = 16
HEAD = 128
ROT = 32
HIST = 8
STREAMS = 4
CORES = 2
CHUNK = 1 << 15
SLACK = 6
TILE = 128
LATE_TILE = 256
LATE_CHUNK = 1 << 16
LATE_SLACK = 4
SPAN = 256
VMEM = 52 << 20
PULL_START = 2
PULL_GAP = 4
GRAD_GAP = 2

highest = lax.Precision.HIGHEST
rope_base = 10000.0
low = jnp.bfloat16
full = jnp.float32


def contract(left, right, left_dim, right_dim):
    return lax.dot_general(
        left, right, (((left_dim,), (right_dim,)), ((), ())), preferred_element_type=full
    )


def contract_high(left, right, left_dim, right_dim):
    return lax.dot_general(
        left,
        right,
        (((left_dim,), (right_dim,)), ((), ())),
        precision=highest,
        preferred_element_type=full,
    )


def batched(left, right, left_dim, right_dim):
    return lax.dot_general(
        left, right, (((left_dim,), (right_dim,)), ((0,), (0,))), preferred_element_type=full
    )


def gelu_exact(values_in):
    return jax.nn.gelu(values_in, approximate=False)


def core_swap(values_in):
    size = lax.axis_size("dp")
    return lax.ppermute(values_in, "dp", [(i, i ^ 1) for i in range(size)])


def outer_shift(values_in, step):
    size = lax.axis_size("dp")
    outer = size // CORES
    pairs = [
        (o * CORES + c, ((o + step) % outer) * CORES + c) for o in range(outer) for c in range(CORES)
    ]
    return lax.ppermute(values_in, "dp", pairs)


def hid_swap(values_in, bit):
    size = lax.axis_size("hid")
    return lax.ppermute(values_in, "hid", [(i, i ^ bit) for i in range(size)])


def ordered(first, values_in, other, axis):
    return jnp.stack(
        [jnp.where(first, values_in, other), jnp.where(first, other, values_in)], axis=axis
    )


def take(values_in, index):
    return lax.dynamic_index_in_dim(values_in, index, 0, keepdims=False)


def put(target, values_in, index):
    return lax.dynamic_update_index_in_dim(target, values_in, index, 0)


def split_ways():
    return 2 if HEADS // lax.axis_size("dp") >= 2 else 1


def gather_ways(values_in, axis):
    if split_ways() == 1:
        return jnp.expand_dims(values_in, axis)
    return ordered(lax.axis_index("hid") % 2 == 0, values_in, hid_swap(values_in, 1), axis)


def gather_dp(values_in):
    size = lax.axis_size("dp")
    outer = size // CORES
    me = lax.axis_index("dp")
    mine, core = me // CORES, me % CORES
    if outer == 2:
        held = ordered(mine == 0, values_in, outer_shift(values_in, 1), 0)
    else:
        held = jnp.zeros((outer,) + values_in.shape, values_in.dtype)
        held = put(held, values_in, mine)
        for step in range(1, outer):
            held = put(held, outer_shift(values_in, step), (mine - step) % outer)
    pair = ordered(core == 0, held, core_swap(held), 1)
    return pair.reshape((size,) + values_in.shape)


def gather_outer(values_in):
    steps = range(1, lax.axis_size("dp") // CORES)
    return [values_in] + [outer_shift(values_in, step) for step in steps]


def gather_cores(held):
    return [v for h in held for v in (h, core_swap(h))]


def gather_turns(values_in):
    return gather_cores(gather_outer(values_in))


def turn_source(turn):
    outer, me = lax.axis_size("dp") // CORES, lax.axis_index("dp")
    there = (me // CORES + outer - turn // CORES) % outer
    return there * CORES + (me + turn) % CORES


def turn_of(index):
    outer, me = lax.axis_size("dp") // CORES, lax.axis_index("dp")
    step = (me // CORES + outer - index // CORES) % outer
    return step * CORES + (me + index) % CORES


def sum_features(values_in):
    if split_ways() == 2:
        values_in = values_in + hid_swap(values_in, 1)
    parts = gather_dp(values_in)
    total = parts[0]
    for i in range(1, parts.shape[0]):
        total = total + parts[i]
    return total


def sum_tokens(values_in):
    size = lax.axis_size("hid")
    ways = split_ways()
    places = size // ways
    mine = lax.axis_index("hid") // ways
    held = put(jnp.zeros((places,) + values_in.shape, values_in.dtype), values_in, mine)
    for step in range(1, places):
        pairs = [(i, (i + step * ways) % size) for i in range(size)]
        held = put(held, lax.ppermute(values_in, "hid", pairs), (mine + places - step) % places)
    return jnp.sum(held, axis=0)


def gather_all(values_in):
    count = lax.axis_size("dp") * lax.axis_size("hid")
    copies = jnp.broadcast_to(values_in[None], (count,) + values_in.shape)
    held = lax.all_to_all(copies, ("dp", "hid"), split_axis=0, concat_axis=0, tiled=True)
    return held.transpose(1, 0, 2).reshape(values_in.shape[0], -1)


def scatter_dp(make):
    size = lax.axis_size("dp")
    outer = size // CORES
    me = lax.axis_index("dp")
    mine, core = me // CORES, me % CORES
    total = None
    for step in list(range(1, outer)) + [0]:
        there = (mine + step) % outer
        away = core_swap(make(there * CORES + 1 - core).astype(low))
        block = make(there * CORES + core) + away.astype(full)
        if step:
            block = outer_shift(block.astype(low), step).astype(full)
        total = block if total is None else total + block
    return total


def exchange(values_in):
    ways, size = split_ways(), lax.axis_size("hid")
    groups = None
    if ways > 1:
        groups = [[t * ways + w for t in range(size // ways)] for w in range(ways)]
    return lax.all_to_all(
        values_in, "hid", split_axis=0, concat_axis=0, tiled=True, axis_index_groups=groups
    )


def turn_heads(values_in, cosine, sine):
    half = ROT // 2
    front, back = values_in[:half], values_in[half:ROT]
    return jnp.concatenate(
        [front * cosine - back * sine, back * cosine + front * sine, values_in[ROT:]], axis=0
    )


def across(left, right, left_dim, right_dim):
    return lax.dot_general(
        left, right, (((left_dim,), (right_dim,)), ((), ())), preferred_element_type=full
    )


def attend_kernel(
    products_ref, cosine_ref, sine_ref, start_ref, heads_ref, attended_ref, tops_ref
):
    tokens = products_ref.shape[2]
    for s in range(2):
        turned = turn_heads(products_ref[s], cosine_ref[...], sine_ref[...])
        heads_ref[s] = turned.astype(low)
    heads_ref[2] = products_ref[2].astype(low)
    for first in range(0, tokens, SPAN):
        stop = first + SPAN
        span = slice(first, stop)
        scores, top = masked_scores(heads_ref, start_ref, first)
        weights = jnp.exp(scores - top)
        total = jnp.sum(weights, axis=0, keepdims=True)
        weights = (weights / total).astype(low)
        mixed = across(heads_ref[2, :, :stop], weights, 1, 0)
        attended_ref[:, span] = mixed.astype(low)
        tops_ref[0, 0:1, span] = top
        tops_ref[0, 1:2, span] = total


def masked_scores(heads_ref, start_ref, first):
    stop = first + SPAN
    span = slice(first, stop)
    scores = across(heads_ref[1, :, :stop], heads_ref[0, :, span], 0, 0) / math.sqrt(HEAD)
    key = lax.broadcasted_iota(jnp.int32, scores.shape, 0)
    query = lax.broadcasted_iota(jnp.int32, scores.shape, 1) + first
    seen = (key >= start_ref[:, span]) & (key <= query)
    scores = jnp.where(seen, scores, -1e30)
    return scores, jnp.max(scores, axis=0, keepdims=True)


def attend_back_kernel(
    heads_ref, gradient_ref, cosine_ref, sine_ref, start_ref, tops_ref, lows_ref, key_sum, value_sum
):
    tokens = heads_ref.shape[2]
    cosine, sine = cosine_ref[...], sine_ref[...]
    scale = 1.0 / math.sqrt(HEAD)
    key_sum[...] = jnp.zeros_like(key_sum)
    value_sum[...] = jnp.zeros_like(value_sum)
    for first in range(0, tokens, SPAN):
        stop = first + SPAN
        span = slice(first, stop)
        scores, _ = masked_scores(heads_ref, start_ref, first)
        probs = jnp.exp(scores - tops_ref[0, 0:1, span]) / tops_ref[0, 1:2, span]
        gradient = gradient_ref[:, span]
        change = across(heads_ref[2, :, :stop], gradient, 0, 0)
        row_total = jnp.sum(probs * change, axis=0, keepdims=True)
        change = (probs * (change - row_total)).astype(low)
        query = across(heads_ref[1, :, :stop], change, 1, 0) * scale
        lows_ref[0, :, span] = turn_heads(query, cosine[:, span], -sine[:, span]).astype(low)
        key_sum[:, :stop] = key_sum[:, :stop] + across(heads_ref[0, :, span], change, 1, 1) * scale
        value_sum[:, :stop] = value_sum[:, :stop] + across(gradient, probs.astype(low), 1, 1)
    lows_ref[1] = turn_heads(key_sum[...], cosine, -sine).astype(low)
    lows_ref[2] = value_sum[...].astype(low)


def attend(products, cosine, sine, start):
    _, n_heads, head, tokens = products.shape
    per_head = pl.BlockSpec((3, None, head, tokens), lambda h: (0, h, 0, 0))
    table = pl.BlockSpec(cosine.shape, lambda h: (0, 0))
    return pl.pallas_call(
        attend_kernel,
        grid=(n_heads,),
        out_shape=[
            jax.ShapeDtypeStruct(products.shape, low),
            jax.ShapeDtypeStruct((n_heads, head, tokens), low),
            jax.ShapeDtypeStruct((n_heads, 2, tokens), full),
        ],
        in_specs=[per_head, table, table, pl.BlockSpec(start.shape, lambda h: (0, 0))],
        out_specs=[
            per_head,
            pl.BlockSpec((None, head, tokens), lambda h: (h, 0, 0)),
            pl.BlockSpec((1, 2, tokens), lambda h: (h, 0, 0)),
        ],
        compiler_params=pltpu.CompilerParams(vmem_limit_bytes=40 << 20),
        cost_estimate=pl.CostEstimate(
            flops=4 * n_heads * head * tokens * tokens,
            bytes_accessed=10 * products.size,
            transcendentals=n_heads * tokens * tokens,
        ),
    )(products, cosine, sine, start)


def attend_back(heads, gradient, cosine, sine, start, tops):
    _, n_heads, head, tokens = heads.shape
    per_head = pl.BlockSpec((3, None, head, tokens), lambda h: (0, h, 0, 0))
    table = pl.BlockSpec(cosine.shape, lambda h: (0, 0))
    return pl.pallas_call(
        attend_back_kernel,
        grid=(n_heads,),
        out_shape=jax.ShapeDtypeStruct(heads.shape, low),
        in_specs=[
            per_head,
            pl.BlockSpec((None, head, tokens), lambda h: (h, 0, 0)),
            table,
            table,
            pl.BlockSpec(start.shape, lambda h: (0, 0)),
            pl.BlockSpec((1, 2, tokens), lambda h: (h, 0, 0)),
        ],
        out_specs=per_head,
        scratch_shapes=[pltpu.VMEM((head, tokens), full)] * 2,
        compiler_params=pltpu.CompilerParams(vmem_limit_bytes=40 << 20),
        cost_estimate=pl.CostEstimate(
            flops=10 * n_heads * head * tokens * tokens,
            bytes_accessed=6 * heads.size,
            transcendentals=n_heads * tokens * tokens,
        ),
    )(heads, gradient, cosine, sine, start, tops)


def forward_kernel(dims, *refs):
    places, piece, group, n_head, n_units = dims
    (send_ref, mom_ref, gains_ref, query_ref, key_ref, value_ref, up_ref), refs = refs[:7], refs[7:]
    cot_ref, refs = refs[0], refs[1:]
    (
        normed_ref,
        own_ref,
        residual_ref,
        own_shift_ref,
        scale_ref,
        active_ref,
        slope_ref,
        heads_ref,
        turned_ref,
        turned_up_ref,
        cot_out,
    ), refs = refs[:11], refs[11:]
    (
        devs,
        shift_ref,
        moms,
        joins,
        weights,
        core_out,
        core_in,
        outer_out,
        outer_in,
        mom_send,
        mom_recv,
        dev_send,
        dev_recv,
        way_send,
        way_recv,
        pair_send,
        pair_recv,
        join_send,
        join_recv,
        weight_sem,
        turned_sem,
        core_send,
        core_recv,
        outer_send,
        outer_recv,
        cot_send,
        cot_recv,
        cot_own,
    ) = refs
    count = weights.shape[0]
    ups = n_units // n_head
    index, hid = lax.axis_index("dp"), lax.axis_index("hid")
    outer, core = index // 2, index % 2
    place, way = hid // 2, hid % 2
    me = index * 2 + way
    partner = {"hid": hid + 1 - 2 * way}
    core_peer = {"dp": index + 1 - 2 * core}
    outer_peer = {"dp": (index + 2) % 4}

    def peer(k):
        return (place + k) % places

    def z_device(k):
        return {"hid": peer(k) * 2 + way}

    others = [(i, j) for i in range(4) for j in range(2) if i or j]

    def join_device(i, j):
        return {"dp": (index + i) % 4, "hid": place * 2 + (way + j) % 2}

    def weight_copy(unit, t):
        there = (1 - outer if t < 2 else outer) * 2 + (core if t % 2 else 1 - core)
        block = there * 2 + way
        if unit < ups:
            source, start = up_ref, block * n_units + unit * n_head
        else:
            source, start = (query_ref, key_ref, value_ref)[unit - ups], block * n_head
        start = pl.multiple_of(start, n_head)
        return pltpu.make_async_copy(
            source.at[:, pl.ds(start, n_head)], weights.at[unit, t], weight_sem.at[unit]
        )

    for unit in range(count):
        for t in range(4):
            weight_copy(unit, t).start()

    barrier = pltpu.get_barrier_semaphore()

    for k in range(1, places):
        greet(z_device(k))
    for i, j in others:
        greet(join_device(i, j))
    pl.semaphore_wait(barrier, places - 1 + len(others))

    def mom_copy(k, sender, target):
        return remote(
            mom_ref.at[target], moms.at[way, sender], mom_send, mom_recv.at[sender], z_device(k)
        )

    def dev_copy(s, k, sender, target):
        return remote(
            send_ref.at[target, s],
            devs.at[s, way, sender],
            dev_send,
            dev_recv.at[s, sender],
            z_device(k),
        )

    for k in range(1, places):
        mom_copy(k, place, peer(k)).start()
    for s in (3, 0, 1, 2):
        for k in range(1, places):
            dev_copy(s, k, place, peer(k)).start()
    for k in range(1, places):
        remote(cot_ref.at[peer(k)], cot_out.at[place], cot_send, cot_recv, z_device(k)).start()
    pltpu.make_async_copy(cot_ref.at[place], cot_out.at[place], cot_own).start()
    moms[way, place] = mom_ref[place]
    for s in range(STREAMS):
        devs[s, way, place] = send_ref[place, s]

    def way_copy(source, s, q):
        return remote(source, devs.at[s, way, q], way_send, way_recv.at[s], partner)

    def forward(s):
        way_copy(send_ref.at[place, s], s, place).start()
        for k in range(1, places):
            q = peer(k)
            dev_copy(s, k, q, q).wait_recv()
            way_copy(devs.at[s, way, q], s, q).start()

    def join_parts(means, parts, size):
        mean = means[0]
        for m in means[1:]:
            mean = mean + m
        mean = mean / len(means)
        total = parts[0]
        for v in parts[1:]:
            total = total + v
        for m in means:
            total = total + size * (m - mean) * (m - mean)
        return mean, total

    for k in range(1, places):
        mom_copy(k, peer(k), place).wait_recv()
    remote(moms.at[way], moms.at[way], pair_send, pair_recv, partner).start()
    mean, total = join_parts(
        [moms[way, q, :STREAMS, :] for q in range(places)],
        [moms[way, q, STREAMS:, :] for q in range(places)],
        piece,
    )
    joins[me, :STREAMS, :] = mean
    joins[me, STREAMS:, :] = total
    for i, j in others:
        remote(joins.at[me], joins.at[me], join_send, join_recv, join_device(i, j)).start()
    forward(3)
    n_others = len(others)
    remote(
        joins.at[pl.ds(0, n_others)], joins.at[pl.ds(0, n_others)], join_send, join_recv, partner
    ).wait_recv()
    remote(moms.at[way], moms.at[1 - way], pair_send, pair_recv, partner).wait_recv()
    mean, total = join_parts(
        [joins[i, :STREAMS, :] for i in range(n_others + 1)],
        [joins[i, STREAMS:, :] for i in range(n_others + 1)],
        piece * places,
    )
    scale = lax.rsqrt(total / (piece * places * (n_others + 1)) + 1e-05)
    for s in range(STREAMS):
        for q in range(places):
            for w in range(2):
                off = moms[w, q, s : s + 1, :] - mean[s : s + 1]
                shift_ref[s, 2 * q + w : 2 * q + w + 1, :] = off * scale[s : s + 1]
        shift_ref[s, 2 * places : 2 * places + 1, :] = scale[s : s + 1]
        scale_ref[s] = scale[s : s + 1]
        for q in range(places):
            first, second = [shift_ref[s, 2 * q + w : 2 * q + w + 1, :] for w in range(2)]
            own_shift_ref[s, q] = jnp.where(way == 0, first, second)

    def normalize(s):
        remote(devs.at[s, 1 - way], devs.at[s, 1 - way], way_send, way_recv.at[s], partner).wait_recv()
        size = shift_ref[s, 2 * places : 2 * places + 1, :]
        for q in range(places):
            for w in range(2):
                block = 2 * q + w
                rows = slice(block * piece, (block + 1) * piece)
                unit = devs[s, w, q].astype(full) * size + shift_ref[s, block : block + 1, :]
                normed_ref[s, rows, :] = (unit * gains_ref[s, rows, :]).astype(low)

    def core_copy(unit, half):
        return remote(
            core_out.at[unit, half],
            core_in.at[unit, half],
            core_send,
            core_recv.at[unit, half],
            core_peer,
        )

    def outer_copy(unit):
        return remote(
            outer_out.at[unit], outer_in.at[unit], outer_send, outer_recv.at[unit], outer_peer
        )

    def project(unit, carry):
        @pl.when(unit == 0)
        def _():
            normalize(3)
            forward(0)

        for s in (1, 2):

            @pl.when(unit == s)
            def _(s=s):
                forward(s)

        @pl.when(unit >= ups)
        def _():
            normalize(unit - ups)

        stream = jnp.where(unit < ups, 3, unit - ups)
        pltpu.make_async_copy(weights.at[unit], weights.at[unit], weight_sem.at[unit]).wait()

        def product(t):
            return lax.dot_general(
                weights[unit, t],
                normed_ref[stream],
                (((0,), (0,)), ((), ())),
                preferred_element_type=full,
            )

        def stage(k, carry):
            core_out[unit, k] = product(2 * k).astype(low)
            core_copy(unit, k).start()
            kept = product(2 * k + 1)
            core_copy(unit, k).wait_recv()
            kept = kept + core_in[unit, k].astype(full)

            @pl.when(k == 0)
            def _():
                outer_out[unit] = kept.astype(low)
                outer_copy(unit).start()

            @pl.when((k == 1) & (unit < ups))
            def _():
                slope_ref[pl.ds(pl.multiple_of(unit * n_head, n_head), n_head), :] = kept

            @pl.when((k == 1) & (unit >= ups))
            def _():
                heads_ref[unit - ups] = kept

            return carry

        lax.fori_loop(0, 2, stage, 0)
        return carry

    lax.fori_loop(0, count, project, 0)

    def turned_copies():
        for unit in range(count):
            for t in range(4):
                turn = 3 - t
                if unit < ups:
                    start = turn * n_units + unit * n_head
                    target = turned_up_ref.at[:, start : start + n_head]
                else:
                    target = turned_ref.at[unit - ups, :, turn * n_head : (turn + 1) * n_head]
                yield pltpu.make_async_copy(weights.at[unit, t], target, turned_sem)

    for copy in turned_copies():
        copy.start()
    for s in range(STREAMS):
        own_ref[s] = devs[s, way]
    for q in range(places):
        offset = moms[way, q, 3:4, :]
        residual_ref[q * piece : (q + 1) * piece, :] = devs[3, way, q].astype(full) + offset

    step = 32

    def finish_up(unit, carry):
        outer_copy(unit).wait_recv()

        def part(i, carry):
            inner = pl.ds(pl.multiple_of(i * step, step), step)
            rows = pl.ds(pl.multiple_of(unit * n_head + i * step, step), step)
            hidden = slope_ref[rows, :] + outer_in[unit, inner, :].astype(full)
            half = 0.5 + 0.5 * lax.erf(hidden * math.sqrt(0.5))
            active_ref[rows, :] = (hidden * half).astype(low)
            bell = jnp.exp(-0.5 * hidden * hidden) * (1.0 / math.sqrt(2.0 * math.pi))
            slope_ref[rows, :] = half + hidden * bell
            return carry

        return lax.fori_loop(0, n_head // step, part, carry)

    lax.fori_loop(0, ups, finish_up, 0)

    def finish_head(unit, carry):
        outer_copy(unit).wait_recv()
        heads_ref[unit - ups] = heads_ref[unit - ups] + outer_in[unit].astype(full)
        return carry

    lax.fori_loop(ups, count, finish_head, 0)

    def sent(ref, sem):
        remote(ref, ref, sem, join_recv, partner).wait_send()

    sent(moms.at[0, pl.ds(0, places - 1)], mom_send)
    sent(send_ref.at[pl.ds(0, places - 1)], dev_send)
    sent(send_ref, way_send)
    sent(moms.at[0], pair_send)
    sent(joins.at[pl.ds(0, n_others)], join_send)
    sent(core_out, core_send)
    sent(outer_out, outer_send)
    moved = cot_ref.at[pl.ds(0, places - 1)]
    sent(moved, cot_send)
    remote(moved, moved, cot_send, cot_recv, partner).wait_recv()
    pltpu.make_async_copy(cot_ref.at[0], cot_out.at[0], cot_own).wait()
    pltpu.make_async_copy(weights, weights, turned_sem).wait()


def forward_projections(deviations, moments, gains, w_query, w_key, w_value, w_up, cotangent):
    places, _, piece, group = deviations.shape
    feats = gains.shape[1]
    n_head = w_query.shape[1] // 8
    n_units = w_up.shape[1] // 8
    count = n_units // n_head + 3
    vmem, dma = pltpu.VMEM, pltpu.SemaphoreType.DMA
    out_types = [
        ((STREAMS, feats, group), low),
        ((STREAMS, places, piece, group), low),
        ((places * piece, group), full),
        ((STREAMS, places, 1, group), full),
        ((STREAMS, 1, group), full),
        ((n_units, group), low),
        ((n_units, group), full),
        ((3, n_head, group), full),
        ((3, feats, 4 * n_head), low),
        ((feats, 4 * n_units), low),
        (cotangent.shape, low),
    ]
    spaces = [vmem] * 8 + [pl.ANY] * 3
    return pl.pallas_call(
        functools.partial(forward_kernel, (places, piece, group, n_head, n_units)),
        out_shape=[jax.ShapeDtypeStruct(*t) for t in out_types],
        in_specs=[pl.BlockSpec(memory_space=vmem)] * 3 + [pl.BlockSpec(memory_space=pl.ANY)] * 5,
        out_specs=[pl.BlockSpec(memory_space=m) for m in spaces],
        scratch_shapes=[
            vmem((STREAMS, 2, places, piece, group), low),
            vmem((STREAMS, 2 * places + 8, group), full),
            vmem((2, places, 2 * STREAMS, group), full),
            vmem((8, 2 * STREAMS, group), full),
            vmem((count, 4, feats, n_head), low),
            vmem((count, 2, n_head, group), low),
            vmem((count, 2, n_head, group), low),
            vmem((count, n_head, group), low),
            vmem((count, n_head, group), low),
            dma,
            dma((places,)),
            dma,
            dma((STREAMS, places)),
            dma,
            dma((STREAMS,)),
            dma,
            dma,
            dma,
            dma,
            dma((count,)),
            dma,
            dma,
            dma((count, 2)),
            dma,
            dma((count,)),
            dma,
            dma,
            dma,
        ],
        compiler_params=pltpu.CompilerParams(
            collective_id=7, has_side_effects=True, vmem_limit_bytes=62 << 20
        ),
        cost_estimate=pl.CostEstimate(
            flops=8 * count * n_head * feats * group,
            bytes_accessed=300 << 20,
            transcendentals=2 * n_units * group,
        ),
    )(
        deviations,
        moments,
        gains,
        w_query,
        w_key,
        w_value,
        w_up,
        cotangent,
    )


def remote(source, target, send, recv, device):
    return pltpu.make_async_remote_copy(
        src_ref=source,
        dst_ref=target,
        send_sem=send,
        recv_sem=recv,
        device_id=device,
        device_id_type=pl.DeviceIdType.MESH,
    )


def greet(device):
    pl.semaphore_signal(
        pltpu.get_barrier_semaphore(),
        inc=1,
        device_id=device,
        device_id_type=pl.DeviceIdType.MESH,
    )


def chain_place(ways, places):
    last = places - 1
    me = lax.axis_index("hid")
    if ways == 2:
        place, way = me // 2, me % 2
        return place, way, me + 2, me - 2, me + 1 - 2 * way
    odd, half = me % 2, places // 2
    place = (1 - odd) * (me // 2) + odd * (last - me // 2)
    turn_up = (place + 1) // half
    turn_down = (place - 1 + places) // half - 2
    above = (1 - turn_up) * 2 * (place + 1) + turn_up * (2 * (last - place - 1) + 1)
    below = (1 - turn_down) * 2 * (place - 1) + turn_down * (2 * (last - place + 1) + 1)
    return place, 0, above, below, me


def chain_semaphores(count):
    dma = pltpu.SemaphoreType.DMA
    return [dma, dma((count,)), dma, dma((count,)), dma, dma, dma, dma, dma((count,))]


def chain_loop(ways, places, out_ref, own, landed, semaphores, compute, slack, hook=None, far=None):
    (
        up_send,
        up_recv,
        down_send,
        down_recv,
        side_send,
        side_recv,
        kept,
        far_send,
        far_recv,
    ) = semaphores
    count, depth = landed.shape[:2]
    per_tile = own.shape[0] // depth
    last = places - 1
    root = last if far is None else places // 2
    place, way, above, below, beside = chain_place(ways, places)
    above, below, beside = {"hid": above}, {"hid": below}, {"hid": beside}

    def send_in(i):
        @pl.when(place < root)
        def _():
            remote(landed.at[i], landed.at[i], up_send, up_recv.at[i], above).start()

        if far is not None:

            @pl.when(place == root + 1)
            def _():
                remote(landed.at[i], far.at[i], up_send, far_recv.at[i], below).start()

            @pl.when(place > root + 1)
            def _():
                remote(landed.at[i], landed.at[i], up_send, up_recv.at[i], below).start()

    def send_out(source, i):
        def to(device, send):
            remote(source, out_ref.at[way, i], send, down_recv.at[i], device).start()

        @pl.when((place <= root) & (place > 0))
        def _():
            to(below, down_send)

        if far is not None:

            @pl.when((place >= root) & (place < last))
            def _():
                to(above, far_send)

        if ways == 2:
            remote(source, out_ref.at[way, i], side_send, side_recv, beside).start()

    def upward(i):
        @pl.when(i % per_tile == 0)
        def _():
            compute(i // per_tile)

        mine = own[pl.ds(pl.multiple_of(i % per_tile * depth, depth), depth), :]
        ends = place == 0 if far is None else (place == 0) | (place == last)

        @pl.when(ends)
        def _():
            landed[i] = mine.astype(low)

        @pl.when(jnp.logical_not(ends))
        def _():
            remote(landed.at[i], landed.at[i], up_send, up_recv.at[i], above).wait_recv()
            total = landed[i].astype(full) + mine
            if far is None:
                landed[i] = total.astype(low)
            else:

                @pl.when(place != root)
                def _():
                    landed[i] = total.astype(low)

                @pl.when(place == root)
                def _():
                    remote(far.at[i], far.at[i], up_send, far_recv.at[i], above).wait_recv()
                    landed[i] = (total + far[i].astype(full)).astype(low)

        @pl.when(place != root)
        def _():
            send_in(i)

        @pl.when(place == root)
        def _():
            send_out(landed.at[i], i)
            pltpu.make_async_copy(landed.at[i], out_ref.at[way, i], kept).start()

    def downward(i):
        done = out_ref.at[way, i]
        remote(done, done, down_send, down_recv.at[i], below).wait_recv()
        send_out(done, i)

    away = root - place if far is None else jnp.where(place < root, root - place, place - root)
    lag = slack * away + 2

    def step(i, carry):
        @pl.when(i < count)
        def _():
            upward(i)

        behind = i - lag

        @pl.when((behind >= 0) & (behind < count) & (place != root))
        def _():
            downward(behind)

        if hook is not None:
            hook(i)
        return carry

    lax.fori_loop(0, count + slack * root + 2, step, 0)

    def sent(sem):
        remote(landed, landed, sem, side_recv, beside).wait_send()

    @pl.when(place != root)
    def _():
        sent(up_send)

    @pl.when((place <= root) & (place > 0))
    def _():
        sent(down_send)

    if far is not None:

        @pl.when((place >= root) & (place < last))
        def _():
            sent(far_send)

    @pl.when(place == root)
    def _():
        pltpu.make_async_copy(landed, out_ref.at[way], kept).wait()

    if ways == 2:
        sent(side_send)
        remote(landed, landed, side_send, side_recv, beside).wait_recv()


def chain_kernel(ways, places, blocks, n_operands, *refs):
    operand_refs, out_ref, refs = refs[:n_operands], refs[n_operands], refs[n_operands + 1 :]
    operands, (own, landed, far, fetched, *semaphores) = refs[:n_operands], refs[n_operands:]
    last = places - 1
    place, way, above, below, beside = chain_place(ways, places)

    def fetch(n):
        return pltpu.make_async_copy(operand_refs[n], operands[n], fetched.at[n])

    for n in range(n_operands):
        fetch(n).start()

    barrier = pltpu.get_barrier_semaphore()

    @pl.when(place > 0)
    def _():
        greet({"hid": below})

    @pl.when(place < last)
    def _():
        greet({"hid": above})

    if ways == 2:
        greet({"hid": beside})
    met = jnp.where(place > 0, 1, 0) + jnp.where(place < last, 1, 0) + (ways - 1)
    pl.semaphore_wait(barrier, met)

    def compute(tile):
        seen, first = set(), 0
        for rows, segments in blocks:
            start = first
            first = first + rows // TILE
            fresh = [n for seg in segments for n in (seg[0], seg[2])]
            fresh = [n for n in dict.fromkeys(fresh) if n not in seen]
            seen.update(fresh)

            @pl.when(tile == start)
            def _(fresh=fresh):
                for n in fresh:
                    fetch(n).wait()

            @pl.when((tile >= start) & (tile < first))
            def _(start=start, segments=segments):
                column = 0
                for left, left_row, right, right_row, size in segments:
                    row = pl.multiple_of(left_row + (tile - start) * TILE, TILE)
                    own[:, column : column + size] = lax.dot_general(
                        operands[left][pl.ds(row, TILE), :],
                        operands[right][right_row : right_row + size, :],
                        (((1,), (1,)), ((), ())),
                        preferred_element_type=full,
                    )
                    column += size

    chain_loop(ways, places, out_ref, own, landed, semaphores, compute, SLACK, far=far)


def chain_sum(operands, blocks, collective_id):
    ways, size = split_ways(), lax.axis_size("hid")
    columns = sum(seg[4] for seg in blocks[0][1])
    rows = sum(block[0] for block in blocks)
    depth = max(16, CHUNK // columns)
    count = rows // depth
    tokens = operands[0].shape[1]
    return pl.pallas_call(
        functools.partial(chain_kernel, ways, size // ways, blocks, len(operands)),
        out_shape=jax.ShapeDtypeStruct((ways, count, depth, columns), low),
        in_specs=[pl.BlockSpec(memory_space=pl.ANY)] * len(operands),
        out_specs=pl.BlockSpec(memory_space=pl.ANY),
        scratch_shapes=[pltpu.VMEM(v.shape, low) for v in operands]
        + [
            pltpu.VMEM((TILE, columns), full),
            pltpu.VMEM((count, depth, columns), low),
            pltpu.VMEM((count, depth, columns), low),
            pltpu.SemaphoreType.DMA((len(operands),)),
        ]
        + chain_semaphores(count),
        compiler_params=pltpu.CompilerParams(
            collective_id=collective_id, has_side_effects=True, vmem_limit_bytes=60 << 20
        ),
        cost_estimate=pl.CostEstimate(
            flops=2 * rows * columns * tokens,
            bytes_accessed=300 * rows * columns,
            transcendentals=0,
        ),
    )(*operands)


def branch_kernel(dims, *refs):
    places, piece, group = dims
    (attended_ref, active_ref, residual_ref, mixer_ref, out_w_ref, down_w_ref), refs = refs[:6], refs[6:]
    (output_ref, rounded_ref, sums_ref, turned_out_ref, turned_down_ref), refs = refs[:5], refs[5:]
    (
        weights,
        sums,
        core_out,
        core_in,
        outer_out,
        outer_in,
        side_out,
        side_in,
        parts_out,
        parts_in,
        totals,
        weight_sem,
        turned_sem,
        core_send,
        core_recv,
        outer_send,
        outer_recv,
        side_send,
        side_recv,
        part_send,
        part_recv,
        total_send,
        total_recv,
    ) = refs
    index, hid = lax.axis_index("dp"), lax.axis_index("hid")
    outer, core = index // 2, index % 2
    place, way = hid // 2, hid % 2
    me = index * 2 + way
    partner = {"hid": hid + 1 - 2 * way}
    core_peer = {"dp": index + 1 - 2 * core}
    outer_peer = {"dp": (index + 2) % 4}
    others = [(i, j) for i in range(4) for j in range(2) if i or j]
    n_head, n_units = attended_ref.shape[0], active_ref.shape[0]
    feats = weights.shape[2]
    wide = group // 8

    def peer(i, j):
        there, other = (index + i) % 4, (way + j) % 2
        return there * 2 + other, {"dp": there, "hid": place * 2 + other}

    def weight_copies(t):
        there = (1 - outer if t < 2 else outer) * 2 + (core if t % 2 else 1 - core)
        columns = pl.ds(pl.multiple_of(there * feats, feats), feats)
        for ref, first, size in ((out_w_ref, 0, n_head), (down_w_ref, n_head, n_units)):
            rows = pl.ds(pl.multiple_of(way * size, size), size)
            yield pltpu.make_async_copy(
                ref.at[rows, columns], weights.at[t, first : first + size], weight_sem.at[t]
            )

    def turned_copies(t):
        columns = pl.ds(pl.multiple_of((3 - t) * feats, feats), feats)
        for ref, first, size in ((turned_out_ref, 0, n_head), (turned_down_ref, n_head, n_units)):
            yield pltpu.make_async_copy(
                weights.at[t, first : first + size], ref.at[:, columns], turned_sem
            )

    for t in range(4):
        for copy in weight_copies(t):
            copy.start()
    for i, j in others:
        greet(peer(i, j)[1])
    pl.semaphore_wait(pltpu.get_barrier_semaphore(), len(others))

    def halves(t, target, kind):
        pltpu.make_async_copy(weights.at[t], weights.at[t], weight_sem.at[t]).wait()
        product = across(weights[t, :n_head, :], attended_ref[...], 0, 0)
        product = product + across(weights[t, n_head:, :], active_ref[...], 0, 0)
        for q in range(places):
            first = product[2 * q * piece : (2 * q + 1) * piece]
            second = product[(2 * q + 1) * piece : (2 * q + 2) * piece]
            rows = slice(q * piece, (q + 1) * piece)
            target[0, rows, :] = jnp.where(way == 0, second, first).astype(kind)
            target[1, rows, :] = jnp.where(way == 0, first, second).astype(kind)
        for copy in turned_copies(t):
            copy.start()

    def core_copy(stage, half):
        return remote(
            core_out.at[stage, half],
            core_in.at[stage, half],
            core_send,
            core_recv.at[stage, half],
            core_peer,
        )

    def outer_copy(half):
        return remote(
            outer_out.at[half], outer_in.at[half], outer_send, outer_recv.at[half], outer_peer
        )

    def stage(k, carry):
        halves(2 * k, core_out.at[k], low)
        for half in range(2):
            core_copy(k, half).start()
        halves(2 * k + 1, sums.at[k], full)
        for half in range(2):
            core_copy(k, half).wait_recv()
            sums[k, half] = sums[k, half] + core_in[k, half].astype(full)

            @pl.when(k == 0)
            def _(half=half):
                outer_out[half] = sums[0, half].astype(low)
                outer_copy(half).start()

        return carry

    lax.fori_loop(0, 2, stage, 0)
    kept = sums.at[1]
    kept[1] = kept[1] + residual_ref[...]
    side = remote(side_out, side_in, side_send, side_recv, partner)
    outer_copy(0).wait_recv()
    side_out[...] = (kept[0] + outer_in[0].astype(full)).astype(low)
    side.start()
    outer_copy(1).wait_recv()
    kept[1] = kept[1] + outer_in[1].astype(full)
    side.wait_recv()
    output = kept[1] + side_in[...].astype(full)
    output_ref[...] = output
    rounded = output.astype(low)
    rounded_ref[...] = rounded

    mixed = jnp.dot(mixer_ref[...], rounded, preferred_element_type=full)
    square = jnp.sum(output * output, axis=0, keepdims=True)
    row = lax.broadcasted_iota(jnp.int32, mixed.shape, 0)
    mixed = jnp.where(row == mixed.shape[0] - 1, square, mixed)
    for b in range(8):
        parts_out[b] = mixed[:, b * wide : (b + 1) * wide]
    parts_in[me] = parts_out[me]
    for i, j in others:
        slot, device = peer(i, j)
        remote(parts_out.at[slot], parts_in.at[me], part_send, part_recv, device).start()
    some = pl.ds(0, len(others))

    def whole(ref, send, recv):
        return remote(ref.at[some], ref.at[some], send, recv, partner)

    whole(parts_in, part_send, part_recv).wait_recv()
    total = parts_in[0]
    for b in range(1, 8):
        total = total + parts_in[b]
    totals[me] = total
    for i, j in others:
        remote(totals.at[me], totals.at[me], total_send, total_recv, peer(i, j)[1]).start()
    whole(totals, total_send, total_recv).wait_recv()
    for b in range(8):
        sums_ref[:, b * wide : (b + 1) * wide] = totals[b]

    whole(parts_out, part_send, part_recv).wait_send()
    whole(totals, total_send, total_recv).wait_send()
    remote(core_out, core_out, core_send, side_recv, partner).wait_send()
    remote(outer_out, outer_out, outer_send, side_recv, partner).wait_send()
    side.wait_send()
    pltpu.make_async_copy(weights, weights, turned_sem).wait()


def add_branches(places, attended, active, residual, mixer_rows, w_out, w_down):
    mine, group = residual.shape
    n_head, n_units = attended.shape[0], active.shape[0]
    feats = w_out.shape[0]
    n_sums = 48
    table = jnp.zeros((n_sums, mine), low).at[: mixer_rows.shape[1]].set(mixer_rows.T)
    vmem, dma = pltpu.VMEM, pltpu.SemaphoreType.DMA
    out_types = [
        ((mine, group), full),
        ((mine, group), low),
        ((n_sums, group), full),
        ((n_head, w_out.shape[1]), low),
        ((n_units, w_down.shape[1]), low),
    ]
    spaces = [vmem] * 3 + [pl.ANY] * 2
    block = (2, mine, group)
    slots = (8, n_sums, group // 8)
    return pl.pallas_call(
        functools.partial(branch_kernel, (places, mine // places, group)),
        out_shape=[jax.ShapeDtypeStruct(*t) for t in out_types],
        in_specs=[pl.BlockSpec(memory_space=vmem)] * 4 + [pl.BlockSpec(memory_space=pl.ANY)] * 2,
        out_specs=[pl.BlockSpec(memory_space=m) for m in spaces],
        scratch_shapes=[
            vmem((4, n_head + n_units, feats), low),
            vmem((2,) + block, full),
            vmem((2,) + block, low),
            vmem((2,) + block, low),
            vmem(block, low),
            vmem(block, low),
            vmem(block[1:], low),
            vmem(block[1:], low),
            vmem(slots, full),
            vmem(slots, full),
            vmem(slots, full),
            dma((4,)),
            dma,
            dma,
            dma((2, 2)),
            dma,
            dma((2,)),
            dma,
            dma,
            dma,
            dma,
            dma,
            dma,
        ],
        compiler_params=pltpu.CompilerParams(
            collective_id=8, has_side_effects=True, vmem_limit_bytes=56 << 20
        ),
        cost_estimate=pl.CostEstimate(
            flops=8 * (n_head + n_units) * feats * group, bytes_accessed=100 << 20, transcendentals=0
        ),
    )(attended, active, residual, table, w_out, w_down)


def late_kernel(dims, *refs):
    places, piece, group, n_head, n_units = dims
    (
        hidden_ref,
        hidden_far_ref,
        lows_ref,
        lows_far_ref,
        output_low_ref,
        attended_ref,
        normed_ref,
        turned_ref,
        turned_up_ref,
        devs_ref,
        output_grad_ref,
        shifts,
        scales,
        gains,
    ), refs = refs[:14], refs[14:]
    (out_ref, split_ref, gain_ref), refs = refs[:3], refs[3:]
    (
        hidden,
        lows,
        output_low,
        attended,
        normed,
        turned,
        turned_up,
        devs,
        output_grad,
        kept,
        given,
        taken,
        grads,
        joins,
        totals,
        own,
        pulled,
        landed,
        fetched,
        core_send,
        core_recv,
        side_send,
        side_recv,
        join_send,
        join_recv,
        place_send,
        place_recv,
        own_copy,
        *semaphores,
    ) = refs
    index, hid = lax.axis_index("dp"), lax.axis_index("hid")
    core = index % 2
    place, way = hid // 2, hid % 2
    me = index * 2 + way
    partner = {"hid": hid + 1 - 2 * way}
    core_peer = {"dp": index + 1 - 2 * core}
    others = [(i, j) for i in range(4) for j in range(2) if i or j]
    wide = own.shape[1]
    feats = normed.shape[1]

    def join_device(i, j):
        return {"dp": (index + i) % 4, "hid": place * 2 + (way + j) % 2}

    def head_rows(turn):
        return slice(turn * n_head, (turn + 1) * n_head)

    def unit_rows(turn):
        return slice(turn * n_units, (turn + 1) * n_units)

    fetches = [
        [(output_low_ref, output_low), (attended_ref, attended), (normed_ref, normed)],
        [(hidden_ref, hidden.at[unit_rows(0)])],
        [
            (hidden_far_ref, hidden.at[unit_rows(2)]),
            (turned_ref, turned),
            (turned_up_ref, turned_up),
            (devs_ref, devs),
            (output_grad_ref, output_grad),
        ]
        + [
            (source.at[head_rows(s)], lows.at[s, head_rows(turn)])
            for s in range(3)
            for turn, source in ((0, lows_ref), (2, lows_far_ref))
        ],
    ]

    def fetch(stage):
        return [pltpu.make_async_copy(a, b, fetched.at[stage, n]) for n, (a, b) in enumerate(fetches[stage])]

    for stage in range(len(fetches)):
        for copy in fetch(stage):
            copy.start()

    for k in range(1, places):
        greet({"hid": (place + k) % places * 2 + way})
    for i, j in others:
        greet(join_device(i, j))
    pl.semaphore_wait(pltpu.get_barrier_semaphore(), places - 1 + len(others))

    def core_copies(far):
        source, heads = (hidden_far_ref, lows_far_ref) if far else (hidden_ref, lows_ref)
        turn = 3 if far else 1
        yield remote(source, hidden.at[unit_rows(turn)], core_send.at[far], core_recv.at[far], core_peer)
        for s in range(3):
            yield remote(
                heads.at[head_rows(s)],
                lows.at[s, head_rows(turn)],
                core_send.at[2 + far],
                core_recv.at[2 + far],
                core_peer,
            )

    for far in range(2):
        for copy in core_copies(far):
            copy.start()

    def wait_cores():
        for far in range(2):
            remote(hidden_ref, hidden_ref, core_send.at[far], core_recv.at[far], core_peer).wait_recv()
            remote(lows_ref, lows_ref, core_send.at[2 + far], core_recv.at[2 + far], core_peer).wait_recv()

    per_block = feats // LATE_TILE
    per_out = n_head // LATE_TILE

    def compute(tile):
        @pl.when(tile == 0)
        def _():
            for copy in fetch(0):
                copy.wait()

        @pl.when(tile == per_block)
        def _():
            for copy in fetch(1):
                copy.wait()

        inner = tile % per_block

        def product(left, right):
            own[...] = lax.dot_general(
                left, right, (((1,), (1,)), ((), ())), preferred_element_type=full
            )

        def rows(n):
            return pl.ds(pl.multiple_of(n * LATE_TILE, LATE_TILE), LATE_TILE)

        @pl.when(tile < per_block)
        def _():
            half = pl.ds(pl.multiple_of(inner // per_out * wide, wide), wide)
            product(attended[rows(inner % per_out), :], output_low[half, :])

        block = tile // per_block

        @pl.when((block >= 1) & (block < 5))
        def _():
            turn = (block - 1) // 2 + (block - 1) % 2 * 2
            units = pl.ds(pl.multiple_of(turn * n_units, n_units), n_units)
            product(normed[3, rows(inner), :], hidden[units, :])

        @pl.when(block >= 5)
        def _():
            product(normed[block - 5, rows(inner), :], lows[block - 5])

    totals[...] = jnp.zeros_like(totals)

    def side_copy(s, r):
        return remote(given.at[s, r], taken.at[s, r], side_send, side_recv.at[s], partner)

    def pull(s):
        @pl.when(s < 3)
        def _():
            pulled[...] = jnp.dot(turned[s], lows[s], preferred_element_type=full)

        @pl.when(s == 3)
        def _():
            pulled[...] = jnp.zeros_like(pulled)

            def add_turn(turn, carry):
                units = pl.ds(pl.multiple_of(turn * n_units, n_units), n_units)
                pulled[...] += jnp.dot(
                    turned_up[:, units], hidden[units, :], preferred_element_type=full
                )
                return carry

            lax.fori_loop(0, 4, add_turn, 0)

        def use(r, carry):
            rows = pl.ds(pl.multiple_of(2 * piece * r, 2 * piece), 2 * piece)
            here = pulled[rows, :]
            totals[s, 0:1, :] = totals[s, 0:1, :] + jnp.sum(
                here * gains[s, rows, :], axis=0, keepdims=True
            )
            totals[s, 1:2, :] = totals[s, 1:2, :] + jnp.sum(
                here * normed[s, rows, :].astype(full), axis=0, keepdims=True
            )
            first = way == 0
            kept[s, r] = jnp.where(first, here[:piece], here[piece:])
            given[s, r] = jnp.where(first, here[piece:], here[:piece]).astype(low)
            side_copy(s, r).start()
            return carry

        lax.fori_loop(0, places, use, 0)

    def share_totals():
        joins[me] = totals[...]
        for i, j in others:
            remote(joins.at[me], joins.at[me], join_send, join_recv, join_device(i, j)).start()

    def sum_totals():
        some = joins.at[pl.ds(0, len(others))]
        remote(some, some, join_send, join_recv, partner).wait_recv()
        total = joins[0]
        for i in range(1, len(others) + 1):
            total = total + joins[i]
        totals[...] = total / (feats * 4)

    def stream_grad(s, r):
        @pl.when(r == 0)
        def _():
            remote(given.at[s], taken.at[s], side_send, side_recv.at[s], partner).wait_recv()

        gradient = kept[s, r] + taken[s, r].astype(full)
        unit = devs[s, r].astype(full) * scales[s] + shifts[s, r]
        gain_ref[s, r] = jnp.sum(gradient * unit, axis=1, keepdims=True)
        rows = pl.ds(pl.multiple_of((2 * r + way) * piece, piece), piece)
        result = gradient * gains[s, rows, :] - totals[s, 0:1, :] - unit * totals[s, 1:2, :]
        extra = output_grad[r] * jnp.where(s == 3, 1.0, 0.0)
        grads[s, r] = (result * scales[s] + extra).astype(low)

        @pl.when(r == place)
        def _():
            pltpu.make_async_copy(grads.at[s, r], split_ref.at[s, place], own_copy).start()

        @pl.when(r != place)
        def _():
            remote(
                grads.at[s, r],
                split_ref.at[s, place],
                place_send,
                place_recv,
                {"hid": r * 2 + way},
            ).start()

    n_pulls = STREAMS * places
    middle = PULL_START + PULL_GAP * STREAMS
    resume = middle + 8

    def hook(i):
        @pl.when(i == PULL_START)
        def _():
            for copy in fetch(2):
                copy.wait()
            wait_cores()

        k = (i - PULL_START) // PULL_GAP

        @pl.when((i >= PULL_START) & (i < middle) & ((i - PULL_START) % PULL_GAP == 0))
        def _():
            pull(k)

        @pl.when(i == middle)
        def _():
            share_totals()

        @pl.when(i == resume)
        def _():
            sum_totals()

        n = (i - resume) // GRAD_GAP

        @pl.when((i >= resume) & (n < n_pulls) & ((i - resume) % GRAD_GAP == 0))
        def _():
            stream_grad(n // places, n % places)

    chain_loop(2, places, out_ref, own, landed, semaphores, compute, LATE_SLACK, hook)

    def sent(ref, sem):
        remote(ref, ref, sem, join_recv, partner).wait_send()

    for far in range(2):
        sent(hidden_ref, core_send.at[far])
        sent(lows_ref, core_send.at[2 + far])
    sent(given, side_send)
    sent(joins.at[pl.ds(0, len(others))], join_send)
    moved = grads.at[pl.ds(0, places - 1)]
    sent(moved, place_send)
    remote(moved, moved, place_send, place_recv, partner).wait_recv()
    mine = grads.at[0]
    pltpu.make_async_copy(mine, mine, own_copy).wait()


def late_sums(operands, tables, collective_id):
    hidden, _, lows, _, output_low, attended, normed = operands[:7]
    _, places, piece, group = operands[9].shape
    feats = normed.shape[1]
    n_units, n_head = hidden.shape[0], attended.shape[0]
    wide = n_units
    rows = 8 * feats
    depth = max(16, LATE_CHUNK // wide)
    count = rows // depth
    vmem, dma = pltpu.VMEM, pltpu.SemaphoreType.DMA
    block = (STREAMS, places, piece, group)
    outs = [
        jax.ShapeDtypeStruct((2, count, depth, wide), low),
        jax.ShapeDtypeStruct(block, low),
        jax.ShapeDtypeStruct((STREAMS, places, piece, 1), full),
    ]
    any_space, vmem_space = pl.BlockSpec(memory_space=pl.ANY), pl.BlockSpec(memory_space=vmem)
    total, split, gain_parts = pl.pallas_call(
        functools.partial(late_kernel, (places, piece, group, n_head, n_units)),
        out_shape=outs,
        in_specs=[any_space] * len(operands) + [vmem_space] * len(tables),
        out_specs=[any_space, any_space, vmem_space],
        scratch_shapes=[
            vmem((4 * n_units, group), low),
            vmem((3, 4 * n_head, group), low),
            vmem(output_low.shape, low),
            vmem(attended.shape, low),
            vmem(normed.shape, low),
            vmem(operands[7].shape, low),
            vmem(operands[8].shape, low),
            vmem(block, low),
            vmem(block[1:], full),
            vmem(block, full),
            vmem(block, low),
            vmem(block, low),
            vmem(block, low),
            vmem((8, STREAMS, 2, group), full),
            vmem((STREAMS, 2, group), full),
            vmem((LATE_TILE, wide), full),
            vmem((feats, group), full),
            vmem((count, depth, wide), low),
            dma((3, 11)),
            dma((4,)),
            dma((4,)),
            dma,
            dma((STREAMS,)),
            dma,
            dma,
            dma,
            dma,
            dma,
        ]
        + chain_semaphores(count),
        compiler_params=pltpu.CompilerParams(
            collective_id=collective_id, has_side_effects=True, vmem_limit_bytes=63 << 20
        ),
        cost_estimate=pl.CostEstimate(
            flops=4 * rows * wide * group, bytes_accessed=900 << 20, transcendentals=0
        ),
    )(*operands, *tables)
    return total.reshape(2, 8, feats, wide), split, gain_parts


def chain_sums(operands, blocks, collective_id):
    groups, held, size = [[]], set(), 0
    for rows, segments in blocks:
        used = {n for seg in segments for n in (seg[0], seg[2])}
        more = sum(2 * operands[n].size for n in used - held)
        more += 4 * rows * sum(seg[4] for seg in segments)
        if groups[-1] and size + more > VMEM:
            groups.append([])
            held, size = set(), 0
            more = sum(2 * operands[n].size for n in used)
            more += 4 * rows * sum(seg[4] for seg in segments)
        groups[-1].append((rows, segments))
        held |= used
        size += more
    totals = []
    for i, group in enumerate(groups):
        used = sorted({n for _, segments in group for seg in segments for n in (seg[0], seg[2])})
        place = {n: k for k, n in enumerate(used)}
        own = [
            (rows, [(place[a], b, place[c], d, e) for a, b, c, d, e in segments])
            for rows, segments in group
        ]
        total = chain_sum([operands[n] for n in used], own, collective_id + i)
        totals.append(total.reshape(total.shape[0], -1, total.shape[3]))
    return totals[0] if len(totals) == 1 else jnp.concatenate(totals, axis=1)


def assemble_kernel(ways, dp, fused, own_ref, *refs):
    halves, (up_ref, *head_refs, out_ref) = refs[:ways], refs[ways:]
    rows, wide = own_ref.shape[2:]
    size = up_ref.shape[1] // dp // ways
    blocks = dp * size // wide
    own = wide // dp
    feats = out_ref.shape[1] // dp
    for d in range(dp):
        turn = turn_of(d)
        for w in range(ways):
            start = turn * size
            lanes = pl.ds(pl.multiple_of(start % wide, size), size)
            place = (d * ways + w) * size
            up_block = 1 + turn // 2 + turn % 2 * 2 if fused else start // wide
            up_ref[:, place : place + size] = own_ref[w, up_block, :, lanes].astype(full)
            for s, ref in enumerate(head_refs):
                lanes = pl.ds(pl.multiple_of(turn * own, own), own)
                place = (d * ways + w) * own
                ref[:, place : place + own] = own_ref[w, blocks + s + fused, :, lanes].astype(full)
        start = turn * feats
        lanes = pl.ds(pl.multiple_of(start % wide, feats), feats)
        for w in range(ways):

            @pl.when(start // wide == w)
            def _(w=w, d=d, lanes=lanes):
                out_ref[:, d * feats : (d + 1) * feats] = halves[w][0, 0, :, lanes].astype(full)


def assemble(total, w_up, fused):
    ways, dp = split_ways(), lax.axis_size("dp")
    blocks, rows, wide = total.shape[1:]
    depth = min(64, rows // ways)
    share = rows // ways // depth

    def half_map(half):
        return lambda i: (i // share, 0 if fused else blocks - 1, half * share + i % share, 0)

    widths = [w_up.shape[1]] + [ways * wide] * 4
    return pl.pallas_call(
        functools.partial(assemble_kernel, ways, dp, int(fused)),
        grid=(rows // depth,),
        out_shape=[jax.ShapeDtypeStruct((rows, n), full) for n in widths],
        in_specs=[pl.BlockSpec((ways, blocks, depth, wide), lambda i: (0, 0, i, 0))]
        + [pl.BlockSpec((1, 1, depth, wide), half_map(half)) for half in range(ways)],
        out_specs=[pl.BlockSpec((depth, n), lambda i: (i, 0)) for n in widths],
        compiler_params=pltpu.CompilerParams(vmem_limit_bytes=48 << 20),
        cost_estimate=pl.CostEstimate(
            flops=0, bytes_accessed=6 * total.size, transcendentals=0
        ),
    )(total, *[total] * ways)


def unturn_kernel(dp, own_ref, out_ref):
    size = out_ref.shape[1] // dp
    for d in range(dp):
        lanes = pl.ds(pl.multiple_of(turn_of(d) * size, size), size)
        out_ref[:, d * size : (d + 1) * size] = own_ref[:, lanes].astype(full)


def unturn(total):
    rows, columns = total.shape
    depth = 256
    return pl.pallas_call(
        functools.partial(unturn_kernel, lax.axis_size("dp")),
        grid=(rows // depth,),
        out_shape=jax.ShapeDtypeStruct((rows, columns), full),
        in_specs=[pl.BlockSpec((depth, columns), lambda i: (i, 0))],
        out_specs=pl.BlockSpec((depth, columns), lambda i: (i, 0)),
        cost_estimate=pl.CostEstimate(
            flops=0, bytes_accessed=6 * total.size, transcendentals=0
        ),
    )(total)


def stream_kernel(stored_ref, mix_ref, deviations_ref, moments_ref):
    means, spreads = [], []
    for s in range(STREAMS):
        total = mix_ref[s * HIST : s * HIST + 1, :] * stored_ref[0].astype(full)
        for j in range(1, HIST):
            row = s * HIST + j
            total = total + mix_ref[row : row + 1, :] * stored_ref[j].astype(full)
        mean = jnp.mean(total, axis=0, keepdims=True)
        off = total - mean
        deviations_ref[0, s] = off.astype(low)
        means.append(mean)
        spreads.append(jnp.sum(off * off, axis=0, keepdims=True))
    moments_ref[0] = jnp.concatenate(means + spreads, axis=0)


def mix_streams(stored, mix_all, places):
    _, piece, tokens = stored.shape
    group = tokens // places
    wide = min(512, group)
    per_place = group // wide
    return pl.pallas_call(
        stream_kernel,
        grid=(tokens // wide,),
        out_shape=[
            jax.ShapeDtypeStruct((places, STREAMS, piece, group), low),
            jax.ShapeDtypeStruct((places, 2 * STREAMS, group), full),
        ],
        in_specs=[
            pl.BlockSpec((HIST, piece, wide), lambda i: (0, 0, i)),
            pl.BlockSpec((mix_all.shape[0], wide), lambda i: (0, i)),
        ],
        out_specs=[
            pl.BlockSpec((1, STREAMS, piece, wide), lambda i: (i // per_place, 0, 0, i % per_place)),
            pl.BlockSpec((1, 2 * STREAMS, wide), lambda i: (i // per_place, 0, i % per_place)),
        ],
        compiler_params=pltpu.CompilerParams(vmem_limit_bytes=40 << 20),
        cost_estimate=pl.CostEstimate(
            flops=2 * STREAMS * HIST * piece * tokens,
            bytes_accessed=4 * HIST * piece * tokens,
            transcendentals=0,
        ),
    )(stored, mix_all)


def history_kernel(split_ref, stored_ref, mix_ref, grad_ref, parts_ref):
    streams = [split_ref[s, 0].astype(full) for s in range(STREAMS)]
    rows = [None] * (STREAMS * HIST)
    for j in range(HIST):
        layer = stored_ref[j].astype(full)
        total = mix_ref[j : j + 1, :] * streams[0]
        for s in range(1, STREAMS):
            total = total + mix_ref[s * HIST + j : s * HIST + j + 1, :] * streams[s]
        grad_ref[j] = total
        for s in range(STREAMS):
            rows[s * HIST + j] = jnp.sum(streams[s] * layer, axis=0, keepdims=True)
    parts = jnp.concatenate(rows, axis=0)
    block = parts_ref.shape[2]
    for b in range(parts_ref.shape[0]):
        parts_ref[b] = parts[:, b * block : (b + 1) * block]


def history_gradients(split, stored, mix_all, block):
    _, places, piece, group = split.shape
    n_mix, tokens = mix_all.shape
    wide = min(512, group)
    per_place = group // wide
    return pl.pallas_call(
        history_kernel,
        grid=(tokens // wide,),
        out_shape=[
            jax.ShapeDtypeStruct((HIST, piece, tokens), full),
            jax.ShapeDtypeStruct((tokens // block, n_mix, block), full),
        ],
        in_specs=[
            pl.BlockSpec((STREAMS, 1, piece, wide), lambda i: (0, i // per_place, 0, i % per_place)),
            pl.BlockSpec((HIST, piece, wide), lambda i: (0, 0, i)),
            pl.BlockSpec((n_mix, wide), lambda i: (0, i)),
        ],
        out_specs=[
            pl.BlockSpec((HIST, piece, wide), lambda i: (0, 0, i)),
            pl.BlockSpec((wide // block, n_mix, block), lambda i: (i, 0, 0)),
        ],
        compiler_params=pltpu.CompilerParams(vmem_limit_bytes=40 << 20),
        cost_estimate=pl.CostEstimate(
            flops=4 * STREAMS * HIST * piece * tokens,
            bytes_accessed=6 * HIST * piece * tokens + 2 * split.size,
            transcendentals=0,
        ),
    )(split, stored, mix_all)


def to_owner(values_in):
    dp, hid, ways = lax.axis_size("dp"), lax.axis_size("hid"), split_ways()
    index = lax.axis_index("dp") * ways + lax.axis_index("hid") % ways
    mine = lax.dynamic_index_in_dim(values_in, index, 1, keepdims=False)
    pairs = [
        (d * hid + t * ways + w, (t * dp + d) * ways + w)
        for d in range(dp)
        for t in range(hid // ways)
        for w in range(ways)
    ]
    return lax.ppermute(mine, ("dp", "hid"), pairs)


def rotate(values_in, cosine, sine):
    half = cosine.shape[1]
    front, back = values_in[:, :half], values_in[:, half : 2 * half]
    return jnp.concatenate(
        [
            front * cosine - back * sine,
            back * cosine + front * sine,
            values_in[:, 2 * half :],
        ],
        axis=1,
    )


def local(
    history,
    mix,
    segment_ids,
    norm_gains,
    w_query,
    w_key,
    w_value,
    w_out,
    w_up,
    w_down,
    w_mixer,
    mixer_out,
    mix_static,
    out_cotangent,
    mix_cotangent,
):
    dp, hid, ways = lax.axis_size("dp"), lax.axis_size("hid"), split_ways()
    places = hid // ways
    my_hid = lax.axis_index("hid")
    place, way = my_hid // ways, my_hid % ways
    block = segment_ids.shape[0]
    total_tokens = block * dp * hid
    row = total_tokens // dp
    group = total_tokens // places
    rows = group // row
    piece = history.shape[2]
    mine = piece * places
    feats = piece * hid
    width = feats * dp
    heads = HEADS // dp // ways
    n_mix = mix.shape[1]
    n_cot = mix_cotangent.shape[1]

    def by_place(values_in):
        return jnp.stack(
            [values_in[..., p * group : (p + 1) * group] for p in range(places)], axis=0
        )

    stored = history.swapaxes(1, 2)
    mix_all = gather_all(mix.T)
    fused = dp == 4 and ways == 2 and rows == 1
    if fused:
        gain_columns = norm_gains.T.astype(full)[:, :, None]
        mix_all, gain_columns = lax.optimization_barrier((mix_all, gain_columns))
    deviations, moments = mix_streams(stored, mix_all, places)

    table = jnp.concatenate([mix_cotangent.T, segment_ids.astype(full)[None]], axis=0)
    table = lax.dynamic_slice_in_dim(gather_all(table), place * group, group, 1)
    cot_t = table[:n_cot]
    ids = table[-1].reshape(rows, row)

    there = jnp.arange(row, dtype=jnp.int32)
    same_doc = ids[:, :, None] == ids[:, None, :]
    doc_start = jnp.min(jnp.where(same_doc, there[None, None], row), axis=2)
    position = (there[None] - doc_start).astype(full).reshape(group)
    visible = same_doc & (there[None, None] <= there[None, :, None])
    frequency = rope_base ** (-jnp.arange(ROT // 2, dtype=full) * 2.0 / ROT)
    angle = frequency[:, None] * position[None, :]
    cosine, sine = jnp.cos(angle)[None], jnp.sin(angle)[None]

    def own_rows(values_in):
        parts = values_in.reshape((places, ways, piece) + values_in.shape[1:])
        part = lax.dynamic_index_in_dim(parts, way, 1, keepdims=False)
        return part.reshape((mine,) + values_in.shape[1:])

    def all_rows(values_in):
        parts = values_in.reshape((places, piece) + values_in.shape[1:])
        return gather_ways(parts, 1).reshape((feats,) + values_in.shape[1:])

    own_gains = own_rows(norm_gains).astype(full)
    gains = [own_gains[:, s][:, None] for s in range(STREAMS)]
    all_gains = norm_gains.astype(full)

    def project(weight, left):
        columns = weight.shape[1] // dp // ways

        def make(index):
            start = (index * ways + way) * columns
            part = lax.dynamic_slice_in_dim(weight, start, columns, 1)
            return contract(part, left, 0, 0)

        return scatter_dp(make)

    def way_columns(weight):
        if ways == 1:
            return weight
        size = weight.shape[1] // dp // ways
        parts = [weight[:, i * size : (i + 1) * size] for i in range(dp * ways)]
        pairs = zip(parts[::2], parts[1::2])
        return jnp.concatenate([jnp.where(way == 0, a, b) for a, b in pairs], axis=1)

    def way_rows(weight):
        size = weight.shape[0] // ways
        return lax.dynamic_slice_in_dim(weight, way * size, size, 0)

    def by_head(values_in):
        return values_in.reshape(heads, HEAD, group)

    def turned(weight, stride, offset, size):
        starts = [turn_source(turn) * stride + offset for turn in range(dp)]
        parts = [lax.dynamic_slice_in_dim(weight, start, size, 1) for start in starts]
        return jnp.concatenate(parts, axis=1)

    n_head = heads * HEAD
    n_units = w_up.shape[1] // dp // ways
    if fused:
        normed, deviations, residual, own_shifts, inv_scales, active, slope, products, *ends = (
            forward_projections(
                deviations,
                moments,
                gain_columns,
                w_query,
                w_key,
                w_value,
                w_up,
                by_place(out_cotangent.T),
            )
        )
        turned_heads, turned_up, upstream = ends
        upstream = upstream.reshape(mine, group)
        normed_all = normed
        normed = [normed[s] for s in range(STREAMS)]
        products = products.reshape(3, heads, HEAD, group)
        turned_weights = [turned_heads[s] for s in range(3)] + [turned_up]
    else:
        moments = exchange(moments)
        deviations = exchange(deviations)
        deviations = [deviations[:, s] for s in range(STREAMS)]
        def join_moments(mean_parts, dev_parts, size):
            mean = jnp.mean(mean_parts, axis=0)
            spread = size * jnp.sum(jnp.square(mean_parts - mean), axis=0)
            return mean, jnp.sum(dev_parts, axis=0) + spread

        block_means = moments[:, :STREAMS]
        joined = join_moments(block_means, moments[:, STREAMS:], piece)
        joined = gather_dp(gather_ways(jnp.concatenate(joined, axis=0), 0))
        joined = joined.reshape((dp * ways,) + joined.shape[2:])
        means, variance = join_moments(joined[:, :STREAMS], joined[:, STREAMS:], mine)
        inv_scales = lax.rsqrt(variance / width + 1e-05)
        all_means = gather_ways(block_means, 1)

        def unit(values_in, block_mean, s):
            return (values_in.astype(full) + (block_mean - means[s])[..., None, :]) * inv_scales[s]

        units = [
            unit(deviations[s], block_means[:, s], s).reshape(mine, group) for s in range(STREAMS)
        ]
        normed = []
        for s in range(STREAMS):
            both = unit(gather_ways(deviations[s], 1), all_means[:, :, s], s).reshape(feats, group)
            normed.append((both * all_gains[:, s][:, None]).astype(low))
        residual = (deviations[3].astype(full) + block_means[:, 3][:, None]).reshape(mine, group)
        products = [
            by_head(project(w, normed[s])) for s, w in enumerate((w_query, w_key, w_value))
        ]
        hidden = project(w_up, normed[3])
        active, hidden_pull = jax.vjp(gelu_exact, hidden)
        active = active.astype(low)
        (slope,) = hidden_pull(jnp.ones_like(hidden))
        turned_weights = [
            turned(w, ways * n_head, way * n_head, n_head) for w in (w_query, w_key, w_value)
        ] + [turned(w_up, ways * n_units, way * n_units, n_units)]

    def by_row(values_in):
        if rows == 1:
            return values_in
        return (
            values_in.reshape(heads, HEAD, rows, row)
            .transpose(0, 2, 1, 3)
            .reshape(heads * rows, HEAD, row)
        )

    def from_row(values_in):
        if rows == 1:
            return values_in
        return (
            values_in.reshape(heads, rows, HEAD, row)
            .transpose(0, 2, 1, 3)
            .reshape(heads, HEAD, group)
        )

    if fused:
        starts = doc_start.reshape(1, group)
        turned_values, attended, tops = attend(products, cosine[0], sine[0], starts)
        attended = attended.reshape(n_head, group)
    else:
        queries = rotate(products[0], cosine, sine).astype(low)
        keys = rotate(products[1], cosine, sine).astype(low)
        values = products[2].astype(low)
        q_rows, k_rows, v_rows = by_row(queries), by_row(keys), by_row(values)
        score_scale = 1.0 / math.sqrt(HEAD)
        scores = batched(q_rows, k_rows, 1, 1) * score_scale
        mask = jnp.broadcast_to(visible[None], (heads, rows, row, row)).reshape(scores.shape)
        scores = jnp.where(mask, scores, -1e30)
        probs = jax.nn.softmax(scores, axis=-1)
        probs_low = probs.astype(low)
        attended = from_row(batched(v_rows, probs_low, 2, 2).astype(low)).reshape(heads * HEAD, group)

        cotangent, attended = lax.optimization_barrier((out_cotangent, attended))
        upstream = exchange(by_place(cotangent.T)).reshape(mine, group)

    mixer_rows = own_rows(w_mixer)
    if fused:
        output, output_rounded, sums, *turned_ends = add_branches(
            places, attended, active, residual, mixer_rows, w_out, w_down
        )
        sums = jnp.concatenate([sums[: mixer_rows.shape[1]], sums[-1:]], axis=0)
        turned_weights += turned_ends
    else:
        out_rows, down_rows = way_rows(w_out), way_rows(w_down)
        turned_weights += [turned(out_rows, feats, 0, feats), turned(down_rows, feats, 0, feats)]
        def make_out(index):
            start = index * feats
            left = lax.dynamic_slice_in_dim(out_rows, start, feats, 1)
            other = lax.dynamic_slice_in_dim(down_rows, start, feats, 1)
            return contract(left, attended, 0, 0) + contract(other, active, 0, 0)

        branches = scatter_dp(make_out).reshape(places, ways, piece, group)
        kept = lax.dynamic_index_in_dim(branches, way, 1, keepdims=False)
        if ways == 2:
            given = lax.dynamic_index_in_dim(branches, 1 - way, 1, keepdims=False).astype(low)
            kept = kept + hid_swap(given, 1).astype(full)
        output = residual + kept.reshape(mine, group)
        output, upstream, turned_weights = lax.optimization_barrier(
            (output, upstream, turned_weights)
        )
        output_rounded = output.astype(low)
        square = jnp.sum(output * output, axis=0, keepdims=True)
        mixer_part = contract(mixer_rows, output_rounded, 0, 0)
        sums = sum_features(jnp.concatenate([mixer_part, square], axis=0))
    upstream = upstream.astype(full)

    block_output = exchange(output_rounded.reshape(places, piece, group))

    inv_rms = lax.rsqrt(sums[-1] / width + 1e-06)
    inner_raw = sums[:-1]
    inner_pre = inner_raw * inv_rms
    inner_act, inner_pull = jax.vjp(gelu_exact, inner_pre)
    raw_mix = contract_high(mixer_out, inner_act, 0, 0)
    column = jnp.stack(
        [
            jnp.sum(raw_mix, axis=1),
            jnp.sum(raw_mix * raw_mix, axis=1),
            jnp.sum(cot_t, axis=1),
            jnp.sum(cot_t * raw_mix, axis=1),
        ],
        axis=0,
    )
    act_total = jnp.sum(inner_act, axis=1)
    act_cot = contract_high(inner_act, cot_t, 1, 1)
    act_raw = contract_high(inner_act, raw_mix, 1, 1)
    n_inner = act_total.shape[0]
    flat = sum_tokens(
        jnp.concatenate([column.reshape(-1), act_total, act_cot.reshape(-1), act_raw.reshape(-1)])
    )
    sum_raw, sum_square, sum_grad, sum_grad_raw = flat[: 4 * n_cot].reshape(4, n_cot)
    start = 4 * n_cot
    act_total = flat[start : start + n_inner]
    start += n_inner
    act_cot = flat[start : start + n_inner * n_cot].reshape(n_inner, n_cot)
    start += n_inner * n_cot
    act_raw = flat[start:].reshape(n_inner, n_cot)
    average = sum_raw / total_tokens
    variance_mix = sum_square / total_tokens - average * average
    inv_spread = lax.rsqrt(variance_mix + 1e-05)
    unit_mix = (raw_mix - average[:, None]) * inv_spread[:, None]
    mix_next = mix_static[:, None] + unit_mix
    mix_next = to_owner(mix_next.reshape(n_cot, dp * ways, block)).T
    mean_grad = sum_grad / total_tokens
    sum_grad_unit = inv_spread * (sum_grad_raw - average * sum_grad)
    mean_grad_unit = sum_grad_unit / total_tokens
    raw_grad = inv_spread[:, None] * (
        cot_t - mean_grad[:, None] - unit_mix * mean_grad_unit[:, None]
    )
    act_unit = inv_spread[None, :] * (act_raw - act_total[:, None] * average[None, :])
    mixer_out_grad = inv_spread[None, :] * (
        act_cot - act_total[:, None] * mean_grad[None, :] - act_unit * mean_grad_unit[None, :]
    )
    act_grad = contract_high(mixer_out, raw_grad, 1, 0)
    inner_low = inner_pull(act_grad)[0].astype(low)
    scaled = (output * inv_rms).astype(low)
    mixer_grad_part = contract(inner_low, scaled, 1, 1)
    scaled_grad = contract(mixer_rows, inner_low, 1, 0)
    along = jnp.sum(inner_low.astype(full) * inner_raw, axis=0) / width
    output_grad = upstream + inv_rms * scaled_grad - output * (inv_rms * inv_rms * inv_rms) * along
    if fused:
        near = output_grad.astype(low)
        far = outer_shift(near, 1)
        beside = hid_swap(near, 1)
        far_beside = outer_shift(beside, 1)

        def interleave(values_in, other):
            values_in, other = [v.reshape(places, piece, group) for v in (values_in, other)]
            return ordered(way == 0, values_in, other, 1).reshape(feats, group)

        output_lows = gather_cores([interleave(near, beside), interleave(far, far_beside)])
    else:
        output_lows = gather_turns(all_rows(output_grad.astype(low)))

    output_low = jnp.concatenate(output_lows, axis=0)

    hidden_low = (contract(turned_weights[5], output_low, 1, 0) * slope).astype(low)

    attended_grad = contract(turned_weights[4], output_low, 1, 0).astype(low)
    if fused:
        lows_mine = attend_back(
            turned_values, by_head(attended_grad), cosine[0], sine[0], starts, tops
        ).reshape(3 * n_head, group)
    else:
        a_rows = by_row(by_head(attended_grad))
        prob_grad = batched(a_rows, v_rows, 1, 1)
        row_total = jnp.sum(probs * prob_grad, axis=-1, keepdims=True)
        score_grad = (probs * (prob_grad - row_total)).astype(low)
        query_grad = from_row(batched(k_rows, score_grad, 2, 2) * score_scale)
        key_grad = from_row(batched(q_rows, score_grad, 2, 1) * score_scale)
        value_grad = from_row(batched(a_rows, probs_low, 2, 1))
        query_low = rotate(query_grad, cosine, -sine).astype(low).reshape(heads * HEAD, group)
        key_low = rotate(key_grad, cosine, -sine).astype(low).reshape(heads * HEAD, group)
        value_low = value_grad.astype(low).reshape(heads * HEAD, group)

        lows_mine = jnp.concatenate([query_low, key_low, value_low], axis=0)
    active_kept, hidden_low, lows_mine = lax.optimization_barrier((active, hidden_low, lows_mine))
    hidden_lows, lows = gather_outer(hidden_low), gather_outer(lows_mine)
    blocks = [(active.shape[0], [(0, 0, 1, 0, width)])]
    branch_sum = chain_sum([active_kept, output_low], blocks, 0)
    branch_sum, block_output, hidden_lows, lows = lax.optimization_barrier(
        (branch_sum, block_output, hidden_lows, lows)
    )
    block_output = block_output.transpose(1, 0, 2).reshape(piece, total_tokens).T

    if fused:
        operands = [hidden_lows[0], hidden_lows[1], lows[0], lows[1], output_low, attended]
        operands += [normed_all, turned_heads, turned_up, deviations]
        operands.append(output_grad.reshape(places, piece, group))
        tables = [
            own_shifts,
            inv_scales,
            gain_columns,
        ]
        late_sum, split, gain_parts = late_sums(operands, tables, 1)
        gain_parts = gain_parts.reshape(STREAMS, mine)
        history_grad, mix_parts = history_gradients(split, stored, mix_all, block)
    else:
        hidden_lows, lows = gather_cores(hidden_lows), gather_cores(lows)

        normed_grads, alongs, rights = [], [], []
        for s in range(STREAMS):
            if s < 3:
                right = jnp.concatenate([v[s * n_head : (s + 1) * n_head] for v in lows], axis=0)
            else:
                right = jnp.concatenate(hidden_lows, axis=0)
            rights.append(right)
            part = contract(turned_weights[s], right, 1, 0)
            alongs.append(jnp.sum(part * all_gains[:, s][:, None], axis=0))
            alongs.append(jnp.sum(part * normed[s].astype(full), axis=0))
            part = part.reshape(places, ways, piece, group)
            kept = lax.dynamic_index_in_dim(part, way, 1, keepdims=False)
            if ways == 2:
                given = lax.dynamic_index_in_dim(part, 1 - way, 1, keepdims=False).astype(low)
                kept = kept + hid_swap(given, 1).astype(full)
            normed_grads.append(kept.reshape(mine, group))
        weighted = [normed_grads[s] * gains[s] for s in range(STREAMS)]
        means_back = sum_features(jnp.stack(alongs, axis=0)) / width
        gain_parts = [jnp.sum(g * u, axis=1) for g, u in zip(normed_grads, units)]
        stream_grads = [
            (weighted[s] - means_back[2 * s] - units[s] * means_back[2 * s + 1]) * inv_scales[s]
            for s in range(STREAMS)
        ]
        stream_grads[3] = stream_grads[3] + output_grad
        gain_parts = jnp.stack(gain_parts, axis=0)

        split = jnp.stack([v.astype(low).reshape(places, piece, group) for v in stream_grads], axis=1)
        attended, split = lax.optimization_barrier((attended, split))
        split = exchange(split)
        wide = w_query.shape[1] // ways
        operands = [rights[3]] + rights[:3] + [output_low, normed[3]] + normed[:3] + [attended]
        blocks = [(feats, [(5, 0, 0, i, wide)]) for i in range(0, rights[3].shape[0], wide)]
        blocks += [(feats, [(6 + s, 0, 1 + s, 0, wide)]) for s in range(3)]
        blocks += [(n_head, [(9, 0, 4, i, wide)]) for i in range(0, width, wide)]
        late_sum = chain_sums(operands, blocks, 1).reshape(ways, -1, feats, wide)
        split = jnp.concatenate([split[p] for p in range(places)], axis=-1).astype(full)
        mix_layers = mix_all.reshape(STREAMS, HIST, total_tokens)
        history_grad = sum(mix_layers[s][:, None] * split[s][None] for s in range(STREAMS))
        mix_parts = jnp.concatenate(
            [jnp.sum(split[s][None] * stored.astype(full), axis=1) for s in range(STREAMS)], axis=0
        )
        mix_parts = mix_parts.reshape(n_mix, dp * hid, block).transpose(1, 0, 2)

    history_grad = history_grad.swapaxes(1, 2)
    smalls = jnp.concatenate([mixer_grad_part, gain_parts], axis=0)
    late_sum, mix_parts, smalls = lax.optimization_barrier((late_sum, mix_parts, smalls))
    mix_parts = lax.all_to_all(mix_parts, ("dp", "hid"), split_axis=0, concat_axis=0, tiled=True)
    late_grads = assemble(late_sum, w_up, fused)
    w_down_grad = unturn(branch_sum.reshape(w_down.shape))
    bit = ways
    while bit < hid:
        smalls = smalls + hid_swap(smalls, bit)
        if bit == ways:
            late_grads, smalls = lax.optimization_barrier((late_grads, smalls))
        else:
            w_down_grad, smalls = lax.optimization_barrier((w_down_grad, smalls))
        bit *= 2
    w_up_grad, w_query_grad, w_key_grad, w_value_grad, w_out_grad = late_grads
    smalls = gather_ways(smalls.reshape(-1, places, piece), 2).reshape(-1, feats)
    w_mixer_grad = smalls[:n_inner].T
    norm_gains_grad = smalls[n_inner:].T
    mix_grad = jnp.sum(mix_parts, axis=0).T

    return (
        block_output,
        mix_next,
        history_grad,
        mix_grad,
        norm_gains_grad,
        w_query_grad,
        w_key_grad,
        w_value_grad,
        w_out_grad,
        w_up_grad,
        w_down_grad,
        w_mixer_grad,
        mixer_out_grad,
        sum_grad,
    )


def solution(mesh):
    everywhere = ("dp", "hid")
    placed = (
        P(None, None, everywhere),
        P(everywhere, None),
        P(everywhere),
        P("dp", None),
        P("dp", None),
        P("dp", None),
        P("dp", None),
        P("dp", None),
        P("dp", None),
        P("dp", None),
        P("dp", None),
        P(),
        P(),
        P(None, everywhere),
        P(everywhere, None),
    )
    return jax.shard_map(
        local,
        mesh=mesh,
        in_specs=placed,
        out_specs=(
            P(None, everywhere),
            P(everywhere, None),
            P(None, None, everywhere),
            P(everywhere, None),
            P("dp", None),
            P("dp", None),
            P("dp", None),
            P("dp", None),
            P("dp", None),
            P("dp", None),
            P("dp", None),
            P("dp", None),
            P(),
            P(),
        ),
        check_vma=False,
    )
```
